32 devices in a mesh: fsdp: 8 (over z, x), dp: 4 (over y, core).
Axes of the slice: x: 2, y: 2, z: 4, core: 2. Of those that a mesh axis runs over, the one named last changes fastest.
Arguments:
- inputs: bfloat16 [18464, 1024], P(('fsdp', 'dp')), may hold values from -6 to 6
- cotangent: bfloat16 [18464, 1024], P(('fsdp', 'dp')), may hold values from -6 to 6
- norm1_gain: float32 [1024], P('fsdp'), may hold values from 0.08 to 2.5
- norm1_bias: float32 [1024], P('fsdp'), may hold values from -1.2 to 1.2
- qkv_weight: float32 [1024, 3072], P('fsdp'), may hold values from -0.1875 to 0.1875
- qv_bias: float32 [2048], P('fsdp'), may hold values from -3 to 3
- out_weight: float32 [1024, 1024], P('fsdp'), may hold values from -3 to 3
- out_bias: float32 [1024], P('fsdp'), may hold values from -3 to 3
- norm2_gain: float32 [1024], P('fsdp'), may hold values from 0.08 to 2.5
- norm2_bias: float32 [1024], P('fsdp'), may hold values from -1.2 to 1.2
- in_weight: float32 [1024, 4096], P('fsdp'), may hold values from -0.1875 to 0.1875
- in_bias: float32 [4096], P('fsdp'), may hold values from -3 to 3
- down_weight: float32 [4096, 1024], P('fsdp'), may hold values from -0.09375 to 0.09375
- down_bias: float32 [1024], P('fsdp'), may hold values from -3 to 3
- qkv_rows: float32 [1024], P('fsdp'), may hold values from 0.34375 to 196.875
- qkv_cols: float32 [3072], replicated, may hold values from 0.9375 to 93.75
- out_rows: float32 [1024], P('fsdp'), may hold values from 0.003125 to 2.8125
- out_cols: float32 [1024], replicated, may hold values from 0.009375 to 0.9375
- in_rows: float32 [1024], P('fsdp'), may hold values from 0.05625 to 31.5625
- in_cols: float32 [4096], replicated, may hold values from 0.15625 to 15.625
- down_rows: float32 [4096], P('fsdp'), may hold values from 0.20833333 to 187.5
- down_cols: float32 [1024], replicated, may hold values from 0.625 to 62.5
- norm1_gain_moment: float32 [1024], P('fsdp'), may hold values from 0.104166667 to 281.25
- norm1_bias_moment: float32 [1024], P('fsdp'), may hold values from 0.104166667 to 281.25
- qv_bias_moment: float32 [2048], P('fsdp'), may hold values from 0.104166667 to 281.25
- out_bias_moment: float32 [1024], P('fsdp'), may hold values from 0.104166667 to 281.25
- norm2_gain_moment: float32 [1024], P('fsdp'), may hold values from 0.104166667 to 281.25
- norm2_bias_moment: float32 [1024], P('fsdp'), may hold values from 0.104166667 to 281.25
- in_bias_moment: float32 [4096], P('fsdp'), may hold values from 0.104166667 to 281.25
- down_bias_moment: float32 [1024], P('fsdp'), may hold values from 0.104166667 to 281.25
Outputs:
- output: bfloat16 [18464, 1024], P(('fsdp', 'dp'))
- input_grad: bfloat16 [18464, 1024], P(('fsdp', 'dp'))
- grad_norm1_gain: float32 [1024], P('fsdp')
- grad_norm1_bias: float32 [1024], P('fsdp')
- grad_qkv_weight: float32 [1024, 3072], P('fsdp')
- grad_qv_bias: float32 [2048], P('fsdp')
- grad_out_weight: float32 [1024, 1024], P('fsdp')
- grad_out_bias: float32 [1024], P('fsdp')
- grad_norm2_gain: float32 [1024], P('fsdp')
- grad_norm2_bias: float32 [1024], P('fsdp')
- grad_in_weight: float32 [1024, 4096], P('fsdp')
- grad_in_bias: float32 [4096], P('fsdp')
- grad_down_weight: float32 [4096, 1024], P('fsdp')
- grad_down_bias: float32 [1024], P('fsdp')
- new_qkv_rows: float32 [1024], P('fsdp')
- new_qkv_cols: float32 [3072], replicated
- new_out_rows: float32 [1024], P('fsdp')
- new_out_cols: float32 [1024], replicated
- new_in_rows: float32 [1024], P('fsdp')
- new_in_cols: float32 [4096], replicated
- new_down_rows: float32 [4096], P('fsdp')
- new_down_cols: float32 [1024], replicated
- new_norm1_gain_moment: float32 [1024], P('fsdp')
- new_norm1_bias_moment: float32 [1024], P('fsdp')
- new_qv_bias_moment: float32 [2048], P('fsdp')
- new_out_bias_moment: float32 [1024], P('fsdp')
- new_norm2_gain_moment: float32 [1024], P('fsdp')
- new_norm2_bias_moment: float32 [1024], P('fsdp')
- new_in_bias_moment: float32 [4096], P('fsdp')
- new_down_bias_moment: float32 [1024], P('fsdp')
- new_norm1_gain: float32 [1024], P('fsdp')
- new_norm1_bias: float32 [1024], P('fsdp')
- new_qkv_weight: float32 [1024, 3072], P('fsdp')
- new_qv_bias: float32 [2048], P('fsdp')
- new_out_weight: float32 [1024, 1024], P('fsdp')
- new_out_bias: float32 [1024], P('fsdp')
- new_norm2_gain: float32 [1024], P('fsdp')
- new_norm2_bias: float32 [1024], P('fsdp')
- new_in_weight: float32 [1024, 4096], P('fsdp')
- new_in_bias: float32 [4096], P('fsdp')
- new_down_weight: float32 [4096, 1024], P('fsdp')
- new_down_bias: float32 [1024], P('fsdp')
- clip_factors: float32 [12], replicated
The draws below stay inside these ranges and needn't reach their ends.
All inputs are finite; a program needn't handle non-finite values.
Results may differ from the reference program's by a relative error of at most 0.01.
The reference program's roundings to bfloat16 on the way count: a program that leaves them out, or rounds other values in their place, can miss the bound.
Values may be sent and summed in bfloat16 or wider, within the bound.
No kernel may reach another device: no remote copies, remote signals or barrier semaphores. Data moves between devices by JAX's collectives and lax.ppermute only.
A program may use at most 256 MiB of HBM per device.

```python
import math
import jax
import jax.numpy as jnp
from jax import lax

D = 1024
HEADS = 16
HEAD_DIM = 64
FF = 4096
SEQ = 577
IMAGES = 32
TOKENS = 18464


def ramped(key, count, lower, upper):
    position = jnp.arange(count, dtype=jnp.float32) / float(max(count - 1, 1))
    noise = jax.random.uniform(key, (count,), jnp.float32, math.log(lower), math.log(upper))
    return jnp.exp(noise + position * math.log(9.0)) / 3.0


def gain_profile(key, count):
    position = jnp.arange(count, dtype=jnp.float32) / float(max(count - 1, 1))
    flipped = jax.random.randint(jax.random.fold_in(key, 1), (), 0, 2)
    along = jnp.where(flipped == 1, 1.0 - position, position)
    rough = jnp.exp(jax.random.uniform(jax.random.fold_in(key, 2), (count,), jnp.float32, math.log(0.8), math.log(1.25)))
    return jnp.exp(math.log(0.1) + along * math.log(20.0)) * rough


def row_state(key, gains, level):
    noise = jnp.exp(jax.random.uniform(key, gains.shape, jnp.float32, math.log(0.5), math.log(2.0)))
    return noise * level * (gains * gains + 0.04)


def draw_norm1_gain(key, part):
    return gain_profile(jax.random.fold_in(key, 41), D)


def draw_norm2_gain(key, part):
    return gain_profile(jax.random.fold_in(key, 42), D)


def draw_qkv_rows(key, part):
    gains = gain_profile(jax.random.fold_in(key, 41), D)
    return row_state(jax.random.fold_in(key, 11), gains, 500.0 / IMAGES)


def draw_out_rows(key, part):
    return ramped(jax.random.fold_in(key, 12), D, 0.3 / IMAGES, 30.0 / IMAGES)


def draw_in_rows(key, part):
    gains = gain_profile(jax.random.fold_in(key, 42), D)
    return row_state(jax.random.fold_in(key, 13), gains, 80.0 / IMAGES)


def draw_down_rows(key, part):
    return ramped(jax.random.fold_in(key, 14), FF, 20.0 / IMAGES, 2000.0 / IMAGES)


def draw_norm1_gain_moment(key, part):
    return ramped(jax.random.fold_in(key, 21), D, 10.0 / IMAGES, 3000.0 / IMAGES)


def draw_norm1_bias_moment(key, part):
    return ramped(jax.random.fold_in(key, 22), D, 10.0 / IMAGES, 3000.0 / IMAGES)


def draw_qv_bias_moment(key, part):
    return ramped(jax.random.fold_in(key, 23), 2 * D, 10.0 / IMAGES, 3000.0 / IMAGES)


def draw_out_bias_moment(key, part):
    return ramped(jax.random.fold_in(key, 24), D, 10.0 / IMAGES, 3000.0 / IMAGES)


def draw_norm2_gain_moment(key, part):
    return ramped(jax.random.fold_in(key, 25), D, 10.0 / IMAGES, 3000.0 / IMAGES)


def draw_norm2_bias_moment(key, part):
    return ramped(jax.random.fold_in(key, 26), D, 10.0 / IMAGES, 3000.0 / IMAGES)


def draw_in_bias_moment(key, part):
    return ramped(jax.random.fold_in(key, 27), FF, 10.0 / IMAGES, 3000.0 / IMAGES)


def draw_down_bias_moment(key, part):
    return ramped(jax.random.fold_in(key, 28), D, 10.0 / IMAGES, 3000.0 / IMAGES)


def with_spikes(values, rng, source, target, blocks, factor):
    def block_of(axis_at):
        return (jnp.arange(values.shape[axis_at]) // (values.shape[axis_at] // blocks)).reshape((-1,) + (1,) * (values.ndim - 1 - axis_at))

    first = jax.random.permutation(rng, blocks)[block_of(target)]
    second = (block_of(target) + blocks // 2) % blocks
    return jnp.where((block_of(source) == first) | (block_of(source) == second), factor * values, values)


def level_of(key, dims, split, least, largest):
    def one(axis_at, parts):
        steps = jax.random.uniform(jax.random.fold_in(jax.random.fold_in(key, 6), axis_at), (parts,), jnp.float32, least / len(split), largest / len(split))
        return jnp.repeat(jnp.exp(steps), dims[axis_at] // parts).reshape((-1,) + (1,) * (len(dims) - axis_at - 1))

    gain = one(*split[0])
    for cut in split[1:]:
        gain = gain * one(*cut)
    return gain


def normal_values(rng, dims, scale, most, cuts=(), kind=jnp.bfloat16):
    level = level_of(rng, dims, cuts, -0.22, 0.18) if cuts else 1.0
    values = jax.random.normal(rng, dims, jnp.float32) * scale * level
    return jnp.minimum(jnp.maximum(values, -most), most).astype(kind)


def gaussian_with(rng, dims, scale, most, split, heavy, kind=jnp.bfloat16):
    entries = scale * jax.random.normal(rng, dims, jnp.float32)
    if split:
        entries = entries * level_of(rng, dims, split, -0.22, 0.18)
    return jnp.clip(with_spikes(entries, jax.random.fold_in(rng, 3), *heavy), -most, most).astype(kind)


def setup_inputs(seed: int = 0) -> dict:
    key_of = jax.random.split(jax.random.key(seed), 31)
    inputs = normal_values(key_of[0], (TOKENS, D), 1.0, 6.0, ((0, 32),))
    cotangent = gaussian_with(key_of[1], (TOKENS, D), 1.0, 6.0, ((0, 32),), (0, 1, 32, 2.75))
    norm1_gain = draw_norm1_gain(jax.random.fold_in(key_of[30], 71), 0)
    norm1_bias = normal_values(key_of[3], (D,), 0.2, 1.2, ((0, 8),), jnp.float32)
    qkv_weight = normal_values(key_of[4], (D, 3 * D), D ** -0.5, 0.1875, ((0, 8),), jnp.float32)
    qv_bias = normal_values(key_of[5], (2 * D,), 0.5, 3.0, ((0, 8),), jnp.float32)
    out_weight = normal_values(key_of[6], (D, D), (max(1, D // 256)) ** -0.5, 3.0, ((0, 8),), jnp.float32)
    out_bias = normal_values(key_of[7], (D,), 0.5, 3.0, ((0, 8),), jnp.float32)
    norm2_gain = draw_norm2_gain(jax.random.fold_in(key_of[30], 71), 0)
    norm2_bias = normal_values(key_of[9], (D,), 0.2, 1.2, ((0, 8),), jnp.float32)
    in_weight = normal_values(key_of[10], (D, FF), D ** -0.5, 0.1875, ((0, 8),), jnp.float32)
    in_bias = normal_values(key_of[11], (FF,), 0.5, 3.0, ((0, 8),), jnp.float32)
    down_weight = normal_values(key_of[12], (FF, D), FF ** -0.5, 0.09375, ((0, 8),), jnp.float32)
    down_bias = normal_values(key_of[13], (D,), 0.5, 3.0, ((0, 8),), jnp.float32)
    qkv_rows = draw_qkv_rows(jax.random.fold_in(key_of[30], 71), 0)
    qkv_cols = jnp.clip(jnp.exp(jax.random.uniform(key_of[15], (3 * D,), jnp.float32, math.log(0.9375), math.log(93.75))), 0.9375, 93.75)
    out_rows = draw_out_rows(jax.random.fold_in(key_of[30], 71), 0)
    out_cols = jnp.clip(jnp.exp(jax.random.uniform(key_of[17], (D,), jnp.float32, math.log(0.009375), math.log(0.9375))), 0.009375, 0.9375)
    in_rows = draw_in_rows(jax.random.fold_in(key_of[30], 71), 0)
    in_cols = jnp.clip(jnp.exp(jax.random.uniform(key_of[19], (FF,), jnp.float32, math.log(0.15625), math.log(15.625))), 0.15625, 15.625)
    down_rows = draw_down_rows(jax.random.fold_in(key_of[30], 71), 0)
    down_cols = jnp.clip(jnp.exp(jax.random.uniform(key_of[21], (D,), jnp.float32, math.log(0.625), math.log(62.5))), 0.625, 62.5)
    norm1_gain_moment = draw_norm1_gain_moment(jax.random.fold_in(key_of[30], 71), 0)
    norm1_bias_moment = draw_norm1_bias_moment(jax.random.fold_in(key_of[30], 71), 0)
    qv_bias_moment = draw_qv_bias_moment(jax.random.fold_in(key_of[30], 71), 0)
    out_bias_moment = draw_out_bias_moment(jax.random.fold_in(key_of[30], 71), 0)
    norm2_gain_moment = draw_norm2_gain_moment(jax.random.fold_in(key_of[30], 71), 0)
    norm2_bias_moment = draw_norm2_bias_moment(jax.random.fold_in(key_of[30], 71), 0)
    in_bias_moment = draw_in_bias_moment(jax.random.fold_in(key_of[30], 71), 0)
    down_bias_moment = draw_down_bias_moment(jax.random.fold_in(key_of[30], 71), 0)
    return {"inputs": inputs, "cotangent": cotangent, "norm1_gain": norm1_gain, "norm1_bias": norm1_bias, "qkv_weight": qkv_weight, "qv_bias": qv_bias, "out_weight": out_weight, "out_bias": out_bias, "norm2_gain": norm2_gain, "norm2_bias": norm2_bias, "in_weight": in_weight, "in_bias": in_bias, "down_weight": down_weight, "down_bias": down_bias, "qkv_rows": qkv_rows, "qkv_cols": qkv_cols, "out_rows": out_rows, "out_cols": out_cols, "in_rows": in_rows, "in_cols": in_cols, "down_rows": down_rows, "down_cols": down_cols, "norm1_gain_moment": norm1_gain_moment, "norm1_bias_moment": norm1_bias_moment, "qv_bias_moment": qv_bias_moment, "out_bias_moment": out_bias_moment, "norm2_gain_moment": norm2_gain_moment, "norm2_bias_moment": norm2_bias_moment, "in_bias_moment": in_bias_moment, "down_bias_moment": down_bias_moment}


ln_eps = 1e-06
clip_level = 0.05
step_rate = 4.0

@jax.custom_vjp
def low(v):
    return lax.optimization_barrier(v.astype(jnp.bfloat16)).astype(jnp.float32)

@jax.custom_vjp
def low_back(v):
    return v

def low_keep(v):
    return (low(v), None)

def low_pass(kept, grad):
    return (grad,)

def back_keep(v):
    return (v, None)

def back_low(kept, grad):
    return (low(grad),)
low.defvjp(low_keep, low_pass)
low_back.defvjp(back_keep, back_low)

def norm_rows(values):
    centre = values - lax.optimization_barrier(jnp.mean(values, axis=-1, keepdims=True))
    spread = lax.optimization_barrier(jnp.mean(centre * centre, axis=-1, keepdims=True))
    return centre * lax.rsqrt(spread + ln_eps)

def matmul(left, right):
    return jnp.dot(left, right, precision=lax.Precision.HIGHEST, preferred_element_type=jnp.float32)

def block_forward(params, image_in):
    gain_one, bias_one, weight_qkv, bias_qv, weight_out, bias_out, gain_two, bias_two, weight_in, bias_in, weight_down, bias_down = [low(member) for member in params]
    scale = 1.0 / math.sqrt(HEAD_DIM)
    normed = low(norm_rows(image_in) * gain_one + bias_one)
    qkv = matmul(normed, weight_qkv)
    query = low_back(low(qkv[:, :D] + bias_qv[:D]))
    keys = low_back(low(qkv[:, D:2 * D]))
    values = low_back(low(qkv[:, 2 * D:] + bias_qv[D:]))
    query_h = query.reshape(SEQ, HEADS, HEAD_DIM)
    keys_h = keys.reshape(SEQ, HEADS, HEAD_DIM)
    values_h = values.reshape(SEQ, HEADS, HEAD_DIM)
    scores = low_back(jnp.einsum('qhd,khd->hqk', query_h, keys_h, precision=lax.Precision.HIGHEST) * scale)
    probs = low(jax.nn.softmax(scores, axis=-1))
    attended = jnp.einsum('hqk,khd->qhd', probs, values_h, precision=lax.Precision.HIGHEST).reshape(SEQ, D)
    attended = low_back(low(attended))
    branch_one = low_back(matmul(attended, weight_out) + bias_out)
    middle = image_in + branch_one
    normed_mid = low(norm_rows(middle) * gain_two + bias_two)
    preact = low_back(matmul(normed_mid, weight_in) + bias_in)
    hidden = low(jax.nn.gelu(preact, approximate=False))
    branch_two = low_back(matmul(hidden, weight_down) + bias_down)
    return middle + branch_two

def matrix_update(weight, grad, rows, cols):
    squared = grad * grad
    new_rows = 0.5 * rows + 0.5 * lax.optimization_barrier(jnp.mean(squared, axis=1))
    new_cols = 0.5 * cols + 0.5 * lax.optimization_barrier(jnp.mean(squared, axis=0))
    estimate = new_rows[:, None] * new_cols[None, :] / jnp.mean(new_rows)
    direction = grad * lax.rsqrt(estimate)
    clip_factor = jnp.maximum(1.0, jnp.sqrt(jnp.mean(direction * direction)) / clip_level)
    updated = weight - step_rate * jnp.sqrt(jnp.mean(weight * weight)) * direction / clip_factor
    return (updated, new_rows, new_cols, clip_factor)

def vector_update(weight, grad, moment):
    new_moment = 0.5 * moment + 0.5 * grad * grad
    direction = grad * lax.rsqrt(new_moment)
    clip_factor = jnp.maximum(1.0, jnp.sqrt(jnp.mean(direction * direction)) / clip_level)
    updated = weight - step_rate * jnp.sqrt(jnp.mean(weight * weight)) * direction / clip_factor
    return (updated, new_moment, clip_factor)

def reference(inputs, cotangent, norm1_gain, norm1_bias, qkv_weight, qv_bias, out_weight, out_bias, norm2_gain, norm2_bias, in_weight, in_bias, down_weight, down_bias, qkv_rows, qkv_cols, out_rows, out_cols, in_rows, in_cols, down_rows, down_cols, norm1_gain_moment, norm1_bias_moment, qv_bias_moment, out_bias_moment, norm2_gain_moment, norm2_bias_moment, in_bias_moment, down_bias_moment):
    params = (norm1_gain, norm1_bias, qkv_weight, qv_bias, out_weight, out_bias, norm2_gain, norm2_bias, in_weight, in_bias, down_weight, down_bias)
    images_in = inputs.astype(jnp.float32).reshape(IMAGES, SEQ, D)
    images_cot = cotangent.astype(jnp.float32).reshape(IMAGES, SEQ, D)

    def one_image(running, couple):
        image_in, image_cot = couple
        result, pullback = jax.vjp(block_forward, params, image_in)
        grad_params, grad_in = pullback(image_cot)
        running = tuple((earlier + latest for earlier, latest in zip(running, grad_params)))
        return (running, (result, grad_in))
    initial = tuple((jnp.zeros(member.shape, jnp.float32) for member in params))
    summed, (results, grads_in) = lax.scan(one_image, initial, (images_in, images_cot))
    grads = [member / IMAGES for member in summed]
    output = results.reshape(TOKENS, D).astype(jnp.bfloat16)
    input_grad = grads_in.reshape(TOKENS, D).astype(jnp.bfloat16)
    row_states = [qkv_rows, out_rows, in_rows, down_rows]
    col_states = [qkv_cols, out_cols, in_cols, down_cols]
    moments = [norm1_gain_moment, norm1_bias_moment, qv_bias_moment, out_bias_moment, norm2_gain_moment, norm2_bias_moment, in_bias_moment, down_bias_moment]
    matrix_slots = {2: 0, 4: 1, 8: 2, 10: 3}
    vector_slots = {0: 0, 1: 1, 3: 2, 5: 3, 6: 4, 7: 5, 9: 6, 11: 7}
    new_params = []
    new_rows_all = [None] * 4
    new_cols_all = [None] * 4
    new_moments = [None] * 8
    clips = []
    for number in range(12):
        if number in matrix_slots:
            position = matrix_slots[number]
            updated, new_rows, new_cols, clip_factor = matrix_update(params[number], grads[number], row_states[position], col_states[position])
            new_rows_all[position] = new_rows
            new_cols_all[position] = new_cols
        else:
            position = vector_slots[number]
            updated, new_moment, clip_factor = vector_update(params[number], grads[number], moments[position])
            new_moments[position] = new_moment
        new_params.append(updated)
        clips.append(clip_factor)
    clip_factors = jnp.stack(clips)
    return (output, input_grad, grads[0], grads[1], grads[2], grads[3], grads[4], grads[5], grads[6], grads[7], grads[8], grads[9], grads[10], grads[11], new_rows_all[0], new_cols_all[0], new_rows_all[1], new_cols_all[1], new_rows_all[2], new_cols_all[2], new_rows_all[3], new_cols_all[3], new_moments[0], new_moments[1], new_moments[2], new_moments[3], new_moments[4], new_moments[5], new_moments[6], new_moments[7], new_params[0], new_params[1], new_params[2], new_params[3], new_params[4], new_params[5], new_params[6], new_params[7], new_params[8], new_params[9], new_params[10], new_params[11], clip_factors)
```

```python
import math

import jax
import jax.numpy as jnp
from jax import lax
from jax.experimental import pallas as pl
from jax.experimental.pallas import tpu as pltpu
from jax.sharding import Mesh
from jax.sharding import PartitionSpec as P

HEAD_DIM = 64
SEQ = 577


ln_eps = 1e-06
clip_level = 0.05
step_rate = 4.0


def norm_rows(values):
    centre = values - jnp.mean(values, axis=-1, keepdims=True)
    spread = jnp.mean(centre * centre, axis=-1, keepdims=True)
    return centre * lax.rsqrt(spread + ln_eps)


def norm_affine(values, gain_full, bias_full):
    return norm_rows(values) * gain_full + bias_full


def gelu_exact(values):
    return jax.nn.gelu(values, approximate=False)


def plain_dot(left, right):
    return jnp.dot(left, right, preferred_element_type=jnp.float32)


def lead_dot(left, right):
    return lax.dot_general(
        left, right, (((0,), (0,)), ((), ())), preferred_element_type=jnp.float32
    )


def tail_dot(left, right):
    return lax.dot_general(
        left, right, (((1,), (1,)), ((), ())), preferred_element_type=jnp.float32
    )


def split_heads(rows):
    return rows.reshape(rows.shape[0], rows.shape[1] // HEAD_DIM, HEAD_DIM)


def attend(block):
    query_rows, key_rows, value_rows = block
    length, width = query_rows.shape
    scale = 1.0 / math.sqrt(HEAD_DIM)
    scores = (
        jnp.einsum(
            "qhd,khd->hqk",
            split_heads(query_rows),
            split_heads(key_rows),
            preferred_element_type=jnp.float32,
        )
        * scale
    )
    highest = jnp.max(scores, axis=-1, keepdims=True)
    exponent = jnp.exp(scores - highest)
    summed = jnp.sum(exponent, axis=-1, keepdims=True)
    probs = exponent / summed
    mixed = jnp.einsum(
        "hqk,khd->qhd",
        probs.astype(jnp.bfloat16),
        split_heads(value_rows),
        preferred_element_type=jnp.float32,
    )
    logsum = (highest + jnp.log(summed))[..., 0]
    return (mixed.reshape(length, width).astype(jnp.bfloat16), logsum)


def attend_back(block):
    query_rows, key_rows, value_rows, logsum, grad_rows = block
    length, width = query_rows.shape
    scale = 1.0 / math.sqrt(HEAD_DIM)
    query_h = split_heads(query_rows)
    key_h = split_heads(key_rows)
    value_h = split_heads(value_rows)
    grad_h = split_heads(grad_rows)
    scores = jnp.einsum("qhd,khd->hqk", query_h, key_h, preferred_element_type=jnp.float32) * scale
    probs = jnp.exp(scores - logsum[..., None])
    grad_probs = jnp.einsum("qhd,khd->hqk", grad_h, value_h, preferred_element_type=jnp.float32)
    grad_value = jnp.einsum(
        "hqk,qhd->khd", probs.astype(jnp.bfloat16), grad_h, preferred_element_type=jnp.float32
    )
    inner = jnp.sum(probs * grad_probs, axis=-1, keepdims=True)
    grad_scores = (probs * (grad_probs - inner)).astype(jnp.bfloat16) * jnp.asarray(
        scale, jnp.bfloat16
    )
    grad_query = jnp.einsum("hqk,khd->qhd", grad_scores, key_h, preferred_element_type=jnp.float32)
    grad_key = jnp.einsum("hqk,qhd->khd", grad_scores, query_h, preferred_element_type=jnp.float32)
    joined = jnp.concatenate(
        [
            grad_query.reshape(length, width),
            grad_key.reshape(length, width),
            grad_value.reshape(length, width),
        ],
        axis=1,
    )
    return joined.astype(jnp.bfloat16)


ALL_AXES = ("z", "x", "y", "c")


def swap(value, axis):
    return lax.ppermute(value, axis, [(0, 1), (1, 0)])


def shift(value, axis, step):
    size = lax.axis_size(axis)
    return lax.ppermute(value, axis, [(i, (i + step) % size) for i in range(size)])


def partner(value, axis, step):
    size = lax.axis_size(axis)
    return lax.ppermute(value, axis, [(i, i ^ step) for i in range(size)])


def sum_over(value, axes):
    for axis in axes:
        step = 1
        while step < lax.axis_size(axis):
            value = value + partner(value, axis, step)
            step *= 2
    return value


def gather_small(vector):
    value = vector[None, :]
    for axis in ("x", "z"):
        step = 1
        while step < lax.axis_size(axis):
            other = partner(value, axis, step)
            low = (lax.axis_index(axis) // step) % 2 == 0
            value = jnp.where(
                low,
                jnp.concatenate([value, other], axis=0),
                jnp.concatenate([other, value], axis=0),
            )
            step *= 2
    return value


def gather_pieces(shard):
    half_rows = shard.shape[0] // 2
    core = lax.axis_index("c")
    half = lax.dynamic_slice_in_dim(shard, core * half_rows, half_rows, 0)
    rest = lax.dynamic_slice_in_dim(shard, (1 - core) * half_rows, half_rows, 0)
    along = [half] + [shift(half, "z", k) for k in range(1, lax.axis_size("z"))]
    pieces = []
    for k, near in enumerate(along):
        across = swap(near, "x")
        pieces.append(
            [[near, rest if k == 0 else swap(near, "c")], [across, swap(across, "c")]]
        )
    return pieces


def assemble(pieces, widths):
    count = len(pieces)
    flat = [piece for by_x in pieces for by_core in by_x for piece in by_core]
    half_rows = flat[0].shape[0]
    rows = half_rows * len(flat)
    place = jnp.stack(
        [lax.axis_index("z"), lax.axis_index("x"), lax.axis_index("c")]
    ).astype(jnp.int32)

    def body(place_ref, *refs):
        ins = refs[: len(flat)]
        outs = refs[len(flat) : len(flat) + len(widths)]
        sem = refs[-1]
        copies = []
        for number, ref in enumerate(ins):
            k, dx, h = number // 4, (number // 2) % 2, number % 2
            z = lax.rem(place_ref[0] + (count - k), count)
            x = dx + (1 - 2 * dx) * place_ref[1]
            c = h + (1 - 2 * h) * place_ref[2]
            row = pl.multiple_of(((z * 2 + x) * 2 + c) * half_rows, half_rows)
            at = 0
            for slot, width in enumerate(widths):
                source = ref if len(widths) == 1 else ref.at[:, pl.ds(at, width)]
                copy = pltpu.make_async_copy(
                    source,
                    outs[slot].at[pl.ds(row, half_rows), :],
                    sem.at[number * len(widths) + slot],
                )
                copy.start()
                copies.append(copy)
                at += width
        for copy in copies:
            copy.wait()

    return pl.pallas_call(
        body,
        out_shape=[jax.ShapeDtypeStruct((rows, width), jnp.bfloat16) for width in widths],
        in_specs=[pl.BlockSpec(memory_space=pltpu.SMEM)]
        + [pl.BlockSpec(memory_space=pl.ANY)] * len(flat),
        out_specs=[pl.BlockSpec(memory_space=pl.ANY)] * len(widths),
        scratch_shapes=[pltpu.SemaphoreType.DMA((len(flat) * len(widths),))],
        name="assemble",
    )(place, *flat)


def scatter_sum(term):
    low = lambda value: value.astype(jnp.bfloat16)
    z_size = lax.axis_size("z")
    z, x, core = lax.axis_index("z"), lax.axis_index("x"), lax.axis_index("c")
    half = term.shape[0] // (z_size * 4)
    cut = term.reshape(z_size, 2, 2, half, term.shape[1])
    pick = lax.dynamic_index_in_dim
    got = swap(low(pick(cut, 1 - core, 2, False)), "c")
    kept = pick(cut, core, 2, False) + got
    got = swap(low(pick(kept, 1 - x, 1, False)), "x")
    kept = pick(kept, x, 1, False) + got
    total = pick(kept, z, 0, False)
    for k in range(1, z_size):
        total = total + shift(low(pick(kept, (z + k) % z_size, 0, False)), "z", k)
    if lax.axis_size("y") == 2:
        mine = low(total)
        total = mine.astype(jnp.float32) + swap(mine, "y").astype(jnp.float32)
    else:
        total = lax.psum(total, "y")
    other = swap(total, "c")
    return jnp.where(
        core == 0,
        jnp.concatenate([total, other], axis=0),
        jnp.concatenate([other, total], axis=0),
    )


def on_device(
    inputs,
    cotangent,
    norm1_gain,
    norm1_bias,
    qkv_weight,
    qv_bias,
    out_weight,
    out_bias,
    norm2_gain,
    norm2_bias,
    in_weight,
    in_bias,
    down_weight,
    down_bias,
    qkv_rows,
    qkv_cols,
    out_rows,
    out_cols,
    in_rows,
    in_cols,
    down_rows,
    down_cols,
    norm1_gain_moment,
    norm1_bias_moment,
    qv_bias_moment,
    out_bias_moment,
    norm2_gain_moment,
    norm2_bias_moment,
    in_bias_moment,
    down_bias_moment,
):
    masters = [
        norm1_gain,
        norm1_bias,
        qkv_weight,
        qv_bias,
        out_weight,
        out_bias,
        norm2_gain,
        norm2_bias,
        in_weight,
        in_bias,
        down_weight,
        down_bias,
    ]
    halves = [member.astype(jnp.bfloat16) for member in masters]
    vectors = [0, 1, 3, 5, 6, 7, 9, 11]
    sizes = [masters[number].shape[0] for number in vectors]
    small = gather_small(jnp.concatenate([halves[number] for number in vectors]))
    full = {}
    at = 0
    for number, size in zip(vectors, sizes):
        full[number] = small[:, at : at + size].reshape(-1)
        at += size
    gain_one, bias_one, bias_qv, bias_out = full[0], full[1], full[3], full[5]
    gain_two, bias_two, bias_in, bias_down = full[6], full[7], full[9], full[11]
    (weight_qkv,) = assemble(gather_pieces(halves[2]), [halves[2].shape[1]])
    weight_out, weight_in = assemble(
        gather_pieces(jnp.concatenate([halves[4], halves[8]], axis=1)),
        [halves[4].shape[1], halves[8].shape[1]],
    )
    (weight_down,) = assemble(gather_pieces(halves[10]), [halves[10].shape[1]])
    tokens, width = inputs.shape
    images = tokens // SEQ
    rows_in = inputs.astype(jnp.float32)
    normed_f, pull_one = jax.vjp(
        norm_affine, rows_in, gain_one.astype(jnp.float32), bias_one.astype(jnp.float32)
    )
    normed = normed_f.astype(jnp.bfloat16)
    qkv = plain_dot(normed, weight_qkv)
    bias_pair = bias_qv.astype(jnp.float32)
    query = (qkv[:, :width] + bias_pair[:width]).astype(jnp.bfloat16)
    keys = qkv[:, width : 2 * width].astype(jnp.bfloat16)
    values = (qkv[:, 2 * width :] + bias_pair[width:]).astype(jnp.bfloat16)
    query_img = query.reshape(images, SEQ, width)
    keys_img = keys.reshape(images, SEQ, width)
    values_img = values.reshape(images, SEQ, width)
    attended_img, logsum = lax.map(attend, (query_img, keys_img, values_img))
    attended = attended_img.reshape(tokens, width)
    middle = rows_in + plain_dot(attended, weight_out) + bias_out.astype(jnp.float32)
    normed_mid_f, pull_two = jax.vjp(
        norm_affine, middle, gain_two.astype(jnp.float32), bias_two.astype(jnp.float32)
    )
    normed_mid = normed_mid_f.astype(jnp.bfloat16)
    preact = plain_dot(normed_mid, weight_in) + bias_in.astype(jnp.float32)
    hidden_f, pull_gelu = jax.vjp(gelu_exact, preact)
    hidden = hidden_f.astype(jnp.bfloat16)
    final = middle + plain_dot(hidden, weight_down) + bias_down.astype(jnp.float32)
    output = final.astype(jnp.bfloat16)
    grad_out_rows = cotangent.astype(jnp.float32)
    term_down_weight = lead_dot(hidden, cotangent)
    term_down_bias = jnp.sum(grad_out_rows, axis=0)
    grad_hidden = tail_dot(cotangent, weight_down)
    (grad_preact,) = pull_gelu(grad_hidden)
    grad_preact_low = grad_preact.astype(jnp.bfloat16)
    term_in_weight = lead_dot(normed_mid, grad_preact_low)
    term_in_bias = jnp.sum(grad_preact_low.astype(jnp.float32), axis=0)
    grad_normed_mid = tail_dot(grad_preact_low, weight_in)
    grad_mid_norm, term_gain_two, term_bias_two = pull_two(grad_normed_mid)
    grad_mid = grad_out_rows + grad_mid_norm
    grad_mid_low = grad_mid.astype(jnp.bfloat16)
    term_out_weight = lead_dot(attended, grad_mid_low)
    term_out_bias = jnp.sum(grad_mid_low.astype(jnp.float32), axis=0)
    grad_attended = tail_dot(grad_mid_low, weight_out).astype(jnp.bfloat16)
    grad_qkv_img = lax.map(
        attend_back,
        (query_img, keys_img, values_img, logsum, grad_attended.reshape(images, SEQ, width)),
    )
    grad_qkv = grad_qkv_img.reshape(tokens, 3 * width)
    term_qkv_weight = lead_dot(normed, grad_qkv)
    column_sums = jnp.sum(grad_qkv.astype(jnp.float32), axis=0)
    term_qv_bias = jnp.concatenate([column_sums[:width], column_sums[2 * width :]])
    grad_normed = tail_dot(grad_qkv, weight_qkv)
    grad_in_norm, term_gain_one, term_bias_one = pull_one(grad_normed)
    input_grad = (grad_mid + grad_in_norm).astype(jnp.bfloat16)
    group_size = lax.axis_size("z") * lax.axis_size("x")
    images_all = images * group_size * lax.axis_size("y") * lax.axis_size("c")
    grads = [None] * 12
    for number, term in (
        (10, term_down_weight),
        (8, term_in_weight),
        (4, term_out_weight),
        (2, term_qkv_weight),
    ):
        grads[number] = scatter_sum(term) / images_all
    vector_terms = {
        0: term_gain_one,
        1: term_bias_one,
        3: term_qv_bias,
        5: term_out_bias,
        6: term_gain_two,
        7: term_bias_two,
        9: term_in_bias,
        11: term_down_bias,
    }
    summed = sum_over(
        jnp.concatenate(
            [vector_terms[number].reshape(group_size, -1) for number in vectors], axis=1
        ),
        ("c", "x", "z", "y"),
    )
    here = lax.axis_index("z") * lax.axis_size("x") + lax.axis_index("x")
    mine = lax.dynamic_index_in_dim(summed, here, 0, False) / images_all
    at = 0
    for number, size in zip(vectors, sizes):
        grads[number] = mine[at : at + size]
        at += size
    row_states = [qkv_rows, out_rows, in_rows, down_rows]
    col_states = [qkv_cols, out_cols, in_cols, down_cols]
    moments = [
        norm1_gain_moment,
        norm1_bias_moment,
        qv_bias_moment,
        out_bias_moment,
        norm2_gain_moment,
        norm2_bias_moment,
        in_bias_moment,
        down_bias_moment,
    ]
    matrix_slots = {2: 0, 4: 1, 8: 2, 10: 3}
    vector_slots = {0: 0, 1: 1, 3: 2, 5: 3, 6: 4, 7: 5, 9: 6, 11: 7}
    prepared = [None] * 12
    new_params = [None] * 12
    clips = [None] * 12
    new_cols_all = [None] * 4

    def finish(number, direction, direction_total, weight_total, count):
        clip_factor = jnp.maximum(1.0, jnp.sqrt(direction_total / count) / clip_level)
        rms_weight = jnp.sqrt(weight_total / count)
        clips[number] = clip_factor
        new_params[number] = masters[number] - step_rate * rms_weight * direction / clip_factor

    for number in (10, 8, 4, 2):
        position = matrix_slots[number]
        weight, grad = masters[number], grads[number]
        squared = grad * grad
        new_rows = 0.5 * row_states[position] + 0.5 * jnp.mean(squared, axis=1)
        prepared[number] = new_rows
        pack = jnp.concatenate(
            [
                jnp.sum(squared, axis=0),
                jnp.sum(squared / new_rows[:, None], axis=0),
                jnp.stack([jnp.sum(new_rows), jnp.sum(weight * weight)]),
            ]
        )
        total = sum_over(pack, ("x", "z"))
        rows_total, cols = weight.shape[0] * group_size, weight.shape[1]
        new_cols = 0.5 * col_states[position] + 0.5 * total[:cols] / rows_total
        new_cols_all[position] = new_cols
        mean_rows = total[-2] / rows_total
        direction = grad * lax.rsqrt(new_rows[:, None] * new_cols[None, :] / mean_rows)
        direction_total = mean_rows * jnp.sum(total[cols : 2 * cols] / new_cols)
        finish(number, direction, direction_total, total[-1], rows_total * cols)
    sums = []
    directions = {}
    for number in vectors:
        weight, grad = masters[number], grads[number]
        prepared[number] = 0.5 * moments[vector_slots[number]] + 0.5 * grad * grad
        directions[number] = grad * lax.rsqrt(prepared[number])
        sums.append(jnp.sum(weight * weight))
        sums.append(jnp.sum(directions[number] * directions[number]))
    total = sum_over(jnp.stack(sums), ("x", "z"))
    for slot, number in enumerate(vectors):
        finish(
            number,
            directions[number],
            total[2 * slot + 1],
            total[2 * slot],
            masters[number].shape[0] * group_size,
        )
    clip_factors = jnp.stack(clips)
    new_rows_all = [prepared[2], prepared[4], prepared[8], prepared[10]]
    new_moments = [
        prepared[0],
        prepared[1],
        prepared[3],
        prepared[5],
        prepared[6],
        prepared[7],
        prepared[9],
        prepared[11],
    ]
    return (
        output,
        input_grad,
        grads[0],
        grads[1],
        grads[2],
        grads[3],
        grads[4],
        grads[5],
        grads[6],
        grads[7],
        grads[8],
        grads[9],
        grads[10],
        grads[11],
        new_rows_all[0],
        new_cols_all[0],
        new_rows_all[1],
        new_cols_all[1],
        new_rows_all[2],
        new_cols_all[2],
        new_rows_all[3],
        new_cols_all[3],
        new_moments[0],
        new_moments[1],
        new_moments[2],
        new_moments[3],
        new_moments[4],
        new_moments[5],
        new_moments[6],
        new_moments[7],
        new_params[0],
        new_params[1],
        new_params[2],
        new_params[3],
        new_params[4],
        new_params[5],
        new_params[6],
        new_params[7],
        new_params[8],
        new_params[9],
        new_params[10],
        new_params[11],
        clip_factors,
    )


def solution(mesh):
    group = mesh.shape["fsdp"]
    split = Mesh(mesh.devices.reshape(group // 2, 2, mesh.shape["dp"] // 2, 2), ALL_AXES)
    in_specs = (
        P(("z", "x", "y", "c"), None),
        P(("z", "x", "y", "c"), None),
        P(("z", "x")),
        P(("z", "x")),
        P(("z", "x"), None),
        P(("z", "x")),
        P(("z", "x"), None),
        P(("z", "x")),
        P(("z", "x")),
        P(("z", "x")),
        P(("z", "x"), None),
        P(("z", "x")),
        P(("z", "x"), None),
        P(("z", "x")),
        P(("z", "x")),
        P(),
        P(("z", "x")),
        P(),
        P(("z", "x")),
        P(),
        P(("z", "x")),
        P(),
        P(("z", "x")),
        P(("z", "x")),
        P(("z", "x")),
        P(("z", "x")),
        P(("z", "x")),
        P(("z", "x")),
        P(("z", "x")),
        P(("z", "x")),
    )
    out_specs = (
        P(("z", "x", "y", "c"), None),
        P(("z", "x", "y", "c"), None),
        P(("z", "x")),
        P(("z", "x")),
        P(("z", "x"), None),
        P(("z", "x")),
        P(("z", "x"), None),
        P(("z", "x")),
        P(("z", "x")),
        P(("z", "x")),
        P(("z", "x"), None),
        P(("z", "x")),
        P(("z", "x"), None),
        P(("z", "x")),
        P(("z", "x")),
        P(),
        P(("z", "x")),
        P(),
        P(("z", "x")),
        P(),
        P(("z", "x")),
        P(),
        P(("z", "x")),
        P(("z", "x")),
        P(("z", "x")),
        P(("z", "x")),
        P(("z", "x")),
        P(("z", "x")),
        P(("z", "x")),
        P(("z", "x")),
        P(("z", "x")),
        P(("z", "x")),
        P(("z", "x"), None),
        P(("z", "x")),
        P(("z", "x"), None),
        P(("z", "x")),
        P(("z", "x")),
        P(("z", "x")),
        P(("z", "x"), None),
        P(("z", "x")),
        P(("z", "x"), None),
        P(("z", "x")),
        P(),
    )
    return jax.shard_map(
        on_device, mesh=split, in_specs=in_specs, out_specs=out_specs, check_vma=False
    )
```

```python
import math

import jax
import jax.numpy as jnp
from jax import lax
from jax.experimental import pallas as pl
from jax.experimental.pallas import tpu as pltpu
from jax.sharding import Mesh
from jax.sharding import PartitionSpec as P

HEAD_DIM = 64
SEQ = 577
LANES = 128
SPAN = 256
CHUNKS = 2
VMEM_LIMIT = 60 * 1024 * 1024

ALL_AXES = ("z", "x", "y", "c")

ln_eps = 1e-06
clip_level = 0.05
step_rate = 4.0


def swap(value, axis):
    return lax.ppermute(value, axis, [(0, 1), (1, 0)])


def shift(value, axis, step):
    size = lax.axis_size(axis)
    return lax.ppermute(value, axis, [(i, (i + step) % size) for i in range(size)])


def partner(value, axis, step):
    size = lax.axis_size(axis)
    return lax.ppermute(value, axis, [(i, i ^ step) for i in range(size)])


def sum_over(value, axes):
    for axis in axes:
        step = 1
        while step < lax.axis_size(axis):
            value = value + partner(value, axis, step)
            step *= 2
    return value


def gather_small(vector):
    value = vector[None, :]
    for axis in ("x", "z"):
        step = 1
        while step < lax.axis_size(axis):
            other = partner(value, axis, step)
            low = (lax.axis_index(axis) // step) % 2 == 0
            value = jnp.where(
                low,
                jnp.concatenate([value, other], axis=0),
                jnp.concatenate([other, value], axis=0),
            )
            step *= 2
    return value


def gather_pieces(shard):
    along = [shard] + [shift(shard, "z", k) for k in range(1, lax.axis_size("z"))]
    pieces = []
    for near in along:
        pieces += [near, swap(near, "x")]
    return pieces


def scatter_sum(keep, send):
    got = swap(send, "x")
    kept = wide(keep) + wide(got)
    total = kept[0]
    for k in range(1, lax.axis_size("z")):
        total = total + wide(shift(low(kept[k]), "z", k))
    if lax.axis_size("y") == 2:
        mine = low(total)
        return wide(mine) + wide(swap(mine, "y"))
    return lax.psum(total, "y")


def row_pad(length):
    return -(-length // LANES) * LANES


def dot(left, right):
    return jnp.dot(left, right, preferred_element_type=jnp.float32)


def dot_tail(left, right):
    return lax.dot_general(
        left, right, (((1,), (1,)), ((), ())), preferred_element_type=jnp.float32
    )


def low(value):
    return value.astype(jnp.bfloat16)


def wide(value):
    return value.astype(jnp.float32)


def any_spec():
    return pl.BlockSpec(memory_space=pl.ANY)


def whole(shape):
    return pl.BlockSpec(shape, lambda *_: (0,) * len(shape))


def sds(shape, dtype):
    return jax.ShapeDtypeStruct(shape, dtype)


def call(body, place, ins, in_specs, outs, out_specs, scratch, name, grid=(1,)):
    return pl.pallas_call(
        body,
        out_shape=outs,
        grid_spec=pltpu.PrefetchScalarGridSpec(
            num_scalar_prefetch=1,
            grid=grid,
            in_specs=in_specs,
            out_specs=out_specs,
            scratch_shapes=scratch,
        ),
        compiler_params=pltpu.CompilerParams(
            vmem_limit_bytes=VMEM_LIMIT, dimension_semantics=("arbitrary",) * len(grid)
        ),
        name=name,
    )(place, *ins)


def shard_of(place_ref, number, z_size):
    k, dx = number // 2, number % 2
    z = lax.rem(place_ref[0] + (z_size - k), z_size)
    x = dx + (1 - 2 * dx) * place_ref[1]
    return z, x


def normalised(rows):
    centre = rows - jnp.mean(rows, axis=-1, keepdims=True)
    spread = jnp.mean(centre * centre, axis=-1, keepdims=True)
    return centre * lax.rsqrt(spread + ln_eps)


def project_qkv(place, rows, gain, bias, bias_q, bias_v, pieces):
    count = len(pieces)
    z_size = count // 2
    part, cols = pieces[0].shape
    width = part * count
    heads = cols // 3
    length = rows[0].shape[0]
    scale = 1.0 / math.sqrt(HEAD_DIM)

    def body(place_ref, own_ref, other_ref, gain_ref, bias_ref, bq_ref, bv_ref, *refs):
        ins, (normed_ref, q_ref, k_ref, v_ref, weight, sem) = refs[:count], refs[count:]
        copies = []
        for number, ref in enumerate(ins):
            z, x = shard_of(place_ref, number, z_size)
            row = pl.multiple_of((z * 2 + x) * part, part)
            copy = pltpu.make_async_copy(ref, weight.at[pl.ds(row, part), :], sem.at[number])
            copy.start()
            copies.append(copy)
        for image, ref in enumerate((own_ref, other_ref)):
            for at in range(0, length, LANES):
                block = wide(ref[at : at + LANES, :])
                normed_ref[image, at : at + LANES, :] = low(
                    normalised(block) * gain_ref[...] + bias_ref[...]
                )
        for copy in copies:
            copy.wait()
        for image in range(2):
            normed = normed_ref[image]
            query = low(dot(normed, weight[:, :heads]) + bq_ref[...])
            q_ref[image] = low(wide(query) * scale)
            k_ref[image] = low(dot(normed, weight[:, heads : 2 * heads]))
            v_ref[image] = low(dot(normed, weight[:, 2 * heads :]) + bv_ref[...])

    part_out = sds((2, length, heads), jnp.bfloat16)
    return call(
        body,
        place,
        (*rows, gain, bias, bias_q, bias_v, *pieces),
        [whole((length, width))] * 2
        + [whole((1, width))] * 2
        + [whole((1, heads))] * 2
        + [any_spec()] * count,
        [sds((2, length, width), jnp.bfloat16)] + [part_out] * 3,
        [whole((2, length, width))] + [whole((2, length, heads))] * 3,
        [pltpu.VMEM((width, cols), jnp.bfloat16), pltpu.SemaphoreType.DMA((count,))],
        "project_qkv",
    )


def attention(place, query, keys, values):
    _, length, heads = query.shape
    pairs = heads // LANES

    def body(place_ref, q_ref, k_ref, v_ref, out_ref, probs_ref):
        lane = lax.broadcasted_iota(jnp.int32, (length, LANES), 1)
        keys_block = k_ref[0]
        values_t = v_ref[0].T
        query_block = q_ref[0]
        mixed = []
        for head in range(2):
            inside = (lane >= head * HEAD_DIM) & (lane < (head + 1) * HEAD_DIM)
            query_head = jnp.where(inside, query_block, jnp.zeros_like(query_block))
            values_head = values_t[head * HEAD_DIM : (head + 1) * HEAD_DIM, :]
            parts = []
            for at in range(0, length, SPAN):
                span = min(SPAN, length - at)
                scores = dot_tail(keys_block, query_head[at : at + span, :])
                key_row = lax.broadcasted_iota(jnp.int32, scores.shape, 0)
                scores = jnp.where(key_row < SEQ, scores, -1e30)
                highest = jnp.max(scores, axis=0, keepdims=True)
                exponent = jnp.exp(scores - highest)
                summed = jnp.sum(exponent, axis=0, keepdims=True)
                probs = low(exponent * (1.0 / summed))
                probs_ref[0, 0, head, :, at : at + span] = probs
                parts.append(dot(values_head, probs))
            mixed.append(jnp.concatenate(parts, axis=1))
        out_ref[0] = low(jnp.concatenate(mixed, axis=0).T)

    block = pl.BlockSpec((1, length, LANES), lambda i, j, p: (i, 0, j))
    return call(
        body,
        place,
        (query, keys, values),
        [block] * 3,
        [
            sds((2, length, heads), jnp.bfloat16),
            sds((2, pairs, 2, length, length), jnp.bfloat16),
        ],
        [block, pl.BlockSpec((1, 1, 2, length, length), lambda i, j, p: (i, j, 0, 0, 0))],
        [],
        "attention",
        grid=(2, pairs),
    )


def attention_back(place, query, keys, values, probs, grad):
    _, length, heads = query.shape
    pairs = heads // LANES
    scale = 1.0 / math.sqrt(HEAD_DIM)

    def body(place_ref, q_ref, k_ref, v_ref, p_ref, g_ref, gq_ref, gk_ref, gv_ref):
        lane = lax.broadcasted_iota(jnp.int32, (length, LANES), 1)
        keys_t = k_ref[0].T
        values_block = v_ref[0]
        query_block = q_ref[0]
        grad_block = g_ref[0]
        grad_query = []
        grad_keys = []
        grad_values = []
        for head in range(2):
            inside = (lane >= head * HEAD_DIM) & (lane < (head + 1) * HEAD_DIM)
            grad_head = jnp.where(inside, grad_block, jnp.zeros_like(grad_block))
            keys_head = keys_t[head * HEAD_DIM : (head + 1) * HEAD_DIM, :]
            parts = []
            sum_keys = None
            sum_values = None
            for at in range(0, length, SPAN):
                span = min(SPAN, length - at)
                probs_low = p_ref[0, 0, head, :, at : at + span]
                probs_wide = wide(probs_low)
                grad_probs = dot_tail(values_block, grad_head[at : at + span, :])
                inner = jnp.sum(probs_wide * grad_probs, axis=0, keepdims=True)
                grad_scores = low(probs_wide * (grad_probs - inner))
                parts.append(dot(keys_head, grad_scores))
                to_keys = dot(grad_scores, query_block[at : at + span, :])
                to_values = dot(probs_low, grad_block[at : at + span, :])
                sum_keys = to_keys if sum_keys is None else sum_keys + to_keys
                sum_values = to_values if sum_values is None else sum_values + to_values
            grad_query.append(jnp.concatenate(parts, axis=1))
            grad_keys.append(sum_keys)
            grad_values.append(sum_values)
        first = lane < HEAD_DIM
        gq_ref[0] = low(jnp.concatenate(grad_query, axis=0).T * scale)
        gk_ref[0] = low(jnp.where(first, grad_keys[0], grad_keys[1]))
        gv_ref[0] = low(jnp.where(first, grad_values[0], grad_values[1]))

    block = pl.BlockSpec((1, length, LANES), lambda i, j, p: (i, 0, j))
    return call(
        body,
        place,
        (query, keys, values, probs, grad),
        [block] * 3
        + [pl.BlockSpec((1, 1, 2, length, length), lambda i, j, p: (i, j, 0, 0, 0)), block],
        [sds((2, length, heads), jnp.bfloat16)] * 3,
        [block] * 3,
        [],
        "attention_back",
        grid=(2, pairs),
    )


def project_out(place, mine, theirs, weight_mine, weight_theirs, rows, bias, gain, norm_bias):
    count, part, half = weight_mine.shape
    z_size = count // 2
    width = part * count
    _, length, heads = mine.shape

    def body(
        place_ref, mine_ref, theirs_ref, wm_ref, wt_ref, own_ref, other_ref, bias_ref, gain_ref,
        nb_ref, middle_ref, normed_ref, weight, total, sem,
    ):
        copies = []
        for number in range(count):
            z, x = shard_of(place_ref, number, z_size)
            row = pl.multiple_of((z * 2 + x) * part, part)
            for slot, ref in enumerate((wm_ref, wt_ref)):
                copy = pltpu.make_async_copy(
                    ref.at[number],
                    weight.at[slot, pl.ds(row, part), :],
                    sem.at[2 * number + slot],
                )
                copy.start()
                copies.append(copy)
        for copy in copies:
            copy.wait()
        core = place_ref[2]
        at_mine = pl.multiple_of(core * heads, heads)
        at_theirs = pl.multiple_of((1 - core) * heads, heads)
        for image, ref in enumerate((own_ref, other_ref)):
            for slot in range(2):
                branch = dot(mine_ref[image], weight[slot, pl.ds(at_mine, heads), :]) + dot(
                    theirs_ref[1 - image], weight[slot, pl.ds(at_theirs, heads), :]
                )
                total[slot] = branch
            for at in range(0, length, LANES):
                upto = at + LANES
                first, second = total[0, at:upto, :], total[1, at:upto, :]
                left = jnp.where(core == 0, first, second)
                right = jnp.where(core == 0, second, first)
                middle = (
                    wide(ref[at:upto, :])
                    + jnp.concatenate([left, right], axis=1)
                    + bias_ref[...]
                )
                if image == 0:
                    middle_ref[at:upto, :] = middle
                normed_ref[image, at:upto, :] = low(
                    normalised(middle) * gain_ref[...] + nb_ref[...]
                )

    return call(
        body,
        place,
        (mine, theirs, weight_mine, weight_theirs, *rows, bias, gain, norm_bias),
        [whole((2, length, heads))] * 2
        + [any_spec()] * 2
        + [whole((length, width))] * 2
        + [whole((1, width))] * 3,
        [sds((length, width), jnp.float32), sds((2, length, width), jnp.bfloat16)],
        [whole((length, width)), whole((2, length, width))],
        [
            pltpu.VMEM((2, width, half), jnp.bfloat16),
            pltpu.VMEM((2, length, half), jnp.float32),
            pltpu.SemaphoreType.DMA((2 * count,)),
        ],
        "project_out",
    )


def feed_forward(place, normed, cotangent, pieces, bias, running):
    count = len(pieces)
    z_size = count // 2
    blocks, part, wide_block = pieces[0].shape
    half_blocks = blocks // 2
    width = part * count
    _, length, _ = normed.shape
    first_call = running is None

    def body(place_ref, normed_ref, own_cot, other_cot, bias_ref, *refs):
        ins = refs[:count]
        refs = refs[count:]
        if not first_call:
            before, refs = refs[:4], refs[4:]
        out_own, out_other, gn_own, gn_other, bsum_ref, keep_ref, send_ref = refs[:7]
        w_in, w_down, normed_t, grads, sem, out_sem = refs[7:]
        step = pl.program_id(0)

        def copies():
            made = []
            for number, ref in enumerate(ins):
                z, x = shard_of(place_ref, number, z_size)
                row = pl.multiple_of((z * 2 + x) * part, part)
                row_in = pl.multiple_of(x * part, part)
                for b in range(half_blocks):
                    made.append(
                        pltpu.make_async_copy(
                            ref.at[b], w_in.at[b, pl.ds(row, part), :], sem.at[number * blocks + b]
                        )
                    )
                    made.append(
                        pltpu.make_async_copy(
                            ref.at[half_blocks + b],
                            w_down.at[z, pl.ds(row_in, part), pl.ds(b * wide_block, wide_block)],
                            sem.at[number * blocks + half_blocks + b],
                        )
                    )
            return made

        @pl.when(step == 0)
        def _():
            for copy in copies():
                copy.start()
            for image in range(2):
                normed_t[:, image * length : (image + 1) * length] = normed_ref[image].T
            for copy in copies():
                copy.wait()

        weight_in = w_in[step]
        weight_down = w_down[step]
        into = None
        down = None
        column_sum = None
        for image, cot_ref in enumerate((own_cot, other_cot)):
            preact = dot(normed_ref[image], weight_in) + bias_ref[0]
            phi = 0.5 * (1.0 + lax.erf(preact * math.sqrt(0.5)))
            density = jnp.exp(-0.5 * preact * preact) * (1.0 / math.sqrt(2.0 * math.pi))
            hidden = low(preact * phi)
            slope = phi + preact * density
            cot = cot_ref[...]
            grad = low(dot_tail(cot, weight_down) * slope)
            out_ref, gn_ref = ((out_own, gn_own), (out_other, gn_other))[image]
            to_out = dot(hidden, weight_down)
            to_normed = dot_tail(grad, weight_in)

            @pl.when(step == 0)
            def _():
                if first_call:
                    out_ref[...] = to_out
                    gn_ref[...] = to_normed
                else:
                    out_ref[...] = before[image][...] + to_out
                    gn_ref[...] = before[2 + image][...] + to_normed

            @pl.when(step > 0)
            def _():
                out_ref[...] += to_out
                gn_ref[...] += to_normed

            partial = jnp.sum(wide(grad), axis=0, keepdims=True)
            column_sum = partial if image == 0 else column_sum + partial
            to_in = dot(normed_t[:, image * length : (image + 1) * length], grad)
            into = to_in if image == 0 else into + to_in
            to_down = dot(hidden.T, cot)
            down = to_down if image == 0 else down + to_down
        bsum_ref[0] = column_sum
        for z in range(z_size):
            for x in range(2):
                k = lax.rem(z + z_size - place_ref[0], z_size)
                dx = x + (1 - 2 * x) * place_ref[1]
                at = (z * 2 + x) * part
                grads[dx, k, step] = low(into[at : at + part, :])
        for x in range(2):
            k = lax.rem(step + z_size - place_ref[0], z_size)
            dx = x + (1 - 2 * x) * place_ref[1]
            for b in range(half_blocks):
                grads[dx, k, half_blocks + b] = low(
                    down[x * part : (x + 1) * part, b * wide_block : (b + 1) * wide_block]
                )

        @pl.when(step == half_blocks - 1)
        def _():
            for slot, ref in enumerate((keep_ref, send_ref)):
                pltpu.make_async_copy(grads.at[slot], ref, out_sem.at[slot]).start()
            for slot, ref in enumerate((keep_ref, send_ref)):
                pltpu.make_async_copy(grads.at[slot], ref, out_sem.at[slot]).wait()

    total = sds((length, width), jnp.float32)
    piece_out = sds((z_size, blocks, part, wide_block), jnp.bfloat16)
    carried = () if first_call else tuple(running)
    return call(
        body,
        place,
        (normed, *cotangent, bias, *pieces, *carried),
        [whole((2, length, width))]
        + [whole((length, width))] * 2
        + [pl.BlockSpec((1, 1, wide_block), lambda b, p: (b, 0, 0))]
        + [any_spec()] * count
        + [whole((length, width))] * len(carried),
        [total] * 4 + [sds((half_blocks, 1, wide_block), jnp.float32)] + [piece_out] * 2,
        [whole((length, width))] * 4
        + [pl.BlockSpec((1, 1, wide_block), lambda b, p: (b, 0, 0))]
        + [any_spec()] * 2,
        [
            pltpu.VMEM((half_blocks, width, wide_block), jnp.bfloat16),
            pltpu.VMEM((half_blocks, wide_block, width), jnp.bfloat16),
            pltpu.VMEM((width, 2 * length), jnp.bfloat16),
            pltpu.VMEM((2, z_size, blocks, part, wide_block), jnp.bfloat16),
            pltpu.SemaphoreType.DMA((count * blocks,)),
            pltpu.SemaphoreType.DMA((2,)),
        ],
        "feed_forward",
        grid=(half_blocks,),
    )


def norm_back(place, rows, gain, grad_own, grad_other, passed, last):
    length, width = rows.shape
    sums = 2 if last else 3

    def body(place_ref, rows_ref, gain_ref, own_ref, other_ref, pass_ref, *refs):
        out_refs, sum_ref = refs[:-1], refs[-1]
        step = pl.program_id(0)
        values = wide(rows_ref[...])
        centre = values - jnp.mean(values, axis=-1, keepdims=True)
        spread = jnp.mean(centre * centre, axis=-1, keepdims=True)
        inverse = lax.rsqrt(spread + ln_eps)
        unit = centre * inverse
        grad = own_ref[...] + other_ref[...]
        scaled = grad * gain_ref[...]
        mean_one = jnp.mean(scaled, axis=-1, keepdims=True)
        mean_two = jnp.mean(scaled * unit, axis=-1, keepdims=True)
        result = wide(pass_ref[...]) + (scaled - mean_one - unit * mean_two) * inverse
        parts = [
            jnp.sum(grad * unit, axis=0, keepdims=True),
            jnp.sum(grad, axis=0, keepdims=True),
        ]
        if last:
            out_refs[0][...] = low(result)
        else:
            out_refs[0][...] = result
            rounded = low(result)
            out_refs[1][...] = rounded
            parts.append(jnp.sum(wide(rounded), axis=0, keepdims=True))
        joined = jnp.concatenate(parts, axis=0)

        @pl.when(step == 0)
        def _():
            sum_ref[...] = joined

        @pl.when(step > 0)
        def _():
            sum_ref[...] += joined

    block = pl.BlockSpec((LANES, width), lambda i, p: (i, 0))
    if last:
        outs = [sds((length, width), jnp.bfloat16)]
    else:
        outs = [sds((length, width), jnp.float32), sds((length, width), jnp.bfloat16)]
    return call(
        body,
        place,
        (rows, gain, grad_own, grad_other, passed),
        [block, whole((1, width)), block, block, block],
        outs + [sds((sums, width), jnp.float32)],
        [block] * len(outs) + [whole((sums, width))],
        [],
        "norm_back",
        grid=(length // LANES,),
    )


def out_back(place, grad_own, grad_other, mine, theirs, weight_mine, weight_theirs):
    count, part, half = weight_mine.shape
    z_size = count // 2
    width = part * count
    _, length, heads = mine.shape

    def body(
        place_ref, own_ref, other_ref, own_half, other_half, mine_ref, theirs_ref, wm_ref, wt_ref,
        ga_ref, keep_ref, send_ref, weight, turned, grads, sem, out_sem,
    ):
        copies = []
        for number in range(count):
            z, x = shard_of(place_ref, number, z_size)
            row = pl.multiple_of((z * 2 + x) * part, part)
            for slot, ref in enumerate((wm_ref, wt_ref)):
                copy = pltpu.make_async_copy(
                    ref.at[number],
                    weight.at[slot, pl.ds(row, part), :],
                    sem.at[2 * number + slot],
                )
                copy.start()
                copies.append(copy)
        core = place_ref[2]
        at_mine = pl.multiple_of(core * heads, heads)
        at_theirs = pl.multiple_of((1 - core) * heads, heads)
        for image in range(2):
            lanes = slice(image * length, (image + 1) * length)
            turned[pl.ds(at_mine, heads), lanes] = mine_ref[image].T
            turned[pl.ds(at_theirs, heads), lanes] = theirs_ref[1 - image].T
        term = dot(turned[:, :length], own_half[...]) + dot(turned[:, length:], other_half[...])
        for z in range(z_size):
            for x in range(2):
                k = lax.rem(z + z_size - place_ref[0], z_size)
                dx = x + (1 - 2 * x) * place_ref[1]
                at = (z * 2 + x) * part
                grads[dx, k] = low(term[at : at + part, :])
        for slot, ref in enumerate((keep_ref, send_ref)):
            pltpu.make_async_copy(grads.at[slot], ref, out_sem.at[slot]).start()
        for copy in copies:
            copy.wait()
        for image, ref in enumerate((own_ref, other_ref)):
            first, second = ref[:, :half], ref[:, half:]
            left = jnp.where(core == 0, first, second)
            right = jnp.where(core == 0, second, first)
            ga_ref[image] = low(
                dot_tail(left, weight[0, pl.ds(at_mine, heads), :])
                + dot_tail(right, weight[1, pl.ds(at_mine, heads), :])
            )
        for slot, ref in enumerate((keep_ref, send_ref)):
            pltpu.make_async_copy(grads.at[slot], ref, out_sem.at[slot]).wait()

    half_block = pl.BlockSpec((length, half), lambda i, p: (0, p[2]))
    piece_out = sds((z_size, part, half), jnp.bfloat16)
    return call(
        body,
        place,
        (
            grad_own,
            grad_other,
            grad_own,
            grad_other,
            mine,
            theirs,
            weight_mine,
            weight_theirs,
        ),
        [whole((length, width))] * 2
        + [half_block] * 2
        + [whole((2, length, heads))] * 2
        + [any_spec()] * 2,
        [sds((2, length, heads), jnp.bfloat16)] + [piece_out] * 2,
        [whole((2, length, heads))] + [any_spec()] * 2,
        [
            pltpu.VMEM((2, width, half), jnp.bfloat16),
            pltpu.VMEM((width, 2 * length), jnp.bfloat16),
            pltpu.VMEM((2, z_size, part, half), jnp.bfloat16),
            pltpu.SemaphoreType.DMA((2 * count,)),
            pltpu.SemaphoreType.DMA((2,)),
        ],
        "out_back",
    )


def qkv_term(place, normed, grad_q, grad_k, grad_v):
    _, length, width = normed.shape
    heads = grad_q.shape[-1]
    cols = 3 * heads

    def body(place_ref, normed_ref, gq_ref, gk_ref, gv_ref, sum_ref, keep_ref, send_ref, turned, grads, sem):
        z_size = grads.shape[1]
        part = grads.shape[2]
        for image in range(2):
            turned[:, image * length : (image + 1) * length] = normed_ref[image].T
        for slot, ref in enumerate((gq_ref, gk_ref, gv_ref)):
            term = dot(turned[:, :length], ref[0]) + dot(turned[:, length:], ref[1])
            for z in range(z_size):
                for x in range(2):
                    k = lax.rem(z + z_size - place_ref[0], z_size)
                    dx = x + (1 - 2 * x) * place_ref[1]
                    at = (z * 2 + x) * part
                    grads[dx, k, :, slot * heads : (slot + 1) * heads] = low(
                        term[at : at + part, :]
                    )
            sum_ref[slot : slot + 1, :] = jnp.sum(wide(ref[0]), axis=0, keepdims=True) + jnp.sum(
                wide(ref[1]), axis=0, keepdims=True
            )
        for slot, ref in enumerate((keep_ref, send_ref)):
            pltpu.make_async_copy(grads.at[slot], ref, sem.at[slot]).start()
        for slot, ref in enumerate((keep_ref, send_ref)):
            pltpu.make_async_copy(grads.at[slot], ref, sem.at[slot]).wait()

    z_size = lax.axis_size("z")
    part = width // (2 * z_size)
    piece_out = sds((z_size, part, cols), jnp.bfloat16)
    return call(
        body,
        place,
        (normed, grad_q, grad_k, grad_v),
        [whole((2, length, width))] + [whole((2, length, heads))] * 3,
        [sds((3, heads), jnp.float32)] + [piece_out] * 2,
        [whole((3, heads))] + [any_spec()] * 2,
        [
            pltpu.VMEM((width, 2 * length), jnp.bfloat16),
            pltpu.VMEM((2, z_size, part, cols), jnp.bfloat16),
            pltpu.SemaphoreType.DMA((2,)),
        ],
        "qkv_term",
    )


def qkv_back(place, grad_q, grad_k, grad_v, pieces):
    count = len(pieces)
    z_size = count // 2
    part, cols = pieces[0].shape
    width = part * count
    heads = cols // 3
    length = grad_q.shape[1]

    def body(place_ref, gq_ref, gk_ref, gv_ref, *refs):
        ins, (own_ref, other_ref, weight, sem) = refs[:count], refs[count:]
        copies = []
        for number, ref in enumerate(ins):
            z, x = shard_of(place_ref, number, z_size)
            row = pl.multiple_of((z * 2 + x) * part, part)
            copy = pltpu.make_async_copy(ref, weight.at[pl.ds(row, part), :], sem.at[number])
            copy.start()
            copies.append(copy)
        for copy in copies:
            copy.wait()
        for image, out_ref in enumerate((own_ref, other_ref)):
            out_ref[...] = (
                dot_tail(gq_ref[image], weight[:, :heads])
                + dot_tail(gk_ref[image], weight[:, heads : 2 * heads])
                + dot_tail(gv_ref[image], weight[:, 2 * heads :])
            )

    return call(
        body,
        place,
        (grad_q, grad_k, grad_v, *pieces),
        [whole((2, length, heads))] * 3 + [any_spec()] * count,
        [sds((length, width), jnp.float32)] * 2,
        [whole((length, width))] * 2,
        [pltpu.VMEM((width, cols), jnp.bfloat16), pltpu.SemaphoreType.DMA((count,))],
        "qkv_back",
    )


def on_device(
    inputs,
    cotangent,
    norm1_gain,
    norm1_bias,
    qkv_weight,
    qv_bias,
    out_weight,
    out_bias,
    norm2_gain,
    norm2_bias,
    in_weight,
    in_bias,
    down_weight,
    down_bias,
    qkv_rows,
    qkv_cols,
    out_rows,
    out_cols,
    in_rows,
    in_cols,
    down_rows,
    down_cols,
    norm1_gain_moment,
    norm1_bias_moment,
    qv_bias_moment,
    out_bias_moment,
    norm2_gain_moment,
    norm2_bias_moment,
    in_bias_moment,
    down_bias_moment,
):
    masters = [
        norm1_gain,
        norm1_bias,
        qkv_weight,
        qv_bias,
        out_weight,
        out_bias,
        norm2_gain,
        norm2_bias,
        in_weight,
        in_bias,
        down_weight,
        down_bias,
    ]
    core = lax.axis_index("c")
    place = jnp.stack([lax.axis_index("z"), lax.axis_index("x"), core]).astype(jnp.int32)
    group_size = lax.axis_size("z") * lax.axis_size("x")
    tokens, width = inputs.shape
    images_all = (tokens // SEQ) * group_size * lax.axis_size("y") * lax.axis_size("c")
    padding = ((0, row_pad(tokens) - tokens), (0, 0))
    rows_own = jnp.pad(inputs, padding)
    cot_own = jnp.pad(cotangent, padding)
    rows = (rows_own, swap(rows_own, "c"))
    cot = (cot_own, swap(cot_own, "c"))

    def half_cols(shard, groups):
        cut = shard.reshape(shard.shape[0], groups, 2, -1)
        return lax.dynamic_index_in_dim(cut, core, 2, False)

    def halves_of(pair):
        mine, theirs = pair
        return jnp.where(core == 0, mine, theirs), jnp.where(core == 0, theirs, mine)

    vectors = [0, 1, 3, 5, 6, 7, 9, 11]
    sizes = [masters[number].shape[0] for number in vectors]
    small = wide(gather_small(low(jnp.concatenate([masters[number] for number in vectors]))))
    full = {}
    at = 0
    for number, size in zip(vectors, sizes):
        full[number] = small[:, at : at + size].reshape(1, -1)
        at += size
    heads_bias = lax.dynamic_index_in_dim(
        full[3].reshape(2, 2, 1, width // 2), core, 1, False
    )

    rows_qkv = low(half_cols(qkv_weight, 3)).reshape(qkv_weight.shape[0], -1)
    pieces_qkv = gather_pieces(rows_qkv)
    pieces_out = gather_pieces(low(half_cols(out_weight, 1)).reshape(out_weight.shape[0], -1))
    weight_mine = jnp.stack(pieces_out)
    weight_theirs = swap(weight_mine, "c")

    part = in_weight.shape[0]
    per_shard = in_weight.shape[1] // group_size // 2 // CHUNKS
    hidden_chunk = per_shard * group_size
    wide_block = hidden_chunk // (group_size // 2)
    blocks = hidden_chunk // wide_block
    in_cut = low(
        lax.dynamic_index_in_dim(
            in_weight.reshape(part, group_size, 2, CHUNKS, per_shard), core, 2, False
        )
    )
    down_cut = low(
        lax.dynamic_index_in_dim(
            down_weight.reshape(2, CHUNKS, per_shard, width // wide_block, wide_block),
            core,
            0,
            False,
        )
    )
    bias_cut = lax.dynamic_index_in_dim(
        full[9].reshape(group_size, 2, CHUNKS, per_shard), core, 1, False
    )
    pieces_ff = []
    bias_ff = []
    for j in range(CHUNKS):
        from_in = in_cut[:, :, j].reshape(part, blocks, wide_block).transpose(1, 0, 2)
        from_down = down_cut[j].transpose(1, 0, 2)
        pieces_ff.append(gather_pieces(jnp.concatenate([from_in, from_down], axis=0)))
        bias_ff.append(bias_cut[:, j].reshape(blocks, 1, wide_block))

    normed, query, keys, values = project_qkv(
        place, rows, full[0], full[1], heads_bias[0], heads_bias[1], pieces_qkv
    )
    attended, probs = attention(place, query, keys, values)
    attended_theirs = swap(attended, "c")
    middle, normed_mid = project_out(
        place,
        attended,
        attended_theirs,
        weight_mine,
        weight_theirs,
        rows,
        full[5],
        full[6],
        full[7],
    )
    running = None
    hidden_sums = []
    grad_ff = []
    for j in range(CHUNKS):
        *running, sums, keep, send = feed_forward(
            place, normed_mid, cot, pieces_ff[j], bias_ff[j], running
        )
        hidden_sums.append(sums)
        grad_ff.append(scatter_sum(keep, send))
    out_share, out_given, normed_share, normed_given = running
    output = low(middle + out_share + swap(out_given, "c") + full[11])[:tokens]
    grad_mid, grad_mid_low, sums_mid = norm_back(
        place, middle, full[6], normed_share, swap(normed_given, "c"), cot_own, False
    )
    grad_mid_other = swap(grad_mid_low, "c")
    grad_attended, keep, send = out_back(
        place,
        grad_mid_low,
        grad_mid_other,
        attended,
        attended_theirs,
        weight_mine,
        weight_theirs,
    )
    grad_out_half = scatter_sum(keep, send)
    grad_q, grad_k, grad_v = attention_back(place, query, keys, values, probs, grad_attended)
    sums_qkv, keep, send = qkv_term(place, normed, grad_q, grad_k, grad_v)
    grad_qkv_half = scatter_sum(keep, send)
    share, given = qkv_back(place, grad_q, grad_k, grad_v, pieces_qkv)
    input_grad, sums_in = norm_back(
        place, rows_own, full[0], share, swap(given, "c"), grad_mid, True
    )
    input_grad = input_grad[:tokens]

    def both_cores(half):
        return halves_of((half, swap(half, "c")))

    grads = [None] * 12
    pair = both_cores(grad_qkv_half / images_all)
    grads[2] = jnp.stack(
        [half.reshape(part, 3, width // 2) for half in pair], axis=2
    ).reshape(qkv_weight.shape)
    pair = both_cores(grad_out_half / images_all)
    grads[4] = jnp.concatenate(pair, axis=1)
    pairs = [both_cores(half / images_all) for half in grad_ff]
    both = jnp.stack([jnp.stack(pair) for pair in pairs])
    by_in = both[:, :, :blocks].reshape(CHUNKS, 2, blocks, part, -1, per_shard)
    grads[8] = by_in.transpose(3, 2, 4, 1, 0, 5).reshape(in_weight.shape)
    grads[10] = both[:, :, blocks:].transpose(1, 0, 3, 2, 4).reshape(down_weight.shape)

    def by_core(cols, axis):
        empty = jnp.zeros_like(cols)
        return jnp.stack(
            [jnp.where(core == 0, cols, empty), jnp.where(core == 0, empty, cols)], axis=axis
        )

    hidden_cols = jnp.stack(hidden_sums).reshape(CHUNKS, group_size, per_shard)
    term_in_bias = by_core(hidden_cols.transpose(1, 0, 2), 1).reshape(-1)
    term_qv_bias = by_core(sums_qkv[::2], 1).reshape(-1)
    term_down_bias = jnp.sum(wide(cotangent), axis=0)
    vector_terms = {
        0: sums_in[0],
        1: sums_in[1],
        3: term_qv_bias,
        5: sums_mid[2],
        6: sums_mid[0],
        7: sums_mid[1],
        9: term_in_bias,
        11: term_down_bias,
    }
    here = lax.axis_index("z") * lax.axis_size("x") + lax.axis_index("x")
    for group in ((5, 6, 7, 9, 11), (0, 1, 3)):
        summed = sum_over(
            jnp.concatenate(
                [vector_terms[number].reshape(group_size, -1) for number in group], axis=1
            ),
            ("c", "x", "z", "y"),
        )
        mine = lax.dynamic_index_in_dim(summed, here, 0, False) / images_all
        at = 0
        for number in group:
            size = masters[number].shape[0]
            grads[number] = mine[at : at + size]
            at += size
    row_states = [qkv_rows, out_rows, in_rows, down_rows]
    col_states = [qkv_cols, out_cols, in_cols, down_cols]
    moments = [
        norm1_gain_moment,
        norm1_bias_moment,
        qv_bias_moment,
        out_bias_moment,
        norm2_gain_moment,
        norm2_bias_moment,
        in_bias_moment,
        down_bias_moment,
    ]
    matrix_slots = {2: 0, 4: 1, 8: 2, 10: 3}
    vector_slots = {0: 0, 1: 1, 3: 2, 5: 3, 6: 4, 7: 5, 9: 6, 11: 7}
    prepared = [None] * 12
    new_params = [None] * 12
    clips = [None] * 12
    new_cols_all = [None] * 4

    def finish(number, direction, direction_total, weight_total, count):
        clip_factor = jnp.maximum(1.0, jnp.sqrt(direction_total / count) / clip_level)
        rms_weight = jnp.sqrt(weight_total / count)
        clips[number] = clip_factor
        new_params[number] = masters[number] - step_rate * rms_weight * direction / clip_factor

    for number in (10, 8, 4, 2):
        position = matrix_slots[number]
        weight, grad = masters[number], grads[number]
        squared = grad * grad
        new_rows = 0.5 * row_states[position] + 0.5 * jnp.mean(squared, axis=1)
        prepared[number] = new_rows
        pack = jnp.concatenate(
            [
                jnp.sum(squared, axis=0),
                jnp.sum(squared / new_rows[:, None], axis=0),
                jnp.stack([jnp.sum(new_rows), jnp.sum(weight * weight)]),
            ]
        )
        total = sum_over(pack, ("x", "z"))
        rows_total, cols = weight.shape[0] * group_size, weight.shape[1]
        new_cols = 0.5 * col_states[position] + 0.5 * total[:cols] / rows_total
        new_cols_all[position] = new_cols
        mean_rows = total[-2] / rows_total
        direction = grad * lax.rsqrt(new_rows[:, None] * new_cols[None, :] / mean_rows)
        direction_total = mean_rows * jnp.sum(total[cols : 2 * cols] / new_cols)
        finish(number, direction, direction_total, total[-1], rows_total * cols)
    sums = []
    directions = {}
    for number in vectors:
        weight, grad = masters[number], grads[number]
        prepared[number] = 0.5 * moments[vector_slots[number]] + 0.5 * grad * grad
        directions[number] = grad * lax.rsqrt(prepared[number])
        sums.append(jnp.sum(weight * weight))
        sums.append(jnp.sum(directions[number] * directions[number]))
    total = sum_over(jnp.stack(sums), ("x", "z"))
    for slot, number in enumerate(vectors):
        finish(
            number,
            directions[number],
            total[2 * slot + 1],
            total[2 * slot],
            masters[number].shape[0] * group_size,
        )
    clip_factors = jnp.stack(clips)
    new_rows_all = [prepared[2], prepared[4], prepared[8], prepared[10]]
    new_moments = [
        prepared[0],
        prepared[1],
        prepared[3],
        prepared[5],
        prepared[6],
        prepared[7],
        prepared[9],
        prepared[11],
    ]
    return (
        output,
        input_grad,
        grads[0],
        grads[1],
        grads[2],
        grads[3],
        grads[4],
        grads[5],
        grads[6],
        grads[7],
        grads[8],
        grads[9],
        grads[10],
        grads[11],
        new_rows_all[0],
        new_cols_all[0],
        new_rows_all[1],
        new_cols_all[1],
        new_rows_all[2],
        new_cols_all[2],
        new_rows_all[3],
        new_cols_all[3],
        new_moments[0],
        new_moments[1],
        new_moments[2],
        new_moments[3],
        new_moments[4],
        new_moments[5],
        new_moments[6],
        new_moments[7],
        new_params[0],
        new_params[1],
        new_params[2],
        new_params[3],
        new_params[4],
        new_params[5],
        new_params[6],
        new_params[7],
        new_params[8],
        new_params[9],
        new_params[10],
        new_params[11],
        clip_factors,
    )


def solution(mesh):
    group = mesh.shape["fsdp"]
    split = Mesh(mesh.devices.reshape(group // 2, 2, mesh.shape["dp"] // 2, 2), ALL_AXES)
    in_specs = (
        P(("z", "x", "y", "c"), None),
        P(("z", "x", "y", "c"), None),
        P(("z", "x")),
        P(("z", "x")),
        P(("z", "x"), None),
        P(("z", "x")),
        P(("z", "x"), None),
        P(("z", "x")),
        P(("z", "x")),
        P(("z", "x")),
        P(("z", "x"), None),
        P(("z", "x")),
        P(("z", "x"), None),
        P(("z", "x")),
        P(("z", "x")),
        P(),
        P(("z", "x")),
        P(),
        P(("z", "x")),
        P(),
        P(("z", "x")),
        P(),
        P(("z", "x")),
        P(("z", "x")),
        P(("z", "x")),
        P(("z", "x")),
        P(("z", "x")),
        P(("z", "x")),
        P(("z", "x")),
        P(("z", "x")),
    )
    out_specs = (
        P(("z", "x", "y", "c"), None),
        P(("z", "x", "y", "c"), None),
        P(("z", "x")),
        P(("z", "x")),
        P(("z", "x"), None),
        P(("z", "x")),
        P(("z", "x"), None),
        P(("z", "x")),
        P(("z", "x")),
        P(("z", "x")),
        P(("z", "x"), None),
        P(("z", "x")),
        P(("z", "x"), None),
        P(("z", "x")),
        P(("z", "x")),
        P(),
        P(("z", "x")),
        P(),
        P(("z", "x")),
        P(),
        P(("z", "x")),
        P(),
        P(("z", "x")),
        P(("z", "x")),
        P(("z", "x")),
        P(("z", "x")),
        P(("z", "x")),
        P(("z", "x")),
        P(("z", "x")),
        P(("z", "x")),
        P(("z", "x")),
        P(("z", "x")),
        P(("z", "x"), None),
        P(("z", "x")),
        P(("z", "x"), None),
        P(("z", "x")),
        P(("z", "x")),
        P(("z", "x")),
        P(("z", "x"), None),
        P(("z", "x")),
        P(("z", "x"), None),
        P(("z", "x")),
        P(),
    )
    return jax.shard_map(
        on_device, mesh=split, in_specs=in_specs, out_specs=out_specs, check_vma=False
    )
```

```python
import math

import jax
import jax.numpy as jnp
from jax import lax
from jax.experimental import pallas as pl
from jax.experimental.pallas import tpu as pltpu
from jax.sharding import Mesh
from jax.sharding import PartitionSpec as P

HEAD_DIM = 64
SEQ = 577
LANES = 128
TILE = 16
SPAN = 256
CHUNKS = 2
VMEM_LIMIT = 60 * 1024 * 1024

ALL_AXES = ("z", "x", "y", "c")

MATRICES = (2, 4, 8, 10)
VECTORS = (0, 1, 3, 5, 6, 7, 9, 11)

ln_eps = 1e-06
clip_level = 0.05
step_rate = 4.0


def swap(value, axis):
    return lax.ppermute(value, axis, [(0, 1), (1, 0)])


def shift(value, axis, step):
    size = lax.axis_size(axis)
    return lax.ppermute(value, axis, [(i, (i + step) % size) for i in range(size)])


def partner(value, axis, step):
    size = lax.axis_size(axis)
    return lax.ppermute(value, axis, [(i, i ^ step) for i in range(size)])


def swap_both(value):
    return lax.ppermute(value, ("y", "c"), [(i, 3 - i) for i in range(4)])


def sum_over(value, axes):
    for axis in axes:
        step = 1
        while step < lax.axis_size(axis):
            value = value + partner(value, axis, step)
            step *= 2
    return value


def gather_pieces(shard):
    along = [shard] + [shift(shard, "z", k) for k in range(1, lax.axis_size("z"))]
    pieces = []
    for near in along:
        pieces += [near, swap(near, "x")]
    return pieces


def scatter_sum(place, keep, send):
    size = lax.axis_size("z")
    held, *parts = fold_x(place, keep, swap(send, "x"))
    mine = fold_z(place, held, [shift(parts[k - 1], "z", k) for k in range(1, size)])
    if lax.axis_size("y") == 2:
        mine = low(mine)
        return [mine, swap(mine, "y")], [swap(mine, "c"), swap_both(mine)]
    total = lax.psum(mine, "y")
    return [total], [swap(total, "c")]


def row_pad(length):
    return -(-length // LANES) * LANES


def dot(left, right):
    return jnp.dot(left, right, preferred_element_type=jnp.float32)


def dot_tail(left, right):
    return lax.dot_general(
        left, right, (((1,), (1,)), ((), ())), preferred_element_type=jnp.float32
    )


def low(value):
    return value.astype(jnp.bfloat16)


def wide(value):
    return value.astype(jnp.float32)


def any_spec():
    return pl.BlockSpec(memory_space=pl.ANY)


def whole(shape):
    return pl.BlockSpec(shape, lambda *_: (0,) * len(shape))


def sds(shape, dtype):
    return jax.ShapeDtypeStruct(shape, dtype)


def call(body, place, ins, in_specs, outs, out_specs, scratch, name, grid=(1,), flops=0):
    moved = sum(math.prod(a.shape) * a.dtype.itemsize for a in [*ins, *outs])
    return pl.pallas_call(
        body,
        out_shape=outs,
        grid_spec=pltpu.PrefetchScalarGridSpec(
            num_scalar_prefetch=1,
            grid=grid,
            in_specs=in_specs,
            out_specs=out_specs,
            scratch_shapes=scratch,
        ),
        compiler_params=pltpu.CompilerParams(
            vmem_limit_bytes=VMEM_LIMIT, dimension_semantics=("arbitrary",) * len(grid)
        ),
        cost_estimate=pl.CostEstimate(flops=flops, bytes_accessed=moved, transcendentals=0),
        name=name,
    )(place, *ins)


def shard_of(place_ref, number, z_size):
    k, dx = number // 2, number % 2
    z = lax.rem(place_ref[0] + (z_size - k), z_size)
    x = dx + (1 - 2 * dx) * place_ref[1]
    return z, x


def normalised(rows):
    centre = rows - jnp.mean(rows, axis=-1, keepdims=True)
    spread = jnp.mean(centre * centre, axis=-1, keepdims=True)
    return centre * lax.rsqrt(spread + ln_eps)


def select(core, first, second):
    return jnp.where(core == 0, first, second)


def prepare_qkv(place, weight, vectors):
    part, cols = weight.shape
    half = cols // 6
    sizes = [vector.shape[-1] for vector in vectors]

    def body(place_ref, weight_ref, *refs):
        out_ref = refs[-1]
        core = place_ref[2]
        for slot in range(3):
            at = 2 * slot * half
            out_ref[:part, slot * half : (slot + 1) * half] = low(
                select(core, weight_ref[:, at : at + half], weight_ref[:, at + half : at + 2 * half])
            )
        at = 0
        for ref, size in zip(refs, sizes):
            out_ref[part:, at : at + size] = low(jnp.broadcast_to(ref[...], (TILE, size)))
            at += size

    shape = (part + TILE, cols // 2)
    return call(
        body,
        place,
        (weight, *vectors),
        [whole((part, cols))] + [whole((1, size)) for size in sizes],
        [sds(shape, jnp.bfloat16)],
        [whole(shape)],
        [],
        "prepare_qkv",
    )[0]


def prepare_rest(place, in_weight, down_weight, out_weight, inputs, cotangent):
    part, hidden = in_weight.shape
    width = down_weight.shape[1]
    per_core = down_weight.shape[0] // 2
    per_shard = per_core // CHUNKS
    shards = hidden // (2 * per_core)
    block = per_shard * 2
    blocks = shards // 2
    tokens = inputs.shape[0]
    length = row_pad(tokens)
    even = tokens // TILE * TILE

    def body(place_ref, in_ref, down_ref, out_w_ref, rows_ref, cot_ref, *refs):
        pieces, (rows_out, cot_out, sum_ref) = refs[:CHUNKS], refs[CHUNKS:]
        core = place_ref[2]
        for j in range(CHUNKS):
            for s in range(shards):
                at = s * 2 * per_core + j * per_shard
                pieces[j][s // 2, :, (s % 2) * per_shard : (s % 2 + 1) * per_shard] = low(
                    select(
                        core,
                        in_ref[:, at : at + per_shard],
                        in_ref[:, at + per_core : at + per_core + per_shard],
                    )
                )
            at = j * per_shard
            for b in range(width // block):
                cols = slice(b * block, (b + 1) * block)
                pieces[j][blocks + b] = low(
                    select(
                        core,
                        down_ref[at : at + per_shard, cols],
                        down_ref[at + per_core : at + per_core + per_shard, cols],
                    )
                )
        half = width // 2
        for b in range(half // block):
            at = b * block
            pieces[0][blocks + width // block + b] = low(
                select(
                    core,
                    out_w_ref[:, at : at + block],
                    out_w_ref[:, half + at : half + at + block],
                )
            )
        row = lax.broadcasted_iota(jnp.int32, (length - even, width), 0)
        for ref, to in ((rows_ref, rows_out), (cot_ref, cot_out)):
            to[:even, :] = ref[:even, :]
            last = jnp.zeros((length - even, width), jnp.float32)
            for extra in range(tokens - even):
                one = wide(ref[even + extra : even + extra + 1, :])
                last = jnp.where(row == extra, one, last)
            to[even:, :] = low(last)
        sum_ref[...] = jnp.sum(wide(cot_out[...]), axis=0, keepdims=True)

    extra = width // 2 // block
    counts = [blocks + width // block + (extra if j == 0 else 0) for j in range(CHUNKS)]
    outs = [sds((count, part, block), jnp.bfloat16) for count in counts]
    outs += [sds((length, width), jnp.bfloat16)] * 2 + [sds((1, width), jnp.float32)]
    ins = (in_weight, down_weight, out_weight, inputs, cotangent)
    return call(
        body,
        place,
        ins,
        [whole(a.shape) for a in ins],
        outs,
        [whole(a.shape) for a in outs],
        [],
        "prepare_rest",
    )


GAIN_ONE, BIAS_ONE, BIAS_OUT, GAIN_TWO, BIAS_TWO, BIAS_DOWN = range(6)


def project_qkv(place, rows, pieces, sizes):
    count = len(pieces)
    z_size = count // 2
    cols = pieces[0].shape[1]
    part = pieces[0].shape[0] - TILE
    width = part * count
    heads = cols // 3
    length = rows[0].shape[0]
    scale = 1.0 / math.sqrt(HEAD_DIM)
    starts = [sum(sizes[:number]) for number in range(len(sizes))]
    per_shard = sizes[6] // 2 // CHUNKS
    blocks = count // 2

    def body(place_ref, own_ref, other_ref, *refs):
        ins, refs = refs[:count], refs[count:]
        normed_ref, q_ref, k_ref, v_ref, vec_ref, hidden_bias_ref, weight, packed, sem = refs
        core = place_ref[2]
        copies = []
        for number, ref in enumerate(ins):
            z, x = shard_of(place_ref, number, z_size)
            row = pl.multiple_of((z * 2 + x) * part, part)
            for slot, copy in enumerate(
                (
                    pltpu.make_async_copy(
                        ref.at[pl.ds(0, part), :], weight.at[pl.ds(row, part), :], sem.at[2 * number]
                    ),
                    pltpu.make_async_copy(
                        ref.at[pl.ds(part, TILE), :], packed.at[z * 2 + x], sem.at[2 * number + 1]
                    ),
                )
            ):
                copy.start()
                copies.append(copy)
        for copy in copies:
            copy.wait()

        def vector(slot, shards=range(count)):
            at, size = starts[slot], sizes[slot]
            return jnp.concatenate(
                [wide(packed[s, 0:1, at : at + size]) for s in shards], axis=1
            )

        gain, bias = vector(0), vector(1)
        for row, value in (
            (GAIN_ONE, gain),
            (BIAS_ONE, bias),
            (BIAS_OUT, vector(3)),
            (GAIN_TWO, vector(4)),
            (BIAS_TWO, vector(5)),
            (BIAS_DOWN, vector(7)),
        ):
            vec_ref[row : row + 1, :] = value
        vec_ref[6:8, :] = jnp.zeros((2, width), jnp.float32)
        for j in range(CHUNKS):
            for b in range(blocks):
                for i in range(2):
                    at = starts[6] + j * per_shard
                    to = at + sizes[6] // 2
                    hidden_bias_ref[j, b, :, i * per_shard : (i + 1) * per_shard] = wide(
                        select(
                            core,
                            wide(packed[2 * b + i, 0:1, at : at + per_shard]),
                            wide(packed[2 * b + i, 0:1, to : to + per_shard]),
                        )
                    )
        bias_q = vector(2, range(blocks))
        bias_v = vector(2, range(blocks, count))
        bias_q = select(core, bias_q[:, :heads], bias_q[:, heads:])
        bias_v = select(core, bias_v[:, :heads], bias_v[:, heads:])
        for image, ref in enumerate((own_ref, other_ref)):
            for at in range(0, length, LANES):
                block = wide(ref[at : at + LANES, :])
                normed_ref[image, at : at + LANES, :] = low(normalised(block) * gain + bias)
            normed = normed_ref[image]
            query = low(dot(normed, weight[:, :heads]) + bias_q)
            q_ref[image] = low(wide(query) * scale)
            k_ref[image] = low(dot(normed, weight[:, heads : 2 * heads]))
            v_ref[image] = low(dot(normed, weight[:, 2 * heads :]) + bias_v)

    part_out = sds((2, length, heads), jnp.bfloat16)
    return call(
        body,
        place,
        (*rows, *pieces),
        [whole((length, width))] * 2 + [any_spec()] * count,
        [sds((2, length, width), jnp.bfloat16)]
        + [part_out] * 3
        + [
            sds((8, width), jnp.float32),
            sds((CHUNKS, blocks, 1, 2 * per_shard), jnp.float32),
        ],
        [whole((2, length, width))]
        + [whole((2, length, heads))] * 3
        + [whole((8, width)), whole((CHUNKS, blocks, 1, 2 * per_shard))],
        [
            pltpu.VMEM((width, cols), jnp.bfloat16),
            pltpu.VMEM((count, TILE, cols), jnp.bfloat16),
            pltpu.SemaphoreType.DMA((2 * count,)),
        ],
        "project_qkv",
        flops=4 * length * width * cols,
    )


def gather_out(place, pieces, first):
    count = len(pieces)
    z_size = count // 2
    total, part, block = pieces[0].shape
    width = part * count

    def body(place_ref, *refs):
        ins, out_ref, sem = refs[:count], refs[count], refs[count + 1]
        copies = []
        for number, ref in enumerate(ins):
            z, x = shard_of(place_ref, number, z_size)
            row = pl.multiple_of((z * 2 + x) * part, part)
            for b in range(total - first):
                copy = pltpu.make_async_copy(
                    ref.at[first + b],
                    out_ref.at[pl.ds(row, part), pl.ds(b * block, block)],
                    sem.at[number * (total - first) + b],
                )
                copy.start()
                copies.append(copy)
        for copy in copies:
            copy.wait()

    shape = (width, (total - first) * block)
    return call(
        body,
        place,
        tuple(pieces),
        [any_spec()] * count,
        [sds(shape, jnp.bfloat16)],
        [whole(shape)],
        [pltpu.SemaphoreType.DMA((count * (total - first),))],
        "gather_out",
    )[0]


def attention(place, query, keys, values):
    _, length, heads = query.shape
    pairs = heads // LANES

    def body(place_ref, q_ref, k_ref, v_ref, out_ref, probs_ref):
        lane = lax.broadcasted_iota(jnp.int32, (length, LANES), 1)
        keys_block = k_ref[0]
        values_t = v_ref[0].T
        query_block = q_ref[0]
        mixed = []
        for head in range(2):
            inside = (lane >= head * HEAD_DIM) & (lane < (head + 1) * HEAD_DIM)
            query_head = jnp.where(inside, query_block, jnp.zeros_like(query_block))
            values_head = values_t[head * HEAD_DIM : (head + 1) * HEAD_DIM, :]
            parts = []
            for at in range(0, length, SPAN):
                span = min(SPAN, length - at)
                scores = dot_tail(keys_block, query_head[at : at + span, :])
                key_row = lax.broadcasted_iota(jnp.int32, scores.shape, 0)
                scores = jnp.where(key_row < SEQ, scores, -1e30)
                highest = jnp.max(scores, axis=0, keepdims=True)
                exponent = jnp.exp(scores - highest)
                summed = jnp.sum(exponent, axis=0, keepdims=True)
                probs = low(exponent * (1.0 / summed))
                probs_ref[0, 0, head, :, at : at + span] = probs
                parts.append(dot(values_head, probs))
            mixed.append(jnp.concatenate(parts, axis=1))
        out_ref[0] = low(jnp.concatenate(mixed, axis=0).T)

    block = pl.BlockSpec((1, length, LANES), lambda i, j, p: (i, 0, j))
    return call(
        body,
        place,
        (query, keys, values),
        [block] * 3,
        [
            sds((2, length, heads), jnp.bfloat16),
            sds((2, pairs, 2, length, length), jnp.bfloat16),
        ],
        [block, pl.BlockSpec((1, 1, 2, length, length), lambda i, j, p: (i, j, 0, 0, 0))],
        [],
        "attention",
        grid=(2, pairs),
        flops=2 * pairs * 2 * 8 * length * length * LANES,
    )


def attention_back(place, query, keys, values, probs, grad):
    _, length, heads = query.shape
    pairs = heads // LANES
    scale = 1.0 / math.sqrt(HEAD_DIM)

    def body(place_ref, q_ref, k_ref, v_ref, p_ref, g_ref, gq_ref, gk_ref, gv_ref):
        lane = lax.broadcasted_iota(jnp.int32, (length, LANES), 1)
        keys_t = k_ref[0].T
        values_block = v_ref[0]
        query_block = q_ref[0]
        grad_block = g_ref[0]
        grad_query = []
        grad_keys = []
        grad_values = []
        for head in range(2):
            inside = (lane >= head * HEAD_DIM) & (lane < (head + 1) * HEAD_DIM)
            grad_head = jnp.where(inside, grad_block, jnp.zeros_like(grad_block))
            keys_head = keys_t[head * HEAD_DIM : (head + 1) * HEAD_DIM, :]
            parts = []
            sum_keys = None
            sum_values = None
            for at in range(0, length, SPAN):
                span = min(SPAN, length - at)
                probs_low = p_ref[0, 0, head, :, at : at + span]
                probs_wide = wide(probs_low)
                grad_probs = dot_tail(values_block, grad_head[at : at + span, :])
                inner = jnp.sum(probs_wide * grad_probs, axis=0, keepdims=True)
                grad_scores = low(probs_wide * (grad_probs - inner))
                parts.append(dot(keys_head, grad_scores))
                to_keys = dot(grad_scores, query_block[at : at + span, :])
                to_values = dot(probs_low, grad_block[at : at + span, :])
                sum_keys = to_keys if sum_keys is None else sum_keys + to_keys
                sum_values = to_values if sum_values is None else sum_values + to_values
            grad_query.append(jnp.concatenate(parts, axis=1))
            grad_keys.append(sum_keys)
            grad_values.append(sum_values)
        first = lane < HEAD_DIM
        gq_ref[0] = low(jnp.concatenate(grad_query, axis=0).T * scale)
        gk_ref[0] = low(jnp.where(first, grad_keys[0], grad_keys[1]))
        gv_ref[0] = low(jnp.where(first, grad_values[0], grad_values[1]))

    block = pl.BlockSpec((1, length, LANES), lambda i, j, p: (i, 0, j))
    return call(
        body,
        place,
        (query, keys, values, probs, grad),
        [block] * 3
        + [pl.BlockSpec((1, 1, 2, length, length), lambda i, j, p: (i, j, 0, 0, 0)), block],
        [sds((2, length, heads), jnp.bfloat16)] * 3,
        [block] * 3,
        [],
        "attention_back",
        grid=(2, pairs),
        flops=2 * pairs * 2 * 10 * length * length * LANES,
    )


def project_out(place, mine, theirs, weight_mine, weight_theirs, rows, vectors):
    width, half = weight_mine.shape
    _, length, heads = mine.shape

    def body(
        place_ref, mine_ref, theirs_ref, wm_ref, wt_ref, own_ref, other_ref, vec_ref, middle_ref,
        normed_ref, total,
    ):
        core = place_ref[2]
        at_mine = pl.multiple_of(core * heads, heads)
        at_theirs = pl.multiple_of((1 - core) * heads, heads)
        for image, ref in enumerate((own_ref, other_ref)):
            for slot, weight in enumerate((wm_ref, wt_ref)):
                total[slot] = dot(mine_ref[image], weight[pl.ds(at_mine, heads), :]) + dot(
                    theirs_ref[1 - image], weight[pl.ds(at_theirs, heads), :]
                )
            for at in range(0, length, LANES):
                upto = at + LANES
                first, second = total[0, at:upto, :], total[1, at:upto, :]
                left = select(core, first, second)
                right = select(core, second, first)
                middle = (
                    wide(ref[at:upto, :])
                    + jnp.concatenate([left, right], axis=1)
                    + vec_ref[BIAS_OUT : BIAS_OUT + 1, :]
                )
                if image == 0:
                    middle_ref[at:upto, :] = middle
                normed_ref[image, at:upto, :] = low(
                    normalised(middle) * vec_ref[GAIN_TWO : GAIN_TWO + 1, :]
                    + vec_ref[BIAS_TWO : BIAS_TWO + 1, :]
                )

    return call(
        body,
        place,
        (mine, theirs, weight_mine, weight_theirs, *rows, vectors),
        [whole((2, length, heads))] * 2
        + [whole((width, half))] * 2
        + [whole((length, width))] * 2
        + [whole(vectors.shape)],
        [sds((length, width), jnp.float32), sds((2, length, width), jnp.bfloat16)],
        [whole((length, width)), whole((2, length, width))],
        [pltpu.VMEM((2, length, half), jnp.float32)],
        "project_out",
        flops=8 * length * width * half,
    )


def feed_forward(place, normed, cotangent, pieces, bias, chunk, running):
    count = len(pieces)
    z_size = count // 2
    _, part, wide_block = pieces[0].shape
    half_blocks = bias.shape[1]
    width = part * count
    blocks = half_blocks + width // wide_block
    _, length, _ = normed.shape
    first_call = running is None

    def body(place_ref, normed_ref, own_cot, other_cot, bias_ref, *refs):
        ins = refs[:count]
        refs = refs[count:]
        if not first_call:
            before, refs = refs[:4], refs[4:]
        out_own, out_other, gn_own, gn_other, bsum_ref, keep_ref, send_ref = refs[:7]
        w_in, w_down, normed_t, grads, sem, out_sem = refs[7:]
        step = pl.program_id(0)

        def copies():
            made = []
            for number, ref in enumerate(ins):
                z, x = shard_of(place_ref, number, z_size)
                row = pl.multiple_of((z * 2 + x) * part, part)
                row_in = pl.multiple_of(x * part, part)
                for b in range(half_blocks):
                    made.append(
                        pltpu.make_async_copy(
                            ref.at[b], w_in.at[b, pl.ds(row, part), :], sem.at[number * blocks + b]
                        )
                    )
                    made.append(
                        pltpu.make_async_copy(
                            ref.at[half_blocks + b],
                            w_down.at[z, pl.ds(row_in, part), pl.ds(b * wide_block, wide_block)],
                            sem.at[number * blocks + half_blocks + b],
                        )
                    )
            return made

        @pl.when(step == 0)
        def _():
            for copy in copies():
                copy.start()
            for image in range(2):
                normed_t[:, image * length : (image + 1) * length] = normed_ref[image].T
            for copy in copies():
                copy.wait()

        weight_in = w_in[step]
        weight_down = w_down[step]
        into = None
        down = None
        column_sum = None
        for image, cot_ref in enumerate((own_cot, other_cot)):
            preact = dot(normed_ref[image], weight_in) + bias_ref[0, 0]
            phi = 0.5 * (1.0 + lax.erf(preact * math.sqrt(0.5)))
            density = jnp.exp(-0.5 * preact * preact) * (1.0 / math.sqrt(2.0 * math.pi))
            hidden = low(preact * phi)
            slope = phi + preact * density
            cot = cot_ref[...]
            grad = low(dot_tail(cot, weight_down) * slope)
            out_ref, gn_ref = ((out_own, gn_own), (out_other, gn_other))[image]
            to_out = dot(hidden, weight_down)
            to_normed = dot_tail(grad, weight_in)

            @pl.when(step == 0)
            def _():
                if first_call:
                    out_ref[...] = to_out
                    gn_ref[...] = to_normed
                else:
                    out_ref[...] = before[image][...] + to_out
                    gn_ref[...] = before[2 + image][...] + to_normed

            @pl.when(step > 0)
            def _():
                out_ref[...] += to_out
                gn_ref[...] += to_normed

            partial = jnp.sum(wide(grad), axis=0, keepdims=True)
            column_sum = partial if image == 0 else column_sum + partial
            to_in = dot(normed_t[:, image * length : (image + 1) * length], grad)
            into = to_in if image == 0 else into + to_in
            to_down = dot(hidden.T, cot)
            down = to_down if image == 0 else down + to_down
        bsum_ref[0] = column_sum
        for z in range(z_size):
            for x in range(2):
                k = lax.rem(z + z_size - place_ref[0], z_size)
                dx = x + (1 - 2 * x) * place_ref[1]
                at = (z * 2 + x) * part
                grads[dx, k, step] = low(into[at : at + part, :])
        for x in range(2):
            k = lax.rem(step + z_size - place_ref[0], z_size)
            dx = x + (1 - 2 * x) * place_ref[1]
            for b in range(half_blocks):
                grads[dx, k, half_blocks + b] = low(
                    down[x * part : (x + 1) * part, b * wide_block : (b + 1) * wide_block]
                )

        @pl.when(step == half_blocks - 1)
        def _():
            for slot, ref in enumerate((keep_ref, send_ref)):
                pltpu.make_async_copy(grads.at[slot], ref, out_sem.at[slot]).start()
            for slot, ref in enumerate((keep_ref, send_ref)):
                pltpu.make_async_copy(grads.at[slot], ref, out_sem.at[slot]).wait()

    total = sds((length, width), jnp.float32)
    piece_out = sds((z_size, blocks, part, wide_block), jnp.bfloat16)
    carried = () if first_call else tuple(running)
    return call(
        body,
        place,
        (normed, *cotangent, bias, *pieces, *carried),
        [whole((2, length, width))]
        + [whole((length, width))] * 2
        + [pl.BlockSpec((1, 1, 1, wide_block), lambda b, p: (chunk, b, 0, 0))]
        + [any_spec()] * count
        + [whole((length, width))] * len(carried),
        [total] * 4 + [sds((half_blocks, 1, wide_block), jnp.float32)] + [piece_out] * 2,
        [whole((length, width))] * 4
        + [pl.BlockSpec((1, 1, wide_block), lambda b, p: (b, 0, 0))]
        + [any_spec()] * 2,
        [
            pltpu.VMEM((half_blocks, width, wide_block), jnp.bfloat16),
            pltpu.VMEM((half_blocks, wide_block, width), jnp.bfloat16),
            pltpu.VMEM((width, 2 * length), jnp.bfloat16),
            pltpu.VMEM((2, z_size, blocks, part, wide_block), jnp.bfloat16),
            pltpu.SemaphoreType.DMA((count * blocks,)),
            pltpu.SemaphoreType.DMA((2,)),
        ],
        "feed_forward",
        grid=(half_blocks,),
        flops=24 * length * width * half_blocks * wide_block,
    )


def norm_back(place, rows, vectors, gain_row, grad_own, grad_other, passed, tokens, finish=None):
    length, width = rows.shape

    def body(place_ref, rows_ref, vec_ref, own_ref, other_ref, pass_ref, *refs):
        step = pl.program_id(0)
        values = wide(rows_ref[...])
        if finish is not None:
            first_ref, second_ref, *refs = refs
            refs[1][...] = low(
                values + first_ref[...] + second_ref[...] + vec_ref[BIAS_DOWN : BIAS_DOWN + 1, :]
            )
        sum_ref = refs[0]
        centre = values - jnp.mean(values, axis=-1, keepdims=True)
        spread = jnp.mean(centre * centre, axis=-1, keepdims=True)
        inverse = lax.rsqrt(spread + ln_eps)
        unit = centre * inverse
        grad = own_ref[...] + other_ref[...]
        scaled = grad * vec_ref[gain_row : gain_row + 1, :]
        mean_one = jnp.mean(scaled, axis=-1, keepdims=True)
        mean_two = jnp.mean(scaled * unit, axis=-1, keepdims=True)
        result = wide(pass_ref[...]) + (scaled - mean_one - unit * mean_two) * inverse
        rounded = low(result)
        parts = [
            jnp.sum(grad * unit, axis=0, keepdims=True),
            jnp.sum(grad, axis=0, keepdims=True),
            jnp.sum(wide(rounded), axis=0, keepdims=True),
            jnp.zeros((5, width), jnp.float32),
        ]
        if finish is None:
            refs[1][...] = rounded
        else:
            refs[2][...] = result
            refs[3][...] = rounded
        joined = jnp.concatenate(parts, axis=0)

        @pl.when(step == 0)
        def _():
            sum_ref[...] = joined

        @pl.when(step > 0)
        def _():
            sum_ref[...] += joined

    block = pl.BlockSpec((LANES, width), lambda i, p: (i, 0))
    outs = [sds((8, width), jnp.float32), sds((tokens, width), jnp.bfloat16)]
    if finish is not None:
        outs += [sds((length, width), jnp.float32), sds((length, width), jnp.bfloat16)]
    ins = (rows, vectors, grad_own, grad_other, passed, *(finish or ()))
    return call(
        body,
        place,
        ins,
        [block, whole(vectors.shape)] + [block] * (len(ins) - 2),
        outs,
        [whole((8, width))] + [block] * (len(outs) - 1),
        [],
        "norm_back",
        grid=(length // LANES,),
    )


def out_back(place, grad_own, grad_other, mine, theirs, weight_mine, weight_theirs):
    width, half = weight_mine.shape
    z_size = lax.axis_size("z")
    part = width // (2 * z_size)
    _, length, heads = mine.shape

    def body(
        place_ref, own_ref, other_ref, own_half, other_half, mine_ref, theirs_ref, wm_ref, wt_ref,
        ga_ref, keep_ref, send_ref, turned, grads, out_sem,
    ):
        core = place_ref[2]
        at_mine = pl.multiple_of(core * heads, heads)
        at_theirs = pl.multiple_of((1 - core) * heads, heads)
        for image in range(2):
            lanes = slice(image * length, (image + 1) * length)
            turned[pl.ds(at_mine, heads), lanes] = mine_ref[image].T
            turned[pl.ds(at_theirs, heads), lanes] = theirs_ref[1 - image].T
        term = dot(turned[:, :length], own_half[...]) + dot(turned[:, length:], other_half[...])
        for z in range(z_size):
            for x in range(2):
                k = lax.rem(z + z_size - place_ref[0], z_size)
                dx = x + (1 - 2 * x) * place_ref[1]
                at = (z * 2 + x) * part
                grads[dx, k] = low(term[at : at + part, :])
        for slot, ref in enumerate((keep_ref, send_ref)):
            pltpu.make_async_copy(grads.at[slot], ref, out_sem.at[slot]).start()
        for image, ref in enumerate((own_ref, other_ref)):
            first, second = ref[:, :half], ref[:, half:]
            left = select(core, first, second)
            right = select(core, second, first)
            ga_ref[image] = low(
                dot_tail(left, wm_ref[pl.ds(at_mine, heads), :])
                + dot_tail(right, wt_ref[pl.ds(at_mine, heads), :])
            )
        for slot, ref in enumerate((keep_ref, send_ref)):
            pltpu.make_async_copy(grads.at[slot], ref, out_sem.at[slot]).wait()

    half_block = pl.BlockSpec((length, half), lambda i, p: (0, p[2]))
    piece_out = sds((z_size, part, half), jnp.bfloat16)
    return call(
        body,
        place,
        (grad_own, grad_other, grad_own, grad_other, mine, theirs, weight_mine, weight_theirs),
        [whole((length, width))] * 2
        + [half_block] * 2
        + [whole((2, length, heads))] * 2
        + [whole((width, half))] * 2,
        [sds((2, length, heads), jnp.bfloat16)] + [piece_out] * 2,
        [whole((2, length, heads))] + [any_spec()] * 2,
        [
            pltpu.VMEM((width, 2 * length), jnp.bfloat16),
            pltpu.VMEM((2, z_size, part, half), jnp.bfloat16),
            pltpu.SemaphoreType.DMA((2,)),
        ],
        "out_back",
        flops=8 * length * width * half,
    )


def qkv_term(place, normed, grad_q, grad_k, grad_v):
    _, length, width = normed.shape
    heads = grad_q.shape[-1]
    cols = 3 * heads

    def body(place_ref, normed_ref, gq_ref, gk_ref, gv_ref, sum_ref, keep_ref, send_ref, turned, grads, sem):
        z_size = grads.shape[1]
        part = grads.shape[2]
        for image in range(2):
            turned[:, image * length : (image + 1) * length] = normed_ref[image].T
        for slot, ref in enumerate((gq_ref, gk_ref, gv_ref)):
            term = dot(turned[:, :length], ref[0]) + dot(turned[:, length:], ref[1])
            for z in range(z_size):
                for x in range(2):
                    k = lax.rem(z + z_size - place_ref[0], z_size)
                    dx = x + (1 - 2 * x) * place_ref[1]
                    at = (z * 2 + x) * part
                    grads[dx, k, :, slot * heads : (slot + 1) * heads] = low(
                        term[at : at + part, :]
                    )
            sum_ref[slot : slot + 1, :] = jnp.sum(wide(ref[0]), axis=0, keepdims=True) + jnp.sum(
                wide(ref[1]), axis=0, keepdims=True
            )
        for slot, ref in enumerate((keep_ref, send_ref)):
            pltpu.make_async_copy(grads.at[slot], ref, sem.at[slot]).start()
        for slot, ref in enumerate((keep_ref, send_ref)):
            pltpu.make_async_copy(grads.at[slot], ref, sem.at[slot]).wait()

    z_size = lax.axis_size("z")
    part = width // (2 * z_size)
    piece_out = sds((z_size, part, cols), jnp.bfloat16)
    return call(
        body,
        place,
        (normed, grad_q, grad_k, grad_v),
        [whole((2, length, width))] + [whole((2, length, heads))] * 3,
        [sds((3, heads), jnp.float32)] + [piece_out] * 2,
        [whole((3, heads))] + [any_spec()] * 2,
        [
            pltpu.VMEM((width, 2 * length), jnp.bfloat16),
            pltpu.VMEM((2, z_size, part, cols), jnp.bfloat16),
            pltpu.SemaphoreType.DMA((2,)),
        ],
        "qkv_term",
        flops=4 * length * width * cols,
    )


def qkv_back(place, grad_q, grad_k, grad_v, pieces):
    count = len(pieces)
    z_size = count // 2
    cols = pieces[0].shape[1]
    part = pieces[0].shape[0] - TILE
    width = part * count
    heads = cols // 3
    length = grad_q.shape[1]

    def body(place_ref, gq_ref, gk_ref, gv_ref, *refs):
        ins, (own_ref, other_ref, weight, sem) = refs[:count], refs[count:]
        copies = []
        for number, ref in enumerate(ins):
            z, x = shard_of(place_ref, number, z_size)
            row = pl.multiple_of((z * 2 + x) * part, part)
            copy = pltpu.make_async_copy(
                ref.at[pl.ds(0, part), :], weight.at[pl.ds(row, part), :], sem.at[number]
            )
            copy.start()
            copies.append(copy)
        for copy in copies:
            copy.wait()
        for image, out_ref in enumerate((own_ref, other_ref)):
            out_ref[...] = (
                dot_tail(gq_ref[image], weight[:, :heads])
                + dot_tail(gk_ref[image], weight[:, heads : 2 * heads])
                + dot_tail(gv_ref[image], weight[:, 2 * heads :])
            )

    return call(
        body,
        place,
        (grad_q, grad_k, grad_v, *pieces),
        [whole((2, length, heads))] * 3 + [any_spec()] * count,
        [sds((length, width), jnp.float32)] * 2,
        [whole((length, width))] * 2,
        [pltpu.VMEM((width, cols), jnp.bfloat16), pltpu.SemaphoreType.DMA((count,))],
        "qkv_back",
        flops=4 * length * width * cols,
    )


def fold_x(place, keep, got):
    size = keep.shape[0]

    def body(place_ref, keep_ref, got_ref, *outs):
        for k, out in enumerate(outs):
            total = wide(keep_ref[k]) + wide(got_ref[k])
            out[...] = total if k == 0 else low(total)

    rest = keep.shape[1:]
    outs = [sds(rest, jnp.float32)] + [sds(rest, jnp.bfloat16)] * (size - 1)
    return call(
        body,
        place,
        (keep, got),
        [whole(keep.shape)] * 2,
        outs,
        [whole(rest)] * size,
        [],
        "fold_x",
    )


def fold_z(place, held, got):
    final = jnp.bfloat16 if lax.axis_size("y") == 2 else jnp.float32

    def body(place_ref, held_ref, *refs):
        total = held_ref[...]
        for ref in refs[:-1]:
            total = total + wide(ref[...])
        refs[-1][...] = total.astype(final)

    return call(
        body,
        place,
        (held, *got),
        [whole(held.shape)] * (1 + len(got)),
        [sds(held.shape, final)],
        [whole(held.shape)],
        [],
        "fold_z",
    )[0]


def to_column(row):
    return jnp.concatenate(
        [
            jnp.broadcast_to(row[:, at : at + LANES], (LANES, LANES)).T[:, :1]
            for at in range(0, row.shape[1], LANES)
        ],
        axis=0,
    )


def to_row(column):
    return jnp.concatenate(
        [
            jnp.broadcast_to(column[at : at + LANES, :], (LANES, LANES)).T[:1, :]
            for at in range(0, column.shape[0], LANES)
        ],
        axis=1,
    )


def statistics(place, kinds, shares, weights, states, images, extra=None):
    flat = [a for chunks in shares for pair in chunks for side in pair for a in side]
    counts = [[[len(side) for side in pair] for pair in chunks] for chunks in shares]
    amount = len(kinds)
    vectors = 0 if extra is None else len(extra[1])

    def body(place_ref, *refs):
        core = place_ref[2]
        refs = list(refs)

        def take(n):
            taken = refs[:n]
            del refs[:n]
            return taken

        share_refs = take(len(flat))
        weight_refs, state_refs = take(amount), take(amount)
        if vectors:
            (terms_ref,) = take(1)
            param_refs, moment_refs = take(vectors), take(vectors)
        grad_refs, row_refs = take(amount), take(amount)
        (pack_ref,) = take(1)
        if vectors:
            vector_grads, new_moments = take(vectors), take(vectors)
        at_pack = 0
        for number, kind in enumerate(kinds):
            grad_ref, weight_ref = grad_refs[number], weight_refs[number]
            rows, cols = weights[number].shape
            for chunk, pair in enumerate(counts[number]):
                sides = []
                for n in pair:
                    sides.append(share_refs[:n])
                    del share_refs[:n]

                def halves(index):
                    mine, theirs = [
                        sum([wide(ref[index]) for ref in side[1:]], wide(side[0][index]))
                        * (1.0 / images)
                        for side in sides
                    ]
                    return select(core, mine, theirs), select(core, theirs, mine)

                shape = sides[0][0].shape
                if kind == "in":
                    blocks, _, block = cols // 2 // CHUNKS // shape[2], shape[1], shape[2]
                    per = block // 2
                    for b in range(blocks):
                        for c, half in enumerate(halves(b)):
                            for i in range(2):
                                at = ((2 * b + i) * 2 + c) * CHUNKS * per + chunk * per
                                grad_ref[:, at : at + per] = half[:, i * per : (i + 1) * per]
                elif kind == "down":
                    _, part, block = shape
                    first = shape[0] - cols // block
                    for b in range(cols // block):
                        for c, half in enumerate(halves(first + b)):
                            at = (c * CHUNKS + chunk) * part
                            grad_ref[at : at + part, b * block : (b + 1) * block] = half
                else:
                    groups = cols // (2 * SPLIT[kind])
                    for slot in range(SPLIT[kind]):
                        lanes = slice(slot * groups, (slot + 1) * groups)
                        for c, half in enumerate(halves((slice(None), lanes))):
                            at = (2 * slot + c) * groups
                            grad_ref[:, at : at + groups] = half
            squared = grad_ref[...] * grad_ref[...]
            new_rows = 0.5 * to_column(state_refs[number][...]) + 0.5 * jnp.mean(
                squared, axis=1, keepdims=True
            )
            row_refs[number][...] = to_row(new_rows)
            pack_ref[0:1, at_pack : at_pack + cols] = jnp.sum(squared, axis=0, keepdims=True)
            pack_ref[1:2, at_pack : at_pack + cols] = jnp.sum(
                squared * (1.0 / new_rows), axis=0, keepdims=True
            )
            at_pack += cols
            weight = weight_ref[...]
            pack_ref[0:1, at_pack : at_pack + LANES] = jnp.broadcast_to(
                jnp.sum(new_rows, axis=0, keepdims=True), (1, LANES)
            )
            pack_ref[1:2, at_pack : at_pack + LANES] = jnp.broadcast_to(
                jnp.sum(jnp.sum(weight * weight, axis=0, keepdims=True), axis=1, keepdims=True),
                (1, LANES),
            )
            at_pack += LANES
        at = 0
        if vectors:
            place_row = lax.broadcasted_iota(jnp.int32, extra[0].shape, 0)
            here = place_row == place_ref[0] * 2 + place_ref[1]
            mine = jnp.sum(
                jnp.where(here, terms_ref[...], 0.0), axis=0, keepdims=True
            )
        for number in range(vectors):
            size = extra[1][number].shape[1]
            grad = mine[:, at : at + size] * (1.0 / images)
            at += size
            param = param_refs[number][...]
            moment = 0.5 * moment_refs[number][...] + 0.5 * grad * grad
            direction = grad * lax.rsqrt(moment)
            vector_grads[number][...] = grad
            new_moments[number][...] = moment
            for row, value in enumerate((direction, param)):
                pack_ref[row : row + 1, at_pack : at_pack + LANES] = jnp.broadcast_to(
                    jnp.sum(value * value, axis=1, keepdims=True), (1, LANES)
                )
            at_pack += LANES

    lanes = sum(weight.shape[1] + LANES for weight in weights) + vectors * LANES
    ins = [*flat, *weights, *states]
    outs = [sds(weight.shape, jnp.float32) for weight in weights]
    outs += [sds(state.shape, jnp.float32) for state in states]
    outs.append(sds((2, lanes), jnp.float32))
    if vectors:
        terms, params, moments = extra
        ins += [terms, *params, *moments]
        outs += [sds(a.shape, jnp.float32) for a in (*params, *moments)]
    results = call(
        body,
        place,
        tuple(ins),
        [whole(a.shape) for a in ins],
        outs,
        [whole(a.shape) for a in outs],
        [],
        "statistics",
    )
    return (
        results[:amount],
        results[amount : 2 * amount],
        results[2 * amount],
        results[2 * amount + 1 : 2 * amount + 1 + vectors],
        results[2 * amount + 1 + vectors :],
    )


SPLIT = {"out": 1, "qkv": 3}


def update(place, grads, new_rows, weights, cols_states, pack, group, extra=None):
    amount = len(weights)
    vectors = 0 if extra is None else len(extra[0])

    def body(place_ref, *refs):
        refs = list(refs)

        def take(n):
            taken = refs[:n]
            del refs[:n]
            return taken

        grad_refs, row_refs, weight_refs, state_refs = [take(amount) for _ in range(4)]
        (pack_ref,) = take(1)
        if vectors:
            vector_grads, moment_refs, param_refs = [take(vectors) for _ in range(3)]
        new_refs, col_refs = take(amount), take(amount)
        (clip_ref,) = take(1)
        param_outs = take(vectors)
        at_pack = 0
        clip_ref[...] = jnp.zeros(clip_ref.shape, jnp.float32)
        for number in range(amount):
            rows, cols = weights[number].shape
            rows_total = rows * group
            count = rows_total * cols
            new_cols = (
                0.5 * state_refs[number][...]
                + 0.5 * pack_ref[0:1, at_pack : at_pack + cols] / rows_total
            )
            col_refs[number][...] = new_cols
            by_rows = pack_ref[1:2, at_pack : at_pack + cols]
            at_pack += cols
            mean_rows = pack_ref[0:1, at_pack : at_pack + 1] / rows_total
            weight_total = pack_ref[1:2, at_pack : at_pack + 1]
            at_pack += LANES
            total = mean_rows * jnp.sum(by_rows / new_cols, axis=1, keepdims=True)
            clip = jnp.maximum(1.0, jnp.sqrt(total / count) / clip_level)
            step = step_rate * jnp.sqrt(weight_total / count) / clip
            clip_ref[number : number + 1, :] = jnp.broadcast_to(clip, (1, LANES))
            estimate = to_column(row_refs[number][...]) * (new_cols / mean_rows)
            new_refs[number][...] = weight_refs[number][...] - step * (
                grad_refs[number][...] * lax.rsqrt(estimate)
            )
        for number in range(vectors):
            count = extra[2][number].shape[1] * group
            total = pack_ref[0:1, at_pack : at_pack + 1]
            weight_total = pack_ref[1:2, at_pack : at_pack + 1]
            at_pack += LANES
            clip = jnp.maximum(1.0, jnp.sqrt(total / count) / clip_level)
            step = step_rate * jnp.sqrt(weight_total / count) / clip
            slot = amount + number
            clip_ref[slot : slot + 1, :] = jnp.broadcast_to(clip, (1, LANES))
            direction = vector_grads[number][...] * lax.rsqrt(moment_refs[number][...])
            param_outs[number][...] = param_refs[number][...] - step * direction

    ins = [*grads, *new_rows, *weights, *cols_states, pack]
    outs = [sds(a.shape, jnp.float32) for a in (*weights, *cols_states)]
    outs.append(sds((TILE, LANES), jnp.float32))
    if vectors:
        ins += [*extra[0], *extra[1], *extra[2]]
        outs += [sds(a.shape, jnp.float32) for a in extra[2]]
    results = call(
        body,
        place,
        tuple(ins),
        [whole(a.shape) for a in ins],
        outs,
        [whole(a.shape) for a in outs],
        [],
        "update",
    )
    return (
        results[:amount],
        results[amount : 2 * amount],
        results[2 * amount],
        results[2 * amount + 1 :],
    )


def pack_terms(place, sums_mid, sums_in, sums_qkv, hidden_sums, down_sums, sizes):
    z_size = lax.axis_size("z")
    shards = 2 * z_size
    per_shard = sizes[6] // 2 // CHUNKS
    heads = sums_qkv.shape[1]

    def body(place_ref, mid_ref, in_ref, qkv_ref, *refs):
        hidden_refs, (down_ref, out_ref) = refs[:CHUNKS], refs[CHUNKS:]
        core = place_ref[2]

        def put(slot, row):
            at, size = sum(sizes[:slot]), sizes[slot]
            for s in range(shards):
                out_ref[s : s + 1, at : at + size] = row[:, s * size : (s + 1) * size]

        put(0, in_ref[0:1, :])
        put(1, in_ref[1:2, :])
        zero = jnp.zeros((1, heads), jnp.float32)
        halves = []
        for slot in (0, 2):
            row = qkv_ref[slot : slot + 1, :]
            halves += [select(core, row, zero), select(core, zero, row)]
        put(2, jnp.concatenate(halves, axis=1))
        put(3, mid_ref[2:3, :])
        put(4, mid_ref[0:1, :])
        put(5, mid_ref[1:2, :])
        put(7, down_ref[...])
        none = jnp.zeros((1, per_shard), jnp.float32)
        for s in range(shards):
            for j in range(CHUNKS):
                i = s % 2
                row = hidden_refs[j][s // 2, :, i * per_shard : (i + 1) * per_shard]
                for c in range(2):
                    at = sum(sizes[:6]) + (c * CHUNKS + j) * per_shard
                    here = select(core, row, none) if c == 0 else select(core, none, row)
                    out_ref[s : s + 1, at : at + per_shard] = here

    ins = (sums_mid, sums_in, sums_qkv, *hidden_sums, down_sums)
    shape = (shards, sum(sizes))
    return call(
        body,
        place,
        ins,
        [whole(a.shape) for a in ins],
        [sds(shape, jnp.float32)],
        [whole(shape)],
        [],
        "pack_terms",
    )[0]


def on_device(
    inputs,
    cotangent,
    norm1_gain,
    norm1_bias,
    qkv_weight,
    qv_bias,
    out_weight,
    out_bias,
    norm2_gain,
    norm2_bias,
    in_weight,
    in_bias,
    down_weight,
    down_bias,
    qkv_rows,
    qkv_cols,
    out_rows,
    out_cols,
    in_rows,
    in_cols,
    down_rows,
    down_cols,
    norm1_gain_moment,
    norm1_bias_moment,
    qv_bias_moment,
    out_bias_moment,
    norm2_gain_moment,
    norm2_bias_moment,
    in_bias_moment,
    down_bias_moment,
):
    masters = [
        norm1_gain,
        norm1_bias,
        qkv_weight,
        qv_bias,
        out_weight,
        out_bias,
        norm2_gain,
        norm2_bias,
        in_weight,
        in_bias,
        down_weight,
        down_bias,
    ]
    moments = [
        norm1_gain_moment,
        norm1_bias_moment,
        qv_bias_moment,
        out_bias_moment,
        norm2_gain_moment,
        norm2_bias_moment,
        in_bias_moment,
        down_bias_moment,
    ]
    place = jnp.stack(
        [lax.axis_index("z"), lax.axis_index("x"), lax.axis_index("c")]
    ).astype(jnp.int32)
    group = lax.axis_size("z") * lax.axis_size("x")
    tokens = inputs.shape[0]
    images = (tokens // SEQ) * group * lax.axis_size("y") * lax.axis_size("c")
    as_row = lambda vector: vector.reshape(1, -1)
    params = [as_row(masters[number]) for number in VECTORS]
    moments = [as_row(moment) for moment in moments]
    sizes = [param.shape[1] for param in params]

    pieces_qkv = gather_pieces(prepare_qkv(place, qkv_weight, params))
    *shards_ff, rows_own, cot_own, down_sums = prepare_rest(
        place, in_weight, down_weight, out_weight, inputs, cotangent
    )
    rows = (rows_own, swap(rows_own, "c"))
    cot = (cot_own, swap(cot_own, "c"))
    pieces_ff = [gather_pieces(shard) for shard in shards_ff]
    weight_mine = gather_out(place, pieces_ff[0], shards_ff[1].shape[0])
    weight_theirs = swap(weight_mine, "c")

    normed, query, keys, values, vectors, hidden_bias = project_qkv(
        place, rows, pieces_qkv, sizes
    )
    attended, probs = attention(place, query, keys, values)
    attended_theirs = swap(attended, "c")
    middle, normed_mid = project_out(
        place, attended, attended_theirs, weight_mine, weight_theirs, rows, vectors
    )
    running = None
    hidden_sums = []
    shares_ff = []
    for j in range(CHUNKS):
        *running, sums, keep, send = feed_forward(
            place, normed_mid, cot, pieces_ff[j], hidden_bias, j, running
        )
        hidden_sums.append(sums)
        shares_ff.append(scatter_sum(place, keep, send))
    out_share, out_given, normed_share, normed_given = running
    sums_mid, output, grad_mid, grad_mid_low = norm_back(
        place,
        middle,
        vectors,
        GAIN_TWO,
        normed_share,
        swap(normed_given, "c"),
        cot_own,
        tokens,
        (out_share, swap(out_given, "c")),
    )
    grad_attended, keep, send = out_back(
        place,
        grad_mid_low,
        swap(grad_mid_low, "c"),
        attended,
        attended_theirs,
        weight_mine,
        weight_theirs,
    )
    share_out = scatter_sum(place, keep, send)
    grad_q, grad_k, grad_v = attention_back(place, query, keys, values, probs, grad_attended)
    sums_qkv, keep, send = qkv_term(place, normed, grad_q, grad_k, grad_v)
    share_qkv = scatter_sum(place, keep, send)
    share, given = qkv_back(place, grad_q, grad_k, grad_v, pieces_qkv)
    sums_in, input_grad = norm_back(
        place, rows_own, vectors, GAIN_ONE, share, swap(given, "c"), grad_mid, tokens
    )
    terms = sum_over(
        pack_terms(place, sums_mid, sums_in, sums_qkv, hidden_sums, down_sums, sizes),
        ("c", "x", "z", "y"),
    )

    early = ("in", "down", "out")
    weights = [in_weight, down_weight, out_weight]
    states = [as_row(state) for state in (in_rows, down_rows, out_rows)]
    grads_early, rows_early, pack, _, _ = statistics(
        place, early, [shares_ff, shares_ff, [share_out]], weights, states, images
    )
    new_early, cols_early, clips_early, _ = update(
        place,
        grads_early,
        rows_early,
        weights,
        [as_row(state) for state in (in_cols, down_cols, out_cols)],
        sum_over(pack, ("x", "z")),
        group,
    )
    grads_late, rows_late, pack, vector_grads, new_moments = statistics(
        place,
        ("qkv",),
        [[share_qkv]],
        [qkv_weight],
        [as_row(qkv_rows)],
        images,
        (terms, params, moments),
    )
    new_late, cols_late, clips_late, new_vectors = update(
        place,
        grads_late,
        rows_late,
        [qkv_weight],
        [as_row(qkv_cols)],
        sum_over(pack, ("x", "z")),
        group,
        (vector_grads, new_moments, params),
    )

    flat = lambda value: value.reshape(-1)
    grads = [None] * 12
    new_params = [None] * 12
    for number, slot in ((8, 0), (10, 1), (4, 2)):
        grads[number], new_params[number] = grads_early[slot], new_early[slot]
    grads[2], new_params[2] = grads_late[0], new_late[0]
    for slot, number in enumerate(VECTORS):
        grads[number] = flat(vector_grads[slot])
        new_params[number] = flat(new_vectors[slot])
    late, first = clips_late[:, 0], clips_early[:, 0]
    clip_factors = jnp.stack(
        [
            late[1],
            late[2],
            late[0],
            late[3],
            first[2],
            late[4],
            late[5],
            late[6],
            first[0],
            late[7],
            first[1],
            late[8],
        ]
    )
    return (
        output,
        input_grad,
        *grads,
        flat(rows_late[0]),
        flat(cols_late[0]),
        flat(rows_early[2]),
        flat(cols_early[2]),
        flat(rows_early[0]),
        flat(cols_early[0]),
        flat(rows_early[1]),
        flat(cols_early[1]),
        *[flat(moment) for moment in new_moments],
        *new_params,
        clip_factors,
    )


def solution(mesh):
    group = mesh.shape["fsdp"]
    split = Mesh(mesh.devices.reshape(group // 2, 2, mesh.shape["dp"] // 2, 2), ALL_AXES)
    in_specs = (
        P(("z", "x", "y", "c"), None),
        P(("z", "x", "y", "c"), None),
        P(("z", "x")),
        P(("z", "x")),
        P(("z", "x"), None),
        P(("z", "x")),
        P(("z", "x"), None),
        P(("z", "x")),
        P(("z", "x")),
        P(("z", "x")),
        P(("z", "x"), None),
        P(("z", "x")),
        P(("z", "x"), None),
        P(("z", "x")),
        P(("z", "x")),
        P(),
        P(("z", "x")),
        P(),
        P(("z", "x")),
        P(),
        P(("z", "x")),
        P(),
        P(("z", "x")),
        P(("z", "x")),
        P(("z", "x")),
        P(("z", "x")),
        P(("z", "x")),
        P(("z", "x")),
        P(("z", "x")),
        P(("z", "x")),
    )
    out_specs = (
        P(("z", "x", "y", "c"), None),
        P(("z", "x", "y", "c"), None),
        P(("z", "x")),
        P(("z", "x")),
        P(("z", "x"), None),
        P(("z", "x")),
        P(("z", "x"), None),
        P(("z", "x")),
        P(("z", "x")),
        P(("z", "x")),
        P(("z", "x"), None),
        P(("z", "x")),
        P(("z", "x"), None),
        P(("z", "x")),
        P(("z", "x")),
        P(),
        P(("z", "x")),
        P(),
        P(("z", "x")),
        P(),
        P(("z", "x")),
        P(),
        P(("z", "x")),
        P(("z", "x")),
        P(("z", "x")),
        P(("z", "x")),
        P(("z", "x")),
        P(("z", "x")),
        P(("z", "x")),
        P(("z", "x")),
        P(("z", "x")),
        P(("z", "x")),
        P(("z", "x"), None),
        P(("z", "x")),
        P(("z", "x"), None),
        P(("z", "x")),
        P(("z", "x")),
        P(("z", "x")),
        P(("z", "x"), None),
        P(("z", "x")),
        P(("z", "x"), None),
        P(("z", "x")),
        P(),
    )
    return jax.shard_map(
        on_device, mesh=split, in_specs=in_specs, out_specs=out_specs, check_vma=False
    )
```

```python
import math

import jax
import jax.numpy as jnp
from jax import lax
from jax.experimental import pallas as pl
from jax.experimental.pallas import tpu as pltpu
from jax.sharding import Mesh
from jax.sharding import PartitionSpec as P

HEAD_DIM = 64
SEQ = 577
LANES = 128
TILE = 16
SPAN = 256
CHUNKS = 2
VMEM_LIMIT = 60 * 1024 * 1024

ALL_AXES = ("z", "x", "y", "c")

MATRICES = (2, 4, 8, 10)
VECTORS = (0, 1, 3, 5, 6, 7, 9, 11)

ln_eps = 1e-06
clip_level = 0.05
step_rate = 4.0


def swap(value, axis):
    return lax.ppermute(value, axis, [(0, 1), (1, 0)])


def shift(value, axis, step):
    size = lax.axis_size(axis)
    return lax.ppermute(value, axis, [(i, (i + step) % size) for i in range(size)])


def partner(value, axis, step):
    size = lax.axis_size(axis)
    return lax.ppermute(value, axis, [(i, i ^ step) for i in range(size)])


def swap_both(value):
    return lax.ppermute(value, ("y", "c"), [(i, 3 - i) for i in range(4)])


def sum_over(value, axes):
    for axis in axes:
        step = 1
        while step < lax.axis_size(axis):
            value = value + partner(value, axis, step)
            step *= 2
    return value


def gather_rows(shard, by_y):
    near = lax.all_gather(shard, "z", axis=0, tiled=True)
    near = near.reshape(lax.axis_size("z"), *shard.shape)
    both = [near, swap(near, "x")]
    if not by_y:
        return [[one] for one in both]
    return [[one, swap(one, "y")] for one in both]


def scatter_sum(keep, send):
    total = low(wide(keep) + wide(swap(send, "x")))
    total = total.reshape(-1, total.shape[-1])
    mine = lax.psum_scatter(total, "z", scatter_dimension=0, tiled=True)
    if lax.axis_size("y") == 2:
        return [mine, swap(mine, "y")], [swap(mine, "c"), swap_both(mine)]
    total = lax.psum(wide(mine), "y")
    return [total], [swap(total, "c")]


def row_pad(length):
    return -(-length // LANES) * LANES


def dot(left, right):
    return jnp.dot(left, right, preferred_element_type=jnp.float32)


def dot_tail(left, right):
    return lax.dot_general(
        left, right, (((1,), (1,)), ((), ())), preferred_element_type=jnp.float32
    )


def low(value):
    return value.astype(jnp.bfloat16)


def wide(value):
    return value.astype(jnp.float32)


def any_spec():
    return pl.BlockSpec(memory_space=pl.ANY)


def whole(shape):
    return pl.BlockSpec(shape, lambda *_: (0,) * len(shape))


def sds(shape, dtype):
    return jax.ShapeDtypeStruct(shape, dtype)


def call(body, place, ins, in_specs, outs, out_specs, scratch, name, grid=(1,), flops=0):
    moved = sum(math.prod(a.shape) * a.dtype.itemsize for a in [*ins, *outs])
    return pl.pallas_call(
        body,
        out_shape=outs,
        grid_spec=pltpu.PrefetchScalarGridSpec(
            num_scalar_prefetch=1,
            grid=grid,
            in_specs=in_specs,
            out_specs=out_specs,
            scratch_shapes=scratch,
        ),
        compiler_params=pltpu.CompilerParams(
            vmem_limit_bytes=VMEM_LIMIT, dimension_semantics=("arbitrary",) * len(grid)
        ),
        cost_estimate=pl.CostEstimate(flops=flops, bytes_accessed=moved, transcendentals=0),
        name=name,
    )(place, *ins)


def shard_number(place_ref, z, dx):
    return z * 2 + dx + (1 - 2 * dx) * place_ref[1]


def normalised(rows):
    centre = rows - jnp.mean(rows, axis=-1, keepdims=True)
    spread = jnp.mean(centre * centre, axis=-1, keepdims=True)
    return centre * lax.rsqrt(spread + ln_eps)


def select(core, first, second):
    return jnp.where(core == 0, first, second)


def prepare_qkv(place, weight, vectors):
    part, cols = weight.shape
    width = cols // 2
    half = cols // 6
    parts = 2
    sizes = [vector.shape[-1] for vector in vectors]

    def body(place_ref, weight_ref, *refs):
        refs, (out_ref, *halves) = refs[: len(sizes)], (refs[-1], *refs[len(sizes) : -1])
        core = place_ref[2]
        for slot in range(3):
            at = 2 * slot * half
            out_ref[:part, slot * half : (slot + 1) * half] = low(
                select(core, weight_ref[:, at : at + half], weight_ref[:, at + half : at + 2 * half])
            )
        at = 0
        for ref, size in zip(refs, sizes):
            out_ref[part:, at : at + size] = low(jnp.broadcast_to(ref[...], (TILE, size)))
            at += size
        for number, ref in enumerate(halves):
            ref[...] = out_ref[:, number * width // parts : (number + 1) * width // parts]

    shape = (part + TILE, width // parts)
    return call(
        body,
        place,
        (weight, *vectors),
        [whole((part, cols))] + [whole((1, size)) for size in sizes],
        [sds(shape, jnp.bfloat16)] * parts,
        [whole(shape)] * parts,
        [pltpu.VMEM((part + TILE, width), jnp.bfloat16)],
        "prepare_qkv",
    )


def prepare_rest(place, in_weight, down_weight, out_weight, inputs, cotangent, by_y):
    part, hidden = in_weight.shape
    width = down_weight.shape[1]
    per_core = down_weight.shape[0] // 2
    per_shard = per_core // CHUNKS
    shards = hidden // (2 * per_core)
    tokens = inputs.shape[0]
    length = row_pad(tokens)
    even = tokens // TILE * TILE
    cut = 2 if by_y else 1
    rows_in, rows_down, rows_out = part // cut, per_shard // cut, part // cut // 2

    def body(place_ref, in_ref, down_ref, out_w_ref, rows_ref, cot_ref, *refs):
        pieces, (rows_out_ref, cot_out, sum_ref) = refs[:CHUNKS], refs[CHUNKS:]
        core, y = place_ref[2], place_ref[3]

        def pick(ref, row, count, step, col, cols, by_row):
            def of_core(r):
                if by_row:
                    return select(
                        core, ref[r : r + count, col : col + cols], ref[r + step : r + step + count, col : col + cols]
                    )
                return select(
                    core, ref[r : r + count, col : col + cols], ref[r : r + count, col + step : col + step + cols]
                )

            if cut == 1:
                return low(of_core(row))
            return low(select(y, of_core(row), of_core(row + count)))

        for j in range(CHUNKS):
            for s in range(shards):
                at = s * 2 * per_core + j * per_shard
                pieces[j][:rows_in, s * per_shard : (s + 1) * per_shard] = pick(
                    in_ref, 0, rows_in, per_core, at, per_shard, False
                )
            pieces[j][rows_in : rows_in + rows_down, :] = pick(
                down_ref, j * per_shard, rows_down, per_core, 0, width, True
            )
        half = width // 2
        branch = pick(out_w_ref, 0, 2 * rows_out, half, 0, half, False)
        for side in range(2):
            pieces[0][rows_in + rows_down :, side * half : (side + 1) * half] = branch[
                side * rows_out : (side + 1) * rows_out, :
            ]
        row = lax.broadcasted_iota(jnp.int32, (length - even, width), 0)
        for ref, to in ((rows_ref, rows_out_ref), (cot_ref, cot_out)):
            to[:even, :] = ref[:even, :]
            last = jnp.zeros((length - even, width), jnp.float32)
            for extra in range(tokens - even):
                one = wide(ref[even + extra : even + extra + 1, :])
                last = jnp.where(row == extra, one, last)
            to[even:, :] = low(last)
        sum_ref[...] = jnp.sum(wide(cot_out[...]), axis=0, keepdims=True)

    counts = [rows_in + rows_down + (rows_out if j == 0 else 0) for j in range(CHUNKS)]
    outs = [sds((count, width), jnp.bfloat16) for count in counts]
    outs += [sds((length, width), jnp.bfloat16)] * 2 + [sds((1, width), jnp.float32)]
    ins = (in_weight, down_weight, out_weight, inputs, cotangent)
    return call(
        body,
        place,
        ins,
        [whole(a.shape) for a in ins],
        outs,
        [whole(a.shape) for a in outs],
        [],
        "prepare_rest",
    )


GAIN_ONE, BIAS_ONE, BIAS_OUT, GAIN_TWO, BIAS_TWO, BIAS_DOWN = range(6)


def project_qkv(place, rows, pieces, sizes):
    flat = [one for piece in pieces for (one,) in piece]
    z_size, part, cols_part = flat[0].shape
    part -= TILE
    count = 2 * z_size
    cols = cols_part * len(pieces)
    width = part * count
    heads = cols // 3
    length = rows[0].shape[0]
    scale = 1.0 / math.sqrt(HEAD_DIM)
    starts = [sum(sizes[:number]) for number in range(len(sizes))]
    per_shard = sizes[6] // 2 // CHUNKS
    blocks = count // 2

    def body(place_ref, own_ref, other_ref, *refs):
        ins, refs = refs[: len(flat)], refs[len(flat) :]
        normed_ref, q_ref, k_ref, v_ref, vec_ref, hidden_bias_ref, weight, packed, sem = refs
        core = place_ref[2]
        copies = []
        for number, ref in enumerate(ins):
            lanes = pl.ds(number // 2 * cols_part, cols_part)
            for z in range(z_size):
                s = shard_number(place_ref, z, number % 2)
                row = pl.multiple_of(s * part, part)
                for source, to in (
                    (ref.at[z, pl.ds(0, part), :], weight.at[pl.ds(row, part), lanes]),
                    (ref.at[z, pl.ds(part, TILE), :], packed.at[s, :, lanes]),
                ):
                    copy = pltpu.make_async_copy(source, to, sem.at[len(copies)])
                    copy.start()
                    copies.append(copy)
        for copy in copies:
            copy.wait()

        def vector(slot, shards=range(count)):
            at, size = starts[slot], sizes[slot]
            return jnp.concatenate(
                [wide(packed[s, 0:1, at : at + size]) for s in shards], axis=1
            )

        gain, bias = vector(0), vector(1)
        for row, value in (
            (GAIN_ONE, gain),
            (BIAS_ONE, bias),
            (BIAS_OUT, vector(3)),
            (GAIN_TWO, vector(4)),
            (BIAS_TWO, vector(5)),
            (BIAS_DOWN, vector(7)),
        ):
            vec_ref[row : row + 1, :] = value
        vec_ref[6:8, :] = jnp.zeros((2, width), jnp.float32)
        for j in range(CHUNKS):
            for b in range(blocks):
                for i in range(2):
                    at = starts[6] + j * per_shard
                    to = at + sizes[6] // 2
                    hidden_bias_ref[j, b, :, i * per_shard : (i + 1) * per_shard] = wide(
                        select(
                            core,
                            wide(packed[2 * b + i, 0:1, at : at + per_shard]),
                            wide(packed[2 * b + i, 0:1, to : to + per_shard]),
                        )
                    )
        bias_q = vector(2, range(blocks))
        bias_v = vector(2, range(blocks, count))
        bias_q = select(core, bias_q[:, :heads], bias_q[:, heads:])
        bias_v = select(core, bias_v[:, :heads], bias_v[:, heads:])
        for image, ref in enumerate((own_ref, other_ref)):
            for at in range(0, length, LANES):
                block = wide(ref[at : at + LANES, :])
                normed_ref[image, at : at + LANES, :] = low(normalised(block) * gain + bias)
            normed = normed_ref[image]
            query = low(dot(normed, weight[:, :heads]) + bias_q)
            q_ref[image] = low(wide(query) * scale)
            k_ref[image] = low(dot(normed, weight[:, heads : 2 * heads]))
            v_ref[image] = low(dot(normed, weight[:, 2 * heads :]) + bias_v)

    part_out = sds((2, length, heads), jnp.bfloat16)
    return call(
        body,
        place,
        (*rows, *flat),
        [whole((length, width))] * 2 + [any_spec()] * len(flat),
        [sds((2, length, width), jnp.bfloat16)]
        + [part_out] * 3
        + [
            sds((8, width), jnp.float32),
            sds((CHUNKS, blocks, 1, 2 * per_shard), jnp.float32),
        ],
        [whole((2, length, width))]
        + [whole((2, length, heads))] * 3
        + [whole((8, width)), whole((CHUNKS, blocks, 1, 2 * per_shard))],
        [
            pltpu.VMEM((width, cols), jnp.bfloat16),
            pltpu.VMEM((count, TILE, cols), jnp.bfloat16),
            pltpu.SemaphoreType.DMA((2 * z_size * len(flat),)),
        ],
        "project_qkv",
        flops=4 * length * width * cols,
    )


def gather_out(place, pieces, first):
    cut = len(pieces[0])
    z_size, total, width = pieces[0][0].shape
    rows = total - first
    half = width // 2
    part = width // (2 * z_size)

    def body(place_ref, *refs):
        ins, out_ref, sem = refs[: 2 * cut], refs[2 * cut], refs[2 * cut + 1]
        copies = []
        for number, ref in enumerate(ins):
            dx, h = number // cut, number % cut
            y = h + (1 - 2 * h) * place_ref[3] if cut == 2 else 0
            for z in range(z_size):
                for side in range(2):
                    row = shard_number(place_ref, z, dx) * part + (2 * y + side) * rows
                    copy = pltpu.make_async_copy(
                        ref.at[z, pl.ds(first, rows), pl.ds(side * half, half)],
                        out_ref.at[pl.ds(pl.multiple_of(row, rows), rows), :],
                        sem.at[len(copies)],
                    )
                    copy.start()
                    copies.append(copy)
        for copy in copies:
            copy.wait()

    shape = (width, half)
    return call(
        body,
        place,
        tuple(one for side in pieces for one in side),
        [any_spec()] * (2 * cut),
        [sds(shape, jnp.bfloat16)],
        [whole(shape)],
        [pltpu.SemaphoreType.DMA((2 * cut * z_size * 2,))],
        "gather_out",
    )[0]


def attention(place, query, keys, values):
    _, length, heads = query.shape
    pairs = heads // LANES

    def body(place_ref, q_ref, k_ref, v_ref, out_ref, probs_ref):
        lane = lax.broadcasted_iota(jnp.int32, (length, LANES), 1)
        keys_block = k_ref[0]
        values_t = v_ref[0].T
        query_block = q_ref[0]
        mixed = []
        for head in range(2):
            inside = (lane >= head * HEAD_DIM) & (lane < (head + 1) * HEAD_DIM)
            query_head = jnp.where(inside, query_block, jnp.zeros_like(query_block))
            values_head = values_t[head * HEAD_DIM : (head + 1) * HEAD_DIM, :]
            parts = []
            for at in range(0, length, SPAN):
                span = min(SPAN, length - at)
                scores = dot_tail(keys_block, query_head[at : at + span, :])
                key_row = lax.broadcasted_iota(jnp.int32, scores.shape, 0)
                scores = jnp.where(key_row < SEQ, scores, -1e30)
                highest = jnp.max(scores, axis=0, keepdims=True)
                exponent = jnp.exp(scores - highest)
                summed = jnp.sum(exponent, axis=0, keepdims=True)
                probs = low(exponent * (1.0 / summed))
                probs_ref[0, 0, head, :, at : at + span] = probs
                parts.append(dot(values_head, probs))
            mixed.append(jnp.concatenate(parts, axis=1))
        out_ref[0] = low(jnp.concatenate(mixed, axis=0).T)

    block = pl.BlockSpec((1, length, LANES), lambda i, j, p: (i, 0, j))
    return call(
        body,
        place,
        (query, keys, values),
        [block] * 3,
        [
            sds((2, length, heads), jnp.bfloat16),
            sds((2, pairs, 2, length, length), jnp.bfloat16),
        ],
        [block, pl.BlockSpec((1, 1, 2, length, length), lambda i, j, p: (i, j, 0, 0, 0))],
        [],
        "attention",
        grid=(2, pairs),
        flops=2 * pairs * 2 * 8 * length * length * LANES,
    )


def attention_back(place, query, keys, values, probs, grad):
    _, length, heads = query.shape
    pairs = heads // LANES
    scale = 1.0 / math.sqrt(HEAD_DIM)

    def body(place_ref, q_ref, k_ref, v_ref, p_ref, g_ref, gq_ref, gk_ref, gv_ref):
        lane = lax.broadcasted_iota(jnp.int32, (length, LANES), 1)
        keys_t = k_ref[0].T
        values_block = v_ref[0]
        query_block = q_ref[0]
        grad_block = g_ref[0]
        grad_query = []
        grad_keys = []
        grad_values = []
        for head in range(2):
            inside = (lane >= head * HEAD_DIM) & (lane < (head + 1) * HEAD_DIM)
            grad_head = jnp.where(inside, grad_block, jnp.zeros_like(grad_block))
            keys_head = keys_t[head * HEAD_DIM : (head + 1) * HEAD_DIM, :]
            parts = []
            sum_keys = None
            sum_values = None
            for at in range(0, length, SPAN):
                span = min(SPAN, length - at)
                probs_low = p_ref[0, 0, head, :, at : at + span]
                probs_wide = wide(probs_low)
                grad_probs = dot_tail(values_block, grad_head[at : at + span, :])
                inner = jnp.sum(probs_wide * grad_probs, axis=0, keepdims=True)
                grad_scores = low(probs_wide * (grad_probs - inner))
                parts.append(dot(keys_head, grad_scores))
                to_keys = dot(grad_scores, query_block[at : at + span, :])
                to_values = dot(probs_low, grad_block[at : at + span, :])
                sum_keys = to_keys if sum_keys is None else sum_keys + to_keys
                sum_values = to_values if sum_values is None else sum_values + to_values
            grad_query.append(jnp.concatenate(parts, axis=1))
            grad_keys.append(sum_keys)
            grad_values.append(sum_values)
        first = lane < HEAD_DIM
        gq_ref[0] = low(jnp.concatenate(grad_query, axis=0).T * scale)
        gk_ref[0] = low(jnp.where(first, grad_keys[0], grad_keys[1]))
        gv_ref[0] = low(jnp.where(first, grad_values[0], grad_values[1]))

    block = pl.BlockSpec((1, length, LANES), lambda i, j, p: (i, 0, j))
    return call(
        body,
        place,
        (query, keys, values, probs, grad),
        [block] * 3
        + [pl.BlockSpec((1, 1, 2, length, length), lambda i, j, p: (i, j, 0, 0, 0)), block],
        [sds((2, length, heads), jnp.bfloat16)] * 3,
        [block] * 3,
        [],
        "attention_back",
        grid=(2, pairs),
        flops=2 * pairs * 2 * 10 * length * length * LANES,
    )


def project_out(place, mine, theirs, weight_mine, weight_theirs, rows, vectors):
    width, half = weight_mine.shape
    _, length, heads = mine.shape

    def body(
        place_ref, mine_ref, theirs_ref, wm_ref, wt_ref, own_ref, other_ref, vec_ref, middle_ref,
        normed_ref, total,
    ):
        core = place_ref[2]
        at_mine = pl.multiple_of(core * heads, heads)
        at_theirs = pl.multiple_of((1 - core) * heads, heads)
        for image, ref in enumerate((own_ref, other_ref)):
            for slot, weight in enumerate((wm_ref, wt_ref)):
                total[slot] = dot(mine_ref[image], weight[pl.ds(at_mine, heads), :]) + dot(
                    theirs_ref[1 - image], weight[pl.ds(at_theirs, heads), :]
                )
            for at in range(0, length, LANES):
                upto = at + LANES
                first, second = total[0, at:upto, :], total[1, at:upto, :]
                left = select(core, first, second)
                right = select(core, second, first)
                middle = (
                    wide(ref[at:upto, :])
                    + jnp.concatenate([left, right], axis=1)
                    + vec_ref[BIAS_OUT : BIAS_OUT + 1, :]
                )
                if image == 0:
                    middle_ref[at:upto, :] = middle
                normed_ref[image, at:upto, :] = low(
                    normalised(middle) * vec_ref[GAIN_TWO : GAIN_TWO + 1, :]
                    + vec_ref[BIAS_TWO : BIAS_TWO + 1, :]
                )

    return call(
        body,
        place,
        (mine, theirs, weight_mine, weight_theirs, *rows, vectors),
        [whole((2, length, heads))] * 2
        + [whole((width, half))] * 2
        + [whole((length, width))] * 2
        + [whole(vectors.shape)],
        [sds((length, width), jnp.float32), sds((2, length, width), jnp.bfloat16)],
        [whole((length, width)), whole((2, length, width))],
        [pltpu.VMEM((2, length, half), jnp.float32)],
        "project_out",
        flops=8 * length * width * half,
    )


def feed_forward(place, normed, cotangent, pieces, bias, chunk, running):
    cut = len(pieces[0])
    z_size, _, width = pieces[0][0].shape
    blocks, block = bias.shape[1], bias.shape[3]
    hidden_width = blocks * block
    part = width // (2 * z_size)
    per_shard = hidden_width // (2 * z_size)
    rows_in, rows_down = part // cut, per_shard // cut
    in_block = block // per_shard
    _, length, _ = normed.shape
    first_call = running is None

    def body(place_ref, normed_ref, own_cot, other_cot, bias_ref, *refs):
        ins, refs = refs[: 2 * cut], refs[2 * cut :]
        if not first_call:
            before, refs = refs[:4], refs[4:]
        out_own, out_other, gn_own, gn_other, bsum_ref, keep_ref, send_ref = refs[:7]
        w_in, w_down, normed_t, grads, sem, out_sem = refs[7:]
        step = pl.program_id(0)

        def copies():
            made = []
            for number, ref in enumerate(ins):
                dx, h = number // cut, number % cut
                y = h + (1 - 2 * h) * place_ref[3] if cut == 2 else 0
                for z in range(z_size):
                    s = shard_number(place_ref, z, dx)
                    for weight, at, rows, of_shard in (
                        (w_in, 0, rows_in, part),
                        (w_down, rows_in, rows_down, per_shard),
                    ):
                        row = pl.multiple_of(s * of_shard + y * rows, rows)
                        made.append(
                            pltpu.make_async_copy(
                                ref.at[z, pl.ds(at, rows), :],
                                weight.at[pl.ds(row, rows), :],
                                sem.at[len(made)],
                            )
                        )
            return made

        @pl.when(step == 0)
        def _():
            for copy in copies():
                copy.start()
            for image in range(2):
                normed_t[:, image * length : (image + 1) * length] = normed_ref[image].T
            for copy in copies():
                copy.wait()

        at_block = pl.multiple_of(step * block, block)
        weight_in = w_in[:, pl.ds(at_block, block)]
        weight_down = w_down[pl.ds(at_block, block), :]
        into = None
        down = None
        column_sum = None
        for image, cot_ref in enumerate((own_cot, other_cot)):
            preact = dot(normed_ref[image], weight_in) + bias_ref[0, 0]
            phi = 0.5 * (1.0 + lax.erf(preact * math.sqrt(0.5)))
            density = jnp.exp(-0.5 * preact * preact) * (1.0 / math.sqrt(2.0 * math.pi))
            hidden = low(preact * phi)
            slope = phi + preact * density
            cot = cot_ref[...]
            grad = low(dot_tail(cot, weight_down) * slope)
            out_ref, gn_ref = ((out_own, gn_own), (out_other, gn_other))[image]
            to_out = dot(hidden, weight_down)
            to_normed = dot_tail(grad, weight_in)

            @pl.when(step == 0)
            def _():
                if first_call:
                    out_ref[...] = to_out
                    gn_ref[...] = to_normed
                else:
                    out_ref[...] = before[image][...] + to_out
                    gn_ref[...] = before[2 + image][...] + to_normed

            @pl.when(step > 0)
            def _():
                out_ref[...] += to_out
                gn_ref[...] += to_normed

            partial = jnp.sum(wide(grad), axis=0, keepdims=True)
            column_sum = partial if image == 0 else column_sum + partial
            to_in = dot(normed_t[:, image * length : (image + 1) * length], grad)
            into = to_in if image == 0 else into + to_in
            to_down = dot(hidden.T, cot)
            down = to_down if image == 0 else down + to_down
        bsum_ref[0] = column_sum
        for z in range(z_size):
            for x in range(2):
                dx = x + (1 - 2 * x) * place_ref[1]
                at = (z * 2 + x) * part
                grads[dx, z, :part, pl.ds(at_block, block)] = low(into[at : at + part, :])
        for i in range(in_block):
            s = step * in_block + i
            z, x = s // 2, lax.rem(s, 2)
            dx = x + (1 - 2 * x) * place_ref[1]
            grads[dx, z, part:, :] = low(down[i * per_shard : (i + 1) * per_shard, :])

        @pl.when(step == blocks - 1)
        def _():
            for slot, ref in enumerate((keep_ref, send_ref)):
                pltpu.make_async_copy(grads.at[slot], ref, out_sem.at[slot]).start()
            for slot, ref in enumerate((keep_ref, send_ref)):
                pltpu.make_async_copy(grads.at[slot], ref, out_sem.at[slot]).wait()

    total = sds((length, width), jnp.float32)
    piece_out = sds((z_size, part + per_shard, width), jnp.bfloat16)
    carried = () if first_call else tuple(running)
    return call(
        body,
        place,
        (normed, *cotangent, bias, *[one for side in pieces for one in side], *carried),
        [whole((2, length, width))]
        + [whole((length, width))] * 2
        + [pl.BlockSpec((1, 1, 1, block), lambda b, p: (chunk, b, 0, 0))]
        + [any_spec()] * (2 * cut)
        + [whole((length, width))] * len(carried),
        [total] * 4 + [sds((blocks, 1, block), jnp.float32)] + [piece_out] * 2,
        [whole((length, width))] * 4
        + [pl.BlockSpec((1, 1, block), lambda b, p: (b, 0, 0))]
        + [any_spec()] * 2,
        [
            pltpu.VMEM((width, hidden_width), jnp.bfloat16),
            pltpu.VMEM((hidden_width, width), jnp.bfloat16),
            pltpu.VMEM((width, 2 * length), jnp.bfloat16),
            pltpu.VMEM((2, z_size, part + per_shard, width), jnp.bfloat16),
            pltpu.SemaphoreType.DMA((4 * cut * z_size,)),
            pltpu.SemaphoreType.DMA((2,)),
        ],
        "feed_forward",
        grid=(blocks,),
        flops=24 * length * width * hidden_width,
    )


def norm_back(place, rows, vectors, gain_row, grad_own, grad_other, passed, tokens, finish=None):
    length, width = rows.shape

    def body(place_ref, rows_ref, vec_ref, own_ref, other_ref, pass_ref, *refs):
        step = pl.program_id(0)
        values = wide(rows_ref[...])
        if finish is not None:
            first_ref, second_ref, *refs = refs
            refs[1][...] = low(
                values + first_ref[...] + second_ref[...] + vec_ref[BIAS_DOWN : BIAS_DOWN + 1, :]
            )
        sum_ref = refs[0]
        centre = values - jnp.mean(values, axis=-1, keepdims=True)
        spread = jnp.mean(centre * centre, axis=-1, keepdims=True)
        inverse = lax.rsqrt(spread + ln_eps)
        unit = centre * inverse
        grad = own_ref[...] + other_ref[...]
        scaled = grad * vec_ref[gain_row : gain_row + 1, :]
        mean_one = jnp.mean(scaled, axis=-1, keepdims=True)
        mean_two = jnp.mean(scaled * unit, axis=-1, keepdims=True)
        result = wide(pass_ref[...]) + (scaled - mean_one - unit * mean_two) * inverse
        rounded = low(result)
        parts = [
            jnp.sum(grad * unit, axis=0, keepdims=True),
            jnp.sum(grad, axis=0, keepdims=True),
            jnp.sum(wide(rounded), axis=0, keepdims=True),
            jnp.zeros((5, width), jnp.float32),
        ]
        if finish is None:
            refs[1][...] = rounded
        else:
            refs[2][...] = result
            refs[3][...] = rounded
        joined = jnp.concatenate(parts, axis=0)

        @pl.when(step == 0)
        def _():
            sum_ref[...] = joined

        @pl.when(step > 0)
        def _():
            sum_ref[...] += joined

    block = pl.BlockSpec((LANES, width), lambda i, p: (i, 0))
    outs = [sds((8, width), jnp.float32), sds((tokens, width), jnp.bfloat16)]
    if finish is not None:
        outs += [sds((length, width), jnp.float32), sds((length, width), jnp.bfloat16)]
    ins = (rows, vectors, grad_own, grad_other, passed, *(finish or ()))
    return call(
        body,
        place,
        ins,
        [block, whole(vectors.shape)] + [block] * (len(ins) - 2),
        outs,
        [whole((8, width))] + [block] * (len(outs) - 1),
        [],
        "norm_back",
        grid=(length // LANES,),
    )


def out_back(place, grad_own, grad_other, mine, theirs, weight_mine, weight_theirs):
    width, half = weight_mine.shape
    z_size = lax.axis_size("z")
    part = width // (2 * z_size)
    _, length, heads = mine.shape

    def body(
        place_ref, own_ref, other_ref, own_half, other_half, mine_ref, theirs_ref, wm_ref, wt_ref,
        ga_ref, keep_ref, send_ref, turned, grads, out_sem,
    ):
        core = place_ref[2]
        at_mine = pl.multiple_of(core * heads, heads)
        at_theirs = pl.multiple_of((1 - core) * heads, heads)
        for image in range(2):
            lanes = slice(image * length, (image + 1) * length)
            turned[pl.ds(at_mine, heads), lanes] = mine_ref[image].T
            turned[pl.ds(at_theirs, heads), lanes] = theirs_ref[1 - image].T
        term = dot(turned[:, :length], own_half[...]) + dot(turned[:, length:], other_half[...])
        for z in range(z_size):
            for x in range(2):
                dx = x + (1 - 2 * x) * place_ref[1]
                at = (z * 2 + x) * part
                grads[dx, z] = low(term[at : at + part, :])
        for slot, ref in enumerate((keep_ref, send_ref)):
            pltpu.make_async_copy(grads.at[slot], ref, out_sem.at[slot]).start()
        for image, ref in enumerate((own_ref, other_ref)):
            first, second = ref[:, :half], ref[:, half:]
            left = select(core, first, second)
            right = select(core, second, first)
            ga_ref[image] = low(
                dot_tail(left, wm_ref[pl.ds(at_mine, heads), :])
                + dot_tail(right, wt_ref[pl.ds(at_mine, heads), :])
            )
        for slot, ref in enumerate((keep_ref, send_ref)):
            pltpu.make_async_copy(grads.at[slot], ref, out_sem.at[slot]).wait()

    half_block = pl.BlockSpec((length, half), lambda i, p: (0, p[2]))
    piece_out = sds((z_size, part, half), jnp.bfloat16)
    return call(
        body,
        place,
        (grad_own, grad_other, grad_own, grad_other, mine, theirs, weight_mine, weight_theirs),
        [whole((length, width))] * 2
        + [half_block] * 2
        + [whole((2, length, heads))] * 2
        + [whole((width, half))] * 2,
        [sds((2, length, heads), jnp.bfloat16)] + [piece_out] * 2,
        [whole((2, length, heads))] + [any_spec()] * 2,
        [
            pltpu.VMEM((width, 2 * length), jnp.bfloat16),
            pltpu.VMEM((2, z_size, part, half), jnp.bfloat16),
            pltpu.SemaphoreType.DMA((2,)),
        ],
        "out_back",
        flops=8 * length * width * half,
    )


def qkv_term(place, normed, grad_q, grad_k, grad_v):
    _, length, width = normed.shape
    heads = grad_q.shape[-1]
    cols = 3 * heads

    def body(place_ref, normed_ref, gq_ref, gk_ref, gv_ref, sum_ref, keep_ref, send_ref, turned, grads, sem):
        z_size = grads.shape[1]
        part = grads.shape[2]
        for image in range(2):
            turned[:, image * length : (image + 1) * length] = normed_ref[image].T
        for slot, ref in enumerate((gq_ref, gk_ref, gv_ref)):
            term = dot(turned[:, :length], ref[0]) + dot(turned[:, length:], ref[1])
            for z in range(z_size):
                for x in range(2):
                    dx = x + (1 - 2 * x) * place_ref[1]
                    at = (z * 2 + x) * part
                    grads[dx, z, :, slot * heads : (slot + 1) * heads] = low(
                        term[at : at + part, :]
                    )
            sum_ref[slot : slot + 1, :] = jnp.sum(wide(ref[0]), axis=0, keepdims=True) + jnp.sum(
                wide(ref[1]), axis=0, keepdims=True
            )
        for slot, ref in enumerate((keep_ref, send_ref)):
            pltpu.make_async_copy(grads.at[slot], ref, sem.at[slot]).start()
        for slot, ref in enumerate((keep_ref, send_ref)):
            pltpu.make_async_copy(grads.at[slot], ref, sem.at[slot]).wait()

    z_size = lax.axis_size("z")
    part = width // (2 * z_size)
    piece_out = sds((z_size, part, cols), jnp.bfloat16)
    return call(
        body,
        place,
        (normed, grad_q, grad_k, grad_v),
        [whole((2, length, width))] + [whole((2, length, heads))] * 3,
        [sds((3, heads), jnp.float32)] + [piece_out] * 2,
        [whole((3, heads))] + [any_spec()] * 2,
        [
            pltpu.VMEM((width, 2 * length), jnp.bfloat16),
            pltpu.VMEM((2, z_size, part, cols), jnp.bfloat16),
            pltpu.SemaphoreType.DMA((2,)),
        ],
        "qkv_term",
        flops=4 * length * width * cols,
    )


def qkv_back(place, grad_q, grad_k, grad_v, pieces):
    flat = [one for piece in pieces for (one,) in piece]
    z_size, part, cols_part = flat[0].shape
    part -= TILE
    cols = cols_part * len(pieces)
    width = 2 * z_size * part
    heads = cols // 3
    length = grad_q.shape[1]

    def body(place_ref, gq_ref, gk_ref, gv_ref, *refs):
        ins, (own_ref, other_ref, weight, sem) = refs[: len(flat)], refs[len(flat) :]
        copies = []
        for number, ref in enumerate(ins):
            lanes = pl.ds(number // 2 * cols_part, cols_part)
            for z in range(z_size):
                row = pl.multiple_of(shard_number(place_ref, z, number % 2) * part, part)
                copy = pltpu.make_async_copy(
                    ref.at[z, pl.ds(0, part), :],
                    weight.at[pl.ds(row, part), lanes],
                    sem.at[len(copies)],
                )
                copy.start()
                copies.append(copy)
        for copy in copies:
            copy.wait()
        for image, out_ref in enumerate((own_ref, other_ref)):
            out_ref[...] = (
                dot_tail(gq_ref[image], weight[:, :heads])
                + dot_tail(gk_ref[image], weight[:, heads : 2 * heads])
                + dot_tail(gv_ref[image], weight[:, 2 * heads :])
            )

    return call(
        body,
        place,
        (grad_q, grad_k, grad_v, *flat),
        [whole((2, length, heads))] * 3 + [any_spec()] * len(flat),
        [sds((length, width), jnp.float32)] * 2,
        [whole((length, width))] * 2,
        [
            pltpu.VMEM((width, cols), jnp.bfloat16),
            pltpu.SemaphoreType.DMA((z_size * len(flat),)),
        ],
        "qkv_back",
        flops=4 * length * width * cols,
    )


def to_column(row):
    return jnp.concatenate(
        [
            jnp.broadcast_to(row[:, at : at + LANES], (LANES, LANES)).T[:, :1]
            for at in range(0, row.shape[1], LANES)
        ],
        axis=0,
    )


def to_row(column):
    return jnp.concatenate(
        [
            jnp.broadcast_to(column[at : at + LANES, :], (LANES, LANES)).T[:1, :]
            for at in range(0, column.shape[0], LANES)
        ],
        axis=1,
    )


def statistics(place, kinds, shares, weights, states, images, group, extra=None):
    flat = []
    places = []
    for chunks in shares:
        if not any(chunks is done for done, _ in places):
            places.append((chunks, len(flat)))
            flat += [a for pair in chunks for side in pair for a in side]
    starts = [next(at for done, at in places if done is chunks) for chunks in shares]
    amount = len(kinds)
    vectors = 0 if extra is None else len(extra[1])

    def body(place_ref, *refs):
        core = place_ref[2]
        refs = list(refs)

        def take(n):
            taken = refs[:n]
            del refs[:n]
            return taken

        share_refs = take(len(flat))
        weight_refs, state_refs = take(amount), take(amount)
        if vectors:
            (terms_ref,) = take(1)
            param_refs, moment_refs = take(vectors), take(vectors)
        grad_refs, row_refs = take(amount), take(amount)
        (pack_ref,) = take(1)
        if vectors:
            vector_grads, new_moments = take(vectors), take(vectors)
        at_pack = 0
        for number, kind in enumerate(kinds):
            grad_ref, weight_ref = grad_refs[number], weight_refs[number]
            rows, cols = weights[number].shape
            at_share = starts[number]
            for chunk, pair in enumerate(shares[number]):
                sides = []
                for side in pair:
                    sides.append(share_refs[at_share : at_share + len(side)])
                    at_share += len(side)

                def halves(index):
                    mine, theirs = [
                        sum([wide(ref[index]) for ref in side[1:]], wide(side[0][index]))
                        * (1.0 / images)
                        for side in sides
                    ]
                    return select(core, mine, theirs), select(core, theirs, mine)

                if kind == "in":
                    per = cols // (2 * CHUNKS * group)
                    for c, half in enumerate(halves((slice(0, rows), slice(None)))):
                        for s in range(group):
                            at = ((s * 2 + c) * CHUNKS + chunk) * per
                            grad_ref[:, at : at + per] = half[:, s * per : (s + 1) * per]
                elif kind == "down":
                    per = rows // (2 * CHUNKS)
                    first = sides[0][0].shape[0] - per
                    for c, half in enumerate(halves((slice(first, first + per), slice(None)))):
                        at = (c * CHUNKS + chunk) * per
                        grad_ref[at : at + per, :] = half
                else:
                    groups = cols // (2 * SPLIT[kind])
                    for slot in range(SPLIT[kind]):
                        lanes = slice(slot * groups, (slot + 1) * groups)
                        for c, half in enumerate(halves((slice(None), lanes))):
                            at = (2 * slot + c) * groups
                            grad_ref[:, at : at + groups] = half
            squared = grad_ref[...] * grad_ref[...]
            new_rows = 0.5 * to_column(state_refs[number][...]) + 0.5 * jnp.mean(
                squared, axis=1, keepdims=True
            )
            row_refs[number][...] = to_row(new_rows)
            pack_ref[0:1, at_pack : at_pack + cols] = jnp.sum(squared, axis=0, keepdims=True)
            pack_ref[1:2, at_pack : at_pack + cols] = jnp.sum(
                squared * (1.0 / new_rows), axis=0, keepdims=True
            )
            at_pack += cols
            weight = weight_ref[...]
            pack_ref[0:1, at_pack : at_pack + LANES] = jnp.broadcast_to(
                jnp.sum(new_rows, axis=0, keepdims=True), (1, LANES)
            )
            pack_ref[1:2, at_pack : at_pack + LANES] = jnp.broadcast_to(
                jnp.sum(jnp.sum(weight * weight, axis=0, keepdims=True), axis=1, keepdims=True),
                (1, LANES),
            )
            at_pack += LANES
        at = 0
        if vectors:
            place_row = lax.broadcasted_iota(jnp.int32, extra[0].shape, 0)
            here = place_row == place_ref[0] * 2 + place_ref[1]
            mine = jnp.sum(
                jnp.where(here, terms_ref[...], 0.0), axis=0, keepdims=True
            )
        for number in range(vectors):
            size = extra[1][number].shape[1]
            grad = mine[:, at : at + size] * (1.0 / images)
            at += size
            param = param_refs[number][...]
            moment = 0.5 * moment_refs[number][...] + 0.5 * grad * grad
            direction = grad * lax.rsqrt(moment)
            vector_grads[number][...] = grad
            new_moments[number][...] = moment
            for row, value in enumerate((direction, param)):
                pack_ref[row : row + 1, at_pack : at_pack + LANES] = jnp.broadcast_to(
                    jnp.sum(value * value, axis=1, keepdims=True), (1, LANES)
                )
            at_pack += LANES

    lanes = sum(weight.shape[1] + LANES for weight in weights) + vectors * LANES
    ins = [*flat, *weights, *states]
    outs = [sds(weight.shape, jnp.float32) for weight in weights]
    outs += [sds(state.shape, jnp.float32) for state in states]
    outs.append(sds((2, lanes), jnp.float32))
    if vectors:
        terms, params, moments = extra
        ins += [terms, *params, *moments]
        outs += [sds(a.shape, jnp.float32) for a in (*params, *moments)]
    results = call(
        body,
        place,
        tuple(ins),
        [whole(a.shape) for a in ins],
        outs,
        [whole(a.shape) for a in outs],
        [],
        "statistics",
    )
    return (
        results[:amount],
        results[amount : 2 * amount],
        results[2 * amount],
        results[2 * amount + 1 : 2 * amount + 1 + vectors],
        results[2 * amount + 1 + vectors :],
    )


SPLIT = {"out": 1, "qkv": 3}


def update(place, grads, new_rows, weights, cols_states, pack, group, extra=None):
    amount = len(weights)
    vectors = 0 if extra is None else len(extra[0])

    def body(place_ref, *refs):
        refs = list(refs)

        def take(n):
            taken = refs[:n]
            del refs[:n]
            return taken

        grad_refs, row_refs, weight_refs, state_refs = [take(amount) for _ in range(4)]
        (pack_ref,) = take(1)
        if vectors:
            vector_grads, moment_refs, param_refs = [take(vectors) for _ in range(3)]
        new_refs, col_refs = take(amount), take(amount)
        (clip_ref,) = take(1)
        param_outs = take(vectors)
        at_pack = 0
        clip_ref[...] = jnp.zeros(clip_ref.shape, jnp.float32)
        for number in range(amount):
            rows, cols = weights[number].shape
            rows_total = rows * group
            count = rows_total * cols
            new_cols = (
                0.5 * state_refs[number][...]
                + 0.5 * pack_ref[0:1, at_pack : at_pack + cols] / rows_total
            )
            col_refs[number][...] = new_cols
            by_rows = pack_ref[1:2, at_pack : at_pack + cols]
            at_pack += cols
            mean_rows = pack_ref[0:1, at_pack : at_pack + 1] / rows_total
            weight_total = pack_ref[1:2, at_pack : at_pack + 1]
            at_pack += LANES
            total = mean_rows * jnp.sum(by_rows / new_cols, axis=1, keepdims=True)
            clip = jnp.maximum(1.0, jnp.sqrt(total / count) / clip_level)
            step = step_rate * jnp.sqrt(weight_total / count) / clip
            clip_ref[number : number + 1, :] = jnp.broadcast_to(clip, (1, LANES))
            estimate = to_column(row_refs[number][...]) * (new_cols / mean_rows)
            new_refs[number][...] = weight_refs[number][...] - step * (
                grad_refs[number][...] * lax.rsqrt(estimate)
            )
        for number in range(vectors):
            count = extra[2][number].shape[1] * group
            total = pack_ref[0:1, at_pack : at_pack + 1]
            weight_total = pack_ref[1:2, at_pack : at_pack + 1]
            at_pack += LANES
            clip = jnp.maximum(1.0, jnp.sqrt(total / count) / clip_level)
            step = step_rate * jnp.sqrt(weight_total / count) / clip
            slot = amount + number
            clip_ref[slot : slot + 1, :] = jnp.broadcast_to(clip, (1, LANES))
            direction = vector_grads[number][...] * lax.rsqrt(moment_refs[number][...])
            param_outs[number][...] = param_refs[number][...] - step * direction

    ins = [*grads, *new_rows, *weights, *cols_states, pack]
    outs = [sds(a.shape, jnp.float32) for a in (*weights, *cols_states)]
    outs.append(sds((TILE, LANES), jnp.float32))
    if vectors:
        ins += [*extra[0], *extra[1], *extra[2]]
        outs += [sds(a.shape, jnp.float32) for a in extra[2]]
    results = call(
        body,
        place,
        tuple(ins),
        [whole(a.shape) for a in ins],
        outs,
        [whole(a.shape) for a in outs],
        [],
        "update",
    )
    return (
        results[:amount],
        results[amount : 2 * amount],
        results[2 * amount],
        results[2 * amount + 1 :],
    )


def pack_terms(place, sums_mid, sums_in, sums_qkv, hidden_sums, down_sums, sizes):
    z_size = lax.axis_size("z")
    shards = 2 * z_size
    per_shard = sizes[6] // 2 // CHUNKS
    heads = sums_qkv.shape[1]

    def body(place_ref, mid_ref, in_ref, qkv_ref, *refs):
        hidden_refs, (down_ref, out_ref) = refs[:CHUNKS], refs[CHUNKS:]
        core = place_ref[2]

        def put(slot, row):
            at, size = sum(sizes[:slot]), sizes[slot]
            for s in range(shards):
                out_ref[s : s + 1, at : at + size] = row[:, s * size : (s + 1) * size]

        put(0, in_ref[0:1, :])
        put(1, in_ref[1:2, :])
        zero = jnp.zeros((1, heads), jnp.float32)
        halves = []
        for slot in (0, 2):
            row = qkv_ref[slot : slot + 1, :]
            halves += [select(core, row, zero), select(core, zero, row)]
        put(2, jnp.concatenate(halves, axis=1))
        put(3, mid_ref[2:3, :])
        put(4, mid_ref[0:1, :])
        put(5, mid_ref[1:2, :])
        put(7, down_ref[...])
        none = jnp.zeros((1, per_shard), jnp.float32)
        for s in range(shards):
            for j in range(CHUNKS):
                i = s % 2
                row = hidden_refs[j][s // 2, :, i * per_shard : (i + 1) * per_shard]
                for c in range(2):
                    at = sum(sizes[:6]) + (c * CHUNKS + j) * per_shard
                    here = select(core, row, none) if c == 0 else select(core, none, row)
                    out_ref[s : s + 1, at : at + per_shard] = here

    ins = (sums_mid, sums_in, sums_qkv, *hidden_sums, down_sums)
    shape = (shards, sum(sizes))
    return call(
        body,
        place,
        ins,
        [whole(a.shape) for a in ins],
        [sds(shape, jnp.float32)],
        [whole(shape)],
        [],
        "pack_terms",
    )[0]


def on_device(
    inputs,
    cotangent,
    norm1_gain,
    norm1_bias,
    qkv_weight,
    qv_bias,
    out_weight,
    out_bias,
    norm2_gain,
    norm2_bias,
    in_weight,
    in_bias,
    down_weight,
    down_bias,
    qkv_rows,
    qkv_cols,
    out_rows,
    out_cols,
    in_rows,
    in_cols,
    down_rows,
    down_cols,
    norm1_gain_moment,
    norm1_bias_moment,
    qv_bias_moment,
    out_bias_moment,
    norm2_gain_moment,
    norm2_bias_moment,
    in_bias_moment,
    down_bias_moment,
):
    masters = [
        norm1_gain,
        norm1_bias,
        qkv_weight,
        qv_bias,
        out_weight,
        out_bias,
        norm2_gain,
        norm2_bias,
        in_weight,
        in_bias,
        down_weight,
        down_bias,
    ]
    moments = [
        norm1_gain_moment,
        norm1_bias_moment,
        qv_bias_moment,
        out_bias_moment,
        norm2_gain_moment,
        norm2_bias_moment,
        in_bias_moment,
        down_bias_moment,
    ]
    place = jnp.stack([lax.axis_index(axis) for axis in ("z", "x", "c", "y")]).astype(jnp.int32)
    by_y = lax.axis_size("y") == 2
    group = lax.axis_size("z") * lax.axis_size("x")
    tokens = inputs.shape[0]
    images = (tokens // SEQ) * group * lax.axis_size("y") * lax.axis_size("c")
    as_row = lambda vector: vector.reshape(1, -1)
    params = [as_row(masters[number]) for number in VECTORS]
    moments = [as_row(moment) for moment in moments]
    sizes = [param.shape[1] for param in params]

    pieces_qkv = [gather_rows(one, False) for one in prepare_qkv(place, qkv_weight, params)]
    *shards_ff, rows_own, cot_own, down_sums = prepare_rest(
        place, in_weight, down_weight, out_weight, inputs, cotangent, by_y
    )
    rows = (rows_own, swap(rows_own, "c"))
    cot = (cot_own, swap(cot_own, "c"))
    pieces_ff = [gather_rows(shard, by_y) for shard in shards_ff]
    weight_mine = gather_out(place, pieces_ff[0], shards_ff[1].shape[0])
    weight_theirs = swap(weight_mine, "c")

    normed, query, keys, values, vectors, hidden_bias = project_qkv(
        place, rows, pieces_qkv, sizes
    )
    attended, probs = attention(place, query, keys, values)
    attended_theirs = swap(attended, "c")
    middle, normed_mid = project_out(
        place, attended, attended_theirs, weight_mine, weight_theirs, rows, vectors
    )
    running = None
    hidden_sums = []
    shares_ff = []
    for j in range(CHUNKS):
        *running, sums, keep, send = feed_forward(
            place, normed_mid, cot, pieces_ff[j], hidden_bias, j, running
        )
        hidden_sums.append(sums)
        shares_ff.append(scatter_sum(keep, send))
    out_share, out_given, normed_share, normed_given = running
    sums_mid, output, grad_mid, grad_mid_low = norm_back(
        place,
        middle,
        vectors,
        GAIN_TWO,
        normed_share,
        swap(normed_given, "c"),
        cot_own,
        tokens,
        (out_share, swap(out_given, "c")),
    )
    grad_attended, keep, send = out_back(
        place,
        grad_mid_low,
        swap(grad_mid_low, "c"),
        attended,
        attended_theirs,
        weight_mine,
        weight_theirs,
    )
    share_out = scatter_sum(keep, send)
    grad_q, grad_k, grad_v = attention_back(place, query, keys, values, probs, grad_attended)
    sums_qkv, keep, send = qkv_term(place, normed, grad_q, grad_k, grad_v)
    share_qkv = scatter_sum(keep, send)
    share, given = qkv_back(place, grad_q, grad_k, grad_v, pieces_qkv)
    sums_in, input_grad = norm_back(
        place, rows_own, vectors, GAIN_ONE, share, swap(given, "c"), grad_mid, tokens
    )
    terms = sum_over(
        pack_terms(place, sums_mid, sums_in, sums_qkv, hidden_sums, down_sums, sizes),
        ("c", "x", "z", "y"),
    )

    early = ("in", "down", "out")
    weights = [in_weight, down_weight, out_weight]
    states = [as_row(state) for state in (in_rows, down_rows, out_rows)]
    grads_early, rows_early, pack, _, _ = statistics(
        place, early, [shares_ff, shares_ff, [share_out]], weights, states, images, group
    )
    new_early, cols_early, clips_early, _ = update(
        place,
        grads_early,
        rows_early,
        weights,
        [as_row(state) for state in (in_cols, down_cols, out_cols)],
        sum_over(pack, ("x", "z")),
        group,
    )
    grads_late, rows_late, pack, vector_grads, new_moments = statistics(
        place,
        ("qkv",),
        [[share_qkv]],
        [qkv_weight],
        [as_row(qkv_rows)],
        images,
        group,
        (terms, params, moments),
    )
    new_late, cols_late, clips_late, new_vectors = update(
        place,
        grads_late,
        rows_late,
        [qkv_weight],
        [as_row(qkv_cols)],
        sum_over(pack, ("x", "z")),
        group,
        (vector_grads, new_moments, params),
    )

    flat = lambda value: value.reshape(-1)
    grads = [None] * 12
    new_params = [None] * 12
    for number, slot in ((8, 0), (10, 1), (4, 2)):
        grads[number], new_params[number] = grads_early[slot], new_early[slot]
    grads[2], new_params[2] = grads_late[0], new_late[0]
    for slot, number in enumerate(VECTORS):
        grads[number] = flat(vector_grads[slot])
        new_params[number] = flat(new_vectors[slot])
    late, first = clips_late[:, 0], clips_early[:, 0]
    clip_factors = jnp.stack(
        [
            late[1],
            late[2],
            late[0],
            late[3],
            first[2],
            late[4],
            late[5],
            late[6],
            first[0],
            late[7],
            first[1],
            late[8],
        ]
    )
    return (
        output,
        input_grad,
        *grads,
        flat(rows_late[0]),
        flat(cols_late[0]),
        flat(rows_early[2]),
        flat(cols_early[2]),
        flat(rows_early[0]),
        flat(cols_early[0]),
        flat(rows_early[1]),
        flat(cols_early[1]),
        *[flat(moment) for moment in new_moments],
        *new_params,
        clip_factors,
    )


def solution(mesh):
    group = mesh.shape["fsdp"]
    split = Mesh(mesh.devices.reshape(group // 2, 2, mesh.shape["dp"] // 2, 2), ALL_AXES)
    in_specs = (
        P(("z", "x", "y", "c"), None),
        P(("z", "x", "y", "c"), None),
        P(("z", "x")),
        P(("z", "x")),
        P(("z", "x"), None),
        P(("z", "x")),
        P(("z", "x"), None),
        P(("z", "x")),
        P(("z", "x")),
        P(("z", "x")),
        P(("z", "x"), None),
        P(("z", "x")),
        P(("z", "x"), None),
        P(("z", "x")),
        P(("z", "x")),
        P(),
        P(("z", "x")),
        P(),
        P(("z", "x")),
        P(),
        P(("z", "x")),
        P(),
        P(("z", "x")),
        P(("z", "x")),
        P(("z", "x")),
        P(("z", "x")),
        P(("z", "x")),
        P(("z", "x")),
        P(("z", "x")),
        P(("z", "x")),
    )
    out_specs = (
        P(("z", "x", "y", "c"), None),
        P(("z", "x", "y", "c"), None),
        P(("z", "x")),
        P(("z", "x")),
        P(("z", "x"), None),
        P(("z", "x")),
        P(("z", "x"), None),
        P(("z", "x")),
        P(("z", "x")),
        P(("z", "x")),
        P(("z", "x"), None),
        P(("z", "x")),
        P(("z", "x"), None),
        P(("z", "x")),
        P(("z", "x")),
        P(),
        P(("z", "x")),
        P(),
        P(("z", "x")),
        P(),
        P(("z", "x")),
        P(),
        P(("z", "x")),
        P(("z", "x")),
        P(("z", "x")),
        P(("z", "x")),
        P(("z", "x")),
        P(("z", "x")),
        P(("z", "x")),
        P(("z", "x")),
        P(("z", "x")),
        P(("z", "x")),
        P(("z", "x"), None),
        P(("z", "x")),
        P(("z", "x"), None),
        P(("z", "x")),
        P(("z", "x")),
        P(("z", "x")),
        P(("z", "x"), None),
        P(("z", "x")),
        P(("z", "x"), None),
        P(("z", "x")),
        P(),
    )
    return jax.shard_map(
        on_device, mesh=split, in_specs=in_specs, out_specs=out_specs, check_vma=False
    )
```

```python
import math

import jax
import jax.numpy as jnp
from jax import lax
from jax.experimental import pallas as pl
from jax.experimental.pallas import tpu as pltpu
from jax.sharding import Mesh
from jax.sharding import PartitionSpec as P

HEAD_DIM = 64
SEQ = 577
LANES = 128
TILE = 16
SPAN = 256
CHUNKS = 2
GROUPS = 2
GIVEN = 2
VMEM_LIMIT = 60 * 1024 * 1024

ALL_AXES = ("z", "x", "y", "c")

MATRICES = (2, 4, 8, 10)
VECTORS = (0, 1, 3, 5, 6, 7, 9, 11)

ln_eps = 1e-06
clip_level = 0.05
step_rate = 4.0


def swap(value, axis):
    return lax.ppermute(value, axis, [(0, 1), (1, 0)])


def shift(value, axis, step):
    size = lax.axis_size(axis)
    return lax.ppermute(value, axis, [(i, (i + step) % size) for i in range(size)])


def partner(value, axis, step):
    size = lax.axis_size(axis)
    return lax.ppermute(value, axis, [(i, i ^ step) for i in range(size)])


def sum_over(value, axes):
    for axis in axes:
        if lax.axis_size(axis) == 4:
            got = [shift(value, axis, step) for step in (1, 2, 3)]
            value = (value + got[1]) + (got[0] + got[2])
            continue
        step = 1
        while step < lax.axis_size(axis):
            value = value + partner(value, axis, step)
            step *= 2
    return value


def along_z(shard):
    near = lax.all_gather(shard, "z", axis=0, tiled=True)
    return near.reshape(lax.axis_size("z"), *shard.shape)


def by_x(near):
    return [[near], [swap(near, "x")]]


def by_y_too(pieces, by_y):
    return [[one, swap(one, "y")] if by_y else [one] for (one,) in pieces]


def after(values, token):
    return lax.optimization_barrier((values, token))[0]


def fold(keep, got):
    total = low(wide(keep) + wide(got))
    return total.reshape(-1, total.shape[-1])


def scatter_z(total):
    return lax.psum_scatter(total, "z", scatter_dimension=0, tiled=True)


def finish_sum(mine):
    if lax.axis_size("y") == 2:
        own = [mine, swap(mine, "y")]
    else:
        own = [lax.psum(wide(mine), "y")]
    return own, [swap(one, "c") for one in own]


def row_pad(length):
    return -(-length // LANES) * LANES


def dot(left, right):
    return jnp.dot(left, right, preferred_element_type=jnp.float32)


def dot_tail(left, right):
    return lax.dot_general(
        left, right, (((1,), (1,)), ((), ())), preferred_element_type=jnp.float32
    )


def low(value):
    return value.astype(jnp.bfloat16)


def wide(value):
    return value.astype(jnp.float32)


def any_spec():
    return pl.BlockSpec(memory_space=pl.ANY)


def whole(shape):
    return pl.BlockSpec(shape, lambda *_: (0,) * len(shape))


def sds(shape, dtype):
    return jax.ShapeDtypeStruct(shape, dtype)


def call(body, place, ins, in_specs, outs, out_specs, scratch, name, grid=(1,)):
    return pl.pallas_call(
        body,
        out_shape=outs,
        grid_spec=pltpu.PrefetchScalarGridSpec(
            num_scalar_prefetch=1,
            grid=grid,
            in_specs=in_specs,
            out_specs=out_specs,
            scratch_shapes=scratch,
        ),
        compiler_params=pltpu.CompilerParams(
            vmem_limit_bytes=VMEM_LIMIT, dimension_semantics=("arbitrary",) * len(grid)
        ),
        name=name,
    )(place, *ins)


def shard_number(place_ref, z, dx):
    return z * 2 + dx + (1 - 2 * dx) * place_ref[1]


def normalised(rows):
    centre = rows - jnp.mean(rows, axis=-1, keepdims=True)
    spread = jnp.mean(centre * centre, axis=-1, keepdims=True)
    return centre * lax.rsqrt(spread + ln_eps)


def select(core, first, second):
    return jnp.where(core == 0, first, second)


def prepare_qkv(place, weight, out_weight, vectors):
    part, cols = weight.shape
    half = cols // 6
    heads = half // GROUPS
    width = 3 * heads
    sizes = [vector.shape[-1] for vector in vectors]
    tiles = -(-sum(sizes) // width)

    out_half = out_weight.shape[1] // 2

    def body(place_ref, weight_ref, out_ref, *refs):
        refs, groups = refs[: len(sizes)], refs[len(sizes) :]
        core = place_ref[2]
        for number, ref in enumerate(groups):
            for slot in range(3):
                at = 2 * slot * half + number * heads
                ref[:part, slot * heads : (slot + 1) * heads] = low(
                    select(
                        core,
                        weight_ref[:, at : at + heads],
                        weight_ref[:, at + half : at + half + heads],
                    )
                )
        groups[-1][:, width:] = low(select(core, out_ref[:, :out_half], out_ref[:, out_half:]))
        at = 0
        for ref, size in zip(refs, sizes):
            done = 0
            while done < size:
                tile, lane = divmod(at + done, width)
                count = min(size - done, width - lane)
                row = part + tile * TILE
                groups[0][row : row + TILE, lane : lane + count] = low(
                    jnp.broadcast_to(ref[:, done : done + count], (TILE, count))
                )
                done += count
            at += size

    shapes = [
        (part + (tiles * TILE if g == 0 else 0), width + (out_half if g == GROUPS - 1 else 0))
        for g in range(GROUPS)
    ]
    return call(
        body,
        place,
        (weight, out_weight, *vectors),
        [whole((part, cols)), whole(out_weight.shape)] + [whole((1, size)) for size in sizes],
        [sds(shape, jnp.bfloat16) for shape in shapes],
        [whole(shape) for shape in shapes],
        [],
        "prepare_qkv",
    )


def pad_rows(place, rows):
    tokens, width = rows.shape
    length = row_pad(tokens)
    even = tokens // TILE * TILE

    def body(place_ref, ref, to):
        row = lax.broadcasted_iota(jnp.int32, (length - even, width), 0)
        to[:even, :] = ref[:even, :]
        last = jnp.zeros((length - even, width), jnp.float32)
        for extra in range(tokens - even):
            one = wide(ref[even + extra : even + extra + 1, :])
            last = jnp.where(row == extra, one, last)
        to[even:, :] = low(last)

    shape = (length, width)
    return call(
        body,
        place,
        (rows,),
        [whole(rows.shape)],
        [sds(shape, jnp.bfloat16)],
        [whole(shape)],
        [],
        "pad_rows",
    )[0]


def prepare_rest(place, in_weight, down_weight, cotangent, cuts):
    part, hidden = in_weight.shape
    width = down_weight.shape[1]
    per_core = down_weight.shape[0] // 2
    per_shard = per_core // CHUNKS
    shards = hidden // (2 * per_core)
    def body(place_ref, in_ref, down_ref, cot_ref, *refs):
        pieces, (sum_ref,) = refs[:CHUNKS], refs[CHUNKS:]
        core, y = place_ref[2], place_ref[3]

        def pick(ref, row, count, step, col, cols, by_row, cut):
            def of_core(r):
                if by_row:
                    return select(
                        core, ref[r : r + count, col : col + cols], ref[r + step : r + step + count, col : col + cols]
                    )
                return select(
                    core, ref[r : r + count, col : col + cols], ref[r : r + count, col + step : col + step + cols]
                )

            if cut == 1:
                return low(of_core(row))
            return low(select(y, of_core(row), of_core(row + count)))

        for j, cut in enumerate(cuts):
            rows_in, rows_down = part // cut, per_shard // cut
            for s in range(shards):
                at = s * 2 * per_core + j * per_shard
                pieces[j][:rows_in, s * per_shard : (s + 1) * per_shard] = pick(
                    in_ref, 0, rows_in, per_core, at, per_shard, False, cut
                )
            pieces[j][rows_in:, :] = pick(
                down_ref, j * per_shard, rows_down, per_core, 0, width, True, cut
            )
        sum_ref[...] = jnp.sum(wide(cot_ref[...]), axis=0, keepdims=True)

    outs = [sds(((part + per_shard) // cut, width), jnp.bfloat16) for cut in cuts]
    outs += [sds((1, width), jnp.float32)]
    ins = (in_weight, down_weight, cotangent)
    return call(
        body,
        place,
        ins,
        [whole(a.shape) for a in ins],
        outs,
        [whole(a.shape) for a in outs],
        [],
        "prepare_rest",
    )


GAIN_ONE, BIAS_ONE, BIAS_OUT, GAIN_TWO, BIAS_TWO, BIAS_DOWN, BIAS_QV = range(7)


def weight_copies(place_ref, ins, weight, part, sem):
    made = []
    for dx, ref in enumerate(ins):
        for z in range(ref.shape[0]):
            row = pl.multiple_of(shard_number(place_ref, z, dx) * part, part)
            made.append(
                pltpu.make_async_copy(
                    ref.at[z, pl.ds(0, part), pl.ds(0, weight.shape[1])],
                    weight.at[pl.ds(row, part), :],
                    sem.at[len(made)],
                )
            )
    return made


def write_qkv(normed, weight, bias_q, bias_v, image, q_ref, k_ref, v_ref):
    heads = weight.shape[1] // 3
    query = low(dot(normed, weight[:, :heads]) + bias_q)
    q_ref[image] = low(wide(query) * (1.0 / math.sqrt(HEAD_DIM)))
    k_ref[image] = low(dot(normed, weight[:, heads : 2 * heads]))
    v_ref[image] = low(dot(normed, weight[:, 2 * heads :]) + bias_v)


def project_first(place, rows, pieces, sizes):
    flat = [one for (one,) in pieces]
    z_size, part, cols = flat[0].shape
    length, width = rows[0].shape
    count = 2 * z_size
    tiles = (part - width // count) // TILE
    part = width // count
    heads = cols // 3
    half = heads * GROUPS
    starts = [sum(sizes[:number]) for number in range(len(sizes))]
    per_shard = sizes[6] // 2 // CHUNKS
    blocks = count // 2

    def body(place_ref, own_ref, other_ref, *refs):
        ins, refs = refs[:2], refs[2:]
        normed_ref, q_ref, k_ref, v_ref, vec_ref, hidden_bias_ref, weight, packed, sem = refs
        core = place_ref[2]
        copies = []
        for dx, ref in enumerate(ins):
            for z in range(z_size):
                copies.append(
                    pltpu.make_async_copy(
                        ref.at[z, pl.ds(part, tiles * TILE), :],
                        packed.at[shard_number(place_ref, z, dx)],
                        sem.at[count + len(copies)],
                    )
                )
        copies += weight_copies(place_ref, ins, weight, part, sem)
        for copy in copies:
            copy.start()
        for copy in copies:
            copy.wait()

        def lanes(s, at, size):
            found = []
            done = 0
            while done < size:
                tile, lane = divmod(at + done, cols)
                take = min(size - done, cols - lane)
                found.append(wide(packed[s, tile * TILE : tile * TILE + 1, lane : lane + take]))
                done += take
            return found

        def vector(slot, shards=range(count)):
            return jnp.concatenate(
                [one for s in shards for one in lanes(s, starts[slot], sizes[slot])], axis=1
            )

        gain, bias = vector(0), vector(1)
        bias_q = vector(2, range(blocks))
        bias_v = vector(2, range(blocks, count))
        bias_q = select(core, bias_q[:, :half], bias_q[:, half:])
        bias_v = select(core, bias_v[:, :half], bias_v[:, half:])
        for row, value in (
            (GAIN_ONE, gain),
            (BIAS_ONE, bias),
            (BIAS_OUT, vector(3)),
            (GAIN_TWO, vector(4)),
            (BIAS_TWO, vector(5)),
            (BIAS_DOWN, vector(7)),
            (BIAS_QV, jnp.concatenate([bias_q, bias_v], axis=1)),
        ):
            vec_ref[row : row + 1, :] = value
        vec_ref[7:8, :] = jnp.zeros((1, width), jnp.float32)
        for j in range(CHUNKS):
            for b in range(blocks):
                for i in range(2):
                    at = starts[6] + j * per_shard
                    to = at + sizes[6] // 2
                    hidden_bias_ref[j, b, :, i * per_shard : (i + 1) * per_shard] = select(
                        core,
                        jnp.concatenate(lanes(2 * b + i, at, per_shard), axis=1),
                        jnp.concatenate(lanes(2 * b + i, to, per_shard), axis=1),
                    )
        for image, ref in enumerate((own_ref, other_ref)):
            for at in range(0, length, LANES):
                block = wide(ref[at : at + LANES, :])
                normed_ref[image, at : at + LANES, :] = low(normalised(block) * gain + bias)
            write_qkv(
                normed_ref[image],
                weight,
                bias_q[:, :heads],
                bias_v[:, :heads],
                image,
                q_ref,
                k_ref,
                v_ref,
            )

    part_out = sds((2, length, heads), jnp.bfloat16)
    return call(
        body,
        place,
        (*rows, *flat),
        [whole((length, width))] * 2 + [any_spec()] * 2,
        [sds((2, length, width), jnp.bfloat16)]
        + [part_out] * 3
        + [
            sds((8, width), jnp.float32),
            sds((CHUNKS, blocks, 1, 2 * per_shard), jnp.float32),
        ],
        [whole((2, length, width))]
        + [whole((2, length, heads))] * 3
        + [whole((8, width)), whole((CHUNKS, blocks, 1, 2 * per_shard))],
        [
            pltpu.VMEM((width, cols), jnp.bfloat16),
            pltpu.VMEM((count, tiles * TILE, cols), jnp.bfloat16),
            pltpu.SemaphoreType.DMA((2 * count,)),
        ],
        "project_first",
    )


def project_next(place, normed, vectors, pieces, group):
    flat = [one for (one,) in pieces]
    z_size, part, _ = flat[0].shape
    _, length, width = normed.shape
    half = width // 2
    heads = half // GROUPS
    cols = 3 * heads

    def body(place_ref, normed_ref, vec_ref, *refs):
        ins, (q_ref, k_ref, v_ref, weight, sem) = refs[:2], refs[2:]
        copies = weight_copies(place_ref, ins, weight, part, sem)
        for copy in copies:
            copy.start()
        for copy in copies:
            copy.wait()
        at = group * heads
        bias_q = vec_ref[BIAS_QV : BIAS_QV + 1, at : at + heads]
        bias_v = vec_ref[BIAS_QV : BIAS_QV + 1, half + at : half + at + heads]
        for image in range(2):
            write_qkv(normed_ref[image], weight, bias_q, bias_v, image, q_ref, k_ref, v_ref)

    return call(
        body,
        place,
        (normed, vectors, *flat),
        [whole(normed.shape), whole(vectors.shape)] + [any_spec()] * 2,
        [sds((2, length, heads), jnp.bfloat16)] * 3,
        [whole((2, length, heads))] * 3,
        [pltpu.VMEM((width, cols), jnp.bfloat16), pltpu.SemaphoreType.DMA((2 * z_size,))],
        "project_next",
    )


def gather_out(place, pieces, first):
    flat = [one for (one,) in pieces]
    z_size, part, total = flat[0].shape
    half = total - first

    def body(place_ref, *refs):
        ins, out_ref, sem = refs[:2], refs[2], refs[3]
        copies = []
        for dx, ref in enumerate(ins):
            for z in range(z_size):
                row = pl.multiple_of(shard_number(place_ref, z, dx) * part, part)
                copy = pltpu.make_async_copy(
                    ref.at[z, :, pl.ds(first, half)],
                    out_ref.at[pl.ds(row, part), :],
                    sem.at[len(copies)],
                )
                copy.start()
                copies.append(copy)
        for copy in copies:
            copy.wait()

    shape = (2 * z_size * part, half)
    return call(
        body,
        place,
        tuple(flat),
        [any_spec()] * 2,
        [sds(shape, jnp.bfloat16)],
        [whole(shape)],
        [pltpu.SemaphoreType.DMA((2 * z_size,))],
        "gather_out",
    )[0]


def attention(place, query, keys, values):
    _, length, heads = query.shape
    pairs = heads // LANES

    def body(place_ref, q_ref, k_ref, v_ref, out_ref, probs_ref):
        lane = lax.broadcasted_iota(jnp.int32, (length, LANES), 1)
        keys_block = k_ref[0]
        values_t = v_ref[0].T
        query_block = q_ref[0]
        mixed = []
        for head in range(2):
            inside = (lane >= head * HEAD_DIM) & (lane < (head + 1) * HEAD_DIM)
            query_head = jnp.where(inside, query_block, jnp.zeros_like(query_block))
            values_head = values_t[head * HEAD_DIM : (head + 1) * HEAD_DIM, :]
            parts = []
            for at in range(0, length, SPAN):
                span = min(SPAN, length - at)
                scores = dot_tail(keys_block, query_head[at : at + span, :])
                key_row = lax.broadcasted_iota(jnp.int32, scores.shape, 0)
                scores = jnp.where(key_row < SEQ, scores, -1e30)
                highest = jnp.max(scores, axis=0, keepdims=True)
                exponent = jnp.exp(scores - highest)
                summed = jnp.sum(exponent, axis=0, keepdims=True)
                probs = low(exponent * (1.0 / summed))
                probs_ref[0, 0, head, :, at : at + span] = probs
                parts.append(dot(values_head, probs))
            mixed.append(jnp.concatenate(parts, axis=1))
        out_ref[0] = low(jnp.concatenate(mixed, axis=0).T)

    block = pl.BlockSpec((1, length, LANES), lambda i, j, p: (i, 0, j))
    return call(
        body,
        place,
        (query, keys, values),
        [block] * 3,
        [
            sds((2, length, heads), jnp.bfloat16),
            sds((2, pairs, 2, length, length), jnp.bfloat16),
        ],
        [block, pl.BlockSpec((1, 1, 2, length, length), lambda i, j, p: (i, j, 0, 0, 0))],
        [],
        "attention",
        grid=(2, pairs),
    )


def attention_back(place, query, keys, values, probs, grad):
    _, length, heads = query.shape
    pairs = heads // LANES
    scale = 1.0 / math.sqrt(HEAD_DIM)

    def body(place_ref, q_ref, k_ref, v_ref, p_ref, g_ref, gq_ref, gk_ref, gv_ref):
        lane = lax.broadcasted_iota(jnp.int32, (length, LANES), 1)
        keys_t = k_ref[0].T
        values_block = v_ref[0]
        query_block = q_ref[0]
        grad_block = g_ref[0]
        grad_query = []
        grad_keys = []
        grad_values = []
        for head in range(2):
            inside = (lane >= head * HEAD_DIM) & (lane < (head + 1) * HEAD_DIM)
            grad_head = jnp.where(inside, grad_block, jnp.zeros_like(grad_block))
            keys_head = keys_t[head * HEAD_DIM : (head + 1) * HEAD_DIM, :]
            parts = []
            sum_keys = None
            sum_values = None
            for at in range(0, length, SPAN):
                span = min(SPAN, length - at)
                probs_low = p_ref[0, 0, head, :, at : at + span]
                probs_wide = wide(probs_low)
                grad_probs = dot_tail(values_block, grad_head[at : at + span, :])
                inner = jnp.sum(probs_wide * grad_probs, axis=0, keepdims=True)
                grad_scores = low(probs_wide * (grad_probs - inner))
                parts.append(dot(keys_head, grad_scores))
                to_keys = dot(grad_scores, query_block[at : at + span, :])
                to_values = dot(probs_low, grad_block[at : at + span, :])
                sum_keys = to_keys if sum_keys is None else sum_keys + to_keys
                sum_values = to_values if sum_values is None else sum_values + to_values
            grad_query.append(jnp.concatenate(parts, axis=1))
            grad_keys.append(sum_keys)
            grad_values.append(sum_values)
        first = lane < HEAD_DIM
        gq_ref[0] = low(jnp.concatenate(grad_query, axis=0).T * scale)
        gk_ref[0] = low(jnp.where(first, grad_keys[0], grad_keys[1]))
        gv_ref[0] = low(jnp.where(first, grad_values[0], grad_values[1]))

    block = pl.BlockSpec((1, length, LANES), lambda i, j, p: (i, 0, j))
    return call(
        body,
        place,
        (query, keys, values, probs, grad),
        [block] * 3
        + [pl.BlockSpec((1, 1, 2, length, length), lambda i, j, p: (i, j, 0, 0, 0)), block],
        [sds((2, length, heads), jnp.bfloat16)] * 3,
        [block] * 3,
        [],
        "attention_back",
        grid=(2, pairs),
    )


def head_rows(core, heads, group):
    mine = pl.multiple_of((core * GROUPS + group) * heads, heads)
    return mine, pl.multiple_of(((1 - core) * GROUPS + group) * heads, heads)


def project_out(place, mine, theirs, weight_mine, weight_theirs, rows, vectors):
    width, half = weight_mine.shape
    _, length, heads = mine[0].shape

    def body(place_ref, *refs):
        mine_refs, theirs_refs, refs = refs[:GROUPS], refs[GROUPS : 2 * GROUPS], refs[2 * GROUPS :]
        wm_ref, wt_ref, own_ref, other_ref, vec_ref, middle_ref, normed_ref, total = refs
        core = place_ref[2]
        for image, ref in enumerate((own_ref, other_ref)):
            for slot, weight in enumerate((wm_ref, wt_ref)):
                branch = None
                for g in range(GROUPS):
                    at_mine, at_theirs = head_rows(core, heads, g)
                    add = dot(mine_refs[g][image], weight[pl.ds(at_mine, heads), :]) + dot(
                        theirs_refs[g][1 - image], weight[pl.ds(at_theirs, heads), :]
                    )
                    branch = add if branch is None else branch + add
                total[slot] = branch
            for at in range(0, length, LANES):
                upto = at + LANES
                first, second = total[0, at:upto, :], total[1, at:upto, :]
                left = select(core, first, second)
                right = select(core, second, first)
                middle = (
                    wide(ref[at:upto, :])
                    + jnp.concatenate([left, right], axis=1)
                    + vec_ref[BIAS_OUT : BIAS_OUT + 1, :]
                )
                if image == 0:
                    middle_ref[at:upto, :] = middle
                normed_ref[image, at:upto, :] = low(
                    normalised(middle) * vec_ref[GAIN_TWO : GAIN_TWO + 1, :]
                    + vec_ref[BIAS_TWO : BIAS_TWO + 1, :]
                )

    return call(
        body,
        place,
        (*mine, *theirs, weight_mine, weight_theirs, *rows, vectors),
        [whole((2, length, heads))] * (2 * GROUPS)
        + [whole((width, half))] * 2
        + [whole((length, width))] * 2
        + [whole(vectors.shape)],
        [sds((length, width), jnp.float32), sds((2, length, width), jnp.bfloat16)],
        [whole((length, width)), whole((2, length, width))],
        [pltpu.VMEM((2, length, half), jnp.float32)],
        "project_out",
    )


def feed_forward(place, normed, cotangent, pieces, bias, chunk, running):
    cut = len(pieces[0])
    z_size, _, width = pieces[0][0].shape
    blocks, block = bias.shape[1], bias.shape[3]
    hidden_width = blocks * block
    part = width // (2 * z_size)
    per_shard = hidden_width // (2 * z_size)
    rows_in, rows_down = part // cut, per_shard // cut
    in_block = block // per_shard
    _, length, _ = normed.shape
    first_call = running is None
    last_call = chunk == CHUNKS - 1

    def body(place_ref, normed_ref, own_cot, other_cot, bias_ref, *refs):
        ins, refs = refs[: 2 * cut], refs[2 * cut :]
        if not first_call:
            before, refs = refs[:4], refs[4:]
        out_own, out_other, gn_own, gn_other, bsum_ref, keep_ref, send_ref = refs[:7]
        w_in, w_down, normed_t, grads, sem, out_sem, *held = refs[7:]
        given = (out_other, gn_other)
        if last_call:
            out_other, gn_other = held
        step = pl.program_id(0)

        def copies():
            made = []
            for number, ref in enumerate(ins):
                dx, h = number // cut, number % cut
                y = h + (1 - 2 * h) * place_ref[3] if cut == 2 else 0
                for z in range(z_size):
                    s = shard_number(place_ref, z, dx)
                    for weight, at, rows, of_shard in (
                        (w_in, 0, rows_in, part),
                        (w_down, rows_in, rows_down, per_shard),
                    ):
                        row = pl.multiple_of(s * of_shard + y * rows, rows)
                        made.append(
                            pltpu.make_async_copy(
                                ref.at[z, pl.ds(at, rows), :],
                                weight.at[pl.ds(row, rows), :],
                                sem.at[len(made)],
                            )
                        )
            return made

        @pl.when(step == 0)
        def _():
            for copy in copies():
                copy.start()
            for image in range(2):
                normed_t[:, image * length : (image + 1) * length] = normed_ref[image].T
            for copy in copies():
                copy.wait()

        at_block = pl.multiple_of(step * block, block)
        weight_in = w_in[:, pl.ds(at_block, block)]
        weight_down = w_down[pl.ds(at_block, block), :]
        into = None
        down = None
        column_sum = None
        for image, cot_ref in enumerate((own_cot, other_cot)):
            preact = dot(normed_ref[image], weight_in) + bias_ref[0, 0]
            phi = 0.5 * (1.0 + lax.erf(preact * math.sqrt(0.5)))
            density = jnp.exp(-0.5 * preact * preact) * (1.0 / math.sqrt(2.0 * math.pi))
            hidden = low(preact * phi)
            slope = phi + preact * density
            cot = cot_ref[...]
            grad = low(dot_tail(cot, weight_down) * slope)
            out_ref, gn_ref = ((out_own, gn_own), (out_other, gn_other))[image]
            to_out = dot(hidden, weight_down)
            to_normed = dot_tail(grad, weight_in)

            @pl.when(step == 0)
            def _():
                if first_call:
                    out_ref[...] = to_out
                    gn_ref[...] = to_normed
                else:
                    out_ref[...] = before[image][...] + to_out
                    gn_ref[...] = before[2 + image][...] + to_normed

            @pl.when(step > 0)
            def _():
                out_ref[...] += to_out
                gn_ref[...] += to_normed

            partial = jnp.sum(wide(grad), axis=0, keepdims=True)
            column_sum = partial if image == 0 else column_sum + partial
            to_in = dot(normed_t[:, image * length : (image + 1) * length], grad)
            into = to_in if image == 0 else into + to_in
            to_down = dot(hidden.T, cot)
            down = to_down if image == 0 else down + to_down
        bsum_ref[0] = column_sum
        for z in range(z_size):
            for x in range(2):
                dx = x + (1 - 2 * x) * place_ref[1]
                at = (z * 2 + x) * part
                grads[dx, z, :part, pl.ds(at_block, block)] = low(into[at : at + part, :])
        for i in range(in_block):
            s = step * in_block + i
            z, x = s // 2, lax.rem(s, 2)
            dx = x + (1 - 2 * x) * place_ref[1]
            grads[dx, z, part:, :] = low(down[i * per_shard : (i + 1) * per_shard, :])

        @pl.when(step == blocks - 1)
        def _():
            for total_ref, ref in zip(held, given):
                ref[...] = low(total_ref[...])
            for slot, ref in enumerate((keep_ref, send_ref)):
                pltpu.make_async_copy(grads.at[slot], ref, out_sem.at[slot]).start()
            for slot, ref in enumerate((keep_ref, send_ref)):
                pltpu.make_async_copy(grads.at[slot], ref, out_sem.at[slot]).wait()

    total = sds((length, width), jnp.float32)
    other = sds((length, width), jnp.bfloat16 if last_call else jnp.float32)
    piece_out = sds((z_size, part + per_shard, width), jnp.bfloat16)
    carried = () if first_call else tuple(running)
    return call(
        body,
        place,
        (normed, *cotangent, bias, *[one for side in pieces for one in side], *carried),
        [whole((2, length, width))]
        + [whole((length, width))] * 2
        + [pl.BlockSpec((1, 1, 1, block), lambda b, p: (chunk, b, 0, 0))]
        + [any_spec()] * (2 * cut)
        + [whole((length, width))] * len(carried),
        [total, other, total, other] + [sds((blocks, 1, block), jnp.float32)] + [piece_out] * 2,
        [whole((length, width))] * 4
        + [pl.BlockSpec((1, 1, block), lambda b, p: (b, 0, 0))]
        + [any_spec()] * 2,
        [
            pltpu.VMEM((width, hidden_width), jnp.bfloat16),
            pltpu.VMEM((hidden_width, width), jnp.bfloat16),
            pltpu.VMEM((width, 2 * length), jnp.bfloat16),
            pltpu.VMEM((2, z_size, part + per_shard, width), jnp.bfloat16),
            pltpu.SemaphoreType.DMA((4 * cut * z_size,)),
            pltpu.SemaphoreType.DMA((2,)),
        ]
        + [pltpu.VMEM((length, width), jnp.float32)] * (2 if last_call else 0),
        "feed_forward",
        grid=(blocks,),
    )


def norm_back(place, rows, vectors, gain_row, grad_own, others, passed, tokens, finish=()):
    length, width = rows.shape

    def body(place_ref, rows_ref, vec_ref, own_ref, pass_ref, *refs):
        other_refs, refs = refs[: len(others)], refs[len(others) :]
        step = pl.program_id(0)
        values = wide(rows_ref[...])
        if finish:
            first_ref, second_ref, *refs = refs
            refs[1][...] = low(
                values + first_ref[...] + wide(second_ref[...]) + vec_ref[BIAS_DOWN : BIAS_DOWN + 1, :]
            )
        sum_ref = refs[0]
        centre = values - jnp.mean(values, axis=-1, keepdims=True)
        spread = jnp.mean(centre * centre, axis=-1, keepdims=True)
        inverse = lax.rsqrt(spread + ln_eps)
        unit = centre * inverse
        grad = own_ref[...] + jnp.concatenate([wide(ref[...]) for ref in other_refs], axis=1)
        scaled = grad * vec_ref[gain_row : gain_row + 1, :]
        mean_one = jnp.mean(scaled, axis=-1, keepdims=True)
        mean_two = jnp.mean(scaled * unit, axis=-1, keepdims=True)
        result = wide(pass_ref[...]) + (scaled - mean_one - unit * mean_two) * inverse
        rounded = low(result)
        parts = [
            jnp.sum(grad * unit, axis=0, keepdims=True),
            jnp.sum(grad, axis=0, keepdims=True),
            jnp.sum(wide(rounded), axis=0, keepdims=True),
            jnp.zeros((5, width), jnp.float32),
        ]
        if not finish:
            refs[1][...] = rounded
        else:
            refs[2][...] = result
            refs[3][...] = rounded
        joined = jnp.concatenate(parts, axis=0)

        @pl.when(step == 0)
        def _():
            sum_ref[...] = joined

        @pl.when(step > 0)
        def _():
            sum_ref[...] += joined

    block = pl.BlockSpec((LANES, width), lambda i, p: (i, 0))
    outs = [sds((8, width), jnp.float32), sds((tokens, width), jnp.bfloat16)]
    if finish:
        outs += [sds((length, width), jnp.float32), sds((length, width), jnp.bfloat16)]
    other_block = pl.BlockSpec((LANES, others[0].shape[1]), lambda i, p: (i, 0))
    ins = (rows, vectors, grad_own, passed, *others, *finish)
    return call(
        body,
        place,
        ins,
        [block, whole(vectors.shape), block, block]
        + [other_block] * len(others)
        + [block] * len(finish),
        outs,
        [whole((8, width))] + [block] * (len(outs) - 1),
        [],
        "norm_back",
        grid=(length // LANES,),
    )


def out_back(place, grad_own, grad_other, mine, theirs, weight_mine, weight_theirs):
    width, half = weight_mine.shape
    z_size = lax.axis_size("z")
    part = width // (2 * z_size)
    _, length, heads = mine[0].shape

    def body(place_ref, own_ref, other_ref, own_half, other_half, *refs):
        mine_refs, theirs_refs, refs = refs[:GROUPS], refs[GROUPS : 2 * GROUPS], refs[2 * GROUPS :]
        wm_ref, wt_ref, *refs = refs
        ga_refs, (keep_ref, send_ref, turned, grads, out_sem) = refs[:GROUPS], refs[GROUPS:]
        core = place_ref[2]
        for image in range(2):
            lanes = slice(image * length, (image + 1) * length)
            for g in range(GROUPS):
                at_mine, at_theirs = head_rows(core, heads, g)
                turned[pl.ds(at_mine, heads), lanes] = mine_refs[g][image].T
                turned[pl.ds(at_theirs, heads), lanes] = theirs_refs[g][1 - image].T
        term = dot(turned[:, :length], own_half[...]) + dot(turned[:, length:], other_half[...])
        for z in range(z_size):
            for x in range(2):
                dx = x + (1 - 2 * x) * place_ref[1]
                at = (z * 2 + x) * part
                grads[dx, z] = low(term[at : at + part, :])
        for slot, ref in enumerate((keep_ref, send_ref)):
            pltpu.make_async_copy(grads.at[slot], ref, out_sem.at[slot]).start()
        for image, ref in enumerate((own_ref, other_ref)):
            first, second = ref[:, :half], ref[:, half:]
            left = select(core, first, second)
            right = select(core, second, first)
            for g in range(GROUPS):
                at_mine, _ = head_rows(core, heads, g)
                ga_refs[g][image] = low(
                    dot_tail(left, wm_ref[pl.ds(at_mine, heads), :])
                    + dot_tail(right, wt_ref[pl.ds(at_mine, heads), :])
                )
        for slot, ref in enumerate((keep_ref, send_ref)):
            pltpu.make_async_copy(grads.at[slot], ref, out_sem.at[slot]).wait()

    half_block = pl.BlockSpec((length, half), lambda i, p: (0, p[2]))
    piece_out = sds((z_size, part, half), jnp.bfloat16)
    return call(
        body,
        place,
        (grad_own, grad_other, grad_own, grad_other, *mine, *theirs, weight_mine, weight_theirs),
        [whole((length, width))] * 2
        + [half_block] * 2
        + [whole((2, length, heads))] * (2 * GROUPS)
        + [whole((width, half))] * 2,
        [sds((2, length, heads), jnp.bfloat16)] * GROUPS + [piece_out] * 2,
        [whole((2, length, heads))] * GROUPS + [any_spec()] * 2,
        [
            pltpu.VMEM((width, 2 * length), jnp.bfloat16),
            pltpu.VMEM((2, z_size, part, half), jnp.bfloat16),
            pltpu.SemaphoreType.DMA((2,)),
        ],
        "out_back",
    )


def qkv_term(place, normed, grad_q, grad_k, grad_v):
    _, length, width = normed.shape
    heads = grad_q.shape[-1]
    cols = 3 * heads

    def body(place_ref, normed_ref, gq_ref, gk_ref, gv_ref, sum_ref, keep_ref, send_ref, turned, grads, sem):
        z_size = grads.shape[1]
        part = grads.shape[2]
        for image in range(2):
            turned[:, image * length : (image + 1) * length] = normed_ref[image].T
        for slot, ref in enumerate((gq_ref, gk_ref, gv_ref)):
            term = dot(turned[:, :length], ref[0]) + dot(turned[:, length:], ref[1])
            for z in range(z_size):
                for x in range(2):
                    dx = x + (1 - 2 * x) * place_ref[1]
                    at = (z * 2 + x) * part
                    grads[dx, z, :, slot * heads : (slot + 1) * heads] = low(
                        term[at : at + part, :]
                    )
            sum_ref[slot : slot + 1, :] = jnp.sum(wide(ref[0]), axis=0, keepdims=True) + jnp.sum(
                wide(ref[1]), axis=0, keepdims=True
            )
        for slot, ref in enumerate((keep_ref, send_ref)):
            pltpu.make_async_copy(grads.at[slot], ref, sem.at[slot]).start()
        for slot, ref in enumerate((keep_ref, send_ref)):
            pltpu.make_async_copy(grads.at[slot], ref, sem.at[slot]).wait()

    z_size = lax.axis_size("z")
    part = width // (2 * z_size)
    piece_out = sds((z_size, part, cols), jnp.bfloat16)
    return call(
        body,
        place,
        (normed, grad_q, grad_k, grad_v),
        [whole((2, length, width))] + [whole((2, length, heads))] * 3,
        [sds((3, heads), jnp.float32)] + [piece_out] * 2,
        [whole((3, heads))] + [any_spec()] * 2,
        [
            pltpu.VMEM((width, 2 * length), jnp.bfloat16),
            pltpu.VMEM((2, z_size, part, cols), jnp.bfloat16),
            pltpu.SemaphoreType.DMA((2,)),
        ],
        "qkv_term",
    )


def qkv_back(place, grads, pieces):
    flat = [one for piece in pieces for (one,) in piece]
    z_size, _, cols = flat[0].shape
    heads = cols // 3
    length = grads[0][0].shape[1]
    part = flat[-1].shape[1]
    width = 2 * z_size * part

    def body(place_ref, *refs):
        grad_refs, refs = refs[: 3 * GROUPS], refs[3 * GROUPS :]
        ins, (own_ref, *other_refs, weight, sem) = refs[: len(flat)], refs[len(flat) :]
        copies = []
        for g in range(GROUPS):
            copies += weight_copies(
                place_ref, ins[2 * g : 2 * g + 2], weight.at[g], part, sem.at[g]
            )
        for copy in copies:
            copy.start()
        for copy in copies:
            copy.wait()
        for image in range(2):
            total = None
            for g in range(GROUPS):
                for slot in range(3):
                    add = dot_tail(
                        grad_refs[3 * g + slot][image],
                        weight[g, :, slot * heads : (slot + 1) * heads],
                    )
                    total = add if total is None else total + add
            if image == 0:
                own_ref[...] = total
            else:
                for number, ref in enumerate(other_refs):
                    at = number * width // GIVEN
                    ref[...] = low(total[:, at : at + width // GIVEN])

    return call(
        body,
        place,
        (*[one for grad in grads for one in grad], *flat),
        [whole((2, length, heads))] * (3 * GROUPS) + [any_spec()] * len(flat),
        [sds((length, width), jnp.float32)] + [sds((length, width // GIVEN), jnp.bfloat16)] * GIVEN,
        [whole((length, width))] + [whole((length, width // GIVEN))] * GIVEN,
        [
            pltpu.VMEM((GROUPS, width, cols), jnp.bfloat16),
            pltpu.SemaphoreType.DMA((GROUPS, 2 * z_size)),
        ],
        "qkv_back",
    )


def to_column(row):
    return jnp.concatenate(
        [
            jnp.broadcast_to(row[:, at : at + LANES], (LANES, LANES)).T[:, :1]
            for at in range(0, row.shape[1], LANES)
        ],
        axis=0,
    )


def to_row(column):
    return jnp.concatenate(
        [
            jnp.broadcast_to(column[at : at + LANES, :], (LANES, LANES)).T[:1, :]
            for at in range(0, column.shape[0], LANES)
        ],
        axis=1,
    )


def statistics(place, kinds, pairs, shares, weights, states, images, group, extra=None):
    flat = [a for pair in pairs for side in pair for a in side]
    amount = len(kinds)
    vectors = 0 if extra is None else len(extra[1])

    def body(place_ref, *refs):
        core = place_ref[2]
        refs = list(refs)

        def take(n):
            taken = refs[:n]
            del refs[:n]
            return taken

        sides_of = [[take(len(side)) for side in pair] for pair in pairs]
        weight_refs, state_refs = take(amount), take(amount)
        if vectors:
            (terms_ref,) = take(1)
            param_refs, moment_refs = take(vectors), take(vectors)
        grad_refs, row_refs = take(amount), take(amount)
        (pack_ref,) = take(1)
        if vectors:
            vector_grads, new_moments = take(vectors), take(vectors)
        at_pack = 0
        for number, kind in enumerate(kinds):
            grad_ref, weight_ref = grad_refs[number], weight_refs[number]
            rows, cols = weights[number].shape
            for chunk, (number_of, row0, col0) in enumerate(shares[number]):
                sides = sides_of[number_of]

                def halves(row, row_count, col, col_count):
                    index = (
                        slice(row0 + row, row0 + row + row_count),
                        slice(col0 + col, col0 + col + col_count),
                    )
                    mine, theirs = [
                        sum([wide(ref[index]) for ref in side[1:]], wide(side[0][index]))
                        * (1.0 / images)
                        for side in sides
                    ]
                    return select(core, mine, theirs), select(core, theirs, mine)

                if kind == "in":
                    per = cols // (2 * CHUNKS * group)
                    for c, half in enumerate(halves(0, rows, 0, per * group)):
                        for s in range(group):
                            at = ((s * 2 + c) * CHUNKS + chunk) * per
                            grad_ref[:, at : at + per] = half[:, s * per : (s + 1) * per]
                elif kind == "down":
                    per = rows // (2 * CHUNKS)
                    for c, half in enumerate(halves(0, per, 0, cols)):
                        at = (c * CHUNKS + chunk) * per
                        grad_ref[at : at + per, :] = half
                else:
                    amount_of = len(shares[number])
                    lanes_of = cols // (2 * SPLIT[kind] * amount_of)
                    for slot in range(SPLIT[kind]):
                        for c, half in enumerate(halves(0, rows, slot * lanes_of, lanes_of)):
                            at = ((2 * slot + c) * amount_of + chunk) * lanes_of
                            grad_ref[:, at : at + lanes_of] = half
            squared = grad_ref[...] * grad_ref[...]
            new_rows = 0.5 * to_column(state_refs[number][...]) + 0.5 * jnp.mean(
                squared, axis=1, keepdims=True
            )
            row_refs[number][...] = to_row(new_rows)
            pack_ref[0:1, at_pack : at_pack + cols] = jnp.sum(squared, axis=0, keepdims=True)
            pack_ref[1:2, at_pack : at_pack + cols] = jnp.sum(
                squared * (1.0 / new_rows), axis=0, keepdims=True
            )
            at_pack += cols
            weight = weight_ref[...]
            pack_ref[0:1, at_pack : at_pack + LANES] = jnp.broadcast_to(
                jnp.sum(new_rows, axis=0, keepdims=True), (1, LANES)
            )
            pack_ref[1:2, at_pack : at_pack + LANES] = jnp.broadcast_to(
                jnp.sum(jnp.sum(weight * weight, axis=0, keepdims=True), axis=1, keepdims=True),
                (1, LANES),
            )
            at_pack += LANES
        at = 0
        if vectors:
            place_row = lax.broadcasted_iota(jnp.int32, extra[0].shape, 0)
            here = place_row == place_ref[0] * 2 + place_ref[1]
            mine = jnp.sum(
                jnp.where(here, terms_ref[...], 0.0), axis=0, keepdims=True
            )
        for number in range(vectors):
            size = extra[1][number].shape[1]
            grad = mine[:, at : at + size] * (1.0 / images)
            at += size
            param = param_refs[number][...]
            moment = 0.5 * moment_refs[number][...] + 0.5 * grad * grad
            direction = grad * lax.rsqrt(moment)
            vector_grads[number][...] = grad
            new_moments[number][...] = moment
            for row, value in enumerate((direction, param)):
                pack_ref[row : row + 1, at_pack : at_pack + LANES] = jnp.broadcast_to(
                    jnp.sum(value * value, axis=1, keepdims=True), (1, LANES)
                )
            at_pack += LANES

    lanes = sum(weight.shape[1] + LANES for weight in weights) + vectors * LANES
    ins = [*flat, *weights, *states]
    outs = [sds(weight.shape, jnp.float32) for weight in weights]
    outs += [sds(state.shape, jnp.float32) for state in states]
    outs.append(sds((2, lanes), jnp.float32))
    if vectors:
        terms, params, moments = extra
        ins += [terms, *params, *moments]
        outs += [sds(a.shape, jnp.float32) for a in (*params, *moments)]
    results = call(
        body,
        place,
        tuple(ins),
        [whole(a.shape) for a in ins],
        outs,
        [whole(a.shape) for a in outs],
        [],
        "statistics",
    )
    return (
        results[:amount],
        results[amount : 2 * amount],
        results[2 * amount],
        results[2 * amount + 1 : 2 * amount + 1 + vectors],
        results[2 * amount + 1 + vectors :],
    )


CLIP_ORDER = (8, 10, 4, 2)
SPLIT = {"out": 1, "qkv": 3}


def update(place, grads, new_rows, weights, cols_states, pack, group, extra=None, clips=None):
    amount = len(weights)
    vectors = 0 if extra is None else len(extra[0])

    def body(place_ref, *refs):
        refs = list(refs)

        def take(n):
            taken = refs[:n]
            del refs[:n]
            return taken

        grad_refs, row_refs, weight_refs, state_refs = [take(amount) for _ in range(4)]
        (pack_ref,) = take(1)
        if vectors:
            vector_grads, moment_refs, param_refs = [take(vectors) for _ in range(3)]
            (clips_ref,) = take(1)
        new_refs, col_refs = take(amount), take(amount)
        (clip_ref,) = take(1)
        param_outs = take(vectors)
        at_pack = 0
        if not vectors:
            clip_ref[...] = jnp.zeros(clip_ref.shape, jnp.float32)
        for number in range(amount):
            rows, cols = weights[number].shape
            rows_total = rows * group
            count = rows_total * cols
            new_cols = (
                0.5 * state_refs[number][...]
                + 0.5 * pack_ref[0:1, at_pack : at_pack + cols] / rows_total
            )
            col_refs[number][...] = new_cols
            by_rows = pack_ref[1:2, at_pack : at_pack + cols]
            at_pack += cols
            mean_rows = pack_ref[0:1, at_pack : at_pack + 1] / rows_total
            weight_total = pack_ref[1:2, at_pack : at_pack + 1]
            at_pack += LANES
            total = mean_rows * jnp.sum(by_rows / new_cols, axis=1, keepdims=True)
            clip = jnp.maximum(1.0, jnp.sqrt(total / count) / clip_level)
            step = step_rate * jnp.sqrt(weight_total / count) / clip
            if vectors:
                if number == 0:
                    found = [clips_ref[at : at + 1, :1] for at in range(len(MATRICES) - amount)]
                found.append(clip)
            else:
                clip_ref[number : number + 1, :] = jnp.broadcast_to(clip, (1, LANES))
            estimate = to_column(row_refs[number][...]) * (new_cols / mean_rows)
            new_refs[number][...] = weight_refs[number][...] - step * (
                grad_refs[number][...] * lax.rsqrt(estimate)
            )
        for number in range(vectors):
            count = extra[2][number].shape[1] * group
            total = pack_ref[0:1, at_pack : at_pack + 1]
            weight_total = pack_ref[1:2, at_pack : at_pack + 1]
            at_pack += LANES
            clip = jnp.maximum(1.0, jnp.sqrt(total / count) / clip_level)
            step = step_rate * jnp.sqrt(weight_total / count) / clip
            found.append(clip)
            direction = vector_grads[number][...] * lax.rsqrt(moment_refs[number][...])
            param_outs[number][...] = param_refs[number][...] - step * direction
        if vectors:
            lane = lax.broadcasted_iota(jnp.int32, (1, LANES), 1)
            row = jnp.zeros((1, LANES), jnp.float32)
            for value, number in zip(found, (*CLIP_ORDER, *VECTORS)):
                row = jnp.where(lane == number, value, row)
            clip_ref[...] = row[:, : len(found)]

    ins = [*grads, *new_rows, *weights, *cols_states, pack]
    outs = [sds(a.shape, jnp.float32) for a in (*weights, *cols_states)]
    outs.append(sds((1, len(MATRICES) + vectors) if vectors else (8, LANES), jnp.float32))
    if vectors:
        ins += [*extra[0], *extra[1], *extra[2], clips]
        outs += [sds(a.shape, jnp.float32) for a in extra[2]]
    results = call(
        body,
        place,
        tuple(ins),
        [whole(a.shape) for a in ins],
        outs,
        [whole(a.shape) for a in outs],
        [],
        "update",
    )
    return (
        results[:amount],
        results[amount : 2 * amount],
        results[2 * amount],
        results[2 * amount + 1 :],
    )


def pack_terms(place, sums_mid, sums_in, sums_qkv, hidden_sums, down_sums, sizes):
    z_size = lax.axis_size("z")
    shards = 2 * z_size
    per_shard = sizes[6] // 2 // CHUNKS
    heads = sums_qkv[0].shape[1]

    def body(place_ref, mid_ref, in_ref, *refs):
        qkv_refs, refs = refs[:GROUPS], refs[GROUPS:]
        hidden_refs, (down_ref, out_ref) = refs[:CHUNKS], refs[CHUNKS:]
        core = place_ref[2]

        def put(slot, row):
            at, size = sum(sizes[:slot]), sizes[slot]
            for s in range(shards):
                out_ref[s : s + 1, at : at + size] = row[:, s * size : (s + 1) * size]

        put(0, in_ref[0:1, :])
        put(1, in_ref[1:2, :])
        zero = jnp.zeros((1, heads * GROUPS), jnp.float32)
        halves = []
        for slot in (0, 2):
            row = jnp.concatenate([ref[slot : slot + 1, :] for ref in qkv_refs], axis=1)
            halves += [select(core, row, zero), select(core, zero, row)]
        put(2, jnp.concatenate(halves, axis=1))
        put(3, mid_ref[2:3, :])
        put(4, mid_ref[0:1, :])
        put(5, mid_ref[1:2, :])
        put(7, down_ref[...])
        none = jnp.zeros((1, per_shard), jnp.float32)
        for s in range(shards):
            for j in range(CHUNKS):
                i = s % 2
                row = hidden_refs[j][s // 2, :, i * per_shard : (i + 1) * per_shard]
                for c in range(2):
                    at = sum(sizes[:6]) + (c * CHUNKS + j) * per_shard
                    here = select(core, row, none) if c == 0 else select(core, none, row)
                    out_ref[s : s + 1, at : at + per_shard] = here

    ins = (sums_mid, sums_in, *sums_qkv, *hidden_sums, down_sums)
    shape = (shards, sum(sizes))
    return call(
        body,
        place,
        ins,
        [whole(a.shape) for a in ins],
        [sds(shape, jnp.float32)],
        [whole(shape)],
        [],
        "pack_terms",
    )[0]


def on_device(
    inputs,
    cotangent,
    norm1_gain,
    norm1_bias,
    qkv_weight,
    qv_bias,
    out_weight,
    out_bias,
    norm2_gain,
    norm2_bias,
    in_weight,
    in_bias,
    down_weight,
    down_bias,
    qkv_rows,
    qkv_cols,
    out_rows,
    out_cols,
    in_rows,
    in_cols,
    down_rows,
    down_cols,
    norm1_gain_moment,
    norm1_bias_moment,
    qv_bias_moment,
    out_bias_moment,
    norm2_gain_moment,
    norm2_bias_moment,
    in_bias_moment,
    down_bias_moment,
):
    masters = [
        norm1_gain,
        norm1_bias,
        qkv_weight,
        qv_bias,
        out_weight,
        out_bias,
        norm2_gain,
        norm2_bias,
        in_weight,
        in_bias,
        down_weight,
        down_bias,
    ]
    moments = [
        norm1_gain_moment,
        norm1_bias_moment,
        qv_bias_moment,
        out_bias_moment,
        norm2_gain_moment,
        norm2_bias_moment,
        in_bias_moment,
        down_bias_moment,
    ]
    place = jnp.stack([lax.axis_index(axis) for axis in ("z", "x", "c", "y")]).astype(jnp.int32)
    by_y = lax.axis_size("y") == 2
    group = lax.axis_size("z") * lax.axis_size("x")
    tokens = inputs.shape[0]
    images = (tokens // SEQ) * group * lax.axis_size("y") * lax.axis_size("c")
    as_row = lambda vector: vector.reshape(1, -1)
    params = [as_row(masters[number]) for number in VECTORS]
    moments = [as_row(moment) for moment in moments]
    sizes = [param.shape[1] for param in params]

    shard_first, shard_next = prepare_qkv(place, qkv_weight, out_weight, params)
    near = along_z(shard_first)
    pieces_first = by_x(near)
    near_next = along_z(after(shard_next, near))
    rows_own = pad_rows(after(place, near), inputs)
    rows = (rows_own, swap(rows_own, "c"))
    *shards_ff, down_sums = prepare_rest(
        after(place, rows_own), in_weight, down_weight, cotangent, (2 if by_y else 1, 1)
    )
    cot_own = pad_rows(after(place, (down_sums, rows[1])), cotangent)
    near_ff = [along_z(shards_ff[0])]

    normed, *first, vectors, hidden_bias = project_first(
        after(place, cot_own), rows, pieces_first, sizes
    )
    near_ff.append(along_z(after(shards_ff[1], normed)))
    cot = (cot_own, swap(after(cot_own, normed), "c"))
    qkv = [first]
    near_next = after(near_next, normed)
    pieces_next = by_x(near_next)
    mixed, prob = attention(after(place, near_next), *first)
    attended = [mixed]
    probs = [prob]
    theirs = [swap(mixed, "c")]
    pieces_next = after(pieces_next, mixed)
    weight_mine = gather_out(place, pieces_next, 3 * first[0].shape[-1])
    weight_theirs = swap(weight_mine, "c")
    near_ff[0] = after(near_ff[0], weight_mine)
    across = swap(near_ff[0], "x")
    near_too = swap(near_ff[0], "y") if by_y else None
    qkv.append(
        project_next(after(place, near_ff[0]), normed, vectors, pieces_next, 1)
    )
    mixed, prob = attention(place, *qkv[1])
    attended.append(mixed)
    probs.append(prob)
    theirs.append(swap(mixed, "c"))
    across = after(across, mixed)
    if by_y:
        pieces_ff = [[near_ff[0], near_too], [across, swap(across, "y")]]
    else:
        pieces_ff = [[near_ff[0]], [across]]
    middle, normed_mid = project_out(
        after(place, across), attended, theirs, weight_mine, weight_theirs, rows, vectors
    )
    near_ff[1] = after(near_ff[1], normed_mid)
    pieces_next_ff = by_x(near_ff[1])
    *running, sums, keep, send = feed_forward(
        after(place, near_ff[1]), normed_mid, cot, pieces_ff, hidden_bias, 0, None
    )
    hidden_sums = [sums]
    got = swap(send, "x")
    *running, sums, keep_next, send_next = feed_forward(
        place, normed_mid, cot, pieces_next_ff, hidden_bias, 1, running
    )
    hidden_sums.append(sums)
    folded = [fold(*after((keep, got), sums))]
    got_next = swap(send_next, "x")
    scattered = [scatter_z(folded[0])]
    out_share, out_given, normed_share, normed_given = running
    sums_mid, output, grad_mid, grad_mid_low = norm_back(
        after(place, folded[0]),
        middle,
        vectors,
        GAIN_TWO,
        normed_share,
        [swap(normed_given, "c")],
        cot_own,
        tokens,
        (out_share, swap(out_given, "c")),
    )
    *grad_attended, keep, send = out_back(
        place,
        grad_mid_low,
        swap(grad_mid_low, "c"),
        attended,
        theirs,
        weight_mine,
        weight_theirs,
    )
    got = swap(send, "x")
    grad_qkv = [attention_back(place, *qkv[0], probs[0], grad_attended[0])]
    sums_first, keep_first, send_first = qkv_term(place, normed, *grad_qkv[0])
    got_first = swap(send_first, "x")
    folded.append(fold(*after((keep_next, got_next), sums_first)))
    scattered.append(scatter_z(folded[1]))
    grad_qkv.append(
        attention_back(after(place, folded[1]), *qkv[1], probs[1], grad_attended[1])
    )
    sums_next, keep_next, send_next = qkv_term(place, normed, *grad_qkv[1])
    sums_qkv = [sums_first, sums_next]
    got_next = swap(send_next, "x")
    held = after(((keep, got), (keep_first, got_first)), sums_next)
    folded.append(jnp.concatenate([fold(*one) for one in held], axis=1))
    scattered.append(scatter_z(folded[2]))
    share, *given = qkv_back(after(place, folded[2]), grad_qkv, [pieces_first, pieces_next])
    pairs = [finish_sum(after(scattered[0], share))]
    sums_in, input_grad = norm_back(
        after(place, scattered[0]),
        rows_own,
        vectors,
        GAIN_ONE,
        share,
        [swap(one, "c") for one in given],
        grad_mid,
        tokens,
    )
    packed = pack_terms(
        after(place, scattered[1]), sums_mid, sums_in, sums_qkv, hidden_sums, down_sums, sizes
    )
    folded.append(fold(*after((keep_next, got_next), packed)))
    scattered.append(scatter_z(folded[3]))
    pairs += [finish_sum(one) for one in scattered[1:]]
    terms = sum_over(packed, ("c", "z", "x", "y"))

    weights = [in_weight, down_weight]
    states = [as_row(state) for state in (in_rows, down_rows)]
    part = in_weight.shape[0]
    grads_early, rows_early, pack, _, _ = statistics(
        place,
        ("in", "down"),
        pairs[:CHUNKS],
        [[(j, row, 0) for j in range(CHUNKS)] for row in (0, part)],
        weights,
        states,
        images,
        group,
    )
    new_early, cols_early, clips_early, _ = update(
        place,
        grads_early,
        rows_early,
        weights,
        [as_row(state) for state in (in_cols, down_cols)],
        sum_over(pack, ("z", "x")),
        group,
    )
    weights = [out_weight, qkv_weight]
    grads_late, rows_late, pack, vector_grads, new_moments = statistics(
        after(place, clips_early),
        ("out", "qkv"),
        pairs[CHUNKS:],
        [[(0, 0, 0)], [(0, 0, out_weight.shape[1] // 2), (1, 0, 0)]],
        weights,
        [as_row(state) for state in (out_rows, qkv_rows)],
        images,
        group,
        (terms, params, moments),
    )
    new_late, cols_late, clip_factors, new_vectors = update(
        place,
        grads_late,
        rows_late,
        weights,
        [as_row(state) for state in (out_cols, qkv_cols)],
        sum_over(pack, ("z", "x")),
        group,
        (vector_grads, new_moments, params),
        clips_early,
    )

    flat = lambda value: value.reshape(-1)
    grads = [None] * 12
    new_params = [None] * 12
    for number, slot in ((8, 0), (10, 1)):
        grads[number], new_params[number] = grads_early[slot], new_early[slot]
    for number, slot in ((4, 0), (2, 1)):
        grads[number], new_params[number] = grads_late[slot], new_late[slot]
    for slot, number in enumerate(VECTORS):
        grads[number] = flat(vector_grads[slot])
        new_params[number] = flat(new_vectors[slot])
    return (
        output,
        input_grad,
        *grads,
        flat(rows_late[1]),
        flat(cols_late[1]),
        flat(rows_late[0]),
        flat(cols_late[0]),
        flat(rows_early[0]),
        flat(cols_early[0]),
        flat(rows_early[1]),
        flat(cols_early[1]),
        *[flat(moment) for moment in new_moments],
        *new_params,
        flat(clip_factors),
    )


def solution(mesh):
    group = mesh.shape["fsdp"]
    split = Mesh(mesh.devices.reshape(group // 2, 2, mesh.shape["dp"] // 2, 2), ALL_AXES)
    in_specs = (
        P(("z", "x", "y", "c"), None),
        P(("z", "x", "y", "c"), None),
        P(("z", "x")),
        P(("z", "x")),
        P(("z", "x"), None),
        P(("z", "x")),
        P(("z", "x"), None),
        P(("z", "x")),
        P(("z", "x")),
        P(("z", "x")),
        P(("z", "x"), None),
        P(("z", "x")),
        P(("z", "x"), None),
        P(("z", "x")),
        P(("z", "x")),
        P(),
        P(("z", "x")),
        P(),
        P(("z", "x")),
        P(),
        P(("z", "x")),
        P(),
        P(("z", "x")),
        P(("z", "x")),
        P(("z", "x")),
        P(("z", "x")),
        P(("z", "x")),
        P(("z", "x")),
        P(("z", "x")),
        P(("z", "x")),
    )
    out_specs = (
        P(("z", "x", "y", "c"), None),
        P(("z", "x", "y", "c"), None),
        P(("z", "x")),
        P(("z", "x")),
        P(("z", "x"), None),
        P(("z", "x")),
        P(("z", "x"), None),
        P(("z", "x")),
        P(("z", "x")),
        P(("z", "x")),
        P(("z", "x"), None),
        P(("z", "x")),
        P(("z", "x"), None),
        P(("z", "x")),
        P(("z", "x")),
        P(),
        P(("z", "x")),
        P(),
        P(("z", "x")),
        P(),
        P(("z", "x")),
        P(),
        P(("z", "x")),
        P(("z", "x")),
        P(("z", "x")),
        P(("z", "x")),
        P(("z", "x")),
        P(("z", "x")),
        P(("z", "x")),
        P(("z", "x")),
        P(("z", "x")),
        P(("z", "x")),
        P(("z", "x"), None),
        P(("z", "x")),
        P(("z", "x"), None),
        P(("z", "x")),
        P(("z", "x")),
        P(("z", "x")),
        P(("z", "x"), None),
        P(("z", "x")),
        P(("z", "x"), None),
        P(("z", "x")),
        P(),
    )
    return jax.shard_map(
        on_device, mesh=split, in_specs=in_specs, out_specs=out_specs, check_vma=False
    )
```

```python
import math

import jax
import jax.numpy as jnp
from jax import lax
from jax.experimental import pallas as pl
from jax.experimental.pallas import tpu as pltpu
from jax.sharding import Mesh
from jax.sharding import PartitionSpec as P

HEAD_DIM = 64
SEQ = 577
LANES = 128
TILE = 16
CHUNKS = 2
GROUPS = 2
GIVEN = 2
VMEM_LIMIT = 60
VMEM_LIMITS = {"attention": 40, "attention_back": 40, "qkv_term": 40, "out_back": 40, "norm_back": 40}

ALL_AXES = ("z", "x", "y", "c")

MATRICES = (2, 4, 8, 10)
VECTORS = (0, 1, 3, 5, 6, 7, 9, 11)

ln_eps = 1e-06
clip_level = 0.05
step_rate = 4.0


def swap(value, axis):
    return lax.ppermute(value, axis, [(0, 1), (1, 0)])


def shift(value, axis, step):
    size = lax.axis_size(axis)
    return lax.ppermute(value, axis, [(i, (i + step) % size) for i in range(size)])


def partner(value, axis, step):
    size = lax.axis_size(axis)
    return lax.ppermute(value, axis, [(i, i ^ step) for i in range(size)])


def sum_over(value, axes):
    for axis in axes:
        if lax.axis_size(axis) == 4:
            got = [shift(value, axis, step) for step in (1, 2, 3)]
            value = (value + got[1]) + (got[0] + got[2])
            continue
        step = 1
        while step < lax.axis_size(axis):
            value = value + partner(value, axis, step)
            step *= 2
    return value


def along_z(shard):
    near = lax.all_gather(shard, "z", axis=0, tiled=True)
    return near.reshape(lax.axis_size("z"), *shard.shape)


def by_x(near):
    return [[near], [swap(near, "x")]]


def by_y_too(pieces, by_y):
    return [[one, swap(one, "y")] if by_y else [one] for (one,) in pieces]


def after(values, token):
    return lax.optimization_barrier((values, token))[0]


def fold(keep, got):
    total = low(wide(keep) + wide(got))
    return total.reshape(-1, total.shape[-1])


def scatter_z(total):
    return lax.psum_scatter(total, "z", scatter_dimension=0, tiled=True)


def sum_y(mine):
    if lax.axis_size("y") == 2:
        return [mine, swap(mine, "y")]
    return [lax.psum(wide(mine), "y")]


def with_core(own):
    return own, [swap(one, "c") for one in own]


def row_pad(length):
    return -(-length // LANES) * LANES


def dot(left, right):
    return jnp.dot(left, right, preferred_element_type=jnp.float32)


def dot_tail(left, right):
    return lax.dot_general(
        left, right, (((1,), (1,)), ((), ())), preferred_element_type=jnp.float32
    )


def low(value):
    return value.astype(jnp.bfloat16)


def wide(value):
    return value.astype(jnp.float32)


def any_spec():
    return pl.BlockSpec(memory_space=pl.ANY)


def whole(shape):
    return pl.BlockSpec(shape, lambda *_: (0,) * len(shape))


def sds(shape, dtype):
    return jax.ShapeDtypeStruct(shape, dtype)


def call(body, place, ins, in_specs, outs, out_specs, scratch, name, grid=(1,)):
    return pl.pallas_call(
        body,
        out_shape=outs,
        grid_spec=pltpu.PrefetchScalarGridSpec(
            num_scalar_prefetch=1,
            grid=grid,
            in_specs=in_specs,
            out_specs=out_specs,
            scratch_shapes=scratch,
        ),
        compiler_params=pltpu.CompilerParams(
            vmem_limit_bytes=VMEM_LIMITS.get(name, VMEM_LIMIT) * 1024 * 1024, dimension_semantics=("arbitrary",) * len(grid)
        ),
        name=name,
    )(place, *ins)


def shard_number(place_ref, z, dx):
    return z * 2 + dx + (1 - 2 * dx) * place_ref[1]


def normalised(rows):
    centre = rows - jnp.mean(rows, axis=-1, keepdims=True)
    spread = jnp.mean(centre * centre, axis=-1, keepdims=True)
    return centre * lax.rsqrt(spread + ln_eps)


def select(core, first, second):
    return jnp.where(core == 0, first, second)


def prepare_qkv(place, weight, out_weight, vectors):
    part, cols = weight.shape
    half = cols // 6
    heads = half // GROUPS
    width = 3 * heads
    sizes = [vector.shape[-1] for vector in vectors]
    tiles = -(-sum(sizes) // width)

    out_half = out_weight.shape[1] // 2

    def body(place_ref, weight_ref, out_ref, *refs):
        refs, groups = refs[: len(sizes)], refs[len(sizes) :]
        core = place_ref[2]
        for number, ref in enumerate(groups):
            for slot in range(3):
                at = 2 * slot * half + number * heads
                ref[:part, slot * heads : (slot + 1) * heads] = low(
                    select(
                        core,
                        weight_ref[:, at : at + heads],
                        weight_ref[:, at + half : at + half + heads],
                    )
                )
        groups[-1][:, width:] = low(select(core, out_ref[:, :out_half], out_ref[:, out_half:]))
        at = 0
        for ref, size in zip(refs, sizes):
            done = 0
            while done < size:
                tile, lane = divmod(at + done, width)
                count = min(size - done, width - lane)
                row = part + tile * TILE
                groups[0][row : row + TILE, lane : lane + count] = low(
                    jnp.broadcast_to(ref[:, done : done + count], (TILE, count))
                )
                done += count
            at += size

    shapes = [
        (part + (tiles * TILE if g == 0 else 0), width + (out_half if g == GROUPS - 1 else 0))
        for g in range(GROUPS)
    ]
    return call(
        body,
        place,
        (weight, out_weight, *vectors),
        [whole((part, cols)), whole(out_weight.shape)] + [whole((1, size)) for size in sizes],
        [sds(shape, jnp.bfloat16) for shape in shapes],
        [whole(shape) for shape in shapes],
        [],
        "prepare_qkv",
    )


def pad_rows(place, rows):
    tokens, width = rows.shape
    length = row_pad(tokens)
    even = tokens // TILE * TILE
    cols = width // GIVEN

    def body(place_ref, ref, to, *parts):
        row = lax.broadcasted_iota(jnp.int32, (length - even, width), 0)
        last = jnp.zeros((length - even, width), jnp.float32)
        for extra in range(tokens - even):
            one = wide(ref[even + extra : even + extra + 1, :])
            last = jnp.where(row == extra, one, last)
        to[:even, :] = ref[:even, :]
        to[even:, :] = low(last)
        for number, part in enumerate(parts):
            lanes = slice(number * cols, (number + 1) * cols)
            part[...] = to[:, lanes]

    shapes = [(length, width)] + [(length, cols)] * GIVEN
    whole_rows, *parts = call(
        body,
        place,
        (rows,),
        [whole(rows.shape)],
        [sds(shape, jnp.bfloat16) for shape in shapes],
        [whole(shape) for shape in shapes],
        [],
        "pad_rows",
    )
    return whole_rows, parts


def joined(refs, rows=slice(None)):
    return jnp.concatenate([ref[rows, :] for ref in refs], axis=1)


def prepare_rest(place, in_weight, down_weight, cotangent, cuts):
    part, hidden = in_weight.shape
    width = down_weight.shape[1]
    per_core = down_weight.shape[0] // 2
    per_shard = per_core // CHUNKS
    shards = hidden // (2 * per_core)
    def body(place_ref, in_ref, down_ref, cot_ref, *refs):
        pieces, (sum_ref,) = refs[:CHUNKS], refs[CHUNKS:]
        core, y = place_ref[2], place_ref[3]

        def pick(ref, row, count, step, col, cols, by_row, cut):
            def of_core(r):
                if by_row:
                    return select(
                        core, ref[r : r + count, col : col + cols], ref[r + step : r + step + count, col : col + cols]
                    )
                return select(
                    core, ref[r : r + count, col : col + cols], ref[r : r + count, col + step : col + step + cols]
                )

            if cut == 1:
                return low(of_core(row))
            return low(select(y, of_core(row), of_core(row + count)))

        for j, cut in enumerate(cuts):
            rows_in, rows_down = part // cut, per_shard // cut
            for s in range(shards):
                at = s * 2 * per_core + j * per_shard
                pieces[j][:rows_in, s * per_shard : (s + 1) * per_shard] = pick(
                    in_ref, 0, rows_in, per_core, at, per_shard, False, cut
                )
            pieces[j][rows_in:, :] = pick(
                down_ref, j * per_shard, rows_down, per_core, 0, width, True, cut
            )
        sum_ref[...] = jnp.sum(wide(cot_ref[...]), axis=0, keepdims=True)

    outs = [sds(((part + per_shard) // cut, width), jnp.bfloat16) for cut in cuts]
    outs += [sds((1, width), jnp.float32)]
    ins = (in_weight, down_weight, cotangent)
    return call(
        body,
        place,
        ins,
        [whole(a.shape) for a in ins],
        outs,
        [whole(a.shape) for a in outs],
        [],
        "prepare_rest",
    )


GAIN_ONE, BIAS_ONE, BIAS_OUT, GAIN_TWO, BIAS_TWO, BIAS_DOWN, BIAS_QV = range(7)


def weight_copies(place_ref, ins, weight, part, sem):
    made = []
    for dx, ref in enumerate(ins):
        for z in range(ref.shape[0]):
            row = pl.multiple_of(shard_number(place_ref, z, dx) * part, part)
            made.append(
                pltpu.make_async_copy(
                    ref.at[z, pl.ds(0, part), pl.ds(0, weight.shape[1])],
                    weight.at[pl.ds(row, part), :],
                    sem.at[len(made)],
                )
            )
    return made


def write_qkv(normed, weight, bias_q, bias_v, image, q_ref, k_ref, v_ref):
    heads = weight.shape[1] // 3
    query = low(dot(normed, weight[:, :heads]) + bias_q)
    q_ref[image] = low(wide(query) * (1.0 / math.sqrt(HEAD_DIM)))
    k_ref[image] = low(dot(normed, weight[:, heads : 2 * heads]))
    v_ref[image] = low(dot(normed, weight[:, 2 * heads :]) + bias_v)


def project_first(place, rows, pieces, sizes):
    flat = [one for (one,) in pieces]
    z_size, part, cols = flat[0].shape
    rows_own, rows_other = rows
    length, width = rows_own.shape
    count = 2 * z_size
    tiles = (part - width // count) // TILE
    part = width // count
    heads = cols // 3
    half = heads * GROUPS
    starts = [sum(sizes[:number]) for number in range(len(sizes))]
    per_shard = sizes[6] // 2 // CHUNKS
    blocks = count // 2

    def body(place_ref, own_ref, *refs):
        other_refs, refs = refs[:GIVEN], refs[GIVEN:]
        ins, refs = refs[:2], refs[2:]
        normed_ref, q_ref, k_ref, v_ref, vec_ref, hidden_bias_ref, weight, packed, sem = refs
        core = place_ref[2]
        copies = []
        for dx, ref in enumerate(ins):
            for z in range(z_size):
                copies.append(
                    pltpu.make_async_copy(
                        ref.at[z, pl.ds(part, tiles * TILE), :],
                        packed.at[shard_number(place_ref, z, dx)],
                        sem.at[count + len(copies)],
                    )
                )
        copies += weight_copies(place_ref, ins, weight, part, sem)
        for copy in copies:
            copy.start()
        for copy in copies:
            copy.wait()

        def lanes(s, at, size):
            found = []
            done = 0
            while done < size:
                tile, lane = divmod(at + done, cols)
                take = min(size - done, cols - lane)
                found.append(wide(packed[s, tile * TILE : tile * TILE + 1, lane : lane + take]))
                done += take
            return found

        def vector(slot, shards=range(count)):
            return jnp.concatenate(
                [one for s in shards for one in lanes(s, starts[slot], sizes[slot])], axis=1
            )

        gain, bias = vector(0), vector(1)
        bias_q = vector(2, range(blocks))
        bias_v = vector(2, range(blocks, count))
        bias_q = select(core, bias_q[:, :half], bias_q[:, half:])
        bias_v = select(core, bias_v[:, :half], bias_v[:, half:])
        for row, value in (
            (GAIN_ONE, gain),
            (BIAS_ONE, bias),
            (BIAS_OUT, vector(3)),
            (GAIN_TWO, vector(4)),
            (BIAS_TWO, vector(5)),
            (BIAS_DOWN, vector(7)),
            (BIAS_QV, jnp.concatenate([bias_q, bias_v], axis=1)),
        ):
            vec_ref[row : row + 1, :] = value
        vec_ref[7:8, :] = jnp.zeros((1, width), jnp.float32)
        for j in range(CHUNKS):
            for s in range(count):
                at = starts[6] + j * per_shard
                to = at + sizes[6] // 2
                hidden_bias_ref[j, :, s * per_shard : (s + 1) * per_shard] = select(
                    core,
                    jnp.concatenate(lanes(s, at, per_shard), axis=1),
                    jnp.concatenate(lanes(s, to, per_shard), axis=1),
                )
        for image, part_refs in enumerate(((own_ref,), other_refs)):
            for at in range(0, length, LANES):
                block = wide(joined(part_refs, slice(at, at + LANES)))
                normed_ref[image, at : at + LANES, :] = low(normalised(block) * gain + bias)
            write_qkv(
                normed_ref[image],
                weight,
                bias_q[:, :heads],
                bias_v[:, :heads],
                image,
                q_ref,
                k_ref,
                v_ref,
            )

    part_out = sds((2, length, heads), jnp.bfloat16)
    return call(
        body,
        place,
        (rows_own, *rows_other, *flat),
        [whole((length, width))]
        + [whole((length, width // GIVEN))] * GIVEN
        + [any_spec()] * 2,
        [sds((2, length, width), jnp.bfloat16)]
        + [part_out] * 3
        + [
            sds((8, width), jnp.float32),
            sds((CHUNKS, 1, count * per_shard), jnp.float32),
        ],
        [whole((2, length, width))]
        + [whole((2, length, heads))] * 3
        + [whole((8, width)), whole((CHUNKS, 1, count * per_shard))],
        [
            pltpu.VMEM((width, cols), jnp.bfloat16),
            pltpu.VMEM((count, tiles * TILE, cols), jnp.bfloat16),
            pltpu.SemaphoreType.DMA((2 * count,)),
        ],
        "project_first",
    )


def project_next(place, normed, vectors, pieces, group):
    flat = [one for (one,) in pieces]
    z_size, part, _ = flat[0].shape
    _, length, width = normed.shape
    half = width // 2
    heads = half // GROUPS
    cols = 3 * heads

    def body(place_ref, normed_ref, vec_ref, *refs):
        ins, (q_ref, k_ref, v_ref, weight, sem) = refs[:2], refs[2:]
        copies = weight_copies(place_ref, ins, weight, part, sem)
        for copy in copies:
            copy.start()
        for copy in copies:
            copy.wait()
        at = group * heads
        bias_q = vec_ref[BIAS_QV : BIAS_QV + 1, at : at + heads]
        bias_v = vec_ref[BIAS_QV : BIAS_QV + 1, half + at : half + at + heads]
        for image in range(2):
            write_qkv(normed_ref[image], weight, bias_q, bias_v, image, q_ref, k_ref, v_ref)

    return call(
        body,
        place,
        (normed, vectors, *flat),
        [whole(normed.shape), whole(vectors.shape)] + [any_spec()] * 2,
        [sds((2, length, heads), jnp.bfloat16)] * 3,
        [whole((2, length, heads))] * 3,
        [pltpu.VMEM((width, cols), jnp.bfloat16), pltpu.SemaphoreType.DMA((2 * z_size,))],
        "project_next",
    )


def gather_out(place, pieces, first):
    flat = [one for (one,) in pieces]
    z_size, part, total = flat[0].shape
    half = total - first

    def body(place_ref, *refs):
        ins, out_ref, sem = refs[:2], refs[2], refs[3]
        copies = []
        for dx, ref in enumerate(ins):
            for z in range(z_size):
                row = pl.multiple_of(shard_number(place_ref, z, dx) * part, part)
                copy = pltpu.make_async_copy(
                    ref.at[z, :, pl.ds(first, half)],
                    out_ref.at[pl.ds(row, part), :],
                    sem.at[len(copies)],
                )
                copy.start()
                copies.append(copy)
        for copy in copies:
            copy.wait()

    shape = (2 * z_size * part, half)
    return call(
        body,
        place,
        tuple(flat),
        [any_spec()] * 2,
        [sds(shape, jnp.bfloat16)],
        [whole(shape)],
        [pltpu.SemaphoreType.DMA((2 * z_size,))],
        "gather_out",
    )[0]


def attention(place, query, keys, values):
    _, length, heads = query.shape
    pairs = heads // LANES

    def body(place_ref, q_ref, k_ref, v_ref, out_ref, probs_ref):
        lane = lax.broadcasted_iota(jnp.int32, (length, LANES), 1)
        keys_block = k_ref[0]
        values_t = v_ref[0].T
        query_block = q_ref[0]
        key_row = lax.broadcasted_iota(jnp.int32, (length, length), 0)
        scores = []
        for head in range(2):
            inside = (lane >= head * HEAD_DIM) & (lane < (head + 1) * HEAD_DIM)
            query_head = jnp.where(inside, query_block, jnp.zeros_like(query_block))
            scores.append(jnp.where(key_row < SEQ, dot_tail(keys_block, query_head), -1e30))
        mixed = []
        for head in range(2):
            highest = jnp.max(scores[head], axis=0, keepdims=True)
            exponent = jnp.exp(scores[head] - highest)
            summed = jnp.sum(exponent, axis=0, keepdims=True)
            probs = low(exponent * (1.0 / summed))
            probs_ref[0, 0, head] = probs
            mixed.append(dot(values_t[head * HEAD_DIM : (head + 1) * HEAD_DIM, :], probs))
        out_ref[0] = low(jnp.concatenate(mixed, axis=0).T)

    block = pl.BlockSpec((1, length, LANES), lambda i, j, p: (i, 0, j))
    return call(
        body,
        place,
        (query, keys, values),
        [block] * 3,
        [
            sds((2, length, heads), jnp.bfloat16),
            sds((2, pairs, 2, length, length), jnp.bfloat16),
        ],
        [block, pl.BlockSpec((1, 1, 2, length, length), lambda i, j, p: (i, j, 0, 0, 0))],
        [],
        "attention",
        grid=(2, pairs),
    )


def attention_back(place, query, keys, values, probs, grad):
    _, length, heads = query.shape
    pairs = heads // LANES
    scale = 1.0 / math.sqrt(HEAD_DIM)

    def body(place_ref, q_ref, k_ref, v_ref, p_ref, g_ref, gq_ref, gk_ref, gv_ref):
        lane = lax.broadcasted_iota(jnp.int32, (length, LANES), 1)
        keys_t = k_ref[0].T
        values_block = v_ref[0]
        query_block = q_ref[0]
        grad_block = g_ref[0]
        grad_query = []
        grad_keys = []
        grad_values = []
        for head in range(2):
            inside = (lane >= head * HEAD_DIM) & (lane < (head + 1) * HEAD_DIM)
            grad_head = jnp.where(inside, grad_block, jnp.zeros_like(grad_block))
            probs_low = p_ref[0, 0, head]
            probs_wide = wide(probs_low)
            grad_probs = dot_tail(values_block, grad_head)
            inner = jnp.sum(probs_wide * grad_probs, axis=0, keepdims=True)
            grad_scores = low(probs_wide * (grad_probs - inner))
            keys_head = keys_t[head * HEAD_DIM : (head + 1) * HEAD_DIM, :]
            grad_query.append(dot(keys_head, grad_scores))
            grad_keys.append(dot(grad_scores, query_block))
            grad_values.append(dot(probs_low, grad_block))
        first = lane < HEAD_DIM
        gq_ref[0] = low(jnp.concatenate(grad_query, axis=0).T * scale)
        gk_ref[0] = low(jnp.where(first, grad_keys[0], grad_keys[1]))
        gv_ref[0] = low(jnp.where(first, grad_values[0], grad_values[1]))

    block = pl.BlockSpec((1, length, LANES), lambda i, j, p: (i, 0, j))
    return call(
        body,
        place,
        (query, keys, values, probs, grad),
        [block] * 3
        + [pl.BlockSpec((1, 1, 2, length, length), lambda i, j, p: (i, j, 0, 0, 0)), block],
        [sds((2, length, heads), jnp.bfloat16)] * 3,
        [block] * 3,
        [],
        "attention_back",
        grid=(2, pairs),
    )


def head_rows(core, heads, group):
    mine = pl.multiple_of((core * GROUPS + group) * heads, heads)
    return mine, pl.multiple_of(((1 - core) * GROUPS + group) * heads, heads)


def project_out(place, mine, theirs, weight_mine, weight_theirs, rows, vectors):
    width, half = weight_mine.shape
    _, length, heads = mine[0].shape

    def body(place_ref, *refs):
        mine_refs, theirs_refs, refs = refs[:GROUPS], refs[GROUPS : 2 * GROUPS], refs[2 * GROUPS :]
        wm_ref, wt_ref, own_ref, *other_refs, vec_ref, middle_ref, normed_ref, total = refs
        core = place_ref[2]
        for image, part_refs in enumerate(((own_ref,), other_refs)):
            for slot, weight in enumerate((wm_ref, wt_ref)):
                branch = None
                for g in range(GROUPS):
                    at_mine, at_theirs = head_rows(core, heads, g)
                    add = dot(mine_refs[g][image], weight[pl.ds(at_mine, heads), :]) + dot(
                        theirs_refs[g][1 - image], weight[pl.ds(at_theirs, heads), :]
                    )
                    branch = add if branch is None else branch + add
                total[slot] = branch
            for at in range(0, length, LANES):
                upto = at + LANES
                first, second = total[0, at:upto, :], total[1, at:upto, :]
                left = select(core, first, second)
                right = select(core, second, first)
                middle = (
                    wide(joined(part_refs, slice(at, upto)))
                    + jnp.concatenate([left, right], axis=1)
                    + vec_ref[BIAS_OUT : BIAS_OUT + 1, :]
                )
                if image == 0:
                    middle_ref[at:upto, :] = middle
                normed_ref[image, at:upto, :] = low(
                    normalised(middle) * vec_ref[GAIN_TWO : GAIN_TWO + 1, :]
                    + vec_ref[BIAS_TWO : BIAS_TWO + 1, :]
                )

    return call(
        body,
        place,
        (*mine, *theirs, weight_mine, weight_theirs, rows[0], *rows[1], vectors),
        [whole((2, length, heads))] * (2 * GROUPS)
        + [whole((width, half))] * 2
        + [whole((length, width))]
        + [whole((length, width // GIVEN))] * GIVEN
        + [whole(vectors.shape)],
        [sds((length, width), jnp.float32), sds((2, length, width), jnp.bfloat16)],
        [whole((length, width)), whole((2, length, width))],
        [pltpu.VMEM((2, length, half), jnp.float32)],
        "project_out",
    )


def feed_forward(place, normed, cotangent, pieces, bias, chunk, running):
    cut = len(pieces[0])
    z_size, _, width = pieces[0][0].shape
    hidden_width = bias.shape[2]
    part = width // (2 * z_size)
    per_shard = hidden_width // (2 * z_size)
    rows_in, rows_down = part // cut, per_shard // cut
    _, length, _ = normed.shape
    first_call = running is None
    last_call = chunk == CHUNKS - 1

    def body(place_ref, normed_ref, own_cot, *refs):
        other_cots, (bias_ref, *refs) = refs[:GIVEN], refs[GIVEN:]
        ins, refs = refs[: 2 * cut], refs[2 * cut :]
        if not first_call:
            before, refs = refs[:4], refs[4:]
        out_own, out_other, gn_own, gn_other, bsum_ref, keep_ref, send_ref = refs[:7]
        w_in, w_down, normed_t, grads, sem, out_sem = refs[7:]
        copies = []
        for weight, at, rows, of_shard in (
            (w_in, 0, rows_in, part),
            (w_down, rows_in, rows_down, per_shard),
        ):
            for number, ref in enumerate(ins):
                dx, h = number // cut, number % cut
                y = h + (1 - 2 * h) * place_ref[3] if cut == 2 else 0
                for z in range(z_size):
                    s = shard_number(place_ref, z, dx)
                    row = pl.multiple_of(s * of_shard + y * rows, rows)
                    copy = pltpu.make_async_copy(
                        ref.at[z, pl.ds(at, rows), :],
                        weight.at[pl.ds(row, rows), :],
                        sem.at[len(copies)],
                    )
                    copy.start()
                    copies.append(copy)
        for image in range(2):
            normed_t[:, image * length : (image + 1) * length] = normed_ref[image].T
        for copy in copies:
            copy.wait()
        into = None
        down = None
        column_sum = None
        for image, cot_refs in enumerate(((own_cot,), other_cots)):
            preact = dot(normed_ref[image], w_in[...]) + bias_ref[0]
            phi = 0.5 * (1.0 + lax.erf(preact * math.sqrt(0.5)))
            density = jnp.exp(-0.5 * preact * preact) * (1.0 / math.sqrt(2.0 * math.pi))
            hidden = low(preact * phi)
            slope = phi + preact * density
            cot = joined(cot_refs)
            grad = low(dot_tail(cot, w_down[...]) * slope)
            out_ref, gn_ref = ((out_own, gn_own), (out_other, gn_other))[image]
            to_out = dot(hidden, w_down[...])
            to_normed = dot_tail(grad, w_in[...])
            if not first_call:
                to_out = before[image][...] + to_out
                to_normed = before[2 + image][...] + to_normed
            out_ref[...] = to_out.astype(out_ref.dtype)
            gn_ref[...] = to_normed.astype(gn_ref.dtype)
            partial = jnp.sum(wide(grad), axis=0, keepdims=True)
            column_sum = partial if image == 0 else column_sum + partial
            to_in = dot(normed_t[:, image * length : (image + 1) * length], grad)
            into = to_in if image == 0 else into + to_in
            to_down = dot(hidden.T, cot)
            down = to_down if image == 0 else down + to_down
        bsum_ref[...] = column_sum
        for z in range(z_size):
            for x in range(2):
                dx = x + (1 - 2 * x) * place_ref[1]
                s = z * 2 + x
                grads[dx, z, :part, :] = low(into[s * part : (s + 1) * part, :])
                grads[dx, z, part:, :] = low(down[s * per_shard : (s + 1) * per_shard, :])
        copies = [
            pltpu.make_async_copy(grads.at[slot], ref, out_sem.at[slot])
            for slot, ref in enumerate((keep_ref, send_ref))
        ]
        for copy in copies:
            copy.start()
        for copy in copies:
            copy.wait()

    total = sds((length, width), jnp.float32)
    other = sds((length, width), jnp.bfloat16 if last_call else jnp.float32)
    piece_out = sds((z_size, part + per_shard, width), jnp.bfloat16)
    carried = () if first_call else tuple(running)
    return call(
        body,
        place,
        (normed, cotangent[0], *cotangent[1], bias, *[one for side in pieces for one in side], *carried),
        [whole((2, length, width)), whole((length, width))]
        + [whole((length, width // GIVEN))] * GIVEN
        + [pl.BlockSpec((1, 1, hidden_width), lambda i, p: (chunk, 0, 0))]
        + [any_spec()] * (2 * cut)
        + [whole((length, width))] * len(carried),
        [total, other, total, other] + [sds((1, hidden_width), jnp.float32)] + [piece_out] * 2,
        [whole((length, width))] * 4 + [whole((1, hidden_width))] + [any_spec()] * 2,
        [
            pltpu.VMEM((width, hidden_width), jnp.bfloat16),
            pltpu.VMEM((hidden_width, width), jnp.bfloat16),
            pltpu.VMEM((width, 2 * length), jnp.bfloat16),
            pltpu.VMEM((2, z_size, part + per_shard, width), jnp.bfloat16),
            pltpu.SemaphoreType.DMA((4 * cut * z_size,)),
            pltpu.SemaphoreType.DMA((2,)),
        ],
        "feed_forward",
    )


def norm_back(place, rows, vectors, gain_row, grad_own, others, passed, tokens, finish=()):
    length, width = rows.shape

    def body(place_ref, rows_ref, vec_ref, own_ref, pass_ref, *refs):
        other_refs, refs = refs[: len(others)], refs[len(others) :]
        step = pl.program_id(0)
        values = wide(rows_ref[...])
        if finish:
            first_ref, second_ref, *refs = refs
            refs[1][...] = low(
                values + first_ref[...] + wide(second_ref[...]) + vec_ref[BIAS_DOWN : BIAS_DOWN + 1, :]
            )
        sum_ref = refs[0]
        centre = values - jnp.mean(values, axis=-1, keepdims=True)
        spread = jnp.mean(centre * centre, axis=-1, keepdims=True)
        inverse = lax.rsqrt(spread + ln_eps)
        unit = centre * inverse
        grad = own_ref[...] + jnp.concatenate([wide(ref[...]) for ref in other_refs], axis=1)
        scaled = grad * vec_ref[gain_row : gain_row + 1, :]
        mean_one = jnp.mean(scaled, axis=-1, keepdims=True)
        mean_two = jnp.mean(scaled * unit, axis=-1, keepdims=True)
        result = wide(pass_ref[...]) + (scaled - mean_one - unit * mean_two) * inverse
        rounded = low(result)
        parts = [
            jnp.sum(grad * unit, axis=0, keepdims=True),
            jnp.sum(grad, axis=0, keepdims=True),
            jnp.sum(wide(rounded), axis=0, keepdims=True),
            jnp.zeros((5, width), jnp.float32),
        ]
        if not finish:
            refs[1][...] = rounded
        else:
            refs[2][...] = result
            refs[3][...] = rounded
        joined = jnp.concatenate(parts, axis=0)

        @pl.when(step == 0)
        def _():
            sum_ref[...] = joined

        @pl.when(step > 0)
        def _():
            sum_ref[...] += joined

    block = pl.BlockSpec((LANES, width), lambda i, p: (i, 0))
    outs = [sds((8, width), jnp.float32), sds((tokens, width), jnp.bfloat16)]
    if finish:
        outs += [sds((length, width), jnp.float32), sds((length, width), jnp.bfloat16)]
    other_block = pl.BlockSpec((LANES, others[0].shape[1]), lambda i, p: (i, 0))
    ins = (rows, vectors, grad_own, passed, *others, *finish)
    return call(
        body,
        place,
        ins,
        [block, whole(vectors.shape), block, block]
        + [other_block] * len(others)
        + [block] * len(finish),
        outs,
        [whole((8, width))] + [block] * (len(outs) - 1),
        [],
        "norm_back",
        grid=(length // LANES,),
    )


def out_back(place, grad_own, grad_other, mine, theirs, weight_mine, weight_theirs):
    width, half = weight_mine.shape
    z_size = lax.axis_size("z")
    part = width // (2 * z_size)
    _, length, heads = mine[0].shape

    def body(place_ref, own_ref, other_ref, own_half, other_half, *refs):
        mine_refs, theirs_refs, refs = refs[:GROUPS], refs[GROUPS : 2 * GROUPS], refs[2 * GROUPS :]
        wm_ref, wt_ref, *refs = refs
        ga_refs, (keep_ref, send_ref, turned, grads, out_sem) = refs[:GROUPS], refs[GROUPS:]
        core = place_ref[2]
        for image in range(2):
            lanes = slice(image * length, (image + 1) * length)
            for g in range(GROUPS):
                at_mine, at_theirs = head_rows(core, heads, g)
                turned[pl.ds(at_mine, heads), lanes] = mine_refs[g][image].T
                turned[pl.ds(at_theirs, heads), lanes] = theirs_refs[g][1 - image].T
        term = dot(turned[:, :length], own_half[...]) + dot(turned[:, length:], other_half[...])
        for z in range(z_size):
            for x in range(2):
                dx = x + (1 - 2 * x) * place_ref[1]
                at = (z * 2 + x) * part
                grads[dx, z] = low(term[at : at + part, :])
        for slot, ref in enumerate((keep_ref, send_ref)):
            pltpu.make_async_copy(grads.at[slot], ref, out_sem.at[slot]).start()
        for image, ref in enumerate((own_ref, other_ref)):
            first, second = ref[:, :half], ref[:, half:]
            left = select(core, first, second)
            right = select(core, second, first)
            for g in range(GROUPS):
                at_mine, _ = head_rows(core, heads, g)
                ga_refs[g][image] = low(
                    dot_tail(left, wm_ref[pl.ds(at_mine, heads), :])
                    + dot_tail(right, wt_ref[pl.ds(at_mine, heads), :])
                )
        for slot, ref in enumerate((keep_ref, send_ref)):
            pltpu.make_async_copy(grads.at[slot], ref, out_sem.at[slot]).wait()

    half_block = pl.BlockSpec((length, half), lambda i, p: (0, p[2]))
    piece_out = sds((z_size, part, half), jnp.bfloat16)
    return call(
        body,
        place,
        (grad_own, grad_other, grad_own, grad_other, *mine, *theirs, weight_mine, weight_theirs),
        [whole((length, width))] * 2
        + [half_block] * 2
        + [whole((2, length, heads))] * (2 * GROUPS)
        + [whole((width, half))] * 2,
        [sds((2, length, heads), jnp.bfloat16)] * GROUPS + [piece_out] * 2,
        [whole((2, length, heads))] * GROUPS + [any_spec()] * 2,
        [
            pltpu.VMEM((width, 2 * length), jnp.bfloat16),
            pltpu.VMEM((2, z_size, part, half), jnp.bfloat16),
            pltpu.SemaphoreType.DMA((2,)),
        ],
        "out_back",
    )


def qkv_term(place, normed, grad_q, grad_k, grad_v):
    _, length, width = normed.shape
    heads = grad_q.shape[-1]
    cols = 3 * heads

    def body(place_ref, normed_ref, gq_ref, gk_ref, gv_ref, sum_ref, keep_ref, send_ref, turned, grads, sem):
        z_size = grads.shape[1]
        part = grads.shape[2]
        for image in range(2):
            turned[:, image * length : (image + 1) * length] = normed_ref[image].T
        for slot, ref in enumerate((gq_ref, gk_ref, gv_ref)):
            term = dot(turned[:, :length], ref[0]) + dot(turned[:, length:], ref[1])
            for z in range(z_size):
                for x in range(2):
                    dx = x + (1 - 2 * x) * place_ref[1]
                    at = (z * 2 + x) * part
                    grads[dx, z, :, slot * heads : (slot + 1) * heads] = low(
                        term[at : at + part, :]
                    )
            sum_ref[slot : slot + 1, :] = jnp.sum(wide(ref[0]), axis=0, keepdims=True) + jnp.sum(
                wide(ref[1]), axis=0, keepdims=True
            )
        for slot, ref in enumerate((keep_ref, send_ref)):
            pltpu.make_async_copy(grads.at[slot], ref, sem.at[slot]).start()
        for slot, ref in enumerate((keep_ref, send_ref)):
            pltpu.make_async_copy(grads.at[slot], ref, sem.at[slot]).wait()

    z_size = lax.axis_size("z")
    part = width // (2 * z_size)
    piece_out = sds((z_size, part, cols), jnp.bfloat16)
    return call(
        body,
        place,
        (normed, grad_q, grad_k, grad_v),
        [whole((2, length, width))] + [whole((2, length, heads))] * 3,
        [sds((3, heads), jnp.float32)] + [piece_out] * 2,
        [whole((3, heads))] + [any_spec()] * 2,
        [
            pltpu.VMEM((width, 2 * length), jnp.bfloat16),
            pltpu.VMEM((2, z_size, part, cols), jnp.bfloat16),
            pltpu.SemaphoreType.DMA((2,)),
        ],
        "qkv_term",
    )


def qkv_back(place, grads, pieces):
    flat = [one for piece in pieces for (one,) in piece]
    z_size, _, cols = flat[0].shape
    heads = cols // 3
    length = grads[0][0].shape[1]
    part = flat[-1].shape[1]
    width = 2 * z_size * part

    def body(place_ref, *refs):
        grad_refs, refs = refs[: 3 * GROUPS], refs[3 * GROUPS :]
        ins, (own_ref, *other_refs, weight, sem) = refs[: len(flat)], refs[len(flat) :]
        copies = []
        for g in range(GROUPS):
            copies += weight_copies(
                place_ref, ins[2 * g : 2 * g + 2], weight.at[g], part, sem.at[g]
            )
        for copy in copies:
            copy.start()
        for copy in copies:
            copy.wait()
        for image in range(2):
            total = None
            for g in range(GROUPS):
                for slot in range(3):
                    add = dot_tail(
                        grad_refs[3 * g + slot][image],
                        weight[g, :, slot * heads : (slot + 1) * heads],
                    )
                    total = add if total is None else total + add
            if image == 0:
                own_ref[...] = total
            else:
                for number, ref in enumerate(other_refs):
                    at = number * width // GIVEN
                    ref[...] = low(total[:, at : at + width // GIVEN])

    return call(
        body,
        place,
        (*[one for grad in grads for one in grad], *flat),
        [whole((2, length, heads))] * (3 * GROUPS) + [any_spec()] * len(flat),
        [sds((length, width), jnp.float32)] + [sds((length, width // GIVEN), jnp.bfloat16)] * GIVEN,
        [whole((length, width))] + [whole((length, width // GIVEN))] * GIVEN,
        [
            pltpu.VMEM((GROUPS, width, cols), jnp.bfloat16),
            pltpu.SemaphoreType.DMA((GROUPS, 2 * z_size)),
        ],
        "qkv_back",
    )


def to_column(row):
    return jnp.concatenate(
        [
            jnp.broadcast_to(row[:, at : at + LANES], (LANES, LANES)).T[:, :1]
            for at in range(0, row.shape[1], LANES)
        ],
        axis=0,
    )


def to_row(column):
    return jnp.concatenate(
        [
            jnp.broadcast_to(column[at : at + LANES, :], (LANES, LANES)).T[:1, :]
            for at in range(0, column.shape[0], LANES)
        ],
        axis=1,
    )


def statistics(place, kinds, pairs, shares, weights, states, images, group, extra=None):
    flat = [a for pair in pairs for side in pair for a in side]
    amount = len(kinds)
    vectors = 0 if extra is None else len(extra[1])

    def body(place_ref, *refs):
        core = place_ref[2]
        refs = list(refs)

        def take(n):
            taken = refs[:n]
            del refs[:n]
            return taken

        sides_of = [[take(len(side)) for side in pair] for pair in pairs]
        weight_refs, state_refs = take(amount), take(amount)
        if vectors:
            (terms_ref,) = take(1)
            param_refs, moment_refs = take(vectors), take(vectors)
        grad_refs, row_refs = take(amount), take(amount)
        (pack_ref,) = take(1)
        if vectors:
            vector_grads, new_moments = take(vectors), take(vectors)
        at_pack = 0
        for number, kind in enumerate(kinds):
            grad_ref, weight_ref = grad_refs[number], weight_refs[number]
            rows, cols = weights[number].shape
            for chunk, (number_of, row0, col0) in enumerate(shares[number]):
                sides = sides_of[number_of]

                def halves(row, row_count, col, col_count):
                    index = (
                        slice(row0 + row, row0 + row + row_count),
                        slice(col0 + col, col0 + col + col_count),
                    )
                    mine, theirs = [
                        sum([wide(ref[index]) for ref in side[1:]], wide(side[0][index]))
                        * (1.0 / images)
                        for side in sides
                    ]
                    return select(core, mine, theirs), select(core, theirs, mine)

                if kind == "in":
                    per = cols // (2 * CHUNKS * group)
                    for c, half in enumerate(halves(0, rows, 0, per * group)):
                        for s in range(group):
                            at = ((s * 2 + c) * CHUNKS + chunk) * per
                            grad_ref[:, at : at + per] = half[:, s * per : (s + 1) * per]
                elif kind == "down":
                    per = rows // (2 * CHUNKS)
                    for c, half in enumerate(halves(0, per, 0, cols)):
                        at = (c * CHUNKS + chunk) * per
                        grad_ref[at : at + per, :] = half
                else:
                    amount_of = len(shares[number])
                    lanes_of = cols // (2 * SPLIT[kind] * amount_of)
                    for slot in range(SPLIT[kind]):
                        for c, half in enumerate(halves(0, rows, slot * lanes_of, lanes_of)):
                            at = ((2 * slot + c) * amount_of + chunk) * lanes_of
                            grad_ref[:, at : at + lanes_of] = half
            squared = grad_ref[...] * grad_ref[...]
            new_rows = 0.5 * to_column(state_refs[number][...]) + 0.5 * jnp.mean(
                squared, axis=1, keepdims=True
            )
            row_refs[number][...] = to_row(new_rows)
            pack_ref[0:1, at_pack : at_pack + cols] = jnp.sum(squared, axis=0, keepdims=True)
            pack_ref[1:2, at_pack : at_pack + cols] = jnp.sum(
                squared * (1.0 / new_rows), axis=0, keepdims=True
            )
            at_pack += cols
            weight = weight_ref[...]
            pack_ref[0:1, at_pack : at_pack + LANES] = jnp.broadcast_to(
                jnp.sum(new_rows, axis=0, keepdims=True), (1, LANES)
            )
            pack_ref[1:2, at_pack : at_pack + LANES] = jnp.broadcast_to(
                jnp.sum(jnp.sum(weight * weight, axis=0, keepdims=True), axis=1, keepdims=True),
                (1, LANES),
            )
            at_pack += LANES
        at = 0
        if vectors:
            place_row = lax.broadcasted_iota(jnp.int32, extra[0].shape, 0)
            here = place_row == place_ref[0] * 2 + place_ref[1]
            mine = jnp.sum(
                jnp.where(here, terms_ref[...], 0.0), axis=0, keepdims=True
            )
        for number in range(vectors):
            size = extra[1][number].shape[1]
            grad = mine[:, at : at + size] * (1.0 / images)
            at += size
            param = param_refs[number][...]
            moment = 0.5 * moment_refs[number][...] + 0.5 * grad * grad
            direction = grad * lax.rsqrt(moment)
            vector_grads[number][...] = grad
            new_moments[number][...] = moment
            for row, value in enumerate((direction, param)):
                pack_ref[row : row + 1, at_pack : at_pack + LANES] = jnp.broadcast_to(
                    jnp.sum(value * value, axis=1, keepdims=True), (1, LANES)
                )
            at_pack += LANES

    lanes = sum(weight.shape[1] + LANES for weight in weights) + vectors * LANES
    ins = [*flat, *weights, *states]
    outs = [sds(weight.shape, jnp.float32) for weight in weights]
    outs += [sds(state.shape, jnp.float32) for state in states]
    outs.append(sds((2, lanes), jnp.float32))
    if vectors:
        terms, params, moments = extra
        ins += [terms, *params, *moments]
        outs += [sds(a.shape, jnp.float32) for a in (*params, *moments)]
    results = call(
        body,
        place,
        tuple(ins),
        [whole(a.shape) for a in ins],
        outs,
        [whole(a.shape) for a in outs],
        [],
        "statistics",
    )
    return (
        results[:amount],
        results[amount : 2 * amount],
        results[2 * amount],
        results[2 * amount + 1 : 2 * amount + 1 + vectors],
        results[2 * amount + 1 + vectors :],
    )


CLIP_ORDER = (8, 10, 4, 2)
SPLIT = {"out": 1, "qkv": 3}


def update(place, grads, new_rows, weights, cols_states, pack, group, extra=None, clips=None):
    amount = len(weights)
    vectors = 0 if extra is None else len(extra[0])

    def body(place_ref, *refs):
        refs = list(refs)

        def take(n):
            taken = refs[:n]
            del refs[:n]
            return taken

        grad_refs, row_refs, weight_refs, state_refs = [take(amount) for _ in range(4)]
        (pack_ref,) = take(1)
        if vectors:
            vector_grads, moment_refs, param_refs = [take(vectors) for _ in range(3)]
            (clips_ref,) = take(1)
        new_refs, col_refs = take(amount), take(amount)
        (clip_ref,) = take(1)
        param_outs = take(vectors)
        at_pack = 0
        if not vectors:
            clip_ref[...] = jnp.zeros(clip_ref.shape, jnp.float32)
        for number in range(amount):
            rows, cols = weights[number].shape
            rows_total = rows * group
            count = rows_total * cols
            new_cols = (
                0.5 * state_refs[number][...]
                + 0.5 * pack_ref[0:1, at_pack : at_pack + cols] / rows_total
            )
            col_refs[number][...] = new_cols
            by_rows = pack_ref[1:2, at_pack : at_pack + cols]
            at_pack += cols
            mean_rows = pack_ref[0:1, at_pack : at_pack + 1] / rows_total
            weight_total = pack_ref[1:2, at_pack : at_pack + 1]
            at_pack += LANES
            total = mean_rows * jnp.sum(by_rows / new_cols, axis=1, keepdims=True)
            clip = jnp.maximum(1.0, jnp.sqrt(total / count) / clip_level)
            step = step_rate * jnp.sqrt(weight_total / count) / clip
            if vectors:
                if number == 0:
                    found = [clips_ref[at : at + 1, :1] for at in range(len(MATRICES) - amount)]
                found.append(clip)
            else:
                clip_ref[number : number + 1, :] = jnp.broadcast_to(clip, (1, LANES))
            estimate = to_column(row_refs[number][...]) * (new_cols / mean_rows)
            new_refs[number][...] = weight_refs[number][...] - step * (
                grad_refs[number][...] * lax.rsqrt(estimate)
            )
        for number in range(vectors):
            count = extra[2][number].shape[1] * group
            total = pack_ref[0:1, at_pack : at_pack + 1]
            weight_total = pack_ref[1:2, at_pack : at_pack + 1]
            at_pack += LANES
            clip = jnp.maximum(1.0, jnp.sqrt(total / count) / clip_level)
            step = step_rate * jnp.sqrt(weight_total / count) / clip
            found.append(clip)
            direction = vector_grads[number][...] * lax.rsqrt(moment_refs[number][...])
            param_outs[number][...] = param_refs[number][...] - step * direction
        if vectors:
            lane = lax.broadcasted_iota(jnp.int32, (1, LANES), 1)
            row = jnp.zeros((1, LANES), jnp.float32)
            for value, number in zip(found, (*CLIP_ORDER, *VECTORS)):
                row = jnp.where(lane == number, value, row)
            clip_ref[...] = row[:, : len(found)]

    ins = [*grads, *new_rows, *weights, *cols_states, pack]
    outs = [sds(a.shape, jnp.float32) for a in (*weights, *cols_states)]
    outs.append(sds((1, len(MATRICES) + vectors) if vectors else (8, LANES), jnp.float32))
    if vectors:
        ins += [*extra[0], *extra[1], *extra[2], clips]
        outs += [sds(a.shape, jnp.float32) for a in extra[2]]
    results = call(
        body,
        place,
        tuple(ins),
        [whole(a.shape) for a in ins],
        outs,
        [whole(a.shape) for a in outs],
        [],
        "update",
    )
    return (
        results[:amount],
        results[amount : 2 * amount],
        results[2 * amount],
        results[2 * amount + 1 :],
    )


def pack_terms(place, sums_mid, sums_in, sums_qkv, hidden_sums, down_sums, sizes):
    z_size = lax.axis_size("z")
    shards = 2 * z_size
    per_shard = sizes[6] // 2 // CHUNKS
    heads = sums_qkv[0].shape[1]

    def body(place_ref, mid_ref, in_ref, *refs):
        qkv_refs, refs = refs[:GROUPS], refs[GROUPS:]
        hidden_refs, (down_ref, out_ref) = refs[:CHUNKS], refs[CHUNKS:]
        core = place_ref[2]

        def put(slot, row):
            at, size = sum(sizes[:slot]), sizes[slot]
            for s in range(shards):
                out_ref[s : s + 1, at : at + size] = row[:, s * size : (s + 1) * size]

        put(0, in_ref[0:1, :])
        put(1, in_ref[1:2, :])
        zero = jnp.zeros((1, heads * GROUPS), jnp.float32)
        halves = []
        for slot in (0, 2):
            row = jnp.concatenate([ref[slot : slot + 1, :] for ref in qkv_refs], axis=1)
            halves += [select(core, row, zero), select(core, zero, row)]
        put(2, jnp.concatenate(halves, axis=1))
        put(3, mid_ref[2:3, :])
        put(4, mid_ref[0:1, :])
        put(5, mid_ref[1:2, :])
        put(7, down_ref[...])
        none = jnp.zeros((1, per_shard), jnp.float32)
        for s in range(shards):
            for j in range(CHUNKS):
                row = hidden_refs[j][:, s * per_shard : (s + 1) * per_shard]
                for c in range(2):
                    at = sum(sizes[:6]) + (c * CHUNKS + j) * per_shard
                    here = select(core, row, none) if c == 0 else select(core, none, row)
                    out_ref[s : s + 1, at : at + per_shard] = here

    ins = (sums_mid, sums_in, *sums_qkv, *hidden_sums, down_sums)
    shape = (shards, sum(sizes))
    return call(
        body,
        place,
        ins,
        [whole(a.shape) for a in ins],
        [sds(shape, jnp.float32)],
        [whole(shape)],
        [],
        "pack_terms",
    )[0]


def on_device(
    inputs,
    cotangent,
    norm1_gain,
    norm1_bias,
    qkv_weight,
    qv_bias,
    out_weight,
    out_bias,
    norm2_gain,
    norm2_bias,
    in_weight,
    in_bias,
    down_weight,
    down_bias,
    qkv_rows,
    qkv_cols,
    out_rows,
    out_cols,
    in_rows,
    in_cols,
    down_rows,
    down_cols,
    norm1_gain_moment,
    norm1_bias_moment,
    qv_bias_moment,
    out_bias_moment,
    norm2_gain_moment,
    norm2_bias_moment,
    in_bias_moment,
    down_bias_moment,
):
    masters = [
        norm1_gain,
        norm1_bias,
        qkv_weight,
        qv_bias,
        out_weight,
        out_bias,
        norm2_gain,
        norm2_bias,
        in_weight,
        in_bias,
        down_weight,
        down_bias,
    ]
    moments = [
        norm1_gain_moment,
        norm1_bias_moment,
        qv_bias_moment,
        out_bias_moment,
        norm2_gain_moment,
        norm2_bias_moment,
        in_bias_moment,
        down_bias_moment,
    ]
    place = jnp.stack([lax.axis_index(axis) for axis in ("z", "x", "c", "y")]).astype(jnp.int32)
    by_y = lax.axis_size("y") == 2
    group = lax.axis_size("z") * lax.axis_size("x")
    tokens = inputs.shape[0]
    part = in_weight.shape[0]
    images = (tokens // SEQ) * group * lax.axis_size("y") * lax.axis_size("c")
    as_row = lambda vector: vector.reshape(1, -1)
    params = [as_row(masters[number]) for number in VECTORS]
    moments = [as_row(moment) for moment in moments]
    sizes = [param.shape[1] for param in params]

    shard_first, shard_next = prepare_qkv(place, qkv_weight, out_weight, params)
    near = along_z(shard_first)
    pieces_first = by_x(near)
    near_next = along_z(after(shard_next, near))
    rows_own, parts = pad_rows(after(place, near), inputs)
    rows = (rows_own, [swap(one, "c") for one in parts])
    *shards_ff, down_sums = prepare_rest(
        after(place, rows_own), in_weight, down_weight, cotangent, (2 if by_y else 1, 1)
    )
    cot_own, parts = pad_rows(after(place, (down_sums, rows[1])), cotangent)
    near_ff = [along_z(shards_ff[0])]

    normed, *first, vectors, hidden_bias = project_first(
        after(place, (cot_own, near_next)), rows, pieces_first, sizes
    )
    near_ff.append(along_z(after(shards_ff[1], normed)))
    cot = (cot_own, [swap(one, "c") for one in after(parts, normed)])
    qkv = [first]
    pieces_next = by_x(near_next)
    mixed, prob = attention(place, *first)
    attended = [mixed]
    probs = [prob]
    theirs = [swap(mixed, "c")]
    pieces_next = after(pieces_next, mixed)
    weight_mine = gather_out(place, pieces_next, 3 * first[0].shape[-1])
    weight_theirs = swap(weight_mine, "c")
    near_ff[0] = after(near_ff[0], pieces_next)
    across = swap(near_ff[0], "x")
    near_too = swap(near_ff[0], "y") if by_y else None
    qkv.append(
        project_next(
            after(place, (near_ff[0], weight_mine)), normed, vectors, pieces_next, 1
        )
    )
    mixed, prob = attention(place, *qkv[1])
    attended.append(mixed)
    probs.append(prob)
    theirs.append(swap(mixed, "c"))
    across = after(across, mixed)
    if by_y:
        pieces_ff = [[near_ff[0], near_too], [across, swap(across, "y")]]
    else:
        pieces_ff = [[near_ff[0]], [across]]
    middle, normed_mid = project_out(
        after(place, (across, near_too)), attended, theirs, weight_mine, weight_theirs, rows, vectors
    )
    near_ff[1] = after(near_ff[1], normed_mid)
    pieces_next_ff = by_x(near_ff[1])
    *running, sums, keep, send = feed_forward(
        after(place, near_ff[1]), normed_mid, cot, pieces_ff, hidden_bias, 0, None
    )
    hidden_sums = [sums]
    got = swap(send, "x")
    *running, sums, keep_next, send_next = feed_forward(
        place, normed_mid, cot, pieces_next_ff, hidden_bias, 1, running
    )
    hidden_sums.append(sums)
    folded = [fold(*after((keep, got), sums))]
    got_next = swap(send_next, "x")
    scattered = [scatter_z(folded[0])]
    out_share, out_given, normed_share, normed_given = running
    sums_mid, output, grad_mid, grad_mid_low = norm_back(
        after(place, folded[0]),
        middle,
        vectors,
        GAIN_TWO,
        normed_share,
        [swap(normed_given, "c")],
        cot_own,
        tokens,
        (out_share, swap(out_given, "c")),
    )
    *grad_attended, keep, send = out_back(
        place,
        grad_mid_low,
        swap(grad_mid_low, "c"),
        attended,
        theirs,
        weight_mine,
        weight_theirs,
    )
    got = swap(send, "x")
    grad_qkv = [attention_back(place, *qkv[0], probs[0], grad_attended[0])]
    sums_first, keep_first, send_first = qkv_term(place, normed, *grad_qkv[0])
    got_first = swap(send_first, "x")
    folded.append(fold(*after((keep_next, got_next), sums_first)))
    scattered.append(scatter_z(folded[1]))
    scattered[0] = after(scattered[0], folded[1])
    own_ff = [sum_y(scattered[0])]
    grad_qkv.append(
        attention_back(after(place, scattered[0]), *qkv[1], probs[1], grad_attended[1])
    )
    own_ff[0] = after(own_ff[0], grad_qkv[1][0])
    sums_next, keep_next, send_next = qkv_term(
        after(place, own_ff[0]), normed, *grad_qkv[1]
    )
    sums_qkv = [sums_first, sums_next]
    got_next = swap(send_next, "x")
    held = after(((keep, got), (keep_first, got_first)), sums_next)
    folded.append(jnp.concatenate([fold(*one) for one in held], axis=1))
    scattered.append(scatter_z(folded[2]))
    share, *given = qkv_back(after(place, folded[2]), grad_qkv, [pieces_first, pieces_next])
    pairs = [with_core(own_ff[0])]
    scattered[1] = after(scattered[1], share)
    own_ff.append(sum_y(scattered[1]))
    sums_in, input_grad = norm_back(
        after(place, scattered[1]),
        rows_own,
        vectors,
        GAIN_ONE,
        share,
        [swap(one, "c") for one in given],
        grad_mid,
        tokens,
    )
    packed = pack_terms(
        place, sums_mid, sums_in, sums_qkv, hidden_sums, down_sums, sizes
    )
    folded.append(fold(*after((keep_next, got_next), packed)))
    scattered.append(scatter_z(folded[3]))
    pairs.append(with_core(after(own_ff[1], folded[3])))
    terms = sum_over(packed, ("c", "z", "x", "y"))

    weights = [in_weight, down_weight]
    states = [as_row(state) for state in (in_rows, down_rows)]
    grads_early, rows_early, pack, _, _ = statistics(
        place,
        ("in", "down"),
        pairs[:CHUNKS],
        [[(j, row, 0) for j in range(CHUNKS)] for row in (0, part)],
        weights,
        states,
        images,
        group,
    )
    scattered[2] = after(scattered[2], rows_early[0])
    own_mid = sum_y(scattered[2])
    new_early, cols_early, clips_early, _ = update(
        after(place, (terms, scattered[2])),
        grads_early,
        rows_early,
        weights,
        [as_row(state) for state in (in_cols, down_cols)],
        sum_over(pack, ("z", "x")),
        group,
    )
    pairs.append(with_core(after(own_mid, clips_early)))
    pairs.append(with_core(sum_y(after(scattered[3], clips_early))))
    weights = [out_weight, qkv_weight]
    grads_late, rows_late, pack, vector_grads, new_moments = statistics(
        after(place, clips_early),
        ("out", "qkv"),
        pairs[CHUNKS:],
        [[(0, 0, 0)], [(0, 0, out_weight.shape[1] // 2), (1, 0, 0)]],
        weights,
        [as_row(state) for state in (out_rows, qkv_rows)],
        images,
        group,
        (terms, params, moments),
    )
    new_late, cols_late, clip_factors, new_vectors = update(
        place,
        grads_late,
        rows_late,
        weights,
        [as_row(state) for state in (out_cols, qkv_cols)],
        sum_over(pack, ("z", "x")),
        group,
        (vector_grads, new_moments, params),
        clips_early,
    )

    flat = lambda value: value.reshape(-1)
    grads = [None] * 12
    new_params = [None] * 12
    for number, slot in ((8, 0), (10, 1)):
        grads[number], new_params[number] = grads_early[slot], new_early[slot]
    for number, slot in ((4, 0), (2, 1)):
        grads[number], new_params[number] = grads_late[slot], new_late[slot]
    for slot, number in enumerate(VECTORS):
        grads[number] = flat(vector_grads[slot])
        new_params[number] = flat(new_vectors[slot])
    return (
        output,
        input_grad,
        *grads,
        flat(rows_late[1]),
        flat(cols_late[1]),
        flat(rows_late[0]),
        flat(cols_late[0]),
        flat(rows_early[0]),
        flat(cols_early[0]),
        flat(rows_early[1]),
        flat(cols_early[1]),
        *[flat(moment) for moment in new_moments],
        *new_params,
        flat(clip_factors),
    )


def solution(mesh):
    group = mesh.shape["fsdp"]
    split = Mesh(mesh.devices.reshape(group // 2, 2, mesh.shape["dp"] // 2, 2), ALL_AXES)
    in_specs = (
        P(("z", "x", "y", "c"), None),
        P(("z", "x", "y", "c"), None),
        P(("z", "x")),
        P(("z", "x")),
        P(("z", "x"), None),
        P(("z", "x")),
        P(("z", "x"), None),
        P(("z", "x")),
        P(("z", "x")),
        P(("z", "x")),
        P(("z", "x"), None),
        P(("z", "x")),
        P(("z", "x"), None),
        P(("z", "x")),
        P(("z", "x")),
        P(),
        P(("z", "x")),
        P(),
        P(("z", "x")),
        P(),
        P(("z", "x")),
        P(),
        P(("z", "x")),
        P(("z", "x")),
        P(("z", "x")),
        P(("z", "x")),
        P(("z", "x")),
        P(("z", "x")),
        P(("z", "x")),
        P(("z", "x")),
    )
    out_specs = (
        P(("z", "x", "y", "c"), None),
        P(("z", "x", "y", "c"), None),
        P(("z", "x")),
        P(("z", "x")),
        P(("z", "x"), None),
        P(("z", "x")),
        P(("z", "x"), None),
        P(("z", "x")),
        P(("z", "x")),
        P(("z", "x")),
        P(("z", "x"), None),
        P(("z", "x")),
        P(("z", "x"), None),
        P(("z", "x")),
        P(("z", "x")),
        P(),
        P(("z", "x")),
        P(),
        P(("z", "x")),
        P(),
        P(("z", "x")),
        P(),
        P(("z", "x")),
        P(("z", "x")),
        P(("z", "x")),
        P(("z", "x")),
        P(("z", "x")),
        P(("z", "x")),
        P(("z", "x")),
        P(("z", "x")),
        P(("z", "x")),
        P(("z", "x")),
        P(("z", "x"), None),
        P(("z", "x")),
        P(("z", "x"), None),
        P(("z", "x")),
        P(("z", "x")),
        P(("z", "x")),
        P(("z", "x"), None),
        P(("z", "x")),
        P(("z", "x"), None),
        P(("z", "x")),
        P(),
    )
    return jax.shard_map(
        on_device, mesh=split, in_specs=in_specs, out_specs=out_specs, check_vma=False
    )
```

```python
import math

import jax
import jax.numpy as jnp
from jax import lax
from jax.experimental import pallas as pl
from jax.experimental.pallas import tpu as pltpu
from jax.sharding import Mesh
from jax.sharding import PartitionSpec as P

HEAD_DIM = 64
SEQ = 577
LANES = 128
TILE = 16
CHUNKS = 2
GROUPS = 2
GIVEN = 2
VMEM_LIMIT = 60
VMEM_LIMITS = {
    "attention": 30,
    "attention_back": 30,
    "gather_out": 30,
    "norm_back": 30,
    "out_back": 40,
    "pack_terms": 30,
    "project_next": 40,
    "qkv_term": 30,
}

ALL_AXES = ("z", "x", "y", "c")

MATRICES = (2, 4, 8, 10)
VECTORS = (0, 1, 3, 5, 6, 7, 9, 11)

ln_eps = 1e-06
clip_level = 0.05
step_rate = 4.0


def swap(value, axis):
    return lax.ppermute(value, axis, [(0, 1), (1, 0)])


def shift(value, axis, step):
    size = lax.axis_size(axis)
    return lax.ppermute(value, axis, [(i, (i + step) % size) for i in range(size)])


def partner(value, axis, step):
    size = lax.axis_size(axis)
    return lax.ppermute(value, axis, [(i, i ^ step) for i in range(size)])


def sum_over(value, axes):
    for axis in axes:
        if lax.axis_size(axis) == 4:
            got = [shift(value, axis, step) for step in (1, 2, 3)]
            value = (value + got[1]) + (got[0] + got[2])
            continue
        step = 1
        while step < lax.axis_size(axis):
            value = value + partner(value, axis, step)
            step *= 2
    return value


def along_z(shard):
    near = lax.all_gather(shard, "z", axis=0, tiled=True)
    return near.reshape(lax.axis_size("z"), *shard.shape)


def by_x(near):
    return [[near], [swap(near, "x")]]


def by_y_too(pieces, by_y):
    return [[one, swap(one, "y")] if by_y else [one] for (one,) in pieces]


def after(values, token):
    return lax.optimization_barrier((values, token))[0]


def fold(keep, got):
    total = low(wide(keep) + wide(got))
    return total.reshape(-1, total.shape[-1])


def fold_pair(keep_one, got_one, keep_two, got_two):
    both = [low(wide(keep_one) + wide(got_one)), low(wide(keep_two) + wide(got_two))]
    total = jnp.concatenate(both, axis=1)
    return total.reshape(-1, total.shape[-1])


def scatter_z(total):
    return lax.psum_scatter(total, "z", scatter_dimension=0, tiled=True)


def sum_y(mine):
    if lax.axis_size("y") == 2:
        return [mine, swap(mine, "y")]
    return [lax.psum(wide(mine), "y")]


def with_core(own):
    return own, [swap(one, "c") for one in own]


def sum_y_and_core(mine):
    if lax.axis_size("y") != 2:
        return with_core(sum_y(mine))
    across = lax.ppermute(mine, ("y", "c"), [(i, 3 - i) for i in range(4)])
    return [mine, swap(mine, "y")], [swap(mine, "c"), across]


def row_pad(length):
    return -(-length // LANES) * LANES


def dot(left, right):
    return jnp.dot(left, right, preferred_element_type=jnp.float32)


def dot_tail(left, right):
    return lax.dot_general(
        left, right, (((1,), (1,)), ((), ())), preferred_element_type=jnp.float32
    )


def low(value):
    return value.astype(jnp.bfloat16)


def wide(value):
    return value.astype(jnp.float32)


def any_spec():
    return pl.BlockSpec(memory_space=pl.ANY)


def whole(shape):
    return pl.BlockSpec(shape, lambda *_: (0,) * len(shape))


def sds(shape, dtype):
    return jax.ShapeDtypeStruct(shape, dtype)


def call(body, place, ins, in_specs, outs, out_specs, scratch, name, grid=(1,)):
    return pl.pallas_call(
        body,
        out_shape=outs,
        grid_spec=pltpu.PrefetchScalarGridSpec(
            num_scalar_prefetch=1,
            grid=grid,
            in_specs=in_specs,
            out_specs=out_specs,
            scratch_shapes=scratch,
        ),
        compiler_params=pltpu.CompilerParams(
            vmem_limit_bytes=VMEM_LIMITS.get(name, VMEM_LIMIT) * 1024 * 1024, dimension_semantics=("arbitrary",) * len(grid)
        ),
        name=name,
    )(place, *ins)


def shard_number(place_ref, z, dx):
    return z * 2 + dx + (1 - 2 * dx) * place_ref[1]


def normalised(rows):
    centre = rows - jnp.mean(rows, axis=-1, keepdims=True)
    spread = jnp.mean(centre * centre, axis=-1, keepdims=True)
    return centre * lax.rsqrt(spread + ln_eps)


def select(core, first, second):
    return jnp.where(core == 0, first, second)


def prepare_qkv(place, weight, out_weight, vectors):
    part, cols = weight.shape
    half = cols // 6
    heads = half // GROUPS
    width = 3 * heads
    sizes = [vector.shape[-1] for vector in vectors]
    tiles = -(-sum(sizes) // width)

    out_half = out_weight.shape[1] // 2

    def body(place_ref, weight_ref, out_ref, *refs):
        refs, groups = refs[: len(sizes)], refs[len(sizes) :]
        core = place_ref[2]
        for number, ref in enumerate(groups):
            for slot in range(3):
                at = 2 * slot * half + number * heads
                ref[:part, slot * heads : (slot + 1) * heads] = low(
                    select(
                        core,
                        weight_ref[:, at : at + heads],
                        weight_ref[:, at + half : at + half + heads],
                    )
                )
        groups[-1][:, width:] = low(select(core, out_ref[:, :out_half], out_ref[:, out_half:]))
        at = 0
        for ref, size in zip(refs, sizes):
            done = 0
            while done < size:
                tile, lane = divmod(at + done, width)
                count = min(size - done, width - lane)
                row = part + tile * TILE
                groups[0][row : row + TILE, lane : lane + count] = low(
                    jnp.broadcast_to(ref[:, done : done + count], (TILE, count))
                )
                done += count
            at += size

    shapes = [
        (part + (tiles * TILE if g == 0 else 0), width + (out_half if g == GROUPS - 1 else 0))
        for g in range(GROUPS)
    ]
    return call(
        body,
        place,
        (weight, out_weight, *vectors),
        [whole((part, cols)), whole(out_weight.shape)] + [whole((1, size)) for size in sizes],
        [sds(shape, jnp.bfloat16) for shape in shapes],
        [whole(shape) for shape in shapes],
        [],
        "prepare_qkv",
    )


def pad_rows(place, rows):
    tokens, width = rows.shape
    length = row_pad(tokens)
    even = tokens // TILE * TILE
    cols = width // GIVEN

    def body(place_ref, ref, to, *parts):
        row = lax.broadcasted_iota(jnp.int32, (length - even, width), 0)
        last = jnp.zeros((length - even, width), jnp.float32)
        for extra in range(tokens - even):
            one = wide(ref[even + extra : even + extra + 1, :])
            last = jnp.where(row == extra, one, last)
        to[:even, :] = ref[:even, :]
        to[even:, :] = low(last)
        for number, part in enumerate(parts):
            lanes = slice(number * cols, (number + 1) * cols)
            part[...] = to[:, lanes]

    shapes = [(length, width)] + [(length, cols)] * GIVEN
    whole_rows, *parts = call(
        body,
        place,
        (rows,),
        [whole(rows.shape)],
        [sds(shape, jnp.bfloat16) for shape in shapes],
        [whole(shape) for shape in shapes],
        [],
        "pad_rows",
    )
    return whole_rows, parts


def joined(refs, rows=slice(None)):
    return jnp.concatenate([ref[rows, :] for ref in refs], axis=1)


def prepare_rest(place, in_weight, down_weight, cotangent, cuts):
    part, hidden = in_weight.shape
    width = down_weight.shape[1]
    per_core = down_weight.shape[0] // 2
    per_shard = per_core // CHUNKS
    shards = hidden // (2 * per_core)
    def body(place_ref, in_ref, down_ref, cot_ref, *refs):
        pieces, (sum_ref,) = refs[:CHUNKS], refs[CHUNKS:]
        core, y = place_ref[2], place_ref[3]

        def pick(ref, row, count, step, col, cols, by_row, cut):
            def of_core(r):
                if by_row:
                    return select(
                        core, ref[r : r + count, col : col + cols], ref[r + step : r + step + count, col : col + cols]
                    )
                return select(
                    core, ref[r : r + count, col : col + cols], ref[r : r + count, col + step : col + step + cols]
                )

            if cut == 1:
                return low(of_core(row))
            return low(select(y, of_core(row), of_core(row + count)))

        for j, cut in enumerate(cuts):
            rows_in, rows_down = part // cut, per_shard // cut
            for s in range(shards):
                at = s * 2 * per_core + j * per_shard
                pieces[j][:rows_in, s * per_shard : (s + 1) * per_shard] = pick(
                    in_ref, 0, rows_in, per_core, at, per_shard, False, cut
                )
            pieces[j][rows_in:, :] = pick(
                down_ref, j * per_shard, rows_down, per_core, 0, width, True, cut
            )
        sum_ref[...] = jnp.sum(wide(cot_ref[...]), axis=0, keepdims=True)

    outs = [sds(((part + per_shard) // cut, width), jnp.bfloat16) for cut in cuts]
    outs += [sds((1, width), jnp.float32)]
    ins = (in_weight, down_weight, cotangent)
    return call(
        body,
        place,
        ins,
        [whole(a.shape) for a in ins],
        outs,
        [whole(a.shape) for a in outs],
        [],
        "prepare_rest",
    )


GAIN_ONE, BIAS_ONE, BIAS_OUT, GAIN_TWO, BIAS_TWO, BIAS_DOWN, BIAS_QV = range(7)


def weight_copies(place_ref, ins, weight, part, sem):
    made = []
    for dx, ref in enumerate(ins):
        for z in range(ref.shape[0]):
            row = pl.multiple_of(shard_number(place_ref, z, dx) * part, part)
            made.append(
                pltpu.make_async_copy(
                    ref.at[z, pl.ds(0, part), pl.ds(0, weight.shape[1])],
                    weight.at[pl.ds(row, part), :],
                    sem.at[len(made)],
                )
            )
    return made


def write_qkv(normed, weight, bias_q, bias_v, image, q_ref, k_ref, v_ref):
    heads = weight.shape[1] // 3
    query = low(dot(normed, weight[:, :heads]) + bias_q)
    q_ref[image] = low(wide(query) * (1.0 / math.sqrt(HEAD_DIM)))
    k_ref[image] = low(dot(normed, weight[:, heads : 2 * heads]))
    v_ref[image] = low(dot(normed, weight[:, 2 * heads :]) + bias_v)


def project_first(place, rows, pieces, sizes):
    flat = [one for (one,) in pieces]
    z_size, part, cols = flat[0].shape
    rows_own, rows_other = rows
    length, width = rows_own.shape
    count = 2 * z_size
    tiles = (part - width // count) // TILE
    part = width // count
    heads = cols // 3
    half = heads * GROUPS
    starts = [sum(sizes[:number]) for number in range(len(sizes))]
    per_shard = sizes[6] // 2 // CHUNKS
    blocks = count // 2

    def body(place_ref, own_ref, *refs):
        other_refs, refs = refs[:GIVEN], refs[GIVEN:]
        ins, refs = refs[:2], refs[2:]
        normed_ref, q_ref, k_ref, v_ref, vec_ref, hidden_bias_ref, weight, packed, sem = refs
        core = place_ref[2]
        copies = []
        for dx, ref in enumerate(ins):
            for z in range(z_size):
                copies.append(
                    pltpu.make_async_copy(
                        ref.at[z, pl.ds(part, tiles * TILE), :],
                        packed.at[shard_number(place_ref, z, dx)],
                        sem.at[count + len(copies)],
                    )
                )
        copies += weight_copies(place_ref, ins, weight, part, sem)
        for copy in copies:
            copy.start()
        for copy in copies:
            copy.wait()

        def lanes(s, at, size):
            found = []
            done = 0
            while done < size:
                tile, lane = divmod(at + done, cols)
                take = min(size - done, cols - lane)
                found.append(wide(packed[s, tile * TILE : tile * TILE + 1, lane : lane + take]))
                done += take
            return found

        def vector(slot, shards=range(count)):
            return jnp.concatenate(
                [one for s in shards for one in lanes(s, starts[slot], sizes[slot])], axis=1
            )

        gain, bias = vector(0), vector(1)
        bias_q = vector(2, range(blocks))
        bias_v = vector(2, range(blocks, count))
        bias_q = select(core, bias_q[:, :half], bias_q[:, half:])
        bias_v = select(core, bias_v[:, :half], bias_v[:, half:])
        for row, value in (
            (GAIN_ONE, gain),
            (BIAS_ONE, bias),
            (BIAS_OUT, vector(3)),
            (GAIN_TWO, vector(4)),
            (BIAS_TWO, vector(5)),
            (BIAS_DOWN, vector(7)),
            (BIAS_QV, jnp.concatenate([bias_q, bias_v], axis=1)),
        ):
            vec_ref[row : row + 1, :] = value
        vec_ref[7:8, :] = jnp.zeros((1, width), jnp.float32)
        for j in range(CHUNKS):
            for s in range(count):
                at = starts[6] + j * per_shard
                to = at + sizes[6] // 2
                hidden_bias_ref[j, :, s * per_shard : (s + 1) * per_shard] = select(
                    core,
                    jnp.concatenate(lanes(s, at, per_shard), axis=1),
                    jnp.concatenate(lanes(s, to, per_shard), axis=1),
                )
        for image, part_refs in enumerate(((own_ref,), other_refs)):
            for at in range(0, length, LANES):
                block = wide(joined(part_refs, slice(at, at + LANES)))
                normed_ref[image, at : at + LANES, :] = low(normalised(block) * gain + bias)

        def one_image(image, carry):
            write_qkv(
                normed_ref[image],
                weight,
                bias_q[:, :heads],
                bias_v[:, :heads],
                image,
                q_ref,
                k_ref,
                v_ref,
            )
            return carry

        lax.fori_loop(0, 2, one_image, 0)

    part_out = sds((2, length, heads), jnp.bfloat16)
    return call(
        body,
        place,
        (rows_own, *rows_other, *flat),
        [whole((length, width))]
        + [whole((length, width // GIVEN))] * GIVEN
        + [any_spec()] * 2,
        [sds((2, length, width), jnp.bfloat16)]
        + [part_out] * 3
        + [
            sds((8, width), jnp.float32),
            sds((CHUNKS, 1, count * per_shard), jnp.float32),
        ],
        [whole((2, length, width))]
        + [whole((2, length, heads))] * 3
        + [whole((8, width)), whole((CHUNKS, 1, count * per_shard))],
        [
            pltpu.VMEM((width, cols), jnp.bfloat16),
            pltpu.VMEM((count, tiles * TILE, cols), jnp.bfloat16),
            pltpu.SemaphoreType.DMA((2 * count,)),
        ],
        "project_first",
    )


def project_next(place, normed, vectors, pieces, group):
    flat = [one for (one,) in pieces]
    z_size, part, _ = flat[0].shape
    _, length, width = normed.shape
    half = width // 2
    heads = half // GROUPS
    cols = 3 * heads

    def body(place_ref, normed_ref, vec_ref, *refs):
        ins, (q_ref, k_ref, v_ref, weight, sem) = refs[:2], refs[2:]
        copies = weight_copies(place_ref, ins, weight, part, sem)
        for copy in copies:
            copy.start()
        for copy in copies:
            copy.wait()
        at = group * heads
        bias_q = vec_ref[BIAS_QV : BIAS_QV + 1, at : at + heads]
        bias_v = vec_ref[BIAS_QV : BIAS_QV + 1, half + at : half + at + heads]

        def one_image(image, carry):
            write_qkv(normed_ref[image], weight, bias_q, bias_v, image, q_ref, k_ref, v_ref)
            return carry

        lax.fori_loop(0, 2, one_image, 0)

    return call(
        body,
        place,
        (normed, vectors, *flat),
        [whole(normed.shape), whole(vectors.shape)] + [any_spec()] * 2,
        [sds((2, length, heads), jnp.bfloat16)] * 3,
        [whole((2, length, heads))] * 3,
        [pltpu.VMEM((width, cols), jnp.bfloat16), pltpu.SemaphoreType.DMA((2 * z_size,))],
        "project_next",
    )


def gather_out(place, pieces, first):
    flat = [one for (one,) in pieces]
    z_size, part, total = flat[0].shape
    half = total - first

    def body(place_ref, *refs):
        ins, out_ref, sem = refs[:2], refs[2], refs[3]
        copies = []
        for dx, ref in enumerate(ins):
            for z in range(z_size):
                row = pl.multiple_of(shard_number(place_ref, z, dx) * part, part)
                copy = pltpu.make_async_copy(
                    ref.at[z, :, pl.ds(first, half)],
                    out_ref.at[pl.ds(row, part), :],
                    sem.at[len(copies)],
                )
                copy.start()
                copies.append(copy)
        for copy in copies:
            copy.wait()

    shape = (2 * z_size * part, half)
    return call(
        body,
        place,
        tuple(flat),
        [any_spec()] * 2,
        [sds(shape, jnp.bfloat16)],
        [whole(shape)],
        [pltpu.SemaphoreType.DMA((2 * z_size,))],
        "gather_out",
    )[0]


def attention(place, query, keys, values):
    _, length, heads = query.shape
    pairs = heads // LANES

    def body(place_ref, q_ref, k_ref, v_ref, out_ref, probs_ref):
        lane = lax.broadcasted_iota(jnp.int32, (length, LANES), 1)
        keys_block = k_ref[0]
        values_t = v_ref[0].T
        query_block = q_ref[0]
        key_row = lax.broadcasted_iota(jnp.int32, (length, length), 0)
        scores = []
        for head in range(2):
            inside = (lane >= head * HEAD_DIM) & (lane < (head + 1) * HEAD_DIM)
            query_head = jnp.where(inside, query_block, jnp.zeros_like(query_block))
            scores.append(jnp.where(key_row < SEQ, dot_tail(keys_block, query_head), -1e30))
        mixed = []
        for head in range(2):
            highest = jnp.max(scores[head], axis=0, keepdims=True)
            exponent = jnp.exp(scores[head] - highest)
            summed = jnp.sum(exponent, axis=0, keepdims=True)
            probs = low(exponent * (1.0 / summed))
            probs_ref[0, 0, head] = probs
            mixed.append(dot(values_t[head * HEAD_DIM : (head + 1) * HEAD_DIM, :], probs))
        out_ref[0] = low(jnp.concatenate(mixed, axis=0).T)

    block = pl.BlockSpec((1, length, LANES), lambda i, j, p: (i, 0, j))
    return call(
        body,
        place,
        (query, keys, values),
        [block] * 3,
        [
            sds((2, length, heads), jnp.bfloat16),
            sds((2, pairs, 2, length, length), jnp.bfloat16),
        ],
        [block, pl.BlockSpec((1, 1, 2, length, length), lambda i, j, p: (i, j, 0, 0, 0))],
        [],
        "attention",
        grid=(2, pairs),
    )


def attention_back(place, query, keys, values, probs, grad):
    _, length, heads = query.shape
    pairs = heads // LANES
    scale = 1.0 / math.sqrt(HEAD_DIM)

    def body(place_ref, q_ref, k_ref, v_ref, p_ref, g_ref, gq_ref, gk_ref, gv_ref):
        lane = lax.broadcasted_iota(jnp.int32, (length, LANES), 1)
        keys_t = k_ref[0].T
        values_block = v_ref[0]
        query_block = q_ref[0]
        grad_block = g_ref[0]
        grad_query = []
        grad_keys = []
        grad_values = []
        for head in range(2):
            inside = (lane >= head * HEAD_DIM) & (lane < (head + 1) * HEAD_DIM)
            grad_head = jnp.where(inside, grad_block, jnp.zeros_like(grad_block))
            probs_low = p_ref[0, 0, head]
            probs_wide = wide(probs_low)
            grad_probs = dot_tail(values_block, grad_head)
            inner = jnp.sum(probs_wide * grad_probs, axis=0, keepdims=True)
            grad_scores = low(probs_wide * (grad_probs - inner))
            keys_head = keys_t[head * HEAD_DIM : (head + 1) * HEAD_DIM, :]
            grad_query.append(dot(keys_head, grad_scores))
            grad_keys.append(dot(grad_scores, query_block))
            grad_values.append(dot(probs_low, grad_block))
        first = lane < HEAD_DIM
        gq_ref[0] = low(jnp.concatenate(grad_query, axis=0).T * scale)
        gk_ref[0] = low(jnp.where(first, grad_keys[0], grad_keys[1]))
        gv_ref[0] = low(jnp.where(first, grad_values[0], grad_values[1]))

    block = pl.BlockSpec((1, length, LANES), lambda i, j, p: (i, 0, j))
    return call(
        body,
        place,
        (query, keys, values, probs, grad),
        [block] * 3
        + [pl.BlockSpec((1, 1, 2, length, length), lambda i, j, p: (i, j, 0, 0, 0)), block],
        [sds((2, length, heads), jnp.bfloat16)] * 3,
        [block] * 3,
        [],
        "attention_back",
        grid=(2, pairs),
    )


def head_rows(core, heads, group):
    mine = pl.multiple_of((core * GROUPS + group) * heads, heads)
    return mine, pl.multiple_of(((1 - core) * GROUPS + group) * heads, heads)


def project_out(place, mine, theirs, weight_mine, weight_theirs, rows, vectors):
    width, half = weight_mine.shape
    _, length, heads = mine[0].shape

    def body(place_ref, *refs):
        mine_refs, theirs_refs, refs = refs[:GROUPS], refs[GROUPS : 2 * GROUPS], refs[2 * GROUPS :]
        wm_ref, wt_ref, own_ref, *other_refs, vec_ref, middle_ref, normed_ref, total = refs
        core = place_ref[2]
        for image, part_refs in enumerate(((own_ref,), other_refs)):
            for slot, weight in enumerate((wm_ref, wt_ref)):
                branch = None
                for g in range(GROUPS):
                    at_mine, at_theirs = head_rows(core, heads, g)
                    add = dot(mine_refs[g][image], weight[pl.ds(at_mine, heads), :]) + dot(
                        theirs_refs[g][1 - image], weight[pl.ds(at_theirs, heads), :]
                    )
                    branch = add if branch is None else branch + add
                total[slot] = branch
            for at in range(0, length, LANES):
                upto = at + LANES
                first, second = total[0, at:upto, :], total[1, at:upto, :]
                left = select(core, first, second)
                right = select(core, second, first)
                middle = (
                    wide(joined(part_refs, slice(at, upto)))
                    + jnp.concatenate([left, right], axis=1)
                    + vec_ref[BIAS_OUT : BIAS_OUT + 1, :]
                )
                if image == 0:
                    middle_ref[at:upto, :] = middle
                normed_ref[image, at:upto, :] = low(
                    normalised(middle) * vec_ref[GAIN_TWO : GAIN_TWO + 1, :]
                    + vec_ref[BIAS_TWO : BIAS_TWO + 1, :]
                )

    return call(
        body,
        place,
        (*mine, *theirs, weight_mine, weight_theirs, rows[0], *rows[1], vectors),
        [whole((2, length, heads))] * (2 * GROUPS)
        + [whole((width, half))] * 2
        + [whole((length, width))]
        + [whole((length, width // GIVEN))] * GIVEN
        + [whole(vectors.shape)],
        [sds((length, width), jnp.float32), sds((2, length, width), jnp.bfloat16)],
        [whole((length, width)), whole((2, length, width))],
        [pltpu.VMEM((2, length, half), jnp.float32)],
        "project_out",
    )


def feed_forward(place, normed, cotangent, pieces, bias, chunk, running):
    cut = len(pieces[0])
    z_size, _, width = pieces[0][0].shape
    hidden_width = bias.shape[2]
    part = width // (2 * z_size)
    per_shard = hidden_width // (2 * z_size)
    rows_in, rows_down = part // cut, per_shard // cut
    _, length, _ = normed.shape
    first_call = running is None
    last_call = chunk == CHUNKS - 1
    given = GIVEN if last_call else 1

    def body(place_ref, normed_ref, own_cot, *refs):
        other_cots, (bias_ref, *refs) = refs[:GIVEN], refs[GIVEN:]
        ins, refs = refs[: 2 * cut], refs[2 * cut :]
        if not first_call:
            before, refs = refs[:4], refs[4:]
        out_own, *out_other = refs[: 1 + given]
        gn_own, *gn_other = refs[1 + given : 2 + 2 * given]
        bsum_ref, *refs = refs[2 + 2 * given :]
        term_refs, refs = refs[:4], refs[4:]
        w_in, w_down, cots, into, down, grads, sem, out_sem = refs
        copies = []
        for weight, at, rows, of_shard in (
            (w_in, 0, rows_in, part),
            (w_down, rows_in, rows_down, per_shard),
        ):
            for number, ref in enumerate(ins):
                dx, h = number // cut, number % cut
                y = h + (1 - 2 * h) * place_ref[3] if cut == 2 else 0
                for z in range(z_size):
                    s = shard_number(place_ref, z, dx)
                    row = pl.multiple_of(s * of_shard + y * rows, rows)
                    copy = pltpu.make_async_copy(
                        ref.at[z, pl.ds(at, rows), :],
                        weight.at[pl.ds(row, rows), :],
                        sem.at[len(copies)],
                    )
                    copy.start()
                    copies.append(copy)
        for copy in copies:
            copy.wait()
        cots[0] = own_cot[...]
        cots[1] = joined(other_cots)

        def one_image(image, carry):
            first = image == 0
            normed_rows = normed_ref[image]
            preact = dot(normed_rows, w_in[...]) + bias_ref[0]
            phi = 0.5 * (1.0 + lax.erf(preact * math.sqrt(0.5)))
            density = jnp.exp(-0.5 * preact * preact) * (1.0 / math.sqrt(2.0 * math.pi))
            hidden = low(preact * phi)
            slope = phi + preact * density
            cot = cots[image]
            grad = low(dot_tail(cot, w_down[...]) * slope)
            to_out = dot(hidden, w_down[...])
            to_normed = dot_tail(grad, w_in[...])
            for slot, to_refs in enumerate((([out_own], [gn_own]), (out_other, gn_other))):

                @pl.when(image == slot)
                def _():
                    for number, (refs_of, value) in enumerate(zip(to_refs, (to_out, to_normed))):
                        if not first_call:
                            value = before[2 * number + slot][...] + value
                        cols = width // len(refs_of)
                        for at, ref in enumerate(refs_of):
                            ref[...] = value[:, at * cols : (at + 1) * cols].astype(ref.dtype)

            partial = jnp.sum(wide(grad), axis=0, keepdims=True)
            to_in = dot(normed_rows.T, grad)
            to_down = dot(hidden.T, cot)

            @pl.when(first)
            def _():
                bsum_ref[...] = partial
                into[...] = to_in
                down[...] = to_down

            @pl.when(jnp.logical_not(first))
            def _():
                bsum_ref[...] += partial
                for slot, (held, value, rows) in enumerate(
                    ((into, to_in, part), (down, to_down, per_shard))
                ):
                    whole_term = low(held[...] + value)
                    for z in range(z_size):
                        for x in range(2):
                            dx = x + (1 - 2 * x) * place_ref[1]
                            s = z * 2 + x
                            grads[slot, dx, z] = whole_term[s * rows : (s + 1) * rows, :]

            return carry

        lax.fori_loop(0, 2, one_image, 0)
        copies = [
            pltpu.make_async_copy(grads.at[number // 2, number % 2], ref, out_sem.at[number])
            for number, ref in enumerate(term_refs)
        ]
        for copy in copies:
            copy.start()
        for copy in copies:
            copy.wait()

    total = sds((length, width), jnp.float32)
    other = sds((length, width // given), jnp.bfloat16 if last_call else jnp.float32)
    totals = ([total] + [other] * given) * 2
    if part != per_shard:
        raise ValueError
    piece_out = sds((z_size, part, width), jnp.bfloat16)
    carried = () if first_call else tuple(running)
    return call(
        body,
        place,
        (normed, cotangent[0], *cotangent[1], bias, *[one for side in pieces for one in side], *carried),
        [whole((2, length, width)), whole((length, width))]
        + [whole((length, width // GIVEN))] * GIVEN
        + [pl.BlockSpec((1, 1, hidden_width), lambda i, p: (chunk, 0, 0))]
        + [any_spec()] * (2 * cut)
        + [whole((length, width))] * len(carried),
        totals + [sds((1, hidden_width), jnp.float32)] + [piece_out] * 4,
        [whole(a.shape) for a in totals] + [whole((1, hidden_width))] + [any_spec()] * 4,
        [
            pltpu.VMEM((width, hidden_width), jnp.bfloat16),
            pltpu.VMEM((hidden_width, width), jnp.bfloat16),
            pltpu.VMEM((2, length, width), jnp.bfloat16),
            pltpu.VMEM((width, hidden_width), jnp.float32),
            pltpu.VMEM((hidden_width, width), jnp.float32),
            pltpu.VMEM((2, 2, z_size, part, width), jnp.bfloat16),
            pltpu.SemaphoreType.DMA((4 * cut * z_size,)),
            pltpu.SemaphoreType.DMA((4,)),
        ],
        "feed_forward",
    )


def norm_back(place, rows, vectors, gain_row, grad_own, others, passed, tokens, finish=()):
    length, width = rows.shape

    def body(place_ref, rows_ref, vec_ref, own_ref, pass_ref, *refs):
        other_refs, refs = refs[: len(others)], refs[len(others) :]
        step = pl.program_id(0)
        values = wide(rows_ref[...])
        if finish:
            first_ref, second_refs, refs = refs[0], refs[1 : len(finish)], refs[len(finish) :]
            refs[1][...] = low(
                values
                + first_ref[...]
                + wide(joined(second_refs))
                + vec_ref[BIAS_DOWN : BIAS_DOWN + 1, :]
            )
        sum_ref = refs[0]
        centre = values - jnp.mean(values, axis=-1, keepdims=True)
        spread = jnp.mean(centre * centre, axis=-1, keepdims=True)
        inverse = lax.rsqrt(spread + ln_eps)
        unit = centre * inverse
        grad = own_ref[...] + wide(joined(other_refs))
        scaled = grad * vec_ref[gain_row : gain_row + 1, :]
        mean_one = jnp.mean(scaled, axis=-1, keepdims=True)
        mean_two = jnp.mean(scaled * unit, axis=-1, keepdims=True)
        result = wide(pass_ref[...]) + (scaled - mean_one - unit * mean_two) * inverse
        rounded = low(result)
        parts = [
            jnp.sum(grad * unit, axis=0, keepdims=True),
            jnp.sum(grad, axis=0, keepdims=True),
            jnp.sum(wide(rounded), axis=0, keepdims=True),
            jnp.zeros((5, width), jnp.float32),
        ]
        if not finish:
            refs[1][...] = rounded
        else:
            refs[2][...] = result
            refs[3][...] = rounded
            for number, ref in enumerate(refs[4:]):
                at = number * width // GIVEN
                ref[...] = rounded[:, at : at + width // GIVEN]
        sums = jnp.concatenate(parts, axis=0)

        @pl.when(step == 0)
        def _():
            sum_ref[...] = sums

        @pl.when(step > 0)
        def _():
            sum_ref[...] += sums

    block = pl.BlockSpec((LANES, width), lambda i, p: (i, 0))
    outs = [sds((8, width), jnp.float32), sds((tokens, width), jnp.bfloat16)]
    if finish:
        outs += [sds((length, width), jnp.float32), sds((length, width), jnp.bfloat16)]
        outs += [sds((length, width // GIVEN), jnp.bfloat16)] * GIVEN
    other_block = pl.BlockSpec((LANES, others[0].shape[1]), lambda i, p: (i, 0))
    ins = (rows, vectors, grad_own, passed, *others, *finish)
    return call(
        body,
        place,
        ins,
        [block, whole(vectors.shape), block, block]
        + [other_block] * len(others)
        + ([block] + [other_block] * len(others) if finish else []),
        outs,
        [whole((8, width))]
        + [pl.BlockSpec((LANES, a.shape[1]), lambda i, p: (i, 0)) for a in outs[1:]],
        [],
        "norm_back",
        grid=(length // LANES,),
    )


def out_back(place, grad_own, grad_others, mine, theirs, weight_mine, weight_theirs):
    width, half = weight_mine.shape
    z_size = lax.axis_size("z")
    part = width // (2 * z_size)
    _, length, heads = mine[0].shape

    def body(place_ref, own_ref, own_half, *refs):
        other_refs, refs = refs[:GIVEN], refs[GIVEN:]
        mine_refs, theirs_refs, refs = refs[:GROUPS], refs[GROUPS : 2 * GROUPS], refs[2 * GROUPS :]
        wm_ref, wt_ref, *refs = refs
        ga_refs, (keep_ref, send_ref, turned, grads, out_sem) = refs[:GROUPS], refs[GROUPS:]
        core = place_ref[2]
        for image in range(2):
            lanes = slice(image * length, (image + 1) * length)
            for g in range(GROUPS):
                at_mine, at_theirs = head_rows(core, heads, g)
                turned[pl.ds(at_mine, heads), lanes] = mine_refs[g][image].T
                turned[pl.ds(at_theirs, heads), lanes] = theirs_refs[g][1 - image].T
        other = joined(other_refs)
        other_half = select(core, other[:, :half], other[:, half:])
        term = dot(turned[:, :length], own_half[...]) + dot(turned[:, length:], other_half)
        for z in range(z_size):
            for x in range(2):
                dx = x + (1 - 2 * x) * place_ref[1]
                at = (z * 2 + x) * part
                grads[dx, z] = low(term[at : at + part, :])
        for slot, ref in enumerate((keep_ref, send_ref)):
            pltpu.make_async_copy(grads.at[slot], ref, out_sem.at[slot]).start()
        for image, value in enumerate((own_ref[...], other)):
            first, second = value[:, :half], value[:, half:]
            left = select(core, first, second)
            right = select(core, second, first)
            for g in range(GROUPS):
                at_mine, _ = head_rows(core, heads, g)
                ga_refs[g][image] = low(
                    dot_tail(left, wm_ref[pl.ds(at_mine, heads), :])
                    + dot_tail(right, wt_ref[pl.ds(at_mine, heads), :])
                )
        for slot, ref in enumerate((keep_ref, send_ref)):
            pltpu.make_async_copy(grads.at[slot], ref, out_sem.at[slot]).wait()

    half_block = pl.BlockSpec((length, half), lambda i, p: (0, p[2]))
    piece_out = sds((z_size, part, half), jnp.bfloat16)
    return call(
        body,
        place,
        (grad_own, grad_own, *grad_others, *mine, *theirs, weight_mine, weight_theirs),
        [whole((length, width)), half_block]
        + [whole((length, width // GIVEN))] * GIVEN
        + [whole((2, length, heads))] * (2 * GROUPS)
        + [whole((width, half))] * 2,
        [sds((2, length, heads), jnp.bfloat16)] * GROUPS + [piece_out] * 2,
        [whole((2, length, heads))] * GROUPS + [any_spec()] * 2,
        [
            pltpu.VMEM((width, 2 * length), jnp.bfloat16),
            pltpu.VMEM((2, z_size, part, half), jnp.bfloat16),
            pltpu.SemaphoreType.DMA((2,)),
        ],
        "out_back",
    )


def qkv_term(place, normed, grad_q, grad_k, grad_v):
    _, length, width = normed.shape
    heads = grad_q.shape[-1]
    cols = 3 * heads

    def body(place_ref, normed_ref, gq_ref, gk_ref, gv_ref, sum_ref, keep_ref, send_ref, turned, grads, sem):
        z_size = grads.shape[1]
        part = grads.shape[2]
        for image in range(2):
            turned[:, image * length : (image + 1) * length] = normed_ref[image].T
        for slot, ref in enumerate((gq_ref, gk_ref, gv_ref)):
            term = dot(turned[:, :length], ref[0]) + dot(turned[:, length:], ref[1])
            for z in range(z_size):
                for x in range(2):
                    dx = x + (1 - 2 * x) * place_ref[1]
                    at = (z * 2 + x) * part
                    grads[dx, z, :, slot * heads : (slot + 1) * heads] = low(
                        term[at : at + part, :]
                    )
            sum_ref[slot : slot + 1, :] = jnp.sum(wide(ref[0]), axis=0, keepdims=True) + jnp.sum(
                wide(ref[1]), axis=0, keepdims=True
            )
        for slot, ref in enumerate((keep_ref, send_ref)):
            pltpu.make_async_copy(grads.at[slot], ref, sem.at[slot]).start()
        for slot, ref in enumerate((keep_ref, send_ref)):
            pltpu.make_async_copy(grads.at[slot], ref, sem.at[slot]).wait()

    z_size = lax.axis_size("z")
    part = width // (2 * z_size)
    piece_out = sds((z_size, part, cols), jnp.bfloat16)
    return call(
        body,
        place,
        (normed, grad_q, grad_k, grad_v),
        [whole((2, length, width))] + [whole((2, length, heads))] * 3,
        [sds((3, heads), jnp.float32)] + [piece_out] * 2,
        [whole((3, heads))] + [any_spec()] * 2,
        [
            pltpu.VMEM((width, 2 * length), jnp.bfloat16),
            pltpu.VMEM((2, z_size, part, cols), jnp.bfloat16),
            pltpu.SemaphoreType.DMA((2,)),
        ],
        "qkv_term",
    )


def qkv_back(place, grads, pieces):
    flat = [one for piece in pieces for (one,) in piece]
    z_size, _, cols = flat[0].shape
    heads = cols // 3
    length = grads[0][0].shape[1]
    part = flat[-1].shape[1]
    width = 2 * z_size * part

    def body(place_ref, *refs):
        grad_refs, refs = refs[: 3 * GROUPS], refs[3 * GROUPS :]
        ins, (own_ref, *other_refs, weight, sem) = refs[: len(flat)], refs[len(flat) :]
        copies = []
        for g in range(GROUPS):
            copies += weight_copies(
                place_ref, ins[2 * g : 2 * g + 2], weight.at[g], part, sem.at[g]
            )
        for copy in copies:
            copy.start()
        for copy in copies:
            copy.wait()

        def one_image(image, carry):
            total = None
            for g in range(GROUPS):
                for slot in range(3):
                    add = dot_tail(
                        grad_refs[3 * g + slot][image],
                        weight[g, :, slot * heads : (slot + 1) * heads],
                    )
                    total = add if total is None else total + add

            @pl.when(image == 0)
            def _():
                own_ref[...] = total

            @pl.when(image == 1)
            def _():
                for number, ref in enumerate(other_refs):
                    at = number * width // GIVEN
                    ref[...] = low(total[:, at : at + width // GIVEN])

            return carry

        lax.fori_loop(0, 2, one_image, 0)

    return call(
        body,
        place,
        (*[one for grad in grads for one in grad], *flat),
        [whole((2, length, heads))] * (3 * GROUPS) + [any_spec()] * len(flat),
        [sds((length, width), jnp.float32)] + [sds((length, width // GIVEN), jnp.bfloat16)] * GIVEN,
        [whole((length, width))] + [whole((length, width // GIVEN))] * GIVEN,
        [
            pltpu.VMEM((GROUPS, width, cols), jnp.bfloat16),
            pltpu.SemaphoreType.DMA((GROUPS, 2 * z_size)),
        ],
        "qkv_back",
    )


def to_column(row):
    return jnp.concatenate(
        [
            jnp.broadcast_to(row[:, at : at + LANES], (LANES, LANES)).T[:, :1]
            for at in range(0, row.shape[1], LANES)
        ],
        axis=0,
    )


def to_row(column):
    return jnp.concatenate(
        [
            jnp.broadcast_to(column[at : at + LANES, :], (LANES, LANES)).T[:1, :]
            for at in range(0, column.shape[0], LANES)
        ],
        axis=1,
    )


def statistics(place, kinds, pairs, shares, weights, states, images, group, extra=None):
    flat = [a for pair in pairs for side in pair for a in side]
    amount = len(kinds)
    vectors = 0 if extra is None else len(extra[1])

    def body(place_ref, *refs):
        core = place_ref[2]
        refs = list(refs)

        def take(n):
            taken = refs[:n]
            del refs[:n]
            return taken

        sides_of = [[take(len(side)) for side in pair] for pair in pairs]
        weight_refs, state_refs = take(amount), take(amount)
        if vectors:
            (terms_ref,) = take(1)
            param_refs, moment_refs = take(vectors), take(vectors)
        grad_refs, row_refs = take(amount), take(amount)
        (pack_ref,) = take(1)
        if vectors:
            vector_grads, new_moments = take(vectors), take(vectors)
        at_pack = 0
        for number, kind in enumerate(kinds):
            grad_ref, weight_ref = grad_refs[number], weight_refs[number]
            rows, cols = weights[number].shape
            for chunk, (number_of, row0, col0) in enumerate(shares[number]):
                sides = sides_of[number_of]

                def halves(row, row_count, col, col_count):
                    index = (
                        slice(row0 + row, row0 + row + row_count),
                        slice(col0 + col, col0 + col + col_count),
                    )
                    mine, theirs = [
                        sum([wide(ref[index]) for ref in side[1:]], wide(side[0][index]))
                        * (1.0 / images)
                        for side in sides
                    ]
                    return select(core, mine, theirs), select(core, theirs, mine)

                if kind == "in":
                    per = cols // (2 * CHUNKS * group)
                    for c, half in enumerate(halves(0, rows, 0, per * group)):
                        for s in range(group):
                            at = ((s * 2 + c) * CHUNKS + chunk) * per
                            grad_ref[:, at : at + per] = half[:, s * per : (s + 1) * per]
                elif kind == "down":
                    per = rows // (2 * CHUNKS)
                    for c, half in enumerate(halves(0, per, 0, cols)):
                        at = (c * CHUNKS + chunk) * per
                        grad_ref[at : at + per, :] = half
                else:
                    amount_of = len(shares[number])
                    lanes_of = cols // (2 * SPLIT[kind] * amount_of)
                    for slot in range(SPLIT[kind]):
                        for c, half in enumerate(halves(0, rows, slot * lanes_of, lanes_of)):
                            at = ((2 * slot + c) * amount_of + chunk) * lanes_of
                            grad_ref[:, at : at + lanes_of] = half
            squared = grad_ref[...] * grad_ref[...]
            new_rows = 0.5 * to_column(state_refs[number][...]) + 0.5 * jnp.mean(
                squared, axis=1, keepdims=True
            )
            row_refs[number][...] = to_row(new_rows)
            pack_ref[0:1, at_pack : at_pack + cols] = jnp.sum(squared, axis=0, keepdims=True)
            pack_ref[1:2, at_pack : at_pack + cols] = jnp.sum(
                squared * (1.0 / new_rows), axis=0, keepdims=True
            )
            at_pack += cols
            weight = weight_ref[...]
            pack_ref[0:1, at_pack : at_pack + LANES] = jnp.broadcast_to(
                jnp.sum(new_rows, axis=0, keepdims=True), (1, LANES)
            )
            pack_ref[1:2, at_pack : at_pack + LANES] = jnp.broadcast_to(
                jnp.sum(jnp.sum(weight * weight, axis=0, keepdims=True), axis=1, keepdims=True),
                (1, LANES),
            )
            at_pack += LANES
        at = 0
        if vectors:
            place_row = lax.broadcasted_iota(jnp.int32, extra[0].shape, 0)
            here = place_row == place_ref[0] * 2 + place_ref[1]
            mine = jnp.sum(
                jnp.where(here, terms_ref[...], 0.0), axis=0, keepdims=True
            )
        for number in range(vectors):
            size = extra[1][number].shape[1]
            grad = mine[:, at : at + size] * (1.0 / images)
            at += size
            param = param_refs[number][...]
            moment = 0.5 * moment_refs[number][...] + 0.5 * grad * grad
            direction = grad * lax.rsqrt(moment)
            vector_grads[number][...] = grad
            new_moments[number][...] = moment
            for row, value in enumerate((direction, param)):
                pack_ref[row : row + 1, at_pack : at_pack + LANES] = jnp.broadcast_to(
                    jnp.sum(value * value, axis=1, keepdims=True), (1, LANES)
                )
            at_pack += LANES

    lanes = sum(weight.shape[1] + LANES for weight in weights) + vectors * LANES
    ins = [*flat, *weights, *states]
    outs = [sds(weight.shape, jnp.float32) for weight in weights]
    outs += [sds(state.shape, jnp.float32) for state in states]
    outs.append(sds((2, lanes), jnp.float32))
    if vectors:
        terms, params, moments = extra
        ins += [terms, *params, *moments]
        outs += [sds(a.shape, jnp.float32) for a in (*params, *moments)]
    results = call(
        body,
        place,
        tuple(ins),
        [whole(a.shape) for a in ins],
        outs,
        [whole(a.shape) for a in outs],
        [],
        "statistics",
    )
    return (
        results[:amount],
        results[amount : 2 * amount],
        results[2 * amount],
        results[2 * amount + 1 : 2 * amount + 1 + vectors],
        results[2 * amount + 1 + vectors :],
    )


CLIP_ORDER = (8, 10, 4, 2)
SPLIT = {"out": 1, "qkv": 3}


def update(place, grads, new_rows, weights, cols_states, pack, group, extra=None, clips=None):
    amount = len(weights)
    vectors = 0 if extra is None else len(extra[0])

    def body(place_ref, *refs):
        refs = list(refs)

        def take(n):
            taken = refs[:n]
            del refs[:n]
            return taken

        grad_refs, row_refs, weight_refs, state_refs = [take(amount) for _ in range(4)]
        (pack_ref,) = take(1)
        if vectors:
            vector_grads, moment_refs, param_refs = [take(vectors) for _ in range(3)]
            (clips_ref,) = take(1)
        new_refs, col_refs = take(amount), take(amount)
        (clip_ref,) = take(1)
        param_outs = take(vectors)
        at_pack = 0
        if not vectors:
            clip_ref[...] = jnp.zeros(clip_ref.shape, jnp.float32)
        for number in range(amount):
            rows, cols = weights[number].shape
            rows_total = rows * group
            count = rows_total * cols
            new_cols = (
                0.5 * state_refs[number][...]
                + 0.5 * pack_ref[0:1, at_pack : at_pack + cols] / rows_total
            )
            col_refs[number][...] = new_cols
            by_rows = pack_ref[1:2, at_pack : at_pack + cols]
            at_pack += cols
            mean_rows = pack_ref[0:1, at_pack : at_pack + 1] / rows_total
            weight_total = pack_ref[1:2, at_pack : at_pack + 1]
            at_pack += LANES
            total = mean_rows * jnp.sum(by_rows / new_cols, axis=1, keepdims=True)
            clip = jnp.maximum(1.0, jnp.sqrt(total / count) / clip_level)
            step = step_rate * jnp.sqrt(weight_total / count) / clip
            if vectors:
                if number == 0:
                    found = [clips_ref[at : at + 1, :1] for at in range(len(MATRICES) - amount)]
                found.append(clip)
            else:
                clip_ref[number : number + 1, :] = jnp.broadcast_to(clip, (1, LANES))
            estimate = to_column(row_refs[number][...]) * (new_cols / mean_rows)
            new_refs[number][...] = weight_refs[number][...] - step * (
                grad_refs[number][...] * lax.rsqrt(estimate)
            )
        for number in range(vectors):
            count = extra[2][number].shape[1] * group
            total = pack_ref[0:1, at_pack : at_pack + 1]
            weight_total = pack_ref[1:2, at_pack : at_pack + 1]
            at_pack += LANES
            clip = jnp.maximum(1.0, jnp.sqrt(total / count) / clip_level)
            step = step_rate * jnp.sqrt(weight_total / count) / clip
            found.append(clip)
            direction = vector_grads[number][...] * lax.rsqrt(moment_refs[number][...])
            param_outs[number][...] = param_refs[number][...] - step * direction
        if vectors:
            lane = lax.broadcasted_iota(jnp.int32, (1, LANES), 1)
            row = jnp.zeros((1, LANES), jnp.float32)
            for value, number in zip(found, (*CLIP_ORDER, *VECTORS)):
                row = jnp.where(lane == number, value, row)
            clip_ref[...] = row[:, : len(found)]

    ins = [*grads, *new_rows, *weights, *cols_states, pack]
    outs = [sds(a.shape, jnp.float32) for a in (*weights, *cols_states)]
    outs.append(sds((1, len(MATRICES) + vectors) if vectors else (8, LANES), jnp.float32))
    if vectors:
        ins += [*extra[0], *extra[1], *extra[2], clips]
        outs += [sds(a.shape, jnp.float32) for a in extra[2]]
    results = call(
        body,
        place,
        tuple(ins),
        [whole(a.shape) for a in ins],
        outs,
        [whole(a.shape) for a in outs],
        [],
        "update",
    )
    return (
        results[:amount],
        results[amount : 2 * amount],
        results[2 * amount],
        results[2 * amount + 1 :],
    )


def pack_terms(place, sums_mid, sums_in, sums_qkv, hidden_sums, down_sums, sizes):
    z_size = lax.axis_size("z")
    shards = 2 * z_size
    per_shard = sizes[6] // 2 // CHUNKS
    heads = sums_qkv[0].shape[1]

    def body(place_ref, mid_ref, in_ref, *refs):
        qkv_refs, refs = refs[:GROUPS], refs[GROUPS:]
        hidden_refs, (down_ref, out_ref) = refs[:CHUNKS], refs[CHUNKS:]
        core = place_ref[2]

        def put(slot, row):
            at, size = sum(sizes[:slot]), sizes[slot]
            for s in range(shards):
                out_ref[s : s + 1, at : at + size] = row[:, s * size : (s + 1) * size]

        put(0, in_ref[0:1, :])
        put(1, in_ref[1:2, :])
        zero = jnp.zeros((1, heads * GROUPS), jnp.float32)
        halves = []
        for slot in (0, 2):
            row = jnp.concatenate([ref[slot : slot + 1, :] for ref in qkv_refs], axis=1)
            halves += [select(core, row, zero), select(core, zero, row)]
        put(2, jnp.concatenate(halves, axis=1))
        put(3, mid_ref[2:3, :])
        put(4, mid_ref[0:1, :])
        put(5, mid_ref[1:2, :])
        put(7, down_ref[...])
        none = jnp.zeros((1, per_shard), jnp.float32)
        for s in range(shards):
            for j in range(CHUNKS):
                row = hidden_refs[j][:, s * per_shard : (s + 1) * per_shard]
                for c in range(2):
                    at = sum(sizes[:6]) + (c * CHUNKS + j) * per_shard
                    here = select(core, row, none) if c == 0 else select(core, none, row)
                    out_ref[s : s + 1, at : at + per_shard] = here

    ins = (sums_mid, sums_in, *sums_qkv, *hidden_sums, down_sums)
    shape = (shards, sum(sizes))
    return call(
        body,
        place,
        ins,
        [whole(a.shape) for a in ins],
        [sds(shape, jnp.float32)],
        [whole(shape)],
        [],
        "pack_terms",
    )[0]


def on_device(
    inputs,
    cotangent,
    norm1_gain,
    norm1_bias,
    qkv_weight,
    qv_bias,
    out_weight,
    out_bias,
    norm2_gain,
    norm2_bias,
    in_weight,
    in_bias,
    down_weight,
    down_bias,
    qkv_rows,
    qkv_cols,
    out_rows,
    out_cols,
    in_rows,
    in_cols,
    down_rows,
    down_cols,
    norm1_gain_moment,
    norm1_bias_moment,
    qv_bias_moment,
    out_bias_moment,
    norm2_gain_moment,
    norm2_bias_moment,
    in_bias_moment,
    down_bias_moment,
):
    masters = [
        norm1_gain,
        norm1_bias,
        qkv_weight,
        qv_bias,
        out_weight,
        out_bias,
        norm2_gain,
        norm2_bias,
        in_weight,
        in_bias,
        down_weight,
        down_bias,
    ]
    moments = [
        norm1_gain_moment,
        norm1_bias_moment,
        qv_bias_moment,
        out_bias_moment,
        norm2_gain_moment,
        norm2_bias_moment,
        in_bias_moment,
        down_bias_moment,
    ]
    place = jnp.stack([lax.axis_index(axis) for axis in ("z", "x", "c", "y")]).astype(jnp.int32)
    by_y = lax.axis_size("y") == 2
    group = lax.axis_size("z") * lax.axis_size("x")
    tokens = inputs.shape[0]
    part = in_weight.shape[0]
    images = (tokens // SEQ) * group * lax.axis_size("y") * lax.axis_size("c")
    as_row = lambda vector: vector.reshape(1, -1)
    params = [as_row(masters[number]) for number in VECTORS]
    moments = [as_row(moment) for moment in moments]
    sizes = [param.shape[1] for param in params]

    shard_first, shard_next = prepare_qkv(place, qkv_weight, out_weight, params)
    near = along_z(shard_first)
    pieces_first = by_x(near)
    near_next = along_z(after(shard_next, near))
    rows_own, parts = pad_rows(after(place, near), inputs)
    rows = (rows_own, [swap(one, "c") for one in parts])
    *shards_ff, down_sums = prepare_rest(
        after(place, rows_own), in_weight, down_weight, cotangent, (2 if by_y else 1,) * 2
    )
    cot_own, parts = pad_rows(after(place, (down_sums, rows[1])), cotangent)
    near_ff = [along_z(shards_ff[0])]

    normed, *first, vectors, hidden_bias = project_first(
        after(place, (cot_own, near_next)), rows, pieces_first, sizes
    )
    near_ff.append(along_z(after(shards_ff[1], normed)))
    cot = (cot_own, [swap(one, "c") for one in after(parts, normed)])
    qkv = [first]
    pieces_next = by_x(near_next)
    mixed, prob = attention(place, *first)
    attended = [mixed]
    probs = [prob]
    theirs = [swap(mixed, "c")]
    pieces_next = after(pieces_next, mixed)
    weight_mine = gather_out(place, pieces_next, 3 * first[0].shape[-1])
    weight_theirs = swap(weight_mine, "c")
    near_ff[0] = after(near_ff[0], pieces_next)
    across = swap(near_ff[0], "x")
    near_too = swap(near_ff[0], "y") if by_y else None
    qkv.append(
        project_next(
            after(place, (near_ff[0], weight_mine)), normed, vectors, pieces_next, 1
        )
    )
    mixed, prob = attention(place, *qkv[1])
    attended.append(mixed)
    probs.append(prob)
    theirs.append(swap(mixed, "c"))
    across = after(across, mixed)
    if by_y:
        pieces_ff = [[near_ff[0], near_too], [across, swap(across, "y")]]
    else:
        pieces_ff = [[near_ff[0]], [across]]
    near_ff[1] = after(near_ff[1], across)
    across_next = swap(near_ff[1], "x")
    near_first = near_too
    near_too = (near_too, swap(near_ff[1], "y")) if by_y else None
    middle, normed_mid = project_out(
        after(place, (near_ff[1], near_first)), attended, theirs, weight_mine, weight_theirs, rows, vectors
    )
    across_next = after(across_next, normed_mid)
    if by_y:
        pieces_ff = [
            [[near_ff[0], near_too[0]], pieces_ff[1]],
            [[near_ff[1], near_too[1]], [across_next, swap(across_next, "y")]],
        ]
    else:
        pieces_ff = [[[near_ff[0]], [across]], [[near_ff[1]], [across_next]]]
    *running, sums, keep_in, send_in, keep_down, send_down = feed_forward(
        after(place, across_next), normed_mid, cot, pieces_ff[0], hidden_bias, 0, None
    )
    terms_ff = [(keep_in, swap(send_in, "x"), keep_down, swap(send_down, "x"))]
    hidden_sums = [sums]
    *totals, sums, keep_in, send_in, keep_down, send_down = feed_forward(
        place, normed_mid, cot, pieces_ff[1], hidden_bias, 1, running
    )
    hidden_sums.append(sums)
    folded = [fold_pair(*after(terms_ff[0], sums))]
    terms_ff.append((keep_in, swap(send_in, "x"), keep_down, swap(send_down, "x")))
    scattered = [scatter_z(folded[0])]
    out_share, *out_given = totals[: 1 + GIVEN]
    normed_share, *normed_given = totals[1 + GIVEN :]
    sums_mid, output, grad_mid, grad_mid_low, *parts = norm_back(
        after(place, folded[0]),
        middle,
        vectors,
        GAIN_TWO,
        normed_share,
        [swap(one, "c") for one in normed_given],
        cot_own,
        tokens,
        (out_share, *[swap(one, "c") for one in out_given]),
    )
    *grad_attended, keep, send = out_back(
        place,
        grad_mid_low,
        [swap(one, "c") for one in parts],
        attended,
        theirs,
        weight_mine,
        weight_theirs,
    )
    got = swap(send, "x")
    grad_qkv = [attention_back(place, *qkv[0], probs[0], grad_attended[0])]
    sums_first, keep_first, send_first = qkv_term(place, normed, *grad_qkv[0])
    got_first = swap(send_first, "x")
    folded.append(fold_pair(*after(terms_ff[1], sums_first)))
    scattered.append(scatter_z(folded[1]))
    scattered[0] = after(scattered[0], folded[1])
    own_ff = [sum_y(scattered[0])]
    grad_qkv.append(
        attention_back(after(place, scattered[0]), *qkv[1], probs[1], grad_attended[1])
    )
    own_ff[0] = after(own_ff[0], grad_qkv[1][0])
    sums_next, keep_next, send_next = qkv_term(
        after(place, own_ff[0]), normed, *grad_qkv[1]
    )
    sums_qkv = [sums_first, sums_next]
    got_next = swap(send_next, "x")
    held = after(((keep, got), (keep_first, got_first)), sums_next)
    folded.append(jnp.concatenate([fold(*one) for one in held], axis=1))
    scattered.append(scatter_z(folded[2]))
    share, *given = qkv_back(after(place, folded[2]), grad_qkv, [pieces_first, pieces_next])
    pairs = [with_core(own_ff[0])]
    scattered[1] = after(scattered[1], share)
    own_ff.append(sum_y(scattered[1]))
    sums_in, input_grad = norm_back(
        after(place, scattered[1]),
        rows_own,
        vectors,
        GAIN_ONE,
        share,
        [swap(one, "c") for one in given],
        grad_mid,
        tokens,
    )
    packed = pack_terms(
        place, sums_mid, sums_in, sums_qkv, hidden_sums, down_sums, sizes
    )
    folded.append(fold(*after((keep_next, got_next), packed)))
    scattered.append(scatter_z(folded[3]))
    pairs.append(with_core(after(own_ff[1], folded[3])))
    terms = sum_over(packed, ("c", "z", "x", "y"))

    weights = [in_weight, down_weight]
    states = [as_row(state) for state in (in_rows, down_rows)]
    grads_early, rows_early, pack, _, _ = statistics(
        place,
        ("in", "down"),
        pairs[:CHUNKS],
        [[(j, row, 0) for j in range(CHUNKS)] for row in (0, part)],
        weights,
        states,
        images,
        group,
    )
    scattered[2] = after(scattered[2], rows_early[0])
    own_mid = after(sum_y(scattered[2]), terms)
    pairs.append(with_core(own_mid))
    pack = sum_over(pack, ("z", "x"))
    scattered[3] = after(scattered[3], (pack, pairs[-1]))
    pairs.append(sum_y_and_core(scattered[3]))
    new_early, cols_early, clips_early, _ = update(
        after(place, scattered[3]),
        grads_early,
        rows_early,
        weights,
        [as_row(state) for state in (in_cols, down_cols)],
        pack,
        group,
    )
    weights = [out_weight, qkv_weight]
    grads_late, rows_late, pack, vector_grads, new_moments = statistics(
        after(place, clips_early),
        ("out", "qkv"),
        pairs[CHUNKS:],
        [[(0, 0, 0)], [(0, 0, out_weight.shape[1] // 2), (1, 0, 0)]],
        weights,
        [as_row(state) for state in (out_rows, qkv_rows)],
        images,
        group,
        (terms, params, moments),
    )
    new_late, cols_late, clip_factors, new_vectors = update(
        place,
        grads_late,
        rows_late,
        weights,
        [as_row(state) for state in (out_cols, qkv_cols)],
        sum_over(pack, ("z", "x")),
        group,
        (vector_grads, new_moments, params),
        clips_early,
    )

    flat = lambda value: value.reshape(-1)
    grads = [None] * 12
    new_params = [None] * 12
    for number, slot in ((8, 0), (10, 1)):
        grads[number], new_params[number] = grads_early[slot], new_early[slot]
    for number, slot in ((4, 0), (2, 1)):
        grads[number], new_params[number] = grads_late[slot], new_late[slot]
    for slot, number in enumerate(VECTORS):
        grads[number] = flat(vector_grads[slot])
        new_params[number] = flat(new_vectors[slot])
    return (
        output,
        input_grad,
        *grads,
        flat(rows_late[1]),
        flat(cols_late[1]),
        flat(rows_late[0]),
        flat(cols_late[0]),
        flat(rows_early[0]),
        flat(cols_early[0]),
        flat(rows_early[1]),
        flat(cols_early[1]),
        *[flat(moment) for moment in new_moments],
        *new_params,
        flat(clip_factors),
    )


def solution(mesh):
    group = mesh.shape["fsdp"]
    split = Mesh(mesh.devices.reshape(group // 2, 2, mesh.shape["dp"] // 2, 2), ALL_AXES)
    in_specs = (
        P(("z", "x", "y", "c"), None),
        P(("z", "x", "y", "c"), None),
        P(("z", "x")),
        P(("z", "x")),
        P(("z", "x"), None),
        P(("z", "x")),
        P(("z", "x"), None),
        P(("z", "x")),
        P(("z", "x")),
        P(("z", "x")),
        P(("z", "x"), None),
        P(("z", "x")),
        P(("z", "x"), None),
        P(("z", "x")),
        P(("z", "x")),
        P(),
        P(("z", "x")),
        P(),
        P(("z", "x")),
        P(),
        P(("z", "x")),
        P(),
        P(("z", "x")),
        P(("z", "x")),
        P(("z", "x")),
        P(("z", "x")),
        P(("z", "x")),
        P(("z", "x")),
        P(("z", "x")),
        P(("z", "x")),
    )
    out_specs = (
        P(("z", "x", "y", "c"), None),
        P(("z", "x", "y", "c"), None),
        P(("z", "x")),
        P(("z", "x")),
        P(("z", "x"), None),
        P(("z", "x")),
        P(("z", "x"), None),
        P(("z", "x")),
        P(("z", "x")),
        P(("z", "x")),
        P(("z", "x"), None),
        P(("z", "x")),
        P(("z", "x"), None),
        P(("z", "x")),
        P(("z", "x")),
        P(),
        P(("z", "x")),
        P(),
        P(("z", "x")),
        P(),
        P(("z", "x")),
        P(),
        P(("z", "x")),
        P(("z", "x")),
        P(("z", "x")),
        P(("z", "x")),
        P(("z", "x")),
        P(("z", "x")),
        P(("z", "x")),
        P(("z", "x")),
        P(("z", "x")),
        P(("z", "x")),
        P(("z", "x"), None),
        P(("z", "x")),
        P(("z", "x"), None),
        P(("z", "x")),
        P(("z", "x")),
        P(("z", "x")),
        P(("z", "x"), None),
        P(("z", "x")),
        P(("z", "x"), None),
        P(("z", "x")),
        P(),
    )
    return jax.shard_map(
        on_device, mesh=split, in_specs=in_specs, out_specs=out_specs, check_vma=False
    )
```

```python
import math

import jax
import jax.numpy as jnp
from jax import lax
from jax.experimental import pallas as pl
from jax.experimental.pallas import tpu as pltpu
from jax.sharding import Mesh
from jax.sharding import PartitionSpec as P

HEAD_DIM = 64
SEQ = 577
LANES = 128
TILE = 16
CHUNKS = 2
GROUPS = 2
GIVEN = 2
VMEM_LIMIT = 60
VMEM_LIMITS = {
    "attention": 30,
    "attention_back": 30,
    "gather_out": 30,
    "norm_back": 30,
    "out_back": 40,
    "pack_terms": 30,
    "project_next": 40,
    "qkv_term": 30,
}

ALL_AXES = ("z", "x", "y", "c")

MATRICES = (2, 4, 8, 10)
VECTORS = (0, 1, 3, 5, 6, 7, 9, 11)

ln_eps = 1e-06
clip_level = 0.05
step_rate = 4.0


def swap(value, axis):
    return lax.ppermute(value, axis, [(0, 1), (1, 0)])


def shift(value, axis, step):
    size = lax.axis_size(axis)
    return lax.ppermute(value, axis, [(i, (i + step) % size) for i in range(size)])


def partner(value, axis, step):
    size = lax.axis_size(axis)
    return lax.ppermute(value, axis, [(i, i ^ step) for i in range(size)])


def sum_over(value, axes):
    for axis in axes:
        if lax.axis_size(axis) == 4:
            got = [shift(value, axis, step) for step in (1, 2, 3)]
            value = (value + got[1]) + (got[0] + got[2])
            continue
        step = 1
        while step < lax.axis_size(axis):
            value = value + partner(value, axis, step)
            step *= 2
    return value


def along_z(shard):
    near = lax.all_gather(shard, "z", axis=0, tiled=True)
    return near.reshape(lax.axis_size("z"), *shard.shape)


def by_x(near):
    return [[near], [swap(near, "x")]]


def by_y_too(pieces, by_y):
    return [[one, swap(one, "y")] if by_y else [one] for (one,) in pieces]


def after(values, token):
    return lax.optimization_barrier((values, token))[0]


def fold(keep, got):
    total = low(wide(keep) + wide(got))
    return total.reshape(-1, total.shape[-1])


def fold_pair(keep_one, got_one, keep_two, got_two):
    both = [low(wide(keep_one) + wide(got_one)), low(wide(keep_two) + wide(got_two))]
    total = jnp.concatenate(both, axis=1)
    return total.reshape(-1, total.shape[-1])


def scatter_z(total):
    return lax.psum_scatter(total, "z", scatter_dimension=0, tiled=True)


def sum_y(mine):
    if lax.axis_size("y") == 2:
        return [mine, swap(mine, "y")]
    return [lax.psum(wide(mine), "y")]


def with_core(own):
    return own, [swap(one, "c") for one in own]


def sum_y_and_core(mine):
    if lax.axis_size("y") != 2:
        return with_core(sum_y(mine))
    across = lax.ppermute(mine, ("y", "c"), [(i, 3 - i) for i in range(4)])
    return [mine, swap(mine, "y")], [swap(mine, "c"), across]


def row_pad(length):
    return -(-length // LANES) * LANES


def dot(left, right):
    return jnp.dot(left, right, preferred_element_type=jnp.float32)


def dot_tail(left, right):
    return lax.dot_general(
        left, right, (((1,), (1,)), ((), ())), preferred_element_type=jnp.float32
    )


def low(value):
    return value.astype(jnp.bfloat16)


def wide(value):
    return value.astype(jnp.float32)


def any_spec():
    return pl.BlockSpec(memory_space=pl.ANY)


def whole(shape):
    return pl.BlockSpec(shape, lambda *_: (0,) * len(shape))


def sds(shape, dtype):
    return jax.ShapeDtypeStruct(shape, dtype)


def call(body, place, ins, in_specs, outs, out_specs, scratch, name, grid=(1,)):
    return pl.pallas_call(
        body,
        out_shape=outs,
        grid_spec=pltpu.PrefetchScalarGridSpec(
            num_scalar_prefetch=1,
            grid=grid,
            in_specs=in_specs,
            out_specs=out_specs,
            scratch_shapes=scratch,
        ),
        compiler_params=pltpu.CompilerParams(
            vmem_limit_bytes=VMEM_LIMITS.get(name, VMEM_LIMIT) * 1024 * 1024, dimension_semantics=("arbitrary",) * len(grid)
        ),
        name=name,
    )(place, *ins)


def shard_number(place_ref, z, dx):
    return z * 2 + dx + (1 - 2 * dx) * place_ref[1]


def normalised(rows):
    centre = rows - jnp.mean(rows, axis=-1, keepdims=True)
    spread = jnp.mean(centre * centre, axis=-1, keepdims=True)
    return centre * lax.rsqrt(spread + ln_eps)


def select(core, first, second):
    return jnp.where(core == 0, first, second)


def prepare_qkv(place, weight, out_weight, vectors, cut):
    part, cols = weight.shape
    half = cols // 6
    heads = half // GROUPS
    width = 3 * heads
    sizes = [vector.shape[-1] for vector in vectors]
    tiles = -(-sum(sizes) // width)

    out_half = out_weight.shape[1] // 2

    def body(place_ref, weight_ref, out_ref, *refs):
        refs, groups = refs[: len(sizes)], refs[len(sizes) :]
        core = place_ref[2]

        def of_y(rows):
            if cut == 1:
                return low(rows)
            return low(select(place_ref[3], rows[: part // 2], rows[part // 2 :]))

        for number, ref in enumerate(groups):
            for slot in range(3):
                at = 2 * slot * half + number * heads
                cols_of = select(
                    core,
                    weight_ref[:, at : at + heads],
                    weight_ref[:, at + half : at + half + heads],
                )
                lanes = slice(slot * heads, (slot + 1) * heads)
                if number == GROUPS - 1:
                    ref[:, lanes] = of_y(cols_of)
                else:
                    ref[:part, lanes] = low(cols_of)
        groups[-1][:, width:] = of_y(select(core, out_ref[:, :out_half], out_ref[:, out_half:]))
        at = 0
        for ref, size in zip(refs, sizes):
            done = 0
            while done < size:
                tile, lane = divmod(at + done, width)
                count = min(size - done, width - lane)
                row = part + tile * TILE
                groups[0][row : row + TILE, lane : lane + count] = low(
                    jnp.broadcast_to(ref[:, done : done + count], (TILE, count))
                )
                done += count
            at += size

    shapes = [
        (part + (tiles * TILE if g == 0 else 0), width) if g < GROUPS - 1 else (part // cut, width + out_half)
        for g in range(GROUPS)
    ]
    return call(
        body,
        place,
        (weight, out_weight, *vectors),
        [whole((part, cols)), whole(out_weight.shape)] + [whole((1, size)) for size in sizes],
        [sds(shape, jnp.bfloat16) for shape in shapes],
        [whole(shape) for shape in shapes],
        [],
        "prepare_qkv",
    )


def pad_rows(place, rows):
    tokens, width = rows.shape
    length = row_pad(tokens)
    even = tokens // TILE * TILE
    cols = width // GIVEN

    def body(place_ref, ref, to, *parts):
        row = lax.broadcasted_iota(jnp.int32, (length - even, width), 0)
        last = jnp.zeros((length - even, width), jnp.float32)
        for extra in range(tokens - even):
            one = wide(ref[even + extra : even + extra + 1, :])
            last = jnp.where(row == extra, one, last)
        to[:even, :] = ref[:even, :]
        to[even:, :] = low(last)
        for number, part in enumerate(parts):
            lanes = slice(number * cols, (number + 1) * cols)
            part[...] = to[:, lanes]

    shapes = [(length, width)] + [(length, cols)] * GIVEN
    whole_rows, *parts = call(
        body,
        place,
        (rows,),
        [whole(rows.shape)],
        [sds(shape, jnp.bfloat16) for shape in shapes],
        [whole(shape) for shape in shapes],
        [],
        "pad_rows",
    )
    return whole_rows, parts


def joined(refs, rows=slice(None)):
    return jnp.concatenate([ref[rows, :] for ref in refs], axis=1)


def prepare_rest(place, in_weight, down_weight, cotangent, cuts):
    part, hidden = in_weight.shape
    width = down_weight.shape[1]
    per_core = down_weight.shape[0] // 2
    per_shard = per_core // CHUNKS
    shards = hidden // (2 * per_core)
    def body(place_ref, in_ref, down_ref, cot_ref, *refs):
        pieces, (sum_ref,) = refs[:CHUNKS], refs[CHUNKS:]
        core, y = place_ref[2], place_ref[3]

        def pick(ref, row, count, step, col, cols, by_row, cut):
            def of_core(r):
                if by_row:
                    return select(
                        core, ref[r : r + count, col : col + cols], ref[r + step : r + step + count, col : col + cols]
                    )
                return select(
                    core, ref[r : r + count, col : col + cols], ref[r : r + count, col + step : col + step + cols]
                )

            if cut == 1:
                return low(of_core(row))
            return low(select(y, of_core(row), of_core(row + count)))

        for j, cut in enumerate(cuts):
            rows_in, rows_down = part // cut, per_shard // cut
            for s in range(shards):
                at = s * 2 * per_core + j * per_shard
                pieces[j][:rows_in, s * per_shard : (s + 1) * per_shard] = pick(
                    in_ref, 0, rows_in, per_core, at, per_shard, False, cut
                )
            pieces[j][rows_in:, :] = pick(
                down_ref, j * per_shard, rows_down, per_core, 0, width, True, cut
            )
        sum_ref[...] = jnp.sum(wide(cot_ref[...]), axis=0, keepdims=True)

    outs = [sds(((part + per_shard) // cut, width), jnp.bfloat16) for cut in cuts]
    outs += [sds((1, width), jnp.float32)]
    ins = (in_weight, down_weight, cotangent)
    return call(
        body,
        place,
        ins,
        [whole(a.shape) for a in ins],
        outs,
        [whole(a.shape) for a in outs],
        [],
        "prepare_rest",
    )


GAIN_ONE, BIAS_ONE, BIAS_OUT, GAIN_TWO, BIAS_TWO, BIAS_DOWN, BIAS_QV = range(7)


def row_copies(place_ref, ins, to, part, lanes, sem):
    cut = len(ins) // 2
    rows = part // cut
    made = []
    for number, ref in enumerate(ins):
        dx, h = number // cut, number % cut
        y = h + (1 - 2 * h) * place_ref[3] if cut == 2 else 0
        for z in range(ref.shape[0]):
            row = pl.multiple_of(shard_number(place_ref, z, dx) * part + y * rows, rows)
            made.append(
                pltpu.make_async_copy(
                    ref.at[z, pl.ds(0, rows), lanes], to.at[pl.ds(row, rows), :], sem.at[len(made)]
                )
            )
    return made


def weight_copies(place_ref, ins, weight, part, sem):
    return row_copies(place_ref, ins, weight, part, pl.ds(0, weight.shape[1]), sem)


def write_qkv(normed, weight, bias_q, bias_v, image, q_ref, k_ref, v_ref):
    heads = weight.shape[1] // 3
    query = low(dot(normed, weight[:, :heads]) + bias_q)
    q_ref[image] = low(wide(query) * (1.0 / math.sqrt(HEAD_DIM)))
    k_ref[image] = low(dot(normed, weight[:, heads : 2 * heads]))
    v_ref[image] = low(dot(normed, weight[:, 2 * heads :]) + bias_v)


def project_first(place, rows, pieces, sizes):
    flat = [one for (one,) in pieces]
    z_size, part, cols = flat[0].shape
    rows_own, rows_other = rows
    length, width = rows_own.shape
    count = 2 * z_size
    tiles = (part - width // count) // TILE
    part = width // count
    heads = cols // 3
    half = heads * GROUPS
    starts = [sum(sizes[:number]) for number in range(len(sizes))]
    per_shard = sizes[6] // 2 // CHUNKS
    blocks = count // 2

    def body(place_ref, own_ref, *refs):
        other_refs, refs = refs[:GIVEN], refs[GIVEN:]
        ins, refs = refs[:2], refs[2:]
        normed_ref, q_ref, k_ref, v_ref, vec_ref, hidden_bias_ref, weight, packed, sem = refs
        core = place_ref[2]
        copies = []
        for dx, ref in enumerate(ins):
            for z in range(z_size):
                copies.append(
                    pltpu.make_async_copy(
                        ref.at[z, pl.ds(part, tiles * TILE), :],
                        packed.at[shard_number(place_ref, z, dx)],
                        sem.at[count + len(copies)],
                    )
                )
        copies += weight_copies(place_ref, ins, weight, part, sem)
        for copy in copies:
            copy.start()
        for copy in copies:
            copy.wait()

        def lanes(s, at, size):
            found = []
            done = 0
            while done < size:
                tile, lane = divmod(at + done, cols)
                take = min(size - done, cols - lane)
                found.append(wide(packed[s, tile * TILE : tile * TILE + 1, lane : lane + take]))
                done += take
            return found

        def vector(slot, shards=range(count)):
            return jnp.concatenate(
                [one for s in shards for one in lanes(s, starts[slot], sizes[slot])], axis=1
            )

        gain, bias = vector(0), vector(1)
        bias_q = vector(2, range(blocks))
        bias_v = vector(2, range(blocks, count))
        bias_q = select(core, bias_q[:, :half], bias_q[:, half:])
        bias_v = select(core, bias_v[:, :half], bias_v[:, half:])
        for row, value in (
            (GAIN_ONE, gain),
            (BIAS_ONE, bias),
            (BIAS_OUT, vector(3)),
            (GAIN_TWO, vector(4)),
            (BIAS_TWO, vector(5)),
            (BIAS_DOWN, vector(7)),
            (BIAS_QV, jnp.concatenate([bias_q, bias_v], axis=1)),
        ):
            vec_ref[row : row + 1, :] = value
        vec_ref[7:8, :] = jnp.zeros((1, width), jnp.float32)
        for j in range(CHUNKS):
            for s in range(count):
                at = starts[6] + j * per_shard
                to = at + sizes[6] // 2
                hidden_bias_ref[j, :, s * per_shard : (s + 1) * per_shard] = select(
                    core,
                    jnp.concatenate(lanes(s, at, per_shard), axis=1),
                    jnp.concatenate(lanes(s, to, per_shard), axis=1),
                )
        for image, part_refs in enumerate(((own_ref,), other_refs)):
            for at in range(0, length, LANES):
                block = wide(joined(part_refs, slice(at, at + LANES)))
                normed_ref[image, at : at + LANES, :] = low(normalised(block) * gain + bias)

        def one_image(image, carry):
            write_qkv(
                normed_ref[image],
                weight,
                bias_q[:, :heads],
                bias_v[:, :heads],
                image,
                q_ref,
                k_ref,
                v_ref,
            )
            return carry

        lax.fori_loop(0, 2, one_image, 0)

    part_out = sds((2, length, heads), jnp.bfloat16)
    return call(
        body,
        place,
        (rows_own, *rows_other, *flat),
        [whole((length, width))]
        + [whole((length, width // GIVEN))] * GIVEN
        + [any_spec()] * 2,
        [sds((2, length, width), jnp.bfloat16)]
        + [part_out] * 3
        + [
            sds((8, width), jnp.float32),
            sds((CHUNKS, 1, count * per_shard), jnp.float32),
        ],
        [whole((2, length, width))]
        + [whole((2, length, heads))] * 3
        + [whole((8, width)), whole((CHUNKS, 1, count * per_shard))],
        [
            pltpu.VMEM((width, cols), jnp.bfloat16),
            pltpu.VMEM((count, tiles * TILE, cols), jnp.bfloat16),
            pltpu.SemaphoreType.DMA((2 * count,)),
        ],
        "project_first",
    )


def project_next(place, normed, vectors, pieces, group):
    flat = [one for side in pieces for one in side]
    z_size = flat[0].shape[0]
    _, length, width = normed.shape
    part = width // (2 * z_size)
    half = width // 2
    heads = half // GROUPS
    cols = 3 * heads

    def body(place_ref, normed_ref, vec_ref, *refs):
        ins, (q_ref, k_ref, v_ref, weight, sem) = refs[: len(flat)], refs[len(flat) :]
        copies = weight_copies(place_ref, ins, weight, part, sem)
        for copy in copies:
            copy.start()
        for copy in copies:
            copy.wait()
        at = group * heads
        bias_q = vec_ref[BIAS_QV : BIAS_QV + 1, at : at + heads]
        bias_v = vec_ref[BIAS_QV : BIAS_QV + 1, half + at : half + at + heads]

        def one_image(image, carry):
            write_qkv(normed_ref[image], weight, bias_q, bias_v, image, q_ref, k_ref, v_ref)
            return carry

        lax.fori_loop(0, 2, one_image, 0)

    return call(
        body,
        place,
        (normed, vectors, *flat),
        [whole(normed.shape), whole(vectors.shape)] + [any_spec()] * len(flat),
        [sds((2, length, heads), jnp.bfloat16)] * 3,
        [whole((2, length, heads))] * 3,
        [pltpu.VMEM((width, cols), jnp.bfloat16), pltpu.SemaphoreType.DMA((len(flat) * z_size,))],
        "project_next",
    )


def gather_out(place, pieces, first):
    flat = [one for side in pieces for one in side]
    z_size, rows, total = flat[0].shape
    half = total - first
    part = rows * len(flat) // 2

    def body(place_ref, *refs):
        ins, (out_ref, sem) = refs[: len(flat)], refs[len(flat) :]
        copies = row_copies(place_ref, ins, out_ref, part, pl.ds(first, half), sem)
        for copy in copies:
            copy.start()
        for copy in copies:
            copy.wait()

    shape = (2 * z_size * part, half)
    return call(
        body,
        place,
        tuple(flat),
        [any_spec()] * len(flat),
        [sds(shape, jnp.bfloat16)],
        [whole(shape)],
        [pltpu.SemaphoreType.DMA((len(flat) * z_size,))],
        "gather_out",
    )[0]


def attention(place, query, keys, values):
    _, length, heads = query.shape
    pairs = heads // LANES

    def body(place_ref, q_ref, k_ref, v_ref, out_ref, probs_ref):
        lane = lax.broadcasted_iota(jnp.int32, (length, LANES), 1)
        keys_block = k_ref[0]
        values_t = v_ref[0].T
        query_block = q_ref[0]
        key_row = lax.broadcasted_iota(jnp.int32, (length, length), 0)
        scores = []
        for head in range(2):
            inside = (lane >= head * HEAD_DIM) & (lane < (head + 1) * HEAD_DIM)
            query_head = jnp.where(inside, query_block, jnp.zeros_like(query_block))
            scores.append(jnp.where(key_row < SEQ, dot_tail(keys_block, query_head), -1e30))
        mixed = []
        for head in range(2):
            highest = jnp.max(scores[head], axis=0, keepdims=True)
            exponent = jnp.exp(scores[head] - highest)
            summed = jnp.sum(exponent, axis=0, keepdims=True)
            probs = low(exponent * (1.0 / summed))
            probs_ref[0, 0, head] = probs
            mixed.append(dot(values_t[head * HEAD_DIM : (head + 1) * HEAD_DIM, :], probs))
        out_ref[0] = low(jnp.concatenate(mixed, axis=0).T)

    block = pl.BlockSpec((1, length, LANES), lambda i, j, p: (i, 0, j))
    return call(
        body,
        place,
        (query, keys, values),
        [block] * 3,
        [
            sds((2, length, heads), jnp.bfloat16),
            sds((2, pairs, 2, length, length), jnp.bfloat16),
        ],
        [block, pl.BlockSpec((1, 1, 2, length, length), lambda i, j, p: (i, j, 0, 0, 0))],
        [],
        "attention",
        grid=(2, pairs),
    )


def attention_back(place, query, keys, values, probs, grad):
    _, length, heads = query.shape
    pairs = heads // LANES
    scale = 1.0 / math.sqrt(HEAD_DIM)

    def body(place_ref, q_ref, k_ref, v_ref, p_ref, g_ref, gq_ref, gk_ref, gv_ref):
        lane = lax.broadcasted_iota(jnp.int32, (length, LANES), 1)
        keys_t = k_ref[0].T
        values_block = v_ref[0]
        query_block = q_ref[0]
        grad_block = g_ref[0]
        grad_query = []
        grad_keys = []
        grad_values = []
        for head in range(2):
            inside = (lane >= head * HEAD_DIM) & (lane < (head + 1) * HEAD_DIM)
            grad_head = jnp.where(inside, grad_block, jnp.zeros_like(grad_block))
            probs_low = p_ref[0, 0, head]
            probs_wide = wide(probs_low)
            grad_probs = dot_tail(values_block, grad_head)
            inner = jnp.sum(probs_wide * grad_probs, axis=0, keepdims=True)
            grad_scores = low(probs_wide * (grad_probs - inner))
            keys_head = keys_t[head * HEAD_DIM : (head + 1) * HEAD_DIM, :]
            grad_query.append(dot(keys_head, grad_scores))
            grad_keys.append(dot(grad_scores, query_block))
            grad_values.append(dot(probs_low, grad_block))
        first = lane < HEAD_DIM
        gq_ref[0] = low(jnp.concatenate(grad_query, axis=0).T * scale)
        gk_ref[0] = low(jnp.where(first, grad_keys[0], grad_keys[1]))
        gv_ref[0] = low(jnp.where(first, grad_values[0], grad_values[1]))

    block = pl.BlockSpec((1, length, LANES), lambda i, j, p: (i, 0, j))
    return call(
        body,
        place,
        (query, keys, values, probs, grad),
        [block] * 3
        + [pl.BlockSpec((1, 1, 2, length, length), lambda i, j, p: (i, j, 0, 0, 0)), block],
        [sds((2, length, heads), jnp.bfloat16)] * 3,
        [block] * 3,
        [],
        "attention_back",
        grid=(2, pairs),
    )


def head_rows(core, heads, group):
    mine = pl.multiple_of((core * GROUPS + group) * heads, heads)
    return mine, pl.multiple_of(((1 - core) * GROUPS + group) * heads, heads)


def project_out(place, mine, theirs, weight_mine, weight_theirs, rows, vectors):
    width, half = weight_mine.shape
    _, length, heads = mine[0].shape

    def body(place_ref, *refs):
        mine_refs, theirs_refs, refs = refs[:GROUPS], refs[GROUPS : 2 * GROUPS], refs[2 * GROUPS :]
        wm_ref, wt_ref, own_ref, *other_refs, vec_ref, middle_ref, normed_ref, total = refs
        core = place_ref[2]
        for image, part_refs in enumerate(((own_ref,), other_refs)):
            for slot, weight in enumerate((wm_ref, wt_ref)):
                branch = None
                for g in range(GROUPS):
                    at_mine, at_theirs = head_rows(core, heads, g)
                    add = dot(mine_refs[g][image], weight[pl.ds(at_mine, heads), :]) + dot(
                        theirs_refs[g][1 - image], weight[pl.ds(at_theirs, heads), :]
                    )
                    branch = add if branch is None else branch + add
                total[slot] = branch
            for at in range(0, length, LANES):
                upto = at + LANES
                first, second = total[0, at:upto, :], total[1, at:upto, :]
                left = select(core, first, second)
                right = select(core, second, first)
                middle = (
                    wide(joined(part_refs, slice(at, upto)))
                    + jnp.concatenate([left, right], axis=1)
                    + vec_ref[BIAS_OUT : BIAS_OUT + 1, :]
                )
                if image == 0:
                    middle_ref[at:upto, :] = middle
                normed_ref[image, at:upto, :] = low(
                    normalised(middle) * vec_ref[GAIN_TWO : GAIN_TWO + 1, :]
                    + vec_ref[BIAS_TWO : BIAS_TWO + 1, :]
                )

    return call(
        body,
        place,
        (*mine, *theirs, weight_mine, weight_theirs, rows[0], *rows[1], vectors),
        [whole((2, length, heads))] * (2 * GROUPS)
        + [whole((width, half))] * 2
        + [whole((length, width))]
        + [whole((length, width // GIVEN))] * GIVEN
        + [whole(vectors.shape)],
        [sds((length, width), jnp.float32), sds((2, length, width), jnp.bfloat16)],
        [whole((length, width)), whole((2, length, width))],
        [pltpu.VMEM((2, length, half), jnp.float32)],
        "project_out",
    )


def feed_forward(place, normed, cotangent, pieces, bias, chunk, running):
    cut = len(pieces[0])
    z_size, _, width = pieces[0][0].shape
    hidden_width = bias.shape[2]
    part = width // (2 * z_size)
    per_shard = hidden_width // (2 * z_size)
    rows_in, rows_down = part // cut, per_shard // cut
    _, length, _ = normed.shape
    first_call = running is None
    last_call = chunk == CHUNKS - 1
    given = GIVEN if last_call else 1

    def body(place_ref, normed_ref, own_cot, *refs):
        other_cots, (bias_ref, *refs) = refs[:GIVEN], refs[GIVEN:]
        ins, refs = refs[: 2 * cut], refs[2 * cut :]
        if not first_call:
            before, refs = refs[:4], refs[4:]
        out_own, *out_other = refs[: 1 + given]
        gn_own, *gn_other = refs[1 + given : 2 + 2 * given]
        bsum_ref, *refs = refs[2 + 2 * given :]
        term_refs, refs = refs[:4], refs[4:]
        w_in, w_down, cots, into, down, grads, sem, out_sem = refs
        copies = []
        for weight, at, rows, of_shard in (
            (w_in, 0, rows_in, part),
            (w_down, rows_in, rows_down, per_shard),
        ):
            for number, ref in enumerate(ins):
                dx, h = number // cut, number % cut
                y = h + (1 - 2 * h) * place_ref[3] if cut == 2 else 0
                for z in range(z_size):
                    s = shard_number(place_ref, z, dx)
                    row = pl.multiple_of(s * of_shard + y * rows, rows)
                    copy = pltpu.make_async_copy(
                        ref.at[z, pl.ds(at, rows), :],
                        weight.at[pl.ds(row, rows), :],
                        sem.at[len(copies)],
                    )
                    copy.start()
                    copies.append(copy)
        for copy in copies:
            copy.wait()
        cots[0] = own_cot[...]
        cots[1] = joined(other_cots)

        def one_image(image, carry):
            first = image == 0
            normed_rows = normed_ref[image]
            preact = dot(normed_rows, w_in[...]) + bias_ref[0]
            phi = 0.5 * (1.0 + lax.erf(preact * math.sqrt(0.5)))
            density = jnp.exp(-0.5 * preact * preact) * (1.0 / math.sqrt(2.0 * math.pi))
            hidden = low(preact * phi)
            slope = phi + preact * density
            cot = cots[image]
            grad = low(dot_tail(cot, w_down[...]) * slope)
            to_out = dot(hidden, w_down[...])
            to_normed = dot_tail(grad, w_in[...])
            for slot, to_refs in enumerate((([out_own], [gn_own]), (out_other, gn_other))):

                @pl.when(image == slot)
                def _():
                    for number, (refs_of, value) in enumerate(zip(to_refs, (to_out, to_normed))):
                        if not first_call:
                            value = before[2 * number + slot][...] + value
                        cols = width // len(refs_of)
                        for at, ref in enumerate(refs_of):
                            ref[...] = value[:, at * cols : (at + 1) * cols].astype(ref.dtype)

            partial = jnp.sum(wide(grad), axis=0, keepdims=True)
            to_in = dot(normed_rows.T, grad)
            to_down = dot(hidden.T, cot)

            @pl.when(first)
            def _():
                bsum_ref[...] = partial
                into[...] = to_in
                down[...] = to_down

            @pl.when(jnp.logical_not(first))
            def _():
                bsum_ref[...] += partial
                for slot, (held, value, rows) in enumerate(
                    ((into, to_in, part), (down, to_down, per_shard))
                ):
                    whole_term = low(held[...] + value)
                    for z in range(z_size):
                        for x in range(2):
                            dx = x + (1 - 2 * x) * place_ref[1]
                            s = z * 2 + x
                            grads[slot, dx, z] = whole_term[s * rows : (s + 1) * rows, :]

            return carry

        lax.fori_loop(0, 2, one_image, 0)
        copies = [
            pltpu.make_async_copy(grads.at[number // 2, number % 2], ref, out_sem.at[number])
            for number, ref in enumerate(term_refs)
        ]
        for copy in copies:
            copy.start()
        for copy in copies:
            copy.wait()

    total = sds((length, width), jnp.float32)
    other = sds((length, width // given), jnp.bfloat16 if last_call else jnp.float32)
    totals = ([total] + [other] * given) * 2
    if part != per_shard:
        raise ValueError
    piece_out = sds((z_size, part, width), jnp.bfloat16)
    carried = () if first_call else tuple(running)
    return call(
        body,
        place,
        (normed, cotangent[0], *cotangent[1], bias, *[one for side in pieces for one in side], *carried),
        [whole((2, length, width)), whole((length, width))]
        + [whole((length, width // GIVEN))] * GIVEN
        + [pl.BlockSpec((1, 1, hidden_width), lambda i, p: (chunk, 0, 0))]
        + [any_spec()] * (2 * cut)
        + [whole((length, width))] * len(carried),
        totals + [sds((1, hidden_width), jnp.float32)] + [piece_out] * 4,
        [whole(a.shape) for a in totals] + [whole((1, hidden_width))] + [any_spec()] * 4,
        [
            pltpu.VMEM((width, hidden_width), jnp.bfloat16),
            pltpu.VMEM((hidden_width, width), jnp.bfloat16),
            pltpu.VMEM((2, length, width), jnp.bfloat16),
            pltpu.VMEM((width, hidden_width), jnp.float32),
            pltpu.VMEM((hidden_width, width), jnp.float32),
            pltpu.VMEM((2, 2, z_size, part, width), jnp.bfloat16),
            pltpu.SemaphoreType.DMA((4 * cut * z_size,)),
            pltpu.SemaphoreType.DMA((4,)),
        ],
        "feed_forward",
    )


def norm_back(place, rows, vectors, gain_row, grad_own, others, passed, tokens, finish=()):
    length, width = rows.shape

    def body(place_ref, rows_ref, vec_ref, own_ref, pass_ref, *refs):
        other_refs, refs = refs[: len(others)], refs[len(others) :]
        step = pl.program_id(0)
        values = wide(rows_ref[...])
        if finish:
            first_ref, second_refs, refs = refs[0], refs[1 : len(finish)], refs[len(finish) :]
            refs[1][...] = low(
                values
                + first_ref[...]
                + wide(joined(second_refs))
                + vec_ref[BIAS_DOWN : BIAS_DOWN + 1, :]
            )
        sum_ref = refs[0]
        centre = values - jnp.mean(values, axis=-1, keepdims=True)
        spread = jnp.mean(centre * centre, axis=-1, keepdims=True)
        inverse = lax.rsqrt(spread + ln_eps)
        unit = centre * inverse
        grad = own_ref[...] + wide(joined(other_refs))
        scaled = grad * vec_ref[gain_row : gain_row + 1, :]
        mean_one = jnp.mean(scaled, axis=-1, keepdims=True)
        mean_two = jnp.mean(scaled * unit, axis=-1, keepdims=True)
        result = wide(pass_ref[...]) + (scaled - mean_one - unit * mean_two) * inverse
        rounded = low(result)
        parts = [
            jnp.sum(grad * unit, axis=0, keepdims=True),
            jnp.sum(grad, axis=0, keepdims=True),
            jnp.sum(wide(rounded), axis=0, keepdims=True),
            jnp.zeros((5, width), jnp.float32),
        ]
        if not finish:
            refs[1][...] = rounded
        else:
            refs[2][...] = result
            refs[3][...] = rounded
            for number, ref in enumerate(refs[4:]):
                at = number * width // GIVEN
                ref[...] = rounded[:, at : at + width // GIVEN]
        sums = jnp.concatenate(parts, axis=0)

        @pl.when(step == 0)
        def _():
            sum_ref[...] = sums

        @pl.when(step > 0)
        def _():
            sum_ref[...] += sums

    block = pl.BlockSpec((LANES, width), lambda i, p: (i, 0))
    outs = [sds((8, width), jnp.float32), sds((tokens, width), jnp.bfloat16)]
    if finish:
        outs += [sds((length, width), jnp.float32), sds((length, width), jnp.bfloat16)]
        outs += [sds((length, width // GIVEN), jnp.bfloat16)] * GIVEN
    other_block = pl.BlockSpec((LANES, others[0].shape[1]), lambda i, p: (i, 0))
    ins = (rows, vectors, grad_own, passed, *others, *finish)
    return call(
        body,
        place,
        ins,
        [block, whole(vectors.shape), block, block]
        + [other_block] * len(others)
        + ([block] + [other_block] * len(others) if finish else []),
        outs,
        [whole((8, width))]
        + [pl.BlockSpec((LANES, a.shape[1]), lambda i, p: (i, 0)) for a in outs[1:]],
        [],
        "norm_back",
        grid=(length // LANES,),
    )


def out_back(place, grad_own, grad_others, mine, theirs, weight_mine, weight_theirs):
    width, half = weight_mine.shape
    z_size = lax.axis_size("z")
    part = width // (2 * z_size)
    _, length, heads = mine[0].shape

    def body(place_ref, own_ref, own_half, *refs):
        other_refs, refs = refs[:GIVEN], refs[GIVEN:]
        mine_refs, theirs_refs, refs = refs[:GROUPS], refs[GROUPS : 2 * GROUPS], refs[2 * GROUPS :]
        wm_ref, wt_ref, *refs = refs
        ga_refs, (keep_ref, send_ref, turned, grads, out_sem) = refs[:GROUPS], refs[GROUPS:]
        core = place_ref[2]
        for image in range(2):
            lanes = slice(image * length, (image + 1) * length)
            for g in range(GROUPS):
                at_mine, at_theirs = head_rows(core, heads, g)
                turned[pl.ds(at_mine, heads), lanes] = mine_refs[g][image].T
                turned[pl.ds(at_theirs, heads), lanes] = theirs_refs[g][1 - image].T
        other = joined(other_refs)
        other_half = select(core, other[:, :half], other[:, half:])
        term = dot(turned[:, :length], own_half[...]) + dot(turned[:, length:], other_half)
        for z in range(z_size):
            for x in range(2):
                dx = x + (1 - 2 * x) * place_ref[1]
                at = (z * 2 + x) * part
                grads[dx, z] = low(term[at : at + part, :])
        for slot, ref in enumerate((keep_ref, send_ref)):
            pltpu.make_async_copy(grads.at[slot], ref, out_sem.at[slot]).start()
        for image, value in enumerate((own_ref[...], other)):
            first, second = value[:, :half], value[:, half:]
            left = select(core, first, second)
            right = select(core, second, first)
            for g in range(GROUPS):
                at_mine, _ = head_rows(core, heads, g)
                ga_refs[g][image] = low(
                    dot_tail(left, wm_ref[pl.ds(at_mine, heads), :])
                    + dot_tail(right, wt_ref[pl.ds(at_mine, heads), :])
                )
        for slot, ref in enumerate((keep_ref, send_ref)):
            pltpu.make_async_copy(grads.at[slot], ref, out_sem.at[slot]).wait()

    half_block = pl.BlockSpec((length, half), lambda i, p: (0, p[2]))
    piece_out = sds((z_size, part, half), jnp.bfloat16)
    return call(
        body,
        place,
        (grad_own, grad_own, *grad_others, *mine, *theirs, weight_mine, weight_theirs),
        [whole((length, width)), half_block]
        + [whole((length, width // GIVEN))] * GIVEN
        + [whole((2, length, heads))] * (2 * GROUPS)
        + [whole((width, half))] * 2,
        [sds((2, length, heads), jnp.bfloat16)] * GROUPS + [piece_out] * 2,
        [whole((2, length, heads))] * GROUPS + [any_spec()] * 2,
        [
            pltpu.VMEM((width, 2 * length), jnp.bfloat16),
            pltpu.VMEM((2, z_size, part, half), jnp.bfloat16),
            pltpu.SemaphoreType.DMA((2,)),
        ],
        "out_back",
    )


def qkv_term(place, normed, grad_q, grad_k, grad_v):
    _, length, width = normed.shape
    heads = grad_q.shape[-1]
    cols = 3 * heads

    def body(place_ref, normed_ref, gq_ref, gk_ref, gv_ref, sum_ref, keep_ref, send_ref, turned, grads, sem):
        z_size = grads.shape[1]
        part = grads.shape[2]
        for image in range(2):
            turned[:, image * length : (image + 1) * length] = normed_ref[image].T
        for slot, ref in enumerate((gq_ref, gk_ref, gv_ref)):
            term = dot(turned[:, :length], ref[0]) + dot(turned[:, length:], ref[1])
            for z in range(z_size):
                for x in range(2):
                    dx = x + (1 - 2 * x) * place_ref[1]
                    at = (z * 2 + x) * part
                    grads[dx, z, :, slot * heads : (slot + 1) * heads] = low(
                        term[at : at + part, :]
                    )
            sum_ref[slot : slot + 1, :] = jnp.sum(wide(ref[0]), axis=0, keepdims=True) + jnp.sum(
                wide(ref[1]), axis=0, keepdims=True
            )
        for slot, ref in enumerate((keep_ref, send_ref)):
            pltpu.make_async_copy(grads.at[slot], ref, sem.at[slot]).start()
        for slot, ref in enumerate((keep_ref, send_ref)):
            pltpu.make_async_copy(grads.at[slot], ref, sem.at[slot]).wait()

    z_size = lax.axis_size("z")
    part = width // (2 * z_size)
    piece_out = sds((z_size, part, cols), jnp.bfloat16)
    return call(
        body,
        place,
        (normed, grad_q, grad_k, grad_v),
        [whole((2, length, width))] + [whole((2, length, heads))] * 3,
        [sds((3, heads), jnp.float32)] + [piece_out] * 2,
        [whole((3, heads))] + [any_spec()] * 2,
        [
            pltpu.VMEM((width, 2 * length), jnp.bfloat16),
            pltpu.VMEM((2, z_size, part, cols), jnp.bfloat16),
            pltpu.SemaphoreType.DMA((2,)),
        ],
        "qkv_term",
    )


def qkv_back(place, grads, pieces):
    flat = [one for piece in pieces for side in piece for one in side]
    counts = [sum(len(side) for side in piece) for piece in pieces]
    z_size, _, cols = flat[0].shape
    heads = cols // 3
    length = grads[0][0].shape[1]
    part = flat[-1].shape[1] * counts[-1] // 2
    width = 2 * z_size * part

    def body(place_ref, *refs):
        grad_refs, refs = refs[: 3 * GROUPS], refs[3 * GROUPS :]
        ins, (own_ref, *other_refs, weight, sem) = refs[: len(flat)], refs[len(flat) :]
        copies = []
        for g in range(GROUPS):
            at = sum(counts[:g])
            copies += weight_copies(
                place_ref, ins[at : at + counts[g]], weight.at[g], part, sem.at[g]
            )
        for copy in copies:
            copy.start()
        for copy in copies:
            copy.wait()

        def one_image(image, carry):
            total = None
            for g in range(GROUPS):
                for slot in range(3):
                    add = dot_tail(
                        grad_refs[3 * g + slot][image],
                        weight[g, :, slot * heads : (slot + 1) * heads],
                    )
                    total = add if total is None else total + add

            @pl.when(image == 0)
            def _():
                own_ref[...] = total

            @pl.when(image == 1)
            def _():
                for number, ref in enumerate(other_refs):
                    at = number * width // GIVEN
                    ref[...] = low(total[:, at : at + width // GIVEN])

            return carry

        lax.fori_loop(0, 2, one_image, 0)

    return call(
        body,
        place,
        (*[one for grad in grads for one in grad], *flat),
        [whole((2, length, heads))] * (3 * GROUPS) + [any_spec()] * len(flat),
        [sds((length, width), jnp.float32)] + [sds((length, width // GIVEN), jnp.bfloat16)] * GIVEN,
        [whole((length, width))] + [whole((length, width // GIVEN))] * GIVEN,
        [
            pltpu.VMEM((GROUPS, width, cols), jnp.bfloat16),
            pltpu.SemaphoreType.DMA((GROUPS, max(counts) * z_size)),
        ],
        "qkv_back",
    )


def to_column(row):
    return jnp.concatenate(
        [
            jnp.broadcast_to(row[:, at : at + LANES], (LANES, LANES)).T[:, :1]
            for at in range(0, row.shape[1], LANES)
        ],
        axis=0,
    )


def to_row(column):
    return jnp.concatenate(
        [
            jnp.broadcast_to(column[at : at + LANES, :], (LANES, LANES)).T[:1, :]
            for at in range(0, column.shape[0], LANES)
        ],
        axis=1,
    )


def statistics(place, kinds, pairs, shares, weights, states, images, group, extra=None):
    flat = [a for pair in pairs for side in pair for a in side]
    amount = len(kinds)
    vectors = 0 if extra is None else len(extra[1])

    def body(place_ref, *refs):
        core = place_ref[2]
        refs = list(refs)

        def take(n):
            taken = refs[:n]
            del refs[:n]
            return taken

        sides_of = [[take(len(side)) for side in pair] for pair in pairs]
        weight_refs, state_refs = take(amount), take(amount)
        if vectors:
            (terms_ref,) = take(1)
            param_refs, moment_refs = take(vectors), take(vectors)
        grad_refs, row_refs = take(amount), take(amount)
        (pack_ref,) = take(1)
        if vectors:
            vector_grads, new_moments = take(vectors), take(vectors)
        at_pack = 0
        for number, kind in enumerate(kinds):
            grad_ref, weight_ref = grad_refs[number], weight_refs[number]
            rows, cols = weights[number].shape
            for chunk, (number_of, row0, col0) in enumerate(shares[number]):
                sides = sides_of[number_of]

                def halves(row, row_count, col, col_count):
                    index = (
                        slice(row0 + row, row0 + row + row_count),
                        slice(col0 + col, col0 + col + col_count),
                    )
                    mine, theirs = [
                        sum([wide(ref[index]) for ref in side[1:]], wide(side[0][index]))
                        * (1.0 / images)
                        for side in sides
                    ]
                    return select(core, mine, theirs), select(core, theirs, mine)

                if kind == "in":
                    per = cols // (2 * CHUNKS * group)
                    for c, half in enumerate(halves(0, rows, 0, per * group)):
                        for s in range(group):
                            at = ((s * 2 + c) * CHUNKS + chunk) * per
                            grad_ref[:, at : at + per] = half[:, s * per : (s + 1) * per]
                elif kind == "down":
                    per = rows // (2 * CHUNKS)
                    for c, half in enumerate(halves(0, per, 0, cols)):
                        at = (c * CHUNKS + chunk) * per
                        grad_ref[at : at + per, :] = half
                else:
                    amount_of = len(shares[number])
                    lanes_of = cols // (2 * SPLIT[kind] * amount_of)
                    for slot in range(SPLIT[kind]):
                        for c, half in enumerate(halves(0, rows, slot * lanes_of, lanes_of)):
                            at = ((2 * slot + c) * amount_of + chunk) * lanes_of
                            grad_ref[:, at : at + lanes_of] = half
            squared = grad_ref[...] * grad_ref[...]
            new_rows = 0.5 * to_column(state_refs[number][...]) + 0.5 * jnp.mean(
                squared, axis=1, keepdims=True
            )
            row_refs[number][...] = to_row(new_rows)
            pack_ref[0:1, at_pack : at_pack + cols] = jnp.sum(squared, axis=0, keepdims=True)
            pack_ref[1:2, at_pack : at_pack + cols] = jnp.sum(
                squared * (1.0 / new_rows), axis=0, keepdims=True
            )
            at_pack += cols
            weight = weight_ref[...]
            pack_ref[0:1, at_pack : at_pack + LANES] = jnp.broadcast_to(
                jnp.sum(new_rows, axis=0, keepdims=True), (1, LANES)
            )
            pack_ref[1:2, at_pack : at_pack + LANES] = jnp.broadcast_to(
                jnp.sum(jnp.sum(weight * weight, axis=0, keepdims=True), axis=1, keepdims=True),
                (1, LANES),
            )
            at_pack += LANES
        at = 0
        if vectors:
            place_row = lax.broadcasted_iota(jnp.int32, extra[0].shape, 0)
            here = place_row == place_ref[0] * 2 + place_ref[1]
            mine = jnp.sum(
                jnp.where(here, terms_ref[...], 0.0), axis=0, keepdims=True
            )
        for number in range(vectors):
            size = extra[1][number].shape[1]
            grad = mine[:, at : at + size] * (1.0 / images)
            at += size
            param = param_refs[number][...]
            moment = 0.5 * moment_refs[number][...] + 0.5 * grad * grad
            direction = grad * lax.rsqrt(moment)
            vector_grads[number][...] = grad
            new_moments[number][...] = moment
            for row, value in enumerate((direction, param)):
                pack_ref[row : row + 1, at_pack : at_pack + LANES] = jnp.broadcast_to(
                    jnp.sum(value * value, axis=1, keepdims=True), (1, LANES)
                )
            at_pack += LANES

    lanes = sum(weight.shape[1] + LANES for weight in weights) + vectors * LANES
    ins = [*flat, *weights, *states]
    outs = [sds(weight.shape, jnp.float32) for weight in weights]
    outs += [sds(state.shape, jnp.float32) for state in states]
    outs.append(sds((2, lanes), jnp.float32))
    if vectors:
        terms, params, moments = extra
        ins += [terms, *params, *moments]
        outs += [sds(a.shape, jnp.float32) for a in (*params, *moments)]
    results = call(
        body,
        place,
        tuple(ins),
        [whole(a.shape) for a in ins],
        outs,
        [whole(a.shape) for a in outs],
        [],
        "statistics",
    )
    return (
        results[:amount],
        results[amount : 2 * amount],
        results[2 * amount],
        results[2 * amount + 1 : 2 * amount + 1 + vectors],
        results[2 * amount + 1 + vectors :],
    )


CLIP_ORDER = (8, 10, 4, 2)
SPLIT = {"out": 1, "qkv": 3}


def update(place, grads, new_rows, weights, cols_states, pack, group, extra=None, clips=None):
    amount = len(weights)
    vectors = 0 if extra is None else len(extra[0])

    def body(place_ref, *refs):
        refs = list(refs)

        def take(n):
            taken = refs[:n]
            del refs[:n]
            return taken

        grad_refs, row_refs, weight_refs, state_refs = [take(amount) for _ in range(4)]
        (pack_ref,) = take(1)
        if vectors:
            vector_grads, moment_refs, param_refs = [take(vectors) for _ in range(3)]
            (clips_ref,) = take(1)
        new_refs, col_refs = take(amount), take(amount)
        (clip_ref,) = take(1)
        param_outs = take(vectors)
        at_pack = 0
        if not vectors:
            clip_ref[...] = jnp.zeros(clip_ref.shape, jnp.float32)
        for number in range(amount):
            rows, cols = weights[number].shape
            rows_total = rows * group
            count = rows_total * cols
            new_cols = (
                0.5 * state_refs[number][...]
                + 0.5 * pack_ref[0:1, at_pack : at_pack + cols] / rows_total
            )
            col_refs[number][...] = new_cols
            by_rows = pack_ref[1:2, at_pack : at_pack + cols]
            at_pack += cols
            mean_rows = pack_ref[0:1, at_pack : at_pack + 1] / rows_total
            weight_total = pack_ref[1:2, at_pack : at_pack + 1]
            at_pack += LANES
            total = mean_rows * jnp.sum(by_rows / new_cols, axis=1, keepdims=True)
            clip = jnp.maximum(1.0, jnp.sqrt(total / count) / clip_level)
            step = step_rate * jnp.sqrt(weight_total / count) / clip
            if vectors:
                if number == 0:
                    found = [clips_ref[at : at + 1, :1] for at in range(len(MATRICES) - amount)]
                found.append(clip)
            else:
                clip_ref[number : number + 1, :] = jnp.broadcast_to(clip, (1, LANES))
            estimate = to_column(row_refs[number][...]) * (new_cols / mean_rows)
            new_refs[number][...] = weight_refs[number][...] - step * (
                grad_refs[number][...] * lax.rsqrt(estimate)
            )
        for number in range(vectors):
            count = extra[2][number].shape[1] * group
            total = pack_ref[0:1, at_pack : at_pack + 1]
            weight_total = pack_ref[1:2, at_pack : at_pack + 1]
            at_pack += LANES
            clip = jnp.maximum(1.0, jnp.sqrt(total / count) / clip_level)
            step = step_rate * jnp.sqrt(weight_total / count) / clip
            found.append(clip)
            direction = vector_grads[number][...] * lax.rsqrt(moment_refs[number][...])
            param_outs[number][...] = param_refs[number][...] - step * direction
        if vectors:
            lane = lax.broadcasted_iota(jnp.int32, (1, LANES), 1)
            row = jnp.zeros((1, LANES), jnp.float32)
            for value, number in zip(found, (*CLIP_ORDER, *VECTORS)):
                row = jnp.where(lane == number, value, row)
            clip_ref[...] = row[:, : len(found)]

    ins = [*grads, *new_rows, *weights, *cols_states, pack]
    outs = [sds(a.shape, jnp.float32) for a in (*weights, *cols_states)]
    outs.append(sds((1, len(MATRICES) + vectors) if vectors else (8, LANES), jnp.float32))
    if vectors:
        ins += [*extra[0], *extra[1], *extra[2], clips]
        outs += [sds(a.shape, jnp.float32) for a in extra[2]]
    results = call(
        body,
        place,
        tuple(ins),
        [whole(a.shape) for a in ins],
        outs,
        [whole(a.shape) for a in outs],
        [],
        "update",
    )
    return (
        results[:amount],
        results[amount : 2 * amount],
        results[2 * amount],
        results[2 * amount + 1 :],
    )


def pack_terms(place, sums_mid, sums_in, sums_qkv, hidden_sums, down_sums, sizes):
    z_size = lax.axis_size("z")
    shards = 2 * z_size
    per_shard = sizes[6] // 2 // CHUNKS
    heads = sums_qkv[0].shape[1]

    def body(place_ref, mid_ref, in_ref, *refs):
        qkv_refs, refs = refs[:GROUPS], refs[GROUPS:]
        hidden_refs, (down_ref, out_ref) = refs[:CHUNKS], refs[CHUNKS:]
        core = place_ref[2]

        def put(slot, row):
            at, size = sum(sizes[:slot]), sizes[slot]
            for s in range(shards):
                out_ref[s : s + 1, at : at + size] = row[:, s * size : (s + 1) * size]

        put(0, in_ref[0:1, :])
        put(1, in_ref[1:2, :])
        zero = jnp.zeros((1, heads * GROUPS), jnp.float32)
        halves = []
        for slot in (0, 2):
            row = jnp.concatenate([ref[slot : slot + 1, :] for ref in qkv_refs], axis=1)
            halves += [select(core, row, zero), select(core, zero, row)]
        put(2, jnp.concatenate(halves, axis=1))
        put(3, mid_ref[2:3, :])
        put(4, mid_ref[0:1, :])
        put(5, mid_ref[1:2, :])
        put(7, down_ref[...])
        none = jnp.zeros((1, per_shard), jnp.float32)
        for s in range(shards):
            for j in range(CHUNKS):
                row = hidden_refs[j][:, s * per_shard : (s + 1) * per_shard]
                for c in range(2):
                    at = sum(sizes[:6]) + (c * CHUNKS + j) * per_shard
                    here = select(core, row, none) if c == 0 else select(core, none, row)
                    out_ref[s : s + 1, at : at + per_shard] = here

    ins = (sums_mid, sums_in, *sums_qkv, *hidden_sums, down_sums)
    shape = (shards, sum(sizes))
    return call(
        body,
        place,
        ins,
        [whole(a.shape) for a in ins],
        [sds(shape, jnp.float32)],
        [whole(shape)],
        [],
        "pack_terms",
    )[0]


def on_device(
    inputs,
    cotangent,
    norm1_gain,
    norm1_bias,
    qkv_weight,
    qv_bias,
    out_weight,
    out_bias,
    norm2_gain,
    norm2_bias,
    in_weight,
    in_bias,
    down_weight,
    down_bias,
    qkv_rows,
    qkv_cols,
    out_rows,
    out_cols,
    in_rows,
    in_cols,
    down_rows,
    down_cols,
    norm1_gain_moment,
    norm1_bias_moment,
    qv_bias_moment,
    out_bias_moment,
    norm2_gain_moment,
    norm2_bias_moment,
    in_bias_moment,
    down_bias_moment,
):
    masters = [
        norm1_gain,
        norm1_bias,
        qkv_weight,
        qv_bias,
        out_weight,
        out_bias,
        norm2_gain,
        norm2_bias,
        in_weight,
        in_bias,
        down_weight,
        down_bias,
    ]
    moments = [
        norm1_gain_moment,
        norm1_bias_moment,
        qv_bias_moment,
        out_bias_moment,
        norm2_gain_moment,
        norm2_bias_moment,
        in_bias_moment,
        down_bias_moment,
    ]
    place = jnp.stack([lax.axis_index(axis) for axis in ("z", "x", "c", "y")]).astype(jnp.int32)
    by_y = lax.axis_size("y") == 2
    group = lax.axis_size("z") * lax.axis_size("x")
    tokens = inputs.shape[0]
    part = in_weight.shape[0]
    images = (tokens // SEQ) * group * lax.axis_size("y") * lax.axis_size("c")
    as_row = lambda vector: vector.reshape(1, -1)
    params = [as_row(masters[number]) for number in VECTORS]
    moments = [as_row(moment) for moment in moments]
    sizes = [param.shape[1] for param in params]

    cut = 2 if by_y else 1
    shard_first, shard_next = prepare_qkv(place, qkv_weight, out_weight, params, cut)
    near = along_z(shard_first)
    pieces_first = by_x(near)
    near_next = along_z(after(shard_next, near))
    rows_own, parts = pad_rows(after(place, near), inputs)
    rows = (rows_own, [swap(one, "c") for one in parts])
    *shards_ff, down_sums = prepare_rest(
        after(place, rows_own), in_weight, down_weight, cotangent, (cut,) * 2
    )
    cot_own, parts = pad_rows(after(place, (down_sums, rows[1])), cotangent)
    near_ff = [along_z(shards_ff[0])]

    normed, *first, vectors, hidden_bias = project_first(
        after(place, (cot_own, near_next)), rows, pieces_first, sizes
    )
    near_ff.append(along_z(after(shards_ff[1], normed)))
    cot = (cot_own, [swap(one, "c") for one in after(parts, normed)])
    qkv = [first]
    across_next = after(swap(near_next, "x"), normed)
    pieces_next = by_y_too([[near_next], [across_next]], by_y)
    mixed, prob = attention(after(place, across_next), *first)
    attended = [mixed]
    probs = [prob]
    theirs = [swap(mixed, "c")]
    pieces_next = after(pieces_next, mixed)
    weight_mine = gather_out(place, pieces_next, 3 * first[0].shape[-1])
    weight_theirs = swap(weight_mine, "c")
    near_ff[0] = after(near_ff[0], pieces_next)
    across = swap(near_ff[0], "x")
    near_too = swap(near_ff[0], "y") if by_y else None
    qkv.append(
        project_next(
            after(place, (near_ff[0], weight_mine)), normed, vectors, pieces_next, 1
        )
    )
    mixed, prob = attention(place, *qkv[1])
    attended.append(mixed)
    probs.append(prob)
    theirs.append(swap(mixed, "c"))
    across = after(across, mixed)
    if by_y:
        pieces_ff = [[near_ff[0], near_too], [across, swap(across, "y")]]
    else:
        pieces_ff = [[near_ff[0]], [across]]
    near_ff[1] = after(near_ff[1], across)
    across_next = swap(near_ff[1], "x")
    near_first = near_too
    near_too = (near_too, swap(near_ff[1], "y")) if by_y else None
    middle, normed_mid = project_out(
        after(place, (near_ff[1], near_first)), attended, theirs, weight_mine, weight_theirs, rows, vectors
    )
    across_next = after(across_next, normed_mid)
    if by_y:
        pieces_ff = [
            [[near_ff[0], near_too[0]], pieces_ff[1]],
            [[near_ff[1], near_too[1]], [across_next, swap(across_next, "y")]],
        ]
    else:
        pieces_ff = [[[near_ff[0]], [across]], [[near_ff[1]], [across_next]]]
    *running, sums, keep_in, send_in, keep_down, send_down = feed_forward(
        after(place, across_next), normed_mid, cot, pieces_ff[0], hidden_bias, 0, None
    )
    terms_ff = [(keep_in, swap(send_in, "x"), keep_down, swap(send_down, "x"))]
    hidden_sums = [sums]
    *totals, sums, keep_in, send_in, keep_down, send_down = feed_forward(
        place, normed_mid, cot, pieces_ff[1], hidden_bias, 1, running
    )
    hidden_sums.append(sums)
    folded = [fold_pair(*after(terms_ff[0], sums))]
    terms_ff.append((keep_in, swap(send_in, "x"), keep_down, swap(send_down, "x")))
    scattered = [scatter_z(folded[0])]
    out_share, *out_given = totals[: 1 + GIVEN]
    normed_share, *normed_given = totals[1 + GIVEN :]
    sums_mid, output, grad_mid, grad_mid_low, *parts = norm_back(
        after(place, folded[0]),
        middle,
        vectors,
        GAIN_TWO,
        normed_share,
        [swap(one, "c") for one in normed_given],
        cot_own,
        tokens,
        (out_share, *[swap(one, "c") for one in out_given]),
    )
    *grad_attended, keep, send = out_back(
        place,
        grad_mid_low,
        [swap(one, "c") for one in parts],
        attended,
        theirs,
        weight_mine,
        weight_theirs,
    )
    got = swap(send, "x")
    grad_qkv = [attention_back(place, *qkv[0], probs[0], grad_attended[0])]
    sums_first, keep_first, send_first = qkv_term(place, normed, *grad_qkv[0])
    got_first = swap(send_first, "x")
    folded.append(fold_pair(*after(terms_ff[1], sums_first)))
    scattered.append(scatter_z(folded[1]))
    scattered[0] = after(scattered[0], folded[1])
    own_ff = [sum_y(scattered[0])]
    grad_qkv.append(
        attention_back(after(place, scattered[0]), *qkv[1], probs[1], grad_attended[1])
    )
    own_ff[0] = after(own_ff[0], grad_qkv[1][0])
    sums_next, keep_next, send_next = qkv_term(
        after(place, own_ff[0]), normed, *grad_qkv[1]
    )
    sums_qkv = [sums_first, sums_next]
    got_next = swap(send_next, "x")
    held = after(((keep, got), (keep_first, got_first)), sums_next)
    folded.append(jnp.concatenate([fold(*one) for one in held], axis=1))
    scattered.append(scatter_z(folded[2]))
    share, *given = qkv_back(after(place, folded[2]), grad_qkv, [pieces_first, pieces_next])
    pairs = [with_core(own_ff[0])]
    scattered[1] = after(scattered[1], share)
    own_ff.append(sum_y(scattered[1]))
    sums_in, input_grad = norm_back(
        after(place, scattered[1]),
        rows_own,
        vectors,
        GAIN_ONE,
        share,
        [swap(one, "c") for one in given],
        grad_mid,
        tokens,
    )
    packed = pack_terms(
        place, sums_mid, sums_in, sums_qkv, hidden_sums, down_sums, sizes
    )
    folded.append(fold(*after((keep_next, got_next), packed)))
    scattered.append(scatter_z(folded[3]))
    pairs.append(with_core(after(own_ff[1], folded[3])))
    terms = sum_over(packed, ("c", "z", "x", "y"))

    weights = [in_weight, down_weight]
    states = [as_row(state) for state in (in_rows, down_rows)]
    grads_early, rows_early, pack, _, _ = statistics(
        place,
        ("in", "down"),
        pairs[:CHUNKS],
        [[(j, row, 0) for j in range(CHUNKS)] for row in (0, part)],
        weights,
        states,
        images,
        group,
    )
    scattered[2] = after(scattered[2], rows_early[0])
    own_mid = after(sum_y(scattered[2]), terms)
    pairs.append(with_core(own_mid))
    pack = sum_over(pack, ("z", "x"))
    scattered[3] = after(scattered[3], (pack, pairs[-1]))
    pairs.append(sum_y_and_core(scattered[3]))
    new_early, cols_early, clips_early, _ = update(
        after(place, scattered[3]),
        grads_early,
        rows_early,
        weights,
        [as_row(state) for state in (in_cols, down_cols)],
        pack,
        group,
    )
    weights = [out_weight, qkv_weight]
    grads_late, rows_late, pack, vector_grads, new_moments = statistics(
        after(place, clips_early),
        ("out", "qkv"),
        pairs[CHUNKS:],
        [[(0, 0, 0)], [(0, 0, out_weight.shape[1] // 2), (1, 0, 0)]],
        weights,
        [as_row(state) for state in (out_rows, qkv_rows)],
        images,
        group,
        (terms, params, moments),
    )
    new_late, cols_late, clip_factors, new_vectors = update(
        place,
        grads_late,
        rows_late,
        weights,
        [as_row(state) for state in (out_cols, qkv_cols)],
        sum_over(pack, ("z", "x")),
        group,
        (vector_grads, new_moments, params),
        clips_early,
    )

    flat = lambda value: value.reshape(-1)
    grads = [None] * 12
    new_params = [None] * 12
    for number, slot in ((8, 0), (10, 1)):
        grads[number], new_params[number] = grads_early[slot], new_early[slot]
    for number, slot in ((4, 0), (2, 1)):
        grads[number], new_params[number] = grads_late[slot], new_late[slot]
    for slot, number in enumerate(VECTORS):
        grads[number] = flat(vector_grads[slot])
        new_params[number] = flat(new_vectors[slot])
    return (
        output,
        input_grad,
        *grads,
        flat(rows_late[1]),
        flat(cols_late[1]),
        flat(rows_late[0]),
        flat(cols_late[0]),
        flat(rows_early[0]),
        flat(cols_early[0]),
        flat(rows_early[1]),
        flat(cols_early[1]),
        *[flat(moment) for moment in new_moments],
        *new_params,
        flat(clip_factors),
    )


def solution(mesh):
    group = mesh.shape["fsdp"]
    split = Mesh(mesh.devices.reshape(group // 2, 2, mesh.shape["dp"] // 2, 2), ALL_AXES)
    in_specs = (
        P(("z", "x", "y", "c"), None),
        P(("z", "x", "y", "c"), None),
        P(("z", "x")),
        P(("z", "x")),
        P(("z", "x"), None),
        P(("z", "x")),
        P(("z", "x"), None),
        P(("z", "x")),
        P(("z", "x")),
        P(("z", "x")),
        P(("z", "x"), None),
        P(("z", "x")),
        P(("z", "x"), None),
        P(("z", "x")),
        P(("z", "x")),
        P(),
        P(("z", "x")),
        P(),
        P(("z", "x")),
        P(),
        P(("z", "x")),
        P(),
        P(("z", "x")),
        P(("z", "x")),
        P(("z", "x")),
        P(("z", "x")),
        P(("z", "x")),
        P(("z", "x")),
        P(("z", "x")),
        P(("z", "x")),
    )
    out_specs = (
        P(("z", "x", "y", "c"), None),
        P(("z", "x", "y", "c"), None),
        P(("z", "x")),
        P(("z", "x")),
        P(("z", "x"), None),
        P(("z", "x")),
        P(("z", "x"), None),
        P(("z", "x")),
        P(("z", "x")),
        P(("z", "x")),
        P(("z", "x"), None),
        P(("z", "x")),
        P(("z", "x"), None),
        P(("z", "x")),
        P(("z", "x")),
        P(),
        P(("z", "x")),
        P(),
        P(("z", "x")),
        P(),
        P(("z", "x")),
        P(),
        P(("z", "x")),
        P(("z", "x")),
        P(("z", "x")),
        P(("z", "x")),
        P(("z", "x")),
        P(("z", "x")),
        P(("z", "x")),
        P(("z", "x")),
        P(("z", "x")),
        P(("z", "x")),
        P(("z", "x"), None),
        P(("z", "x")),
        P(("z", "x"), None),
        P(("z", "x")),
        P(("z", "x")),
        P(("z", "x")),
        P(("z", "x"), None),
        P(("z", "x")),
        P(("z", "x"), None),
        P(("z", "x")),
        P(),
    )
    return jax.shard_map(
        on_device, mesh=split, in_specs=in_specs, out_specs=out_specs, check_vma=False
    )
```

```python
import math

import jax
import jax.numpy as jnp
from jax import lax
from jax.experimental import pallas as pl
from jax.experimental.pallas import tpu as pltpu
from jax.sharding import Mesh
from jax.sharding import PartitionSpec as P

HEAD_DIM = 64
SEQ = 577
LANES = 128
TILE = 16
CHUNKS = 2
GROUPS = 2
GIVEN = 2
VMEM_LIMIT = 60
VMEM_LIMITS = {
    "attention": 30,
    "attention_back": 30,
    "gather_out": 30,
    "norm_back": 30,
    "out_back": 40,
    "pack_terms": 30,
    "project_next": 40,
    "qkv_term": 30,
}

ALL_AXES = ("z", "x", "y", "c")

MATRICES = (2, 4, 8, 10)
VECTORS = (0, 1, 3, 5, 6, 7, 9, 11)

ln_eps = 1e-06
clip_level = 0.05
step_rate = 4.0


def swap(value, axis):
    return lax.ppermute(value, axis, [(0, 1), (1, 0)])


def shift(value, axis, step):
    size = lax.axis_size(axis)
    return lax.ppermute(value, axis, [(i, (i + step) % size) for i in range(size)])


def partner(value, axis, step):
    size = lax.axis_size(axis)
    return lax.ppermute(value, axis, [(i, i ^ step) for i in range(size)])


def sum_over(value, axes):
    for axis in axes:
        if lax.axis_size(axis) == 4:
            got = [shift(value, axis, step) for step in (1, 2, 3)]
            value = (value + got[1]) + (got[0] + got[2])
            continue
        step = 1
        while step < lax.axis_size(axis):
            value = value + partner(value, axis, step)
            step *= 2
    return value


def along_z(shard):
    near = lax.all_gather(shard, "z", axis=0, tiled=True)
    return near.reshape(lax.axis_size("z"), *shard.shape)


def by_x(near):
    return [[near], [swap(near, "x")]]


def by_y_too(pieces, by_y):
    return [[one, swap(one, "y")] if by_y else [one] for (one,) in pieces]


def after(values, token):
    return lax.optimization_barrier((values, token))[0]


def fold(keep, got):
    total = low(wide(keep) + wide(got))
    return total.reshape(-1, total.shape[-1])


def fold_pair(keep_one, got_one, keep_two, got_two):
    both = [low(wide(keep_one) + wide(got_one)), low(wide(keep_two) + wide(got_two))]
    total = jnp.concatenate(both, axis=1)
    return total.reshape(-1, total.shape[-1])


def scatter_z(total):
    return lax.psum_scatter(total, "z", scatter_dimension=0, tiled=True)


def sum_y(mine):
    if lax.axis_size("y") == 2:
        return [mine, swap(mine, "y")]
    return [lax.psum(wide(mine), "y")]


def with_core(own):
    return own, [swap(one, "c") for one in own]


def sum_y_and_core(mine):
    if lax.axis_size("y") != 2:
        return with_core(sum_y(mine))
    across = lax.ppermute(mine, ("y", "c"), [(i, 3 - i) for i in range(4)])
    return [mine, swap(mine, "y")], [swap(mine, "c"), across]


def row_pad(length):
    return -(-length // LANES) * LANES


def dot(left, right):
    return jnp.dot(left, right, preferred_element_type=jnp.float32)


def dot_tail(left, right):
    return lax.dot_general(
        left, right, (((1,), (1,)), ((), ())), preferred_element_type=jnp.float32
    )


def low(value):
    return value.astype(jnp.bfloat16)


def wide(value):
    return value.astype(jnp.float32)


def any_spec():
    return pl.BlockSpec(memory_space=pl.ANY)


def whole(shape):
    return pl.BlockSpec(shape, lambda *_: (0,) * len(shape))


def sds(shape, dtype):
    return jax.ShapeDtypeStruct(shape, dtype)


def call(body, place, ins, in_specs, outs, out_specs, scratch, name, grid=(1,)):
    return pl.pallas_call(
        body,
        out_shape=outs,
        grid_spec=pltpu.PrefetchScalarGridSpec(
            num_scalar_prefetch=1,
            grid=grid,
            in_specs=in_specs,
            out_specs=out_specs,
            scratch_shapes=scratch,
        ),
        compiler_params=pltpu.CompilerParams(
            vmem_limit_bytes=VMEM_LIMITS.get(name, VMEM_LIMIT) * 1024 * 1024, dimension_semantics=("arbitrary",) * len(grid)
        ),
        name=name,
    )(place, *ins)


def shard_number(place_ref, z, dx):
    return z * 2 + dx + (1 - 2 * dx) * place_ref[1]


def normalised(rows):
    centre = rows - jnp.mean(rows, axis=-1, keepdims=True)
    spread = jnp.mean(centre * centre, axis=-1, keepdims=True)
    return centre * lax.rsqrt(spread + ln_eps)


def select(core, first, second):
    return jnp.where(core == 0, first, second)


def prepare_qkv(place, weight, out_weight, vectors, cut):
    part, cols = weight.shape
    half = cols // 6
    heads = half // GROUPS
    width = 3 * heads
    sizes = [vector.shape[-1] for vector in vectors]
    tiles = -(-sum(sizes) // width)

    out_half = out_weight.shape[1] // 2

    def body(place_ref, weight_ref, out_ref, *refs):
        refs, groups = refs[: len(sizes)], refs[len(sizes) :]
        core = place_ref[2]

        def of_y(rows):
            if cut == 1:
                return low(rows)
            return low(select(place_ref[3], rows[: part // 2], rows[part // 2 :]))

        for number, ref in enumerate(groups):
            for slot in range(3):
                at = 2 * slot * half + number * heads
                cols_of = select(
                    core,
                    weight_ref[:, at : at + heads],
                    weight_ref[:, at + half : at + half + heads],
                )
                lanes = slice(slot * heads, (slot + 1) * heads)
                if number == GROUPS - 1:
                    ref[:, lanes] = of_y(cols_of)
                else:
                    ref[:part, lanes] = low(cols_of)
        groups[-1][:, width:] = of_y(select(core, out_ref[:, :out_half], out_ref[:, out_half:]))
        at = 0
        for ref, size in zip(refs, sizes):
            done = 0
            while done < size:
                tile, lane = divmod(at + done, width)
                count = min(size - done, width - lane)
                row = part + tile * TILE
                groups[0][row : row + TILE, lane : lane + count] = low(
                    jnp.broadcast_to(ref[:, done : done + count], (TILE, count))
                )
                done += count
            at += size

    shapes = [
        (part + (tiles * TILE if g == 0 else 0), width) if g < GROUPS - 1 else (part // cut, width + out_half)
        for g in range(GROUPS)
    ]
    return call(
        body,
        place,
        (weight, out_weight, *vectors),
        [whole((part, cols)), whole(out_weight.shape)] + [whole((1, size)) for size in sizes],
        [sds(shape, jnp.bfloat16) for shape in shapes],
        [whole(shape) for shape in shapes],
        [],
        "prepare_qkv",
    )


def pad_rows(place, rows):
    tokens, width = rows.shape
    length = row_pad(tokens)
    even = tokens // TILE * TILE
    cols = width // GIVEN

    def body(place_ref, ref, to, *parts):
        row = lax.broadcasted_iota(jnp.int32, (length - even, width), 0)
        last = jnp.zeros((length - even, width), jnp.float32)
        for extra in range(tokens - even):
            one = wide(ref[even + extra : even + extra + 1, :])
            last = jnp.where(row == extra, one, last)
        to[:even, :] = ref[:even, :]
        to[even:, :] = low(last)
        for number, part in enumerate(parts):
            lanes = slice(number * cols, (number + 1) * cols)
            part[...] = to[:, lanes]

    shapes = [(length, width)] + [(length, cols)] * GIVEN
    whole_rows, *parts = call(
        body,
        place,
        (rows,),
        [whole(rows.shape)],
        [sds(shape, jnp.bfloat16) for shape in shapes],
        [whole(shape) for shape in shapes],
        [],
        "pad_rows",
    )
    return whole_rows, parts


def joined(refs, rows=slice(None)):
    return jnp.concatenate([ref[rows, :] for ref in refs], axis=1)


def prepare_rest(place, in_weight, down_weight, cotangent, cuts):
    part, hidden = in_weight.shape
    width = down_weight.shape[1]
    per_core = down_weight.shape[0] // 2
    per_shard = per_core // CHUNKS
    shards = hidden // (2 * per_core)
    def body(place_ref, in_ref, down_ref, cot_ref, *refs):
        pieces, (sum_ref,) = refs[:CHUNKS], refs[CHUNKS:]
        core, y = place_ref[2], place_ref[3]

        def pick(ref, row, count, step, col, cols, by_row, cut):
            def of_core(r):
                if by_row:
                    return select(
                        core, ref[r : r + count, col : col + cols], ref[r + step : r + step + count, col : col + cols]
                    )
                return select(
                    core, ref[r : r + count, col : col + cols], ref[r : r + count, col + step : col + step + cols]
                )

            if cut == 1:
                return low(of_core(row))
            return low(select(y, of_core(row), of_core(row + count)))

        for j, cut in enumerate(cuts):
            rows_in, rows_down = part // cut, per_shard // cut
            for s in range(shards):
                at = s * 2 * per_core + j * per_shard
                pieces[j][:rows_in, s * per_shard : (s + 1) * per_shard] = pick(
                    in_ref, 0, rows_in, per_core, at, per_shard, False, cut
                )
            pieces[j][rows_in:, :] = pick(
                down_ref, j * per_shard, rows_down, per_core, 0, width, True, cut
            )
        sum_ref[...] = jnp.sum(wide(cot_ref[...]), axis=0, keepdims=True)

    outs = [sds(((part + per_shard) // cut, width), jnp.bfloat16) for cut in cuts]
    outs += [sds((1, width), jnp.float32)]
    ins = (in_weight, down_weight, cotangent)
    return call(
        body,
        place,
        ins,
        [whole(a.shape) for a in ins],
        outs,
        [whole(a.shape) for a in outs],
        [],
        "prepare_rest",
    )


GAIN_ONE, BIAS_ONE, BIAS_OUT, GAIN_TWO, BIAS_TWO, BIAS_DOWN, BIAS_QV = range(7)


def row_copies(place_ref, ins, to, part, lanes, sem):
    cut = len(ins) // 2
    rows = part // cut
    made = []
    for number, ref in enumerate(ins):
        dx, h = number // cut, number % cut
        y = h + (1 - 2 * h) * place_ref[3] if cut == 2 else 0
        for z in range(ref.shape[0]):
            row = pl.multiple_of(shard_number(place_ref, z, dx) * part + y * rows, rows)
            made.append(
                pltpu.make_async_copy(
                    ref.at[z, pl.ds(0, rows), lanes], to.at[pl.ds(row, rows), :], sem.at[len(made)]
                )
            )
    return made


def weight_copies(place_ref, ins, weight, part, sem):
    return row_copies(place_ref, ins, weight, part, pl.ds(0, weight.shape[1]), sem)


def write_qkv(normed, weight, bias_q, bias_v, image, q_ref, k_ref, v_ref):
    heads = weight.shape[1] // 3
    query = low(dot(normed, weight[:, :heads]) + bias_q)
    q_ref[image] = low(wide(query) * (1.0 / math.sqrt(HEAD_DIM)))
    k_ref[image] = low(dot(normed, weight[:, heads : 2 * heads]))
    v_ref[image] = low(dot(normed, weight[:, 2 * heads :]) + bias_v)


def project_first(place, rows, pieces, sizes):
    flat = [one for (one,) in pieces]
    z_size, part, cols = flat[0].shape
    rows_own, rows_other = rows
    length, width = rows_own.shape
    count = 2 * z_size
    tiles = (part - width // count) // TILE
    part = width // count
    heads = cols // 3
    half = heads * GROUPS
    starts = [sum(sizes[:number]) for number in range(len(sizes))]
    per_shard = sizes[6] // 2 // CHUNKS
    blocks = count // 2

    def body(place_ref, own_ref, *refs):
        other_refs, refs = refs[:GIVEN], refs[GIVEN:]
        ins, refs = refs[:2], refs[2:]
        normed_ref, q_ref, k_ref, v_ref, vec_ref, hidden_bias_ref, weight, packed, sem = refs
        core = place_ref[2]
        copies = []
        for dx, ref in enumerate(ins):
            for z in range(z_size):
                copies.append(
                    pltpu.make_async_copy(
                        ref.at[z, pl.ds(part, tiles * TILE), :],
                        packed.at[shard_number(place_ref, z, dx)],
                        sem.at[count + len(copies)],
                    )
                )
        copies += weight_copies(place_ref, ins, weight, part, sem)
        for copy in copies:
            copy.start()
        for copy in copies:
            copy.wait()

        def lanes(s, at, size):
            found = []
            done = 0
            while done < size:
                tile, lane = divmod(at + done, cols)
                take = min(size - done, cols - lane)
                found.append(wide(packed[s, tile * TILE : tile * TILE + 1, lane : lane + take]))
                done += take
            return found

        def vector(slot, shards=range(count)):
            return jnp.concatenate(
                [one for s in shards for one in lanes(s, starts[slot], sizes[slot])], axis=1
            )

        gain, bias = vector(0), vector(1)
        bias_q = vector(2, range(blocks))
        bias_v = vector(2, range(blocks, count))
        bias_q = select(core, bias_q[:, :half], bias_q[:, half:])
        bias_v = select(core, bias_v[:, :half], bias_v[:, half:])
        for row, value in (
            (GAIN_ONE, gain),
            (BIAS_ONE, bias),
            (BIAS_OUT, vector(3)),
            (GAIN_TWO, vector(4)),
            (BIAS_TWO, vector(5)),
            (BIAS_DOWN, vector(7)),
            (BIAS_QV, jnp.concatenate([bias_q, bias_v], axis=1)),
        ):
            vec_ref[row : row + 1, :] = value
        vec_ref[7:8, :] = jnp.zeros((1, width), jnp.float32)
        for j in range(CHUNKS):
            for s in range(count):
                at = starts[6] + j * per_shard
                to = at + sizes[6] // 2
                hidden_bias_ref[j, :, s * per_shard : (s + 1) * per_shard] = select(
                    core,
                    jnp.concatenate(lanes(s, at, per_shard), axis=1),
                    jnp.concatenate(lanes(s, to, per_shard), axis=1),
                )
        for image, part_refs in enumerate(((own_ref,), other_refs)):
            for at in range(0, length, LANES):
                block = wide(joined(part_refs, slice(at, at + LANES)))
                normed_ref[image, at : at + LANES, :] = low(normalised(block) * gain + bias)

        def one_image(image, carry):
            write_qkv(
                normed_ref[image],
                weight,
                bias_q[:, :heads],
                bias_v[:, :heads],
                image,
                q_ref,
                k_ref,
                v_ref,
            )
            return carry

        lax.fori_loop(0, 2, one_image, 0)

    part_out = sds((2, length, heads), jnp.bfloat16)
    return call(
        body,
        place,
        (rows_own, *rows_other, *flat),
        [whole((length, width))]
        + [whole((length, width // GIVEN))] * GIVEN
        + [any_spec()] * 2,
        [sds((2, length, width), jnp.bfloat16)]
        + [part_out] * 3
        + [
            sds((8, width), jnp.float32),
            sds((CHUNKS, 1, count * per_shard), jnp.float32),
        ],
        [whole((2, length, width))]
        + [whole((2, length, heads))] * 3
        + [whole((8, width)), whole((CHUNKS, 1, count * per_shard))],
        [
            pltpu.VMEM((width, cols), jnp.bfloat16),
            pltpu.VMEM((count, tiles * TILE, cols), jnp.bfloat16),
            pltpu.SemaphoreType.DMA((2 * count,)),
        ],
        "project_first",
    )


def project_next(place, normed, vectors, pieces, group):
    flat = [one for side in pieces for one in side]
    z_size = flat[0].shape[0]
    _, length, width = normed.shape
    part = width // (2 * z_size)
    half = width // 2
    heads = half // GROUPS
    cols = 3 * heads

    def body(place_ref, normed_ref, vec_ref, *refs):
        ins, (q_ref, k_ref, v_ref, weight, sem) = refs[: len(flat)], refs[len(flat) :]
        copies = weight_copies(place_ref, ins, weight, part, sem)
        for copy in copies:
            copy.start()
        for copy in copies:
            copy.wait()
        at = group * heads
        bias_q = vec_ref[BIAS_QV : BIAS_QV + 1, at : at + heads]
        bias_v = vec_ref[BIAS_QV : BIAS_QV + 1, half + at : half + at + heads]

        def one_image(image, carry):
            write_qkv(normed_ref[image], weight, bias_q, bias_v, image, q_ref, k_ref, v_ref)
            return carry

        lax.fori_loop(0, 2, one_image, 0)

    return call(
        body,
        place,
        (normed, vectors, *flat),
        [whole(normed.shape), whole(vectors.shape)] + [any_spec()] * len(flat),
        [sds((2, length, heads), jnp.bfloat16)] * 3,
        [whole((2, length, heads))] * 3,
        [pltpu.VMEM((width, cols), jnp.bfloat16), pltpu.SemaphoreType.DMA((len(flat) * z_size,))],
        "project_next",
    )


def gather_out(place, pieces, first):
    flat = [one for side in pieces for one in side]
    z_size, rows, total = flat[0].shape
    half = total - first
    part = rows * len(flat) // 2

    def body(place_ref, *refs):
        ins, (out_ref, sem) = refs[: len(flat)], refs[len(flat) :]
        copies = row_copies(place_ref, ins, out_ref, part, pl.ds(first, half), sem)
        for copy in copies:
            copy.start()
        for copy in copies:
            copy.wait()

    shape = (2 * z_size * part, half)
    return call(
        body,
        place,
        tuple(flat),
        [any_spec()] * len(flat),
        [sds(shape, jnp.bfloat16)],
        [whole(shape)],
        [pltpu.SemaphoreType.DMA((len(flat) * z_size,))],
        "gather_out",
    )[0]


def attention(place, query, keys, values):
    _, length, heads = query.shape
    pairs = heads // LANES

    def body(place_ref, q_ref, k_ref, v_ref, out_ref, probs_ref):
        lane = lax.broadcasted_iota(jnp.int32, (length, LANES), 1)
        keys_block = k_ref[0]
        values_t = v_ref[0].T
        query_block = q_ref[0]
        key_row = lax.broadcasted_iota(jnp.int32, (length, length), 0)
        scores = []
        for head in range(2):
            inside = (lane >= head * HEAD_DIM) & (lane < (head + 1) * HEAD_DIM)
            query_head = jnp.where(inside, query_block, jnp.zeros_like(query_block))
            scores.append(jnp.where(key_row < SEQ, dot_tail(keys_block, query_head), -1e30))
        mixed = []
        for head in range(2):
            highest = jnp.max(scores[head], axis=0, keepdims=True)
            exponent = jnp.exp(scores[head] - highest)
            summed = jnp.sum(exponent, axis=0, keepdims=True)
            probs = low(exponent * (1.0 / summed))
            probs_ref[0, 0, head] = probs
            mixed.append(dot(values_t[head * HEAD_DIM : (head + 1) * HEAD_DIM, :], probs))
        out_ref[0] = low(jnp.concatenate(mixed, axis=0).T)

    block = pl.BlockSpec((1, length, LANES), lambda i, j, p: (i, 0, j))
    return call(
        body,
        place,
        (query, keys, values),
        [block] * 3,
        [
            sds((2, length, heads), jnp.bfloat16),
            sds((2, pairs, 2, length, length), jnp.bfloat16),
        ],
        [block, pl.BlockSpec((1, 1, 2, length, length), lambda i, j, p: (i, j, 0, 0, 0))],
        [],
        "attention",
        grid=(2, pairs),
    )


def attention_back(place, query, keys, values, probs, grad):
    _, length, heads = query.shape
    pairs = heads // LANES
    scale = 1.0 / math.sqrt(HEAD_DIM)

    def body(place_ref, q_ref, k_ref, v_ref, p_ref, g_ref, gq_ref, gk_ref, gv_ref):
        lane = lax.broadcasted_iota(jnp.int32, (length, LANES), 1)
        keys_t = k_ref[0].T
        values_block = v_ref[0]
        query_block = q_ref[0]
        grad_block = g_ref[0]
        grad_query = []
        grad_keys = []
        grad_values = []
        for head in range(2):
            inside = (lane >= head * HEAD_DIM) & (lane < (head + 1) * HEAD_DIM)
            grad_head = jnp.where(inside, grad_block, jnp.zeros_like(grad_block))
            probs_low = p_ref[0, 0, head]
            probs_wide = wide(probs_low)
            grad_probs = dot_tail(values_block, grad_head)
            inner = jnp.sum(probs_wide * grad_probs, axis=0, keepdims=True)
            grad_scores = low(probs_wide * (grad_probs - inner))
            keys_head = keys_t[head * HEAD_DIM : (head + 1) * HEAD_DIM, :]
            grad_query.append(dot(keys_head, grad_scores))
            grad_keys.append(dot(grad_scores, query_block))
            grad_values.append(dot(probs_low, grad_block))
        first = lane < HEAD_DIM
        gq_ref[0] = low(jnp.concatenate(grad_query, axis=0).T * scale)
        gk_ref[0] = low(jnp.where(first, grad_keys[0], grad_keys[1]))
        gv_ref[0] = low(jnp.where(first, grad_values[0], grad_values[1]))

    block = pl.BlockSpec((1, length, LANES), lambda i, j, p: (i, 0, j))
    return call(
        body,
        place,
        (query, keys, values, probs, grad),
        [block] * 3
        + [pl.BlockSpec((1, 1, 2, length, length), lambda i, j, p: (i, j, 0, 0, 0)), block],
        [sds((2, length, heads), jnp.bfloat16)] * 3,
        [block] * 3,
        [],
        "attention_back",
        grid=(2, pairs),
    )


def head_rows(core, heads, group):
    mine = pl.multiple_of((core * GROUPS + group) * heads, heads)
    return mine, pl.multiple_of(((1 - core) * GROUPS + group) * heads, heads)


def project_out(place, mine, theirs, weight_mine, weight_theirs, rows, vectors):
    width, half = weight_mine.shape
    _, length, heads = mine[0].shape

    def body(place_ref, *refs):
        mine_refs, theirs_refs, refs = refs[:GROUPS], refs[GROUPS : 2 * GROUPS], refs[2 * GROUPS :]
        wm_ref, wt_ref, own_ref, *other_refs, vec_ref, middle_ref, normed_ref, total = refs
        core = place_ref[2]
        for image, part_refs in enumerate(((own_ref,), other_refs)):
            for slot, weight in enumerate((wm_ref, wt_ref)):
                branch = None
                for g in range(GROUPS):
                    at_mine, at_theirs = head_rows(core, heads, g)
                    add = dot(mine_refs[g][image], weight[pl.ds(at_mine, heads), :]) + dot(
                        theirs_refs[g][1 - image], weight[pl.ds(at_theirs, heads), :]
                    )
                    branch = add if branch is None else branch + add
                total[slot] = branch
            for at in range(0, length, LANES):
                upto = at + LANES
                first, second = total[0, at:upto, :], total[1, at:upto, :]
                left = select(core, first, second)
                right = select(core, second, first)
                middle = (
                    wide(joined(part_refs, slice(at, upto)))
                    + jnp.concatenate([left, right], axis=1)
                    + vec_ref[BIAS_OUT : BIAS_OUT + 1, :]
                )
                if image == 0:
                    middle_ref[at:upto, :] = middle
                normed_ref[image, at:upto, :] = low(
                    normalised(middle) * vec_ref[GAIN_TWO : GAIN_TWO + 1, :]
                    + vec_ref[BIAS_TWO : BIAS_TWO + 1, :]
                )

    return call(
        body,
        place,
        (*mine, *theirs, weight_mine, weight_theirs, rows[0], *rows[1], vectors),
        [whole((2, length, heads))] * (2 * GROUPS)
        + [whole((width, half))] * 2
        + [whole((length, width))]
        + [whole((length, width // GIVEN))] * GIVEN
        + [whole(vectors.shape)],
        [sds((length, width), jnp.float32), sds((2, length, width), jnp.bfloat16)],
        [whole((length, width)), whole((2, length, width))],
        [pltpu.VMEM((2, length, half), jnp.float32)],
        "project_out",
    )


def feed_forward(place, normed, cotangent, pieces, bias, chunk, running):
    cut = len(pieces[0])
    z_size, _, width = pieces[0][0].shape
    hidden_width = bias.shape[2]
    part = width // (2 * z_size)
    per_shard = hidden_width // (2 * z_size)
    rows_in, rows_down = part // cut, per_shard // cut
    _, length, _ = normed.shape
    first_call = running is None
    last_call = chunk == CHUNKS - 1
    given = GIVEN if last_call else 1

    def body(place_ref, normed_ref, own_cot, *refs):
        other_cots, (bias_ref, *refs) = refs[:GIVEN], refs[GIVEN:]
        ins, refs = refs[: 2 * cut], refs[2 * cut :]
        if not first_call:
            before, refs = refs[:4], refs[4:]
        out_own, *out_other = refs[: 1 + given]
        gn_own, *gn_other = refs[1 + given : 2 + 2 * given]
        bsum_ref, *refs = refs[2 + 2 * given :]
        term_refs, refs = refs[:4], refs[4:]
        w_in, w_down, cots, into, down, grads, sem, out_sem = refs
        copies = []
        for weight, at, rows, of_shard in (
            (w_in, 0, rows_in, part),
            (w_down, rows_in, rows_down, per_shard),
        ):
            for number, ref in enumerate(ins):
                dx, h = number // cut, number % cut
                y = h + (1 - 2 * h) * place_ref[3] if cut == 2 else 0
                for z in range(z_size):
                    s = shard_number(place_ref, z, dx)
                    row = pl.multiple_of(s * of_shard + y * rows, rows)
                    copy = pltpu.make_async_copy(
                        ref.at[z, pl.ds(at, rows), :],
                        weight.at[pl.ds(row, rows), :],
                        sem.at[len(copies)],
                    )
                    copy.start()
                    copies.append(copy)
        for copy in copies:
            copy.wait()
        cots[0] = own_cot[...]
        cots[1] = joined(other_cots)

        def one_image(image, carry):
            first = image == 0
            normed_rows = normed_ref[image]
            preact = dot(normed_rows, w_in[...]) + bias_ref[0]
            phi = 0.5 * (1.0 + lax.erf(preact * math.sqrt(0.5)))
            density = jnp.exp(-0.5 * preact * preact) * (1.0 / math.sqrt(2.0 * math.pi))
            hidden = low(preact * phi)
            slope = phi + preact * density
            cot = cots[image]
            grad = low(dot_tail(cot, w_down[...]) * slope)
            to_out = dot(hidden, w_down[...])
            to_normed = dot_tail(grad, w_in[...])
            for slot, to_refs in enumerate((([out_own], [gn_own]), (out_other, gn_other))):

                @pl.when(image == slot)
                def _():
                    for number, (refs_of, value) in enumerate(zip(to_refs, (to_out, to_normed))):
                        if not first_call:
                            value = before[2 * number + slot][...] + value
                        cols = width // len(refs_of)
                        for at, ref in enumerate(refs_of):
                            ref[...] = value[:, at * cols : (at + 1) * cols].astype(ref.dtype)

            partial = jnp.sum(wide(grad), axis=0, keepdims=True)
            to_in = dot(normed_rows.T, grad)
            to_down = dot(hidden.T, cot)

            @pl.when(first)
            def _():
                bsum_ref[...] = partial
                into[...] = to_in
                down[...] = to_down

            @pl.when(jnp.logical_not(first))
            def _():
                bsum_ref[...] += partial
                for slot, (held, value, rows) in enumerate(
                    ((into, to_in, part), (down, to_down, per_shard))
                ):
                    whole_term = low(held[...] + value)
                    for z in range(z_size):
                        for x in range(2):
                            dx = x + (1 - 2 * x) * place_ref[1]
                            s = z * 2 + x
                            grads[slot, dx, z] = whole_term[s * rows : (s + 1) * rows, :]

            return carry

        lax.fori_loop(0, 2, one_image, 0)
        copies = [
            pltpu.make_async_copy(grads.at[number // 2, number % 2], ref, out_sem.at[number])
            for number, ref in enumerate(term_refs)
        ]
        for copy in copies:
            copy.start()
        for copy in copies:
            copy.wait()

    total = sds((length, width), jnp.float32)
    other = sds((length, width // given), jnp.bfloat16 if last_call else jnp.float32)
    totals = ([total] + [other] * given) * 2
    if part != per_shard:
        raise ValueError
    piece_out = sds((z_size, part, width), jnp.bfloat16)
    carried = () if first_call else tuple(running)
    return call(
        body,
        place,
        (normed, cotangent[0], *cotangent[1], bias, *[one for side in pieces for one in side], *carried),
        [whole((2, length, width)), whole((length, width))]
        + [whole((length, width // GIVEN))] * GIVEN
        + [pl.BlockSpec((1, 1, hidden_width), lambda i, p: (chunk, 0, 0))]
        + [any_spec()] * (2 * cut)
        + [whole((length, width))] * len(carried),
        totals + [sds((1, hidden_width), jnp.float32)] + [piece_out] * 4,
        [whole(a.shape) for a in totals] + [whole((1, hidden_width))] + [any_spec()] * 4,
        [
            pltpu.VMEM((width, hidden_width), jnp.bfloat16),
            pltpu.VMEM((hidden_width, width), jnp.bfloat16),
            pltpu.VMEM((2, length, width), jnp.bfloat16),
            pltpu.VMEM((width, hidden_width), jnp.float32),
            pltpu.VMEM((hidden_width, width), jnp.float32),
            pltpu.VMEM((2, 2, z_size, part, width), jnp.bfloat16),
            pltpu.SemaphoreType.DMA((4 * cut * z_size,)),
            pltpu.SemaphoreType.DMA((4,)),
        ],
        "feed_forward",
    )


def norm_back(place, rows, vectors, gain_row, grad_own, others, passed, tokens, finish=()):
    length, width = rows.shape

    def body(place_ref, rows_ref, vec_ref, own_ref, pass_ref, *refs):
        other_refs, refs = refs[: len(others)], refs[len(others) :]
        step = pl.program_id(0)
        values = wide(rows_ref[...])
        if finish:
            first_ref, second_refs, refs = refs[0], refs[1 : len(finish)], refs[len(finish) :]
            refs[1][...] = low(
                values
                + first_ref[...]
                + wide(joined(second_refs))
                + vec_ref[BIAS_DOWN : BIAS_DOWN + 1, :]
            )
        sum_ref = refs[0]
        centre = values - jnp.mean(values, axis=-1, keepdims=True)
        spread = jnp.mean(centre * centre, axis=-1, keepdims=True)
        inverse = lax.rsqrt(spread + ln_eps)
        unit = centre * inverse
        grad = own_ref[...] + wide(joined(other_refs))
        scaled = grad * vec_ref[gain_row : gain_row + 1, :]
        mean_one = jnp.mean(scaled, axis=-1, keepdims=True)
        mean_two = jnp.mean(scaled * unit, axis=-1, keepdims=True)
        result = wide(pass_ref[...]) + (scaled - mean_one - unit * mean_two) * inverse
        rounded = low(result)
        parts = [
            jnp.sum(grad * unit, axis=0, keepdims=True),
            jnp.sum(grad, axis=0, keepdims=True),
            jnp.sum(wide(rounded), axis=0, keepdims=True),
            jnp.zeros((5, width), jnp.float32),
        ]
        if not finish:
            refs[1][...] = rounded
        else:
            refs[2][...] = result
            refs[3][...] = rounded
            for number, ref in enumerate(refs[4:]):
                at = number * width // GIVEN
                ref[...] = rounded[:, at : at + width // GIVEN]
        sums = jnp.concatenate(parts, axis=0)

        @pl.when(step == 0)
        def _():
            sum_ref[...] = sums

        @pl.when(step > 0)
        def _():
            sum_ref[...] += sums

    block = pl.BlockSpec((LANES, width), lambda i, p: (i, 0))
    outs = [sds((8, width), jnp.float32), sds((tokens, width), jnp.bfloat16)]
    if finish:
        outs += [sds((length, width), jnp.float32), sds((length, width), jnp.bfloat16)]
        outs += [sds((length, width // GIVEN), jnp.bfloat16)] * GIVEN
    other_block = pl.BlockSpec((LANES, others[0].shape[1]), lambda i, p: (i, 0))
    ins = (rows, vectors, grad_own, passed, *others, *finish)
    return call(
        body,
        place,
        ins,
        [block, whole(vectors.shape), block, block]
        + [other_block] * len(others)
        + ([block] + [other_block] * len(others) if finish else []),
        outs,
        [whole((8, width))]
        + [pl.BlockSpec((LANES, a.shape[1]), lambda i, p: (i, 0)) for a in outs[1:]],
        [],
        "norm_back",
        grid=(length // LANES,),
    )


def out_back(place, grad_own, grad_others, mine, theirs, weight_mine, weight_theirs):
    width, half = weight_mine.shape
    z_size = lax.axis_size("z")
    part = width // (2 * z_size)
    _, length, heads = mine[0].shape

    def body(place_ref, own_ref, own_half, *refs):
        other_refs, refs = refs[:GIVEN], refs[GIVEN:]
        mine_refs, theirs_refs, refs = refs[:GROUPS], refs[GROUPS : 2 * GROUPS], refs[2 * GROUPS :]
        wm_ref, wt_ref, *refs = refs
        ga_refs, (keep_ref, send_ref, turned, grads, out_sem) = refs[:GROUPS], refs[GROUPS:]
        core = place_ref[2]
        for image in range(2):
            lanes = slice(image * length, (image + 1) * length)
            for g in range(GROUPS):
                at_mine, at_theirs = head_rows(core, heads, g)
                turned[pl.ds(at_mine, heads), lanes] = mine_refs[g][image].T
                turned[pl.ds(at_theirs, heads), lanes] = theirs_refs[g][1 - image].T
        other = joined(other_refs)
        other_half = select(core, other[:, :half], other[:, half:])
        term = dot(turned[:, :length], own_half[...]) + dot(turned[:, length:], other_half)
        for z in range(z_size):
            for x in range(2):
                dx = x + (1 - 2 * x) * place_ref[1]
                at = (z * 2 + x) * part
                grads[dx, z] = low(term[at : at + part, :])
        for slot, ref in enumerate((keep_ref, send_ref)):
            pltpu.make_async_copy(grads.at[slot], ref, out_sem.at[slot]).start()
        for image, value in enumerate((own_ref[...], other)):
            first, second = value[:, :half], value[:, half:]
            left = select(core, first, second)
            right = select(core, second, first)
            for g in range(GROUPS):
                at_mine, _ = head_rows(core, heads, g)
                ga_refs[g][image] = low(
                    dot_tail(left, wm_ref[pl.ds(at_mine, heads), :])
                    + dot_tail(right, wt_ref[pl.ds(at_mine, heads), :])
                )
        for slot, ref in enumerate((keep_ref, send_ref)):
            pltpu.make_async_copy(grads.at[slot], ref, out_sem.at[slot]).wait()

    half_block = pl.BlockSpec((length, half), lambda i, p: (0, p[2]))
    piece_out = sds((z_size, part, half), jnp.bfloat16)
    return call(
        body,
        place,
        (grad_own, grad_own, *grad_others, *mine, *theirs, weight_mine, weight_theirs),
        [whole((length, width)), half_block]
        + [whole((length, width // GIVEN))] * GIVEN
        + [whole((2, length, heads))] * (2 * GROUPS)
        + [whole((width, half))] * 2,
        [sds((2, length, heads), jnp.bfloat16)] * GROUPS + [piece_out] * 2,
        [whole((2, length, heads))] * GROUPS + [any_spec()] * 2,
        [
            pltpu.VMEM((width, 2 * length), jnp.bfloat16),
            pltpu.VMEM((2, z_size, part, half), jnp.bfloat16),
            pltpu.SemaphoreType.DMA((2,)),
        ],
        "out_back",
    )


def qkv_term(place, normed, grad_q, grad_k, grad_v):
    _, length, width = normed.shape
    heads = grad_q.shape[-1]
    cols = 3 * heads

    def body(place_ref, normed_ref, gq_ref, gk_ref, gv_ref, sum_ref, keep_ref, send_ref, turned, grads, sem):
        z_size = grads.shape[1]
        part = grads.shape[2]
        for image in range(2):
            turned[:, image * length : (image + 1) * length] = normed_ref[image].T
        for slot, ref in enumerate((gq_ref, gk_ref, gv_ref)):
            term = dot(turned[:, :length], ref[0]) + dot(turned[:, length:], ref[1])
            for z in range(z_size):
                for x in range(2):
                    dx = x + (1 - 2 * x) * place_ref[1]
                    at = (z * 2 + x) * part
                    grads[dx, z, :, slot * heads : (slot + 1) * heads] = low(
                        term[at : at + part, :]
                    )
            sum_ref[slot : slot + 1, :] = jnp.sum(wide(ref[0]), axis=0, keepdims=True) + jnp.sum(
                wide(ref[1]), axis=0, keepdims=True
            )
        for slot, ref in enumerate((keep_ref, send_ref)):
            pltpu.make_async_copy(grads.at[slot], ref, sem.at[slot]).start()
        for slot, ref in enumerate((keep_ref, send_ref)):
            pltpu.make_async_copy(grads.at[slot], ref, sem.at[slot]).wait()

    z_size = lax.axis_size("z")
    part = width // (2 * z_size)
    piece_out = sds((z_size, part, cols), jnp.bfloat16)
    return call(
        body,
        place,
        (normed, grad_q, grad_k, grad_v),
        [whole((2, length, width))] + [whole((2, length, heads))] * 3,
        [sds((3, heads), jnp.float32)] + [piece_out] * 2,
        [whole((3, heads))] + [any_spec()] * 2,
        [
            pltpu.VMEM((width, 2 * length), jnp.bfloat16),
            pltpu.VMEM((2, z_size, part, cols), jnp.bfloat16),
            pltpu.SemaphoreType.DMA((2,)),
        ],
        "qkv_term",
    )


def qkv_back(place, grads, pieces):
    flat = [one for piece in pieces for side in piece for one in side]
    counts = [sum(len(side) for side in piece) for piece in pieces]
    z_size, _, cols = flat[0].shape
    heads = cols // 3
    length = grads[0][0].shape[1]
    part = flat[-1].shape[1] * counts[-1] // 2
    width = 2 * z_size * part

    def body(place_ref, *refs):
        grad_refs, refs = refs[: 3 * GROUPS], refs[3 * GROUPS :]
        ins, (own_ref, *other_refs, weight, sem) = refs[: len(flat)], refs[len(flat) :]
        copies = []
        for g in range(GROUPS):
            at = sum(counts[:g])
            copies += weight_copies(
                place_ref, ins[at : at + counts[g]], weight.at[g], part, sem.at[g]
            )
        for copy in copies:
            copy.start()
        for copy in copies:
            copy.wait()

        def one_image(image, carry):
            total = None
            for g in range(GROUPS):
                for slot in range(3):
                    add = dot_tail(
                        grad_refs[3 * g + slot][image],
                        weight[g, :, slot * heads : (slot + 1) * heads],
                    )
                    total = add if total is None else total + add

            @pl.when(image == 0)
            def _():
                own_ref[...] = total

            @pl.when(image == 1)
            def _():
                for number, ref in enumerate(other_refs):
                    at = number * width // GIVEN
                    ref[...] = low(total[:, at : at + width // GIVEN])

            return carry

        lax.fori_loop(0, 2, one_image, 0)

    return call(
        body,
        place,
        (*[one for grad in grads for one in grad], *flat),
        [whole((2, length, heads))] * (3 * GROUPS) + [any_spec()] * len(flat),
        [sds((length, width), jnp.float32)] + [sds((length, width // GIVEN), jnp.bfloat16)] * GIVEN,
        [whole((length, width))] + [whole((length, width // GIVEN))] * GIVEN,
        [
            pltpu.VMEM((GROUPS, width, cols), jnp.bfloat16),
            pltpu.SemaphoreType.DMA((GROUPS, max(counts) * z_size)),
        ],
        "qkv_back",
    )


def to_column(row):
    return jnp.concatenate(
        [
            jnp.broadcast_to(row[:, at : at + LANES], (LANES, LANES)).T[:, :1]
            for at in range(0, row.shape[1], LANES)
        ],
        axis=0,
    )


def to_row(column):
    return jnp.concatenate(
        [
            jnp.broadcast_to(column[at : at + LANES, :], (LANES, LANES)).T[:1, :]
            for at in range(0, column.shape[0], LANES)
        ],
        axis=1,
    )


def statistics(place, kinds, pairs, shares, weights, states, images, group, extra=None):
    flat = [a for pair in pairs for side in pair for a in side]
    amount = len(kinds)
    vectors = 0 if extra is None else len(extra[1])

    def body(place_ref, *refs):
        core = place_ref[2]
        refs = list(refs)

        def take(n):
            taken = refs[:n]
            del refs[:n]
            return taken

        sides_of = [[take(len(side)) for side in pair] for pair in pairs]
        weight_refs, state_refs = take(amount), take(amount)
        if vectors:
            (terms_ref,) = take(1)
            param_refs, moment_refs = take(vectors), take(vectors)
        grad_refs, row_refs = take(amount), take(amount)
        (pack_ref,) = take(1)
        if vectors:
            vector_grads, new_moments = take(vectors), take(vectors)
        at_pack = 0
        for number, kind in enumerate(kinds):
            grad_ref, weight_ref = grad_refs[number], weight_refs[number]
            rows, cols = weights[number].shape
            for chunk, (number_of, row0, col0) in enumerate(shares[number]):
                sides = sides_of[number_of]

                def halves(row, row_count, col, col_count):
                    index = (
                        slice(row0 + row, row0 + row + row_count),
                        slice(col0 + col, col0 + col + col_count),
                    )
                    mine, theirs = [
                        sum([wide(ref[index]) for ref in side[1:]], wide(side[0][index]))
                        * (1.0 / images)
                        for side in sides
                    ]
                    return select(core, mine, theirs), select(core, theirs, mine)

                if kind == "in":
                    per = cols // (2 * CHUNKS * group)
                    for c, half in enumerate(halves(0, rows, 0, per * group)):
                        for s in range(group):
                            at = ((s * 2 + c) * CHUNKS + chunk) * per
                            grad_ref[:, at : at + per] = half[:, s * per : (s + 1) * per]
                elif kind == "down":
                    per = rows // (2 * CHUNKS)
                    for c, half in enumerate(halves(0, per, 0, cols)):
                        at = (c * CHUNKS + chunk) * per
                        grad_ref[at : at + per, :] = half
                else:
                    amount_of = len(shares[number])
                    lanes_of = cols // (2 * SPLIT[kind] * amount_of)
                    for slot in range(SPLIT[kind]):
                        for c, half in enumerate(halves(0, rows, slot * lanes_of, lanes_of)):
                            at = ((2 * slot + c) * amount_of + chunk) * lanes_of
                            grad_ref[:, at : at + lanes_of] = half
            squared = grad_ref[...] * grad_ref[...]
            new_rows = 0.5 * to_column(state_refs[number][...]) + 0.5 * jnp.mean(
                squared, axis=1, keepdims=True
            )
            row_refs[number][...] = to_row(new_rows)
            pack_ref[0:1, at_pack : at_pack + cols] = jnp.sum(squared, axis=0, keepdims=True)
            pack_ref[1:2, at_pack : at_pack + cols] = jnp.sum(
                squared * (1.0 / new_rows), axis=0, keepdims=True
            )
            at_pack += cols
            weight = weight_ref[...]
            pack_ref[0:1, at_pack : at_pack + LANES] = jnp.broadcast_to(
                jnp.sum(new_rows, axis=0, keepdims=True), (1, LANES)
            )
            pack_ref[1:2, at_pack : at_pack + LANES] = jnp.broadcast_to(
                jnp.sum(jnp.sum(weight * weight, axis=0, keepdims=True), axis=1, keepdims=True),
                (1, LANES),
            )
            at_pack += LANES
        at = 0
        if vectors:
            place_row = lax.broadcasted_iota(jnp.int32, extra[0].shape, 0)
            here = place_row == place_ref[0] * 2 + place_ref[1]
            mine = jnp.sum(
                jnp.where(here, terms_ref[...], 0.0), axis=0, keepdims=True
            )
        for number in range(vectors):
            size = extra[1][number].shape[1]
            grad = mine[:, at : at + size] * (1.0 / images)
            at += size
            param = param_refs[number][...]
            moment = 0.5 * moment_refs[number][...] + 0.5 * grad * grad
            direction = grad * lax.rsqrt(moment)
            vector_grads[number][...] = grad
            new_moments[number][...] = moment
            for row, value in enumerate((direction, param)):
                pack_ref[row : row + 1, at_pack : at_pack + LANES] = jnp.broadcast_to(
                    jnp.sum(value * value, axis=1, keepdims=True), (1, LANES)
                )
            at_pack += LANES

    lanes = sum(weight.shape[1] + LANES for weight in weights) + vectors * LANES
    ins = [*flat, *weights, *states]
    outs = [sds(weight.shape, jnp.float32) for weight in weights]
    outs += [sds(state.shape, jnp.float32) for state in states]
    outs.append(sds((2, lanes), jnp.float32))
    if vectors:
        terms, params, moments = extra
        ins += [terms, *params, *moments]
        outs += [sds(a.shape, jnp.float32) for a in (*params, *moments)]
    results = call(
        body,
        place,
        tuple(ins),
        [whole(a.shape) for a in ins],
        outs,
        [whole(a.shape) for a in outs],
        [],
        "statistics",
    )
    return (
        results[:amount],
        results[amount : 2 * amount],
        results[2 * amount],
        results[2 * amount + 1 : 2 * amount + 1 + vectors],
        results[2 * amount + 1 + vectors :],
    )


CLIP_ORDER = (8, 10, 4, 2)
SPLIT = {"out": 1, "qkv": 3}


def update(place, grads, new_rows, weights, cols_states, packs, group, extra=None, clips=None):
    amount = len(weights)
    vectors = 0 if extra is None else len(extra[0])

    def body(place_ref, *refs):
        refs = list(refs)

        def take(n):
            taken = refs[:n]
            del refs[:n]
            return taken

        grad_refs, row_refs, weight_refs, state_refs = [take(amount) for _ in range(4)]
        pack_refs = take(len(packs))
        pack_ref = sum([ref[...] for ref in pack_refs[1:]], pack_refs[0][...])
        if vectors:
            vector_grads, moment_refs, param_refs = [take(vectors) for _ in range(3)]
            (clips_ref,) = take(1)
        new_refs, col_refs = take(amount), take(amount)
        (clip_ref,) = take(1)
        param_outs = take(vectors)
        at_pack = 0
        if not vectors:
            clip_ref[...] = jnp.zeros(clip_ref.shape, jnp.float32)
        for number in range(amount):
            rows, cols = weights[number].shape
            rows_total = rows * group
            count = rows_total * cols
            new_cols = (
                0.5 * state_refs[number][...]
                + 0.5 * pack_ref[0:1, at_pack : at_pack + cols] / rows_total
            )
            col_refs[number][...] = new_cols
            by_rows = pack_ref[1:2, at_pack : at_pack + cols]
            at_pack += cols
            mean_rows = pack_ref[0:1, at_pack : at_pack + 1] / rows_total
            weight_total = pack_ref[1:2, at_pack : at_pack + 1]
            at_pack += LANES
            total = mean_rows * jnp.sum(by_rows / new_cols, axis=1, keepdims=True)
            clip = jnp.maximum(1.0, jnp.sqrt(total / count) / clip_level)
            step = step_rate * jnp.sqrt(weight_total / count) / clip
            if vectors:
                if number == 0:
                    found = [clips_ref[at : at + 1, :1] for at in range(len(MATRICES) - amount)]
                found.append(clip)
            else:
                clip_ref[number : number + 1, :] = jnp.broadcast_to(clip, (1, LANES))
            estimate = to_column(row_refs[number][...]) * (new_cols / mean_rows)
            new_refs[number][...] = weight_refs[number][...] - step * (
                grad_refs[number][...] * lax.rsqrt(estimate)
            )
        for number in range(vectors):
            count = extra[2][number].shape[1] * group
            total = pack_ref[0:1, at_pack : at_pack + 1]
            weight_total = pack_ref[1:2, at_pack : at_pack + 1]
            at_pack += LANES
            clip = jnp.maximum(1.0, jnp.sqrt(total / count) / clip_level)
            step = step_rate * jnp.sqrt(weight_total / count) / clip
            found.append(clip)
            direction = vector_grads[number][...] * lax.rsqrt(moment_refs[number][...])
            param_outs[number][...] = param_refs[number][...] - step * direction
        if vectors:
            lane = lax.broadcasted_iota(jnp.int32, (1, LANES), 1)
            row = jnp.zeros((1, LANES), jnp.float32)
            for value, number in zip(found, (*CLIP_ORDER, *VECTORS)):
                row = jnp.where(lane == number, value, row)
            clip_ref[...] = row[:, : len(found)]

    ins = [*grads, *new_rows, *weights, *cols_states, *packs]
    outs = [sds(a.shape, jnp.float32) for a in (*weights, *cols_states)]
    outs.append(sds((1, len(MATRICES) + vectors) if vectors else (8, LANES), jnp.float32))
    if vectors:
        ins += [*extra[0], *extra[1], *extra[2], clips]
        outs += [sds(a.shape, jnp.float32) for a in extra[2]]
    results = call(
        body,
        place,
        tuple(ins),
        [whole(a.shape) for a in ins],
        outs,
        [whole(a.shape) for a in outs],
        [],
        "update",
    )
    return (
        results[:amount],
        results[amount : 2 * amount],
        results[2 * amount],
        results[2 * amount + 1 :],
    )


def pack_terms(place, sums_mid, sums_in, sums_qkv, hidden_sums, down_sums, sizes):
    z_size = lax.axis_size("z")
    shards = 2 * z_size
    per_shard = sizes[6] // 2 // CHUNKS
    heads = sums_qkv[0].shape[1]

    def body(place_ref, mid_ref, in_ref, *refs):
        qkv_refs, refs = refs[:GROUPS], refs[GROUPS:]
        hidden_refs, (down_ref, out_ref) = refs[:CHUNKS], refs[CHUNKS:]
        core = place_ref[2]

        def put(slot, row):
            at, size = sum(sizes[:slot]), sizes[slot]
            for s in range(shards):
                out_ref[s : s + 1, at : at + size] = row[:, s * size : (s + 1) * size]

        put(0, in_ref[0:1, :])
        put(1, in_ref[1:2, :])
        zero = jnp.zeros((1, heads * GROUPS), jnp.float32)
        halves = []
        for slot in (0, 2):
            row = jnp.concatenate([ref[slot : slot + 1, :] for ref in qkv_refs], axis=1)
            halves += [select(core, row, zero), select(core, zero, row)]
        put(2, jnp.concatenate(halves, axis=1))
        put(3, mid_ref[2:3, :])
        put(4, mid_ref[0:1, :])
        put(5, mid_ref[1:2, :])
        put(7, down_ref[...])
        none = jnp.zeros((1, per_shard), jnp.float32)
        for s in range(shards):
            for j in range(CHUNKS):
                row = hidden_refs[j][:, s * per_shard : (s + 1) * per_shard]
                for c in range(2):
                    at = sum(sizes[:6]) + (c * CHUNKS + j) * per_shard
                    here = select(core, row, none) if c == 0 else select(core, none, row)
                    out_ref[s : s + 1, at : at + per_shard] = here

    ins = (sums_mid, sums_in, *sums_qkv, *hidden_sums, down_sums)
    shape = (shards, sum(sizes))
    return call(
        body,
        place,
        ins,
        [whole(a.shape) for a in ins],
        [sds(shape, jnp.float32)],
        [whole(shape)],
        [],
        "pack_terms",
    )[0]


def on_device(
    inputs,
    cotangent,
    norm1_gain,
    norm1_bias,
    qkv_weight,
    qv_bias,
    out_weight,
    out_bias,
    norm2_gain,
    norm2_bias,
    in_weight,
    in_bias,
    down_weight,
    down_bias,
    qkv_rows,
    qkv_cols,
    out_rows,
    out_cols,
    in_rows,
    in_cols,
    down_rows,
    down_cols,
    norm1_gain_moment,
    norm1_bias_moment,
    qv_bias_moment,
    out_bias_moment,
    norm2_gain_moment,
    norm2_bias_moment,
    in_bias_moment,
    down_bias_moment,
):
    masters = [
        norm1_gain,
        norm1_bias,
        qkv_weight,
        qv_bias,
        out_weight,
        out_bias,
        norm2_gain,
        norm2_bias,
        in_weight,
        in_bias,
        down_weight,
        down_bias,
    ]
    moments = [
        norm1_gain_moment,
        norm1_bias_moment,
        qv_bias_moment,
        out_bias_moment,
        norm2_gain_moment,
        norm2_bias_moment,
        in_bias_moment,
        down_bias_moment,
    ]
    place = jnp.stack([lax.axis_index(axis) for axis in ("z", "x", "c", "y")]).astype(jnp.int32)
    by_y = lax.axis_size("y") == 2
    group = lax.axis_size("z") * lax.axis_size("x")
    tokens = inputs.shape[0]
    part = in_weight.shape[0]
    images = (tokens // SEQ) * group * lax.axis_size("y") * lax.axis_size("c")
    as_row = lambda vector: vector.reshape(1, -1)
    params = [as_row(masters[number]) for number in VECTORS]
    moments = [as_row(moment) for moment in moments]
    sizes = [param.shape[1] for param in params]

    cut = 2 if by_y else 1
    shard_first, shard_next = prepare_qkv(place, qkv_weight, out_weight, params, cut)
    near = along_z(shard_first)
    pieces_first = by_x(near)
    near_next = along_z(after(shard_next, near))
    rows_own, parts = pad_rows(after(place, near), inputs)
    rows = (rows_own, [swap(one, "c") for one in parts])
    *shards_ff, down_sums = prepare_rest(
        after(place, rows_own), in_weight, down_weight, cotangent, (cut,) * 2
    )
    cot_own, parts = pad_rows(after(place, (down_sums, rows[1])), cotangent)
    near_ff = [along_z(shards_ff[0])]

    normed, *first, vectors, hidden_bias = project_first(
        after(place, (cot_own, near_next)), rows, pieces_first, sizes
    )
    near_ff.append(along_z(after(shards_ff[1], normed)))
    cot = (cot_own, [swap(one, "c") for one in after(parts, normed)])
    qkv = [first]
    across_next = after(swap(near_next, "x"), normed)
    pieces_next = by_y_too([[near_next], [across_next]], by_y)
    mixed, prob = attention(after(place, across_next), *first)
    attended = [mixed]
    probs = [prob]
    theirs = [swap(mixed, "c")]
    pieces_next = after(pieces_next, mixed)
    weight_mine = gather_out(place, pieces_next, 3 * first[0].shape[-1])
    weight_theirs = swap(weight_mine, "c")
    near_ff[0] = after(near_ff[0], pieces_next)
    across = swap(near_ff[0], "x")
    near_too = swap(near_ff[0], "y") if by_y else None
    qkv.append(
        project_next(
            after(place, (near_ff[0], weight_mine)), normed, vectors, pieces_next, 1
        )
    )
    mixed, prob = attention(place, *qkv[1])
    attended.append(mixed)
    probs.append(prob)
    theirs.append(swap(mixed, "c"))
    across = after(across, mixed)
    if by_y:
        pieces_ff = [[near_ff[0], near_too], [across, swap(across, "y")]]
    else:
        pieces_ff = [[near_ff[0]], [across]]
    near_ff[1] = after(near_ff[1], across)
    across_next = swap(near_ff[1], "x")
    near_first = near_too
    near_too = (near_too, swap(near_ff[1], "y")) if by_y else None
    middle, normed_mid = project_out(
        after(place, (near_ff[1], near_first)), attended, theirs, weight_mine, weight_theirs, rows, vectors
    )
    across_next = after(across_next, normed_mid)
    if by_y:
        pieces_ff = [
            [[near_ff[0], near_too[0]], pieces_ff[1]],
            [[near_ff[1], near_too[1]], [across_next, swap(across_next, "y")]],
        ]
    else:
        pieces_ff = [[[near_ff[0]], [across]], [[near_ff[1]], [across_next]]]
    *running, sums, keep_in, send_in, keep_down, send_down = feed_forward(
        after(place, across_next), normed_mid, cot, pieces_ff[0], hidden_bias, 0, None
    )
    terms_ff = [(keep_in, swap(send_in, "x"), keep_down, swap(send_down, "x"))]
    hidden_sums = [sums]
    *totals, sums, keep_in, send_in, keep_down, send_down = feed_forward(
        place, normed_mid, cot, pieces_ff[1], hidden_bias, 1, running
    )
    hidden_sums.append(sums)
    folded = [fold_pair(*after(terms_ff[0], sums))]
    terms_ff.append((keep_in, swap(send_in, "x"), keep_down, swap(send_down, "x")))
    scattered = [scatter_z(folded[0])]
    out_share, *out_given = totals[: 1 + GIVEN]
    normed_share, *normed_given = totals[1 + GIVEN :]
    sums_mid, output, grad_mid, grad_mid_low, *parts = norm_back(
        after(place, folded[0]),
        middle,
        vectors,
        GAIN_TWO,
        normed_share,
        [swap(one, "c") for one in normed_given],
        cot_own,
        tokens,
        (out_share, *[swap(one, "c") for one in out_given]),
    )
    *grad_attended, keep, send = out_back(
        place,
        grad_mid_low,
        [swap(one, "c") for one in parts],
        attended,
        theirs,
        weight_mine,
        weight_theirs,
    )
    got = swap(send, "x")
    grad_qkv = [attention_back(place, *qkv[0], probs[0], grad_attended[0])]
    sums_first, keep_first, send_first = qkv_term(place, normed, *grad_qkv[0])
    got_first = swap(send_first, "x")
    folded.append(fold_pair(*after(terms_ff[1], sums_first)))
    scattered.append(scatter_z(folded[1]))
    scattered[0] = after(scattered[0], folded[1])
    own_ff = [sum_y(scattered[0])]
    grad_qkv.append(
        attention_back(after(place, scattered[0]), *qkv[1], probs[1], grad_attended[1])
    )
    own_ff[0] = after(own_ff[0], grad_qkv[1][0])
    sums_next, keep_next, send_next = qkv_term(
        after(place, own_ff[0]), normed, *grad_qkv[1]
    )
    sums_qkv = [sums_first, sums_next]
    got_next = swap(send_next, "x")
    held = after(((keep, got), (keep_first, got_first)), sums_next)
    folded.append(jnp.concatenate([fold(*one) for one in held], axis=1))
    scattered.append(scatter_z(folded[2]))
    share, *given = qkv_back(after(place, folded[2]), grad_qkv, [pieces_first, pieces_next])
    pairs = [with_core(own_ff[0])]
    scattered[1] = after(scattered[1], share)
    own_ff.append(sum_y(scattered[1]))
    sums_in, input_grad = norm_back(
        after(place, scattered[1]),
        rows_own,
        vectors,
        GAIN_ONE,
        share,
        [swap(one, "c") for one in given],
        grad_mid,
        tokens,
    )
    packed = pack_terms(
        place, sums_mid, sums_in, sums_qkv, hidden_sums, down_sums, sizes
    )
    folded.append(fold(*after((keep_next, got_next), packed)))
    scattered.append(scatter_z(folded[3]))
    pairs.append(with_core(after(own_ff[1], folded[3])))
    terms = sum_over(packed, ("c", "z", "x", "y"))

    weights = [in_weight, down_weight]
    states = [as_row(state) for state in (in_rows, down_rows)]
    grads_early, rows_early, pack, _, _ = statistics(
        place,
        ("in", "down"),
        pairs[:CHUNKS],
        [[(j, row, 0) for j in range(CHUNKS)] for row in (0, part)],
        weights,
        states,
        images,
        group,
    )
    scattered[2] = after(scattered[2], rows_early[0])
    own_mid = after(sum_y(scattered[2]), terms)
    pairs.append(with_core(own_mid))
    pack = sum_over(pack, ("z",))
    pack = [pack, swap(pack, "x")]
    scattered[3] = after(scattered[3], (pack, pairs[-1]))
    pairs.append(sum_y_and_core(scattered[3]))
    new_early, cols_early, clips_early, _ = update(
        after(place, scattered[3]),
        grads_early,
        rows_early,
        weights,
        [as_row(state) for state in (in_cols, down_cols)],
        pack,
        group,
    )
    weights = [out_weight, qkv_weight]
    grads_late, rows_late, pack, vector_grads, new_moments = statistics(
        after(place, clips_early),
        ("out", "qkv"),
        pairs[CHUNKS:],
        [[(0, 0, 0)], [(0, 0, out_weight.shape[1] // 2), (1, 0, 0)]],
        weights,
        [as_row(state) for state in (out_rows, qkv_rows)],
        images,
        group,
        (terms, params, moments),
    )
    pack = sum_over(pack, ("z",))
    new_late, cols_late, clip_factors, new_vectors = update(
        place,
        grads_late,
        rows_late,
        weights,
        [as_row(state) for state in (out_cols, qkv_cols)],
        [pack, swap(pack, "x")],
        group,
        (vector_grads, new_moments, params),
        clips_early,
    )

    flat = lambda value: value.reshape(-1)
    grads = [None] * 12
    new_params = [None] * 12
    for number, slot in ((8, 0), (10, 1)):
        grads[number], new_params[number] = grads_early[slot], new_early[slot]
    for number, slot in ((4, 0), (2, 1)):
        grads[number], new_params[number] = grads_late[slot], new_late[slot]
    for slot, number in enumerate(VECTORS):
        grads[number] = flat(vector_grads[slot])
        new_params[number] = flat(new_vectors[slot])
    return (
        output,
        input_grad,
        *grads,
        flat(rows_late[1]),
        flat(cols_late[1]),
        flat(rows_late[0]),
        flat(cols_late[0]),
        flat(rows_early[0]),
        flat(cols_early[0]),
        flat(rows_early[1]),
        flat(cols_early[1]),
        *[flat(moment) for moment in new_moments],
        *new_params,
        flat(clip_factors),
    )


def solution(mesh):
    group = mesh.shape["fsdp"]
    split = Mesh(mesh.devices.reshape(group // 2, 2, mesh.shape["dp"] // 2, 2), ALL_AXES)
    in_specs = (
        P(("z", "x", "y", "c"), None),
        P(("z", "x", "y", "c"), None),
        P(("z", "x")),
        P(("z", "x")),
        P(("z", "x"), None),
        P(("z", "x")),
        P(("z", "x"), None),
        P(("z", "x")),
        P(("z", "x")),
        P(("z", "x")),
        P(("z", "x"), None),
        P(("z", "x")),
        P(("z", "x"), None),
        P(("z", "x")),
        P(("z", "x")),
        P(),
        P(("z", "x")),
        P(),
        P(("z", "x")),
        P(),
        P(("z", "x")),
        P(),
        P(("z", "x")),
        P(("z", "x")),
        P(("z", "x")),
        P(("z", "x")),
        P(("z", "x")),
        P(("z", "x")),
        P(("z", "x")),
        P(("z", "x")),
    )
    out_specs = (
        P(("z", "x", "y", "c"), None),
        P(("z", "x", "y", "c"), None),
        P(("z", "x")),
        P(("z", "x")),
        P(("z", "x"), None),
        P(("z", "x")),
        P(("z", "x"), None),
        P(("z", "x")),
        P(("z", "x")),
        P(("z", "x")),
        P(("z", "x"), None),
        P(("z", "x")),
        P(("z", "x"), None),
        P(("z", "x")),
        P(("z", "x")),
        P(),
        P(("z", "x")),
        P(),
        P(("z", "x")),
        P(),
        P(("z", "x")),
        P(),
        P(("z", "x")),
        P(("z", "x")),
        P(("z", "x")),
        P(("z", "x")),
        P(("z", "x")),
        P(("z", "x")),
        P(("z", "x")),
        P(("z", "x")),
        P(("z", "x")),
        P(("z", "x")),
        P(("z", "x"), None),
        P(("z", "x")),
        P(("z", "x"), None),
        P(("z", "x")),
        P(("z", "x")),
        P(("z", "x")),
        P(("z", "x"), None),
        P(("z", "x")),
        P(("z", "x"), None),
        P(("z", "x")),
        P(),
    )
    return jax.shard_map(
        on_device, mesh=split, in_specs=in_specs, out_specs=out_specs, check_vma=False
    )
```
